32 devices in a mesh: wide: 4 (over z), narrow: 4 (over x, core), mlp: 2 (over y).
Axes of the slice: x: 2, y: 2, z: 4, core: 2. Of those that a mesh axis runs over, the one named last changes fastest.
Arguments:
- tokens: bfloat16 [8192, 1152], P(('wide', 'narrow')), may hold values from -6 to 6
- timesteps: int32 [32], P(('wide', 'narrow')), may hold values from 200 to 799
- owners: int32 [16], replicated, may hold values from 0 to 15, each once
- rel_index: int32 [256, 256], replicated, may hold values from 0 to 960
- cotangent: bfloat16 [8192, 1152], P(('wide', 'narrow', 'mlp')), may hold values from -6 to 6
- att_master: float32 [1152, 14976], P(('wide', 'narrow')), may hold values from -1 to 1
- att_moment: float32 [1152, 14976], P(('wide', 'narrow')), may hold values from -0.00012207031 to 0.00012207031
- att_second: float32 [1152, 14976], P(('wide', 'narrow')), may hold values from 3.584437e-11 to 1.4337748e-10
- mlp_master: float32 [1152, 2, 4608], P(('wide', 'narrow'), None, 'mlp'), may hold values from -1 to 1
- mlp_moment: float32 [1152, 2, 4608], P(('wide', 'narrow'), None, 'mlp'), may hold values from -0.00012207031 to 0.00012207031
- mlp_second: float32 [1152, 2, 4608], P(('wide', 'narrow'), None, 'mlp'), may hold values from 3.584437e-11 to 1.4337748e-10
- small_master: float32 [24592], replicated, may hold values from -0.6 to 0.6
- small_moment: float32 [24592], replicated, may hold values from -0.00012207031 to 0.00012207031
- small_second: float32 [24592], replicated, may hold values from 3.584437e-11 to 1.4337748e-10
- bias_master: float32 [4608], P('mlp'), may hold values from -0.5 to 0.5
- bias_moment: float32 [4608], P('mlp'), may hold values from -5.340576e-05 to 5.340576e-05
- bias_second: float32 [4608], P('mlp'), may hold values from 5.3766557e-12 to 2.1506623e-11
Outputs:
- output: bfloat16 [8192, 1152], P(('wide', 'narrow', 'mlp'))
- input_grad: float32 [8192, 1152], P(('wide', 'narrow'))
- att_new: float32 [1152, 14976], P(('wide', 'narrow'))
- att_moment_new: float32 [1152, 14976], P(('wide', 'narrow'))
- att_second_new: float32 [1152, 14976], P(('wide', 'narrow'))
- mlp_new: float32 [1152, 2, 4608], P(('wide', 'narrow'), None, 'mlp')
- mlp_moment_new: float32 [1152, 2, 4608], P(('wide', 'narrow'), None, 'mlp')
- mlp_second_new: float32 [1152, 2, 4608], P(('wide', 'narrow'), None, 'mlp')
- small_new: float32 [24592], replicated
- small_moment_new: float32 [24592], replicated
- small_second_new: float32 [24592], replicated
- bias_new: float32 [4608], P('mlp')
- bias_moment_new: float32 [4608], P('mlp')
- bias_second_new: float32 [4608], P('mlp')
- att_copy: bfloat16 [1152, 14976], P(('wide', 'narrow'))
- mlp_copy: bfloat16 [1152, 2, 4608], P(('wide', 'narrow'), None, 'mlp')
- grad_norm: float32 [], replicated
The draws below stay inside these ranges and needn't reach their ends.
Inputs may be any that keep to these rules, and one draw needn't show every extreme that they name: `owners`: each owner number appears once.
All inputs are finite; a program needn't handle non-finite values.
Results may differ from the reference program's by a relative error of at most 0.017.
The reference program's roundings to bfloat16 on the way count: a program that leaves them out, or rounds other values in their place, can miss the bound.
Values may be sent and summed in bfloat16 or wider, within the bound.
A program may use at most 768 MiB of HBM per device.

```python
import math
import jax
import jax.numpy as jnp
from jax import lax

D = 1152
HEADS = 16
HD = 72
FF = 4608
SEQ = 256
NREL = 961
STEP = 10
IMG_DEV = 2
IMAGES = 32
TOKENS = 8192
NSMALL = 24592
NPARAMS = 27898384
N_WIDE = 4
N_NARROW = 4


def draw_att_master(key, part):
    values = jax.random.truncated_normal(key, -4.0, 4.0, (D, 13 * D), jnp.float32)
    column = jnp.arange(13 * D)
    factor = jnp.where(column < 6 * D, 1.0, 2.0) * D ** (-0.5)
    return values * factor[None, :]


def draw_mlp_master(key, part):
    key_main = jax.random.fold_in(key, 11)
    key_column = jax.random.fold_in(key, 23)
    values = jax.random.truncated_normal(key_main, -4.0, 4.0, (D, 2, FF), jnp.float32)
    factor = jnp.array([D ** (-0.5), FF ** (-0.5)], jnp.float32)
    column_part = jax.random.truncated_normal(key_column, -4.0, 4.0, (FF,), jnp.float32) * (0.7 * D ** (-0.5))
    which = jnp.array([1.0, 0.0], jnp.float32)
    return values * factor[None, :, None] + column_part[None, None, :] * which[None, :, None]


def draw_small_master(key, part):
    values = jax.random.truncated_normal(key, -4.0, 4.0, (NSMALL,), jnp.float32)
    position = jnp.arange(NSMALL)
    factor = jnp.where(position < NREL * HEADS, 0.15, 0.05)
    return values * factor


def set_ends(drawn, own_key, least, top_value):
    dims = drawn.shape
    place = [jax.random.randint(jax.random.fold_in(own_key, axis), (), 0, dims[axis]) for axis in range(len(dims))]
    drawn = drawn.at[tuple(place)].set(least)
    longest = dims.index(max(dims))
    place[longest] = (place[longest] + 1) % dims[longest]
    return drawn.at[tuple(place)].set(top_value)


def shard_levels(key, shape, pieces, smallest, top_value):
    def one(axis_at, parts):
        heights = jax.random.uniform(jax.random.fold_in(jax.random.fold_in(key, 6), axis_at), (parts,), jnp.float32, smallest / len(pieces), top_value / len(pieces))
        return jnp.repeat(jnp.exp(heights), shape[axis_at] // parts).reshape((-1,) + (1,) * (len(shape) - axis_at - 1))

    gain = one(*pieces[0])
    for cut in pieces[1:]:
        gain = gain * one(*cut)
    return gain


def scatter_about(key, shape, scale, bound, split=(), dtype=jnp.bfloat16):
    values = jax.random.normal(key, shape, jnp.float32) * scale
    if len(split) > 0:
        values = shard_levels(key, shape, split, -0.22, 0.18) * values
    return jnp.clip(values, min=-bound, max=bound).astype(dtype)


def setup_inputs(seed: int = 0) -> dict:
    splits = jax.random.split(jax.random.key(seed), 18)
    return {
        "tokens": scatter_about(splits[0], (TOKENS, D), 1.0, 6.0, ((0, 16),)),
        "timesteps": set_ends(jax.random.randint(splits[1], (IMAGES,), 200, 800), jax.random.fold_in(splits[1], 1), 200, 799).astype(jnp.int32),
        "owners": jax.random.permutation(splits[2], N_WIDE * N_NARROW).astype(jnp.int32),
        "rel_index": set_ends(jax.random.randint(splits[3], (SEQ, SEQ), 0, NREL), jax.random.fold_in(splits[3], 1), 0, NREL - 1).astype(jnp.int32),
        "cotangent": scatter_about(splits[4], (TOKENS, D), 1.0, 6.0, ((0, 32),)),
        "att_master": draw_att_master(jax.random.fold_in(splits[17], 71), 0),
        "att_moment": scatter_about(splits[6], (D, 13 * D), (0.111 * NPARAMS ** -0.5), 0.00012207031, ((0, 16),), jnp.float32),
        "att_second": jnp.clip(jnp.exp(math.log(1.4337747655801536e-10) - 1.3862944 * jax.random.uniform(splits[7], (D, 13 * D), jnp.float32) ** shard_levels(splits[7], (D, 13 * D), ((0, 16),), -0.2, 0.2)), 3.584436913950384e-11, 1.4337747655801536e-10),
        "mlp_master": draw_mlp_master(jax.random.fold_in(splits[17], 71), 0),
        "mlp_moment": scatter_about(splits[9], (D, 2, FF), (0.111 * NPARAMS ** -0.5), 0.00012207031, ((0, 16), (2, 2)), jnp.float32),
        "mlp_second": jnp.clip(jnp.exp(math.log(1.4337747655801536e-10) - 1.3862944 * jax.random.uniform(splits[10], (D, 2, FF), jnp.float32) ** shard_levels(splits[10], (D, 2, FF), ((0, 16), (2, 2)), -0.2, 0.2)), 3.584436913950384e-11, 1.4337747655801536e-10),
        "small_master": draw_small_master(jax.random.fold_in(splits[17], 71), 0),
        "small_moment": scatter_about(splits[12], (NSMALL,), (0.111 * NPARAMS ** -0.5), 0.00012207031, (), jnp.float32),
        "small_second": jnp.clip(jnp.exp(jax.random.uniform(splits[13], (NSMALL,), jnp.float32, math.log(3.584436913950384e-11), math.log(1.4337747655801536e-10))), 3.584436913950384e-11, 1.4337747655801536e-10),
        "bias_master": scatter_about(splits[14], (FF,), 0.08, 0.5, ((0, 2),), jnp.float32),
        "bias_moment": scatter_about(splits[15], (FF,), (0.045 * NPARAMS ** -0.5), 5.340576171875e-05, ((0, 2),), jnp.float32),
        "bias_second": jnp.clip(jnp.exp(math.log(2.1506622871481085e-11) - 1.3862944 * jax.random.uniform(splits[16], (FF,), jnp.float32) ** shard_levels(splits[16], (FF,), ((0, 2),), -0.2, 0.2)), 5.376655717870271e-12, 2.1506622871481085e-11),
    }


HIGH = lax.Precision.HIGHEST

@jax.custom_vjp
def low(v):
    return lax.optimization_barrier(v.astype(jnp.bfloat16)).astype(jnp.float32)

@jax.custom_vjp
def low_back(v):
    return v

def low_keep(v):
    return (low(v), None)

def low_pass(kept, grad):
    return (grad,)

def back_keep(v):
    return (v, None)

def back_low(kept, grad):
    return (low(grad),)
low.defvjp(low_keep, low_pass)
low_back.defvjp(back_keep, back_low)

def both_ways(values):
    return low_back(low(values))

def layer_norm(values):
    center = values - lax.optimization_barrier(jnp.mean(values, axis=-1, keepdims=True))
    spread = lax.optimization_barrier(jnp.mean(center * center, axis=-1, keepdims=True))
    return center * lax.rsqrt(spread + 1e-06)

def time_embed(steps_int):
    half_dim = D // 2
    frequency = jnp.exp(-math.log(10000.0) * jnp.arange(half_dim).astype(jnp.float32) / half_dim)
    angles = steps_int.astype(jnp.float32)[:, None] * frequency[None, :]
    return jnp.concatenate([jnp.cos(angles), jnp.sin(angles)], axis=1)

def forward(params, tokens_f, steps_int, rel_index):
    att_w, mlp_w, small_p, bias_one = params
    images = steps_int.shape[0]
    time_emb = time_embed(steps_int)
    w_space = att_w[:, 0:3 * D]
    w_time = att_w[:, 3 * D:6 * D]
    w_out = att_w[:, 6 * D:7 * D]
    w_ada = att_w[:, 7 * D:13 * D]
    w_one = mlp_w[:, 0, :]
    w_two = mlp_w[:, 1, :]
    offset = NREL * HEADS
    rel_table = small_p[0:offset].reshape(NREL, HEADS)
    b_ada = small_p[offset:offset + 6 * D]
    b_out = small_p[offset + 6 * D:offset + 7 * D]
    b_two = small_p[offset + 7 * D:offset + 8 * D]
    silu_low = low(jax.nn.silu(time_emb))
    emb_low = low(time_emb)
    modulation = (jnp.dot(silu_low, w_ada, precision=HIGH) + b_ada).reshape(images, 1, 6, D)
    shift_one, scale_one, gate_one = (modulation[:, :, 0], modulation[:, :, 1], modulation[:, :, 2])
    shift_two, scale_two, gate_two = (modulation[:, :, 3], modulation[:, :, 4], modulation[:, :, 5])
    residual = tokens_f.reshape(images, SEQ, D)
    normed = layer_norm(residual)
    shaped = low(normed * (1.0 + scale_one) + shift_one)
    time_part = jnp.dot(emb_low, w_time, precision=HIGH)
    qkv_all = jnp.dot(shaped.reshape(images * SEQ, D), w_space, precision=HIGH).reshape(images, SEQ, 3 * D)
    qkv_all = both_ways(qkv_all + time_part[:, None, :])
    rel_bias = jnp.transpose(rel_table[rel_index], (2, 0, 1))
    inv_root = 1.0 / math.sqrt(HD)

    def attend(block_qkv):
        per_head = block_qkv.reshape(SEQ, 3, HEADS, HD)
        query_h, key_h, value_h = (per_head[:, 0], per_head[:, 1], per_head[:, 2])
        scores = jnp.einsum('qhd,khd->hqk', query_h, key_h, precision=HIGH) * inv_root + rel_bias
        scores = low_back(scores)
        attn_p = low(jax.nn.softmax(scores, axis=-1))
        return jnp.einsum('hqk,khd->qhd', attn_p, value_h, precision=HIGH).reshape(SEQ, D)
    attended = both_ways(lax.map(jax.checkpoint(attend), qkv_all))
    attn_out = low_back(jnp.dot(attended.reshape(images * SEQ, D), w_out, precision=HIGH) + b_out)
    resid_mid = residual + gate_one * attn_out.reshape(images, SEQ, D)
    normed_two = layer_norm(resid_mid)
    shaped_two = low(normed_two * (1.0 + scale_two) + shift_two).reshape(images * SEQ, D)
    hidden_pre = low_back(jnp.dot(shaped_two, w_one, precision=HIGH) + bias_one)
    hidden = low(jax.nn.gelu(hidden_pre, approximate=True))
    branch = low_back(lax.dot_general(hidden, w_two, (((1,), (1,)), ((), ())), precision=HIGH) + b_two)
    return (resid_mid + gate_two * branch.reshape(images, SEQ, D)).reshape(images * SEQ, D)

def adam_update(weight, moment, second, grad, clip_scale):
    scaled = grad * clip_scale
    moment_new = 0.9 * moment + 0.1 * scaled
    second_new = 0.999 * second + 0.001 * scaled * scaled
    rate = 1.5 / math.sqrt(D)
    direction = moment_new / (1.0 - 0.9 ** STEP) / (jnp.sqrt(second_new / (1.0 - 0.999 ** STEP)) + 1e-08)
    return (weight - rate * (direction + 0.1 * weight), moment_new, second_new)

def reference(tokens, timesteps, owners, rel_index, cotangent, att_master, att_moment, att_second, mlp_master, mlp_moment, mlp_second, small_master, small_moment, small_second, bias_master, bias_moment, bias_second):
    groups = N_WIDE * N_NARROW
    rows_blk = D // groups
    att_w = low(att_master.reshape(groups, rows_blk, 13 * D)[owners].reshape(D, 13 * D))
    mlp_w = low(mlp_master.reshape(groups, rows_blk, 2, FF)[owners].reshape(D, 2, FF))
    params = (att_w, mlp_w, small_master, bias_master)
    tok_f = tokens.astype(jnp.float32).reshape(groups, IMG_DEV * SEQ, D)
    cot_f = cotangent.astype(jnp.float32).reshape(groups, IMG_DEV * SEQ, D)
    step_grp = timesteps.reshape(groups, IMG_DEV)

    def one_group(grad_total, inputs):
        tok_g, step_g, cot_g = inputs

        def run_group(params_in, tok_in):
            return forward(params_in, tok_in, step_g, rel_index)
        result, pull_back = jax.vjp(run_group, params, tok_g)
        grads_g, tok_grad = pull_back(cot_g)
        grad_total = jax.tree.map(lambda acc_val, new_val: acc_val + new_val, grad_total, grads_g)
        return (grad_total, (result, tok_grad))
    zero_tree = jax.tree.map(jnp.zeros_like, params)
    grad_total, (result, tok_grad) = lax.scan(one_group, zero_tree, (tok_f, step_grp, cot_f))
    att_grad = jnp.zeros((groups, rows_blk, 13 * D), jnp.float32).at[owners].set(grad_total[0].reshape(groups, rows_blk, 13 * D)).reshape(D, 13 * D)
    mlp_grad = jnp.zeros((groups, rows_blk, 2, FF), jnp.float32).at[owners].set(grad_total[1].reshape(groups, rows_blk, 2, FF)).reshape(D, 2, FF)
    small_grad = grad_total[2]
    bias_grad = grad_total[3]
    grad_norm = jnp.sqrt(jnp.sum(att_grad * att_grad) + jnp.sum(mlp_grad * mlp_grad) + jnp.sum(small_grad * small_grad) + jnp.sum(bias_grad * bias_grad))
    clip_scale = jnp.minimum(1.0, 1.0 / (grad_norm + 1e-06))
    att_new, att_mom_new, att_sec_new = adam_update(att_master, att_moment, att_second, att_grad, clip_scale)
    mlp_new, mlp_mom_new, mlp_sec_new = adam_update(mlp_master, mlp_moment, mlp_second, mlp_grad, clip_scale)
    small_new, small_mom_new, small_sec_new = adam_update(small_master, small_moment, small_second, small_grad, clip_scale)
    bias_new, bias_mom_new, bias_sec_new = adam_update(bias_master, bias_moment, bias_second, bias_grad, clip_scale)
    output = result.reshape(TOKENS, D).astype(jnp.bfloat16)
    input_grad = tok_grad.reshape(TOKENS, D)
    return (output, input_grad, att_new, att_mom_new, att_sec_new, mlp_new, mlp_mom_new, mlp_sec_new, small_new, small_mom_new, small_sec_new, bias_new, bias_mom_new, bias_sec_new, att_new.astype(jnp.bfloat16), mlp_new.astype(jnp.bfloat16), grad_norm)
```

```python
from functools import partial
import math

import jax
import jax.numpy as jnp
from jax import lax
from jax.experimental import pallas as pl
from jax.experimental.pallas import tpu as pltpu
from jax.sharding import PartitionSpec as P

D = 1152
HEADS = 16
HD = 72
NREL = 961
STEP = 10

HIGH = lax.Precision.HIGHEST
F32 = jnp.float32
BF16 = jnp.bfloat16
GRID = ("wide", "narrow")
NN = (((1,), (0,)), ((), ()))
TN = (((0,), (0,)), ((), ()))
NT = (((1,), (1,)), ((), ()))
INV_ROOT = 1.0 / math.sqrt(HD)


def mm(a, b, dims=NN):
    return lax.dot_general(a, b, dims, preferred_element_type=F32)


def mm_exact(a, b, dims=NN):
    return lax.dot_general(a, b, dims, precision=HIGH, preferred_element_type=F32)


def norm_stats(values):
    center = values - jnp.mean(values, axis=-1, keepdims=True)
    inv_std = lax.rsqrt(jnp.mean(center * center, axis=-1, keepdims=True) + 1e-06)
    return (center * inv_std, inv_std)


def norm_back(grad_normed, normed, inv_std):
    mean_grad = jnp.mean(grad_normed, axis=-1, keepdims=True)
    mean_proj = jnp.mean(grad_normed * normed, axis=-1, keepdims=True)
    return (grad_normed - mean_grad - normed * mean_proj) * inv_std


def adam_update(weight, moment, second, grad, clip_scale):
    scaled = grad * clip_scale
    moment_new = 0.9 * moment + 0.1 * scaled
    second_new = 0.999 * second + 0.001 * scaled * scaled
    rate = 1.5 / math.sqrt(D)
    direction = (
        moment_new / (1.0 - 0.9**STEP) / (jnp.sqrt(second_new / (1.0 - 0.999**STEP)) + 1e-08)
    )
    return (weight - rate * (direction + 0.1 * weight), moment_new, second_new)


def attend_fwd_body(seq, images, qkv_ref, index_ref, table_ref, out_ref, bias_ref, lse_ref):
    low = jnp.bitwise_and(index_ref[...], 127)
    high = jnp.right_shift(index_ref[...], 7)
    cols = []
    for part in range(seq // 128):
        lo = low[:, part * 128 : (part + 1) * 128]
        hi = high[:, part * 128 : (part + 1) * 128]
        total = jnp.zeros(lo.shape, F32)
        for chunk in range(8):
            row = jnp.broadcast_to(table_ref[0, :, chunk * 128 : (chunk + 1) * 128], lo.shape)
            total = jnp.where(hi == chunk, jnp.take_along_axis(row, lo, axis=1), total)
        cols.append(total)
    bias = jnp.concatenate(cols, axis=1)
    bias_ref[0] = bias
    for n in range(images):
        at = pl.ds(n * seq, seq)
        scores = mm(qkv_ref[1, 0, :, at], qkv_ref[0, 0, :, at], TN) * INV_ROOT + bias
        top = jnp.max(scores, axis=0, keepdims=True)
        weights = jnp.exp(scores - top)
        total = jnp.sum(weights, axis=0, keepdims=True)
        probs = (weights / total).astype(BF16)
        out_ref[0, :, at] = mm(qkv_ref[2, 0, :, at], probs).astype(BF16)
        lse_ref[0, :, at] = top + jnp.log(total)


def attend_fwd(qkv, index_t, table_t, seq, images):
    rows = seq * images
    return pl.pallas_call(
        partial(attend_fwd_body, seq, images),
        grid=(HEADS,),
        in_specs=[
            pl.BlockSpec((3, 1, HD, rows), lambda h: (0, h, 0, 0)),
            pl.BlockSpec((seq, seq), lambda h: (0, 0)),
            pl.BlockSpec((1, 1, 1024), lambda h: (h, 0, 0)),
        ],
        out_specs=[
            pl.BlockSpec((1, HD, rows), lambda h: (h, 0, 0)),
            pl.BlockSpec((1, seq, seq), lambda h: (h, 0, 0)),
            pl.BlockSpec((1, 1, rows), lambda h: (h, 0, 0)),
        ],
        out_shape=[
            jax.ShapeDtypeStruct((HEADS, HD, rows), BF16),
            jax.ShapeDtypeStruct((HEADS, seq, seq), F32),
            jax.ShapeDtypeStruct((HEADS, 1, rows), F32),
        ],
        name="attend_fwd",
    )(qkv, index_t, table_t)


def attend_bwd_body(seq, images, qkv_ref, grad_ref, bias_ref, lse_ref, out_ref, ds_ref):
    bias = bias_ref[0]
    for n in range(images):
        at = pl.ds(n * seq, seq)
        query, key, value = (qkv_ref[0, 0, :, at], qkv_ref[1, 0, :, at], qkv_ref[2, 0, :, at])
        grad = grad_ref[0, :, at]
        probs = jnp.exp(mm(key, query, TN) * INV_ROOT + bias - lse_ref[0, :, at])
        grad_probs = mm(value, grad, TN)
        inner = jnp.sum(probs * grad_probs, axis=0, keepdims=True)
        ds = (probs * (grad_probs - inner)).astype(BF16)
        out_ref[0, 0, :, at] = (mm(key, ds) * INV_ROOT).astype(BF16)
        out_ref[1, 0, :, at] = (mm(query, ds, NT) * INV_ROOT).astype(BF16)
        out_ref[2, 0, :, at] = mm(grad, probs.astype(BF16), NT).astype(BF16)
        ds_ref[0, :, at] = ds.astype(F32)


def attend_bwd(qkv, grad, bias, lse, seq, images):
    rows = seq * images
    return pl.pallas_call(
        partial(attend_bwd_body, seq, images),
        grid=(HEADS,),
        in_specs=[
            pl.BlockSpec((3, 1, HD, rows), lambda h: (0, h, 0, 0)),
            pl.BlockSpec((1, HD, rows), lambda h: (h, 0, 0)),
            pl.BlockSpec((1, seq, seq), lambda h: (h, 0, 0)),
            pl.BlockSpec((1, 1, rows), lambda h: (h, 0, 0)),
        ],
        out_specs=[
            pl.BlockSpec((3, 1, HD, rows), lambda h: (0, h, 0, 0)),
            pl.BlockSpec((1, seq, rows), lambda h: (h, 0, 0)),
        ],
        out_shape=[
            jax.ShapeDtypeStruct((3, HEADS, HD, rows), BF16),
            jax.ShapeDtypeStruct((HEADS, seq, rows), F32),
        ],
        name="attend_bwd",
    )(qkv, grad, bias, lse)


def rel_grad_body(seq, images, step, ds_ref, index_ref, out_ref):
    @pl.when(pl.program_id(0) == 0)
    def _():
        out_ref[...] = jnp.zeros_like(out_ref)

    bucket = lax.broadcasted_iota(jnp.int32, (256, seq), 0)
    for j in range(step):
        index = index_ref[j : j + 1, :]
        low = jnp.bitwise_and(index, 255)
        high = jnp.right_shift(index, 8)
        hot = jnp.where(bucket == low, 1.0, 0.0).astype(BF16)
        total = ds_ref[:, j, :]
        picked = []
        for n in range(images):
            for a in range(4):
                picked.append(jnp.where(high == a, total[:, n * seq : (n + 1) * seq], 0.0))
        sums = mm(jnp.concatenate(picked, axis=0).astype(BF16), hot, NT)
        for n in range(images):
            out_ref[...] += sums[n * 4 * HEADS : (n + 1) * 4 * HEADS]


def rel_grad_sum(ds, index_t, seq, images):
    rows = seq * images
    step = 8
    return pl.pallas_call(
        partial(rel_grad_body, seq, images, step),
        grid=(seq // step,),
        in_specs=[
            pl.BlockSpec((HEADS, step, rows), lambda j: (0, j, 0)),
            pl.BlockSpec((step, seq), lambda j: (j, 0)),
        ],
        out_specs=pl.BlockSpec((4 * HEADS, 256), lambda j: (0, 0)),
        out_shape=jax.ShapeDtypeStruct((4 * HEADS, 256), F32),
        name="rel_grad",
    )(ds, index_t)


def on_device(
    tokens,
    timesteps,
    owners,
    rel_index,
    cotangent,
    att_master,
    att_moment,
    att_second,
    mlp_master,
    mlp_moment,
    mlp_second,
    small_master,
    small_moment,
    small_second,
    bias_master,
    bias_moment,
    bias_second,
):
    groups = owners.shape[0]
    rows_blk = att_master.shape[0]
    half_ff = mlp_master.shape[2]
    images = timesteps.shape[0]
    tok_rows = tokens.shape[0]
    half_rows = cotangent.shape[0]
    seq_len = tok_rows // images
    mlp_count = lax.axis_size("mlp")
    mlp_at = lax.axis_index("mlp")
    mine = lax.axis_index(GRID)

    place = (owners[:, None] * rows_blk + jnp.arange(rows_blk)[None, :]).reshape(D)
    perm = (place[:, None] == jnp.arange(D)[None, :]).astype(BF16)
    perm_f = perm.astype(F32)
    my_block = jnp.sum(jnp.where(owners == mine, jnp.arange(groups), 0))

    space_all = lax.all_gather(att_master[:, 0 : 3 * D].astype(BF16), GRID, axis=0, tiled=True)
    out_all = lax.all_gather(att_master[:, 6 * D : 7 * D].astype(BF16), GRID, axis=0, tiled=True)
    one_all = lax.all_gather(mlp_master[:, 0].astype(BF16), GRID, axis=0, tiled=True)
    two_all = lax.all_gather(mlp_master[:, 1].astype(BF16), GRID, axis=0, tiled=True)

    all_steps = lax.all_gather(timesteps, GRID, axis=0, tiled=True)
    half_dim = D // 2
    feature = my_block * rows_blk + jnp.arange(rows_blk)
    slot = jnp.where(feature < half_dim, feature, feature - half_dim)
    frequency = jnp.exp(-math.log(10000.0) * slot.astype(F32) / half_dim)
    angles = all_steps.astype(F32)[:, None] * frequency[None, :]
    time_emb = jnp.where(feature[None, :] < half_dim, jnp.cos(angles), jnp.sin(angles))
    silu_low = jax.nn.silu(time_emb).astype(BF16)
    emb_low = time_emb.astype(BF16)
    parts = jnp.concatenate(
        [
            mm(emb_low, att_master[:, 3 * D : 6 * D].astype(BF16)),
            mm(silu_low, att_master[:, 7 * D : 13 * D].astype(BF16)),
        ],
        axis=1,
    )
    summed = lax.psum_scatter(parts, GRID, scatter_dimension=0, tiled=True)
    time_part = summed[:, 0 : 3 * D]

    offset = NREL * HEADS
    table_t = jnp.pad(small_master[0:offset].reshape(NREL, HEADS).T, ((0, 0), (0, 1024 - NREL)))
    b_ada = small_master[offset : offset + 6 * D]
    b_rest = small_master[offset + 6 * D : offset + 8 * D].reshape(2, D)
    modulation = (summed[:, 3 * D :] + b_ada).reshape(images * 6, D)
    moved = mm_exact(jnp.concatenate([modulation, b_rest], axis=0), perm_f)
    modulation = moved[0 : images * 6].reshape(images, 6, 1, D)
    b_out, b_two = (moved[images * 6], moved[images * 6 + 1])
    shift_one, scale_one, gate_one = (modulation[:, 0], modulation[:, 1], modulation[:, 2])
    shift_two, scale_two, gate_two = (modulation[:, 3], modulation[:, 4], modulation[:, 5])

    residual = mm(tokens, perm).reshape(images, seq_len, D)
    normed, inv_one = norm_stats(residual)
    shaped = (normed * (1.0 + scale_one) + shift_one).astype(BF16).reshape(tok_rows, D)
    time_tok = jnp.repeat(time_part.T, seq_len, axis=1)
    qkv = (
        (lax.dot_general(space_all, shaped, (((0,), (1,)), ((), ())), preferred_element_type=F32) + time_tok)
        .astype(BF16)
        .reshape(3, HEADS, HD, tok_rows)
    )
    index_t = rel_index.T
    attended, bias, lse = attend_fwd(
        qkv, index_t, table_t.reshape(HEADS, 1, 1024), seq_len, images
    )
    attended = mm(perm, attended.reshape(D, tok_rows), TN).astype(BF16)
    w_out = mm(out_all, perm).astype(BF16)
    attn_out = (mm(attended, w_out, TN) + b_out).reshape(images, seq_len, D)
    resid_mid = residual + gate_one * attn_out

    normed_two, inv_two = norm_stats(resid_mid)
    shaped_two = (normed_two * (1.0 + scale_two) + shift_two).astype(BF16).reshape(tok_rows, D)
    hidden_pre = mm(shaped_two, one_all) + bias_master
    hidden_full, gelu_pull = jax.vjp(partial(jax.nn.gelu, approximate=True), hidden_pre)
    hidden_low = hidden_full.astype(BF16)
    branch = (
        lax.psum_scatter(mm(hidden_low, two_all, NT), "mlp", scatter_dimension=0, tiled=True)
        + b_two
    )
    first_row = mlp_at * half_rows
    image_of = (jnp.arange(half_rows) + first_row) // seq_len
    image_pick = (image_of[:, None] == jnp.arange(images)[None, :]).astype(F32)
    mid_half = lax.dynamic_slice_in_dim(resid_mid.reshape(tok_rows, D), first_row, half_rows, 0)
    gate_tok = jnp.broadcast_to(gate_two, (images, seq_len, D)).reshape(tok_rows, D)
    gate_half = lax.dynamic_slice_in_dim(gate_tok, first_row, half_rows, 0)
    output = mm((mid_half + gate_half * branch).astype(BF16), perm, NT).astype(BF16)
    cot_all = lax.all_gather(cotangent, "mlp", axis=0, tiled=True)
    cot_all = mm(cot_all, perm)
    cot_half = lax.dynamic_slice_in_dim(cot_all, first_row, half_rows, 0)
    gate_grad_part = mm_exact(image_pick, cot_half * branch, TN)
    grad_branch = (cot_all * gate_tok).astype(BF16)
    b_two_grad = jnp.sum(grad_branch.astype(F32), axis=0)
    grad_hidden = mm(grad_branch, two_all)
    grad_pre = gelu_pull(grad_hidden)[0].astype(BF16)
    b_one_grad = jnp.sum(grad_pre.astype(F32), axis=0)
    grad_one = mm(shaped_two, grad_pre, TN).astype(BF16)
    grad_two = mm(grad_branch, hidden_low, TN).astype(BF16)
    grad_shaped_two, gate_two_grad = lax.psum((mm(grad_pre, one_all, NT), gate_grad_part), "mlp")
    mlp_grad = lax.psum_scatter(
        jnp.concatenate([grad_one, grad_two], axis=1), GRID, scatter_dimension=0, tiled=True
    )
    grad_shaped_two = grad_shaped_two.reshape(images, seq_len, D)
    scale_two_grad = jnp.sum(grad_shaped_two * normed_two, axis=1)
    shift_two_grad = jnp.sum(grad_shaped_two, axis=1)
    grad_mid = cot_all.reshape(images, seq_len, D) + norm_back(
        grad_shaped_two * (1.0 + scale_two), normed_two, inv_two
    )

    grad_attn = (grad_mid * gate_one).astype(BF16).reshape(tok_rows, D)
    gate_one_grad = jnp.sum(grad_mid * attn_out, axis=1)
    b_out_grad = jnp.sum(grad_attn.astype(F32), axis=0)
    grad_out = mm(attended, grad_attn)
    grad_attended = mm(w_out, grad_attn, NT).astype(BF16)
    grad_attended = mm(perm, grad_attended).astype(BF16)
    grad_qkv, ds = attend_bwd(
        qkv, grad_attended.reshape(HEADS, HD, tok_rows), bias, lse, seq_len, images
    )
    rel_sum = rel_grad_sum(ds, index_t, seq_len, images)
    grad_qkv = grad_qkv.reshape(3 * D, tok_rows)
    rel_grad = (
        rel_sum.reshape(4, HEADS, 256).transpose(0, 2, 1).reshape(1024, HEADS)[0:NREL].reshape(-1)
    )
    time_grad = jnp.sum(grad_qkv.astype(F32).reshape(3 * D, images, seq_len), axis=2).T
    grad_space = lax.dot_general(
        shaped, grad_qkv, (((0,), (1,)), ((), ())), preferred_element_type=F32
    )
    att_part = lax.psum_scatter(
        jnp.concatenate([grad_space.astype(BF16), grad_out.astype(BF16)], axis=1),
        GRID,
        scatter_dimension=0,
        tiled=True,
    )
    grad_shaped = lax.dot_general(
        grad_qkv, space_all, (((0,), (1,)), ((), ())), preferred_element_type=F32
    ).reshape(images, seq_len, D)
    scale_one_grad = jnp.sum(grad_shaped * normed, axis=1)
    shift_one_grad = jnp.sum(grad_shaped, axis=1)
    input_grad = (grad_mid + norm_back(grad_shaped * (1.0 + scale_one), normed, inv_one)).reshape(
        tok_rows, D
    )
    input_grad = mm_exact(input_grad, perm_f, NT)
    moved_grad = jnp.stack(
        [
            shift_one_grad,
            scale_one_grad,
            gate_one_grad,
            shift_two_grad,
            scale_two_grad,
            gate_two_grad,
        ],
        axis=1,
    ).reshape(images * 6, D)
    back = mm_exact(
        jnp.concatenate([moved_grad, b_out_grad[None], b_two_grad[None]], axis=0), perm_f, NT
    )
    modul_grad = back[0 : images * 6].reshape(images, 6 * D)
    image_grads = lax.all_gather(
        jnp.concatenate([time_grad, modul_grad], axis=1), GRID, axis=0, tiled=True
    )
    grad_w_time = mm_exact(emb_low.astype(F32), image_grads[:, 0 : 3 * D], TN)
    grad_w_ada = mm_exact(silu_low.astype(F32), image_grads[:, 3 * D :], TN)
    b_ada_grad = jnp.sum(image_grads[:, 3 * D :], axis=0)

    grad_w_out = mm_exact(att_part[:, 3 * D :].astype(F32), perm_f, NT)
    att_grad = jnp.concatenate(
        [att_part[:, 0 : 3 * D].astype(F32), grad_w_time, grad_w_out, grad_w_ada], axis=1
    )
    mlp_grad = mlp_grad.astype(F32).reshape(rows_blk, 2, half_ff)
    local_rest = jnp.concatenate([rel_grad, back[images * 6], back[images * 6 + 1]])
    local_rest, bias_grad = lax.psum((local_rest, b_one_grad), GRID)
    small_grad = jnp.concatenate([local_rest[0:offset], b_ada_grad, local_rest[offset:]])
    local_sq = (
        jnp.sum(mlp_grad * mlp_grad)
        + jnp.sum(att_grad * att_grad) / mlp_count
        + jnp.sum(small_grad * small_grad) / (groups * mlp_count)
        + jnp.sum(bias_grad * bias_grad) / groups
    )
    grad_norm = jnp.sqrt(lax.psum(local_sq, ("wide", "narrow", "mlp")))
    clip_scale = jnp.minimum(1.0, 1.0 / (grad_norm + 1e-06))
    att_new, att_mom_new, att_sec_new = adam_update(
        att_master, att_moment, att_second, att_grad, clip_scale
    )
    mlp_new, mlp_mom_new, mlp_sec_new = adam_update(
        mlp_master, mlp_moment, mlp_second, mlp_grad, clip_scale
    )
    small_new, small_mom_new, small_sec_new = adam_update(
        small_master, small_moment, small_second, small_grad, clip_scale
    )
    bias_new, bias_mom_new, bias_sec_new = adam_update(
        bias_master, bias_moment, bias_second, bias_grad, clip_scale
    )
    return (
        output,
        input_grad,
        att_new,
        att_mom_new,
        att_sec_new,
        mlp_new,
        mlp_mom_new,
        mlp_sec_new,
        small_new,
        small_mom_new,
        small_sec_new,
        bias_new,
        bias_mom_new,
        bias_sec_new,
        att_new.astype(BF16),
        mlp_new.astype(BF16),
        grad_norm,
    )


def solution(mesh):
    rows = P(GRID, None)
    cube = P(GRID, None, "mlp")
    return jax.shard_map(
        on_device,
        mesh=mesh,
        in_specs=(
            rows,
            P(GRID),
            P(),
            P(),
            P(("wide", "narrow", "mlp"), None),
            rows,
            rows,
            rows,
            cube,
            cube,
            cube,
            P(),
            P(),
            P(),
            P("mlp"),
            P("mlp"),
            P("mlp"),
        ),
        out_specs=(
            P(("wide", "narrow", "mlp"), None),
            rows,
            rows,
            rows,
            rows,
            cube,
            cube,
            cube,
            P(),
            P(),
            P(),
            P("mlp"),
            P("mlp"),
            P("mlp"),
            rows,
            cube,
            P(),
        ),
        check_vma=False,
    )
```

```python
from functools import partial
import math

import jax
import jax.numpy as jnp
from jax import lax
from jax.experimental import pallas as pl
from jax.experimental.pallas import tpu as pltpu
from jax.sharding import PartitionSpec as P

D = 1152
HEADS = 16
HD = 72
NREL = 961
STEP = 10

HIGH = lax.Precision.HIGHEST
F32 = jnp.float32
BF16 = jnp.bfloat16
GRID = ("wide", "narrow")
NN = (((1,), (0,)), ((), ()))
TN = (((0,), (0,)), ((), ()))
NT = (((1,), (1,)), ((), ()))
INV_ROOT = 1.0 / math.sqrt(HD)
MESH = pl.DeviceIdType.MESH
ANY = pl.BlockSpec(memory_space=pl.ANY)
HEADW = 256
SPACE_AT = 1280
ONE_AT = SPACE_AT + HEADS * HEADW
VMEM_BYTES = 58 * 1024 * 1024


def mm(a, b, dims=NN):
    return lax.dot_general(a, b, dims, preferred_element_type=F32)


def mm_exact(a, b, dims=NN):
    return lax.dot_general(a, b, dims, precision=HIGH, preferred_element_type=F32)


def norm_stats(values):
    center = values - jnp.mean(values, axis=-1, keepdims=True)
    inv_std = lax.rsqrt(jnp.mean(center * center, axis=-1, keepdims=True) + 1e-06)
    return (center * inv_std, inv_std)


def norm_back(grad_normed, normed, inv_std):
    mean_grad = jnp.mean(grad_normed, axis=-1, keepdims=True)
    mean_proj = jnp.mean(grad_normed * normed, axis=-1, keepdims=True)
    return (grad_normed - mean_grad - normed * mean_proj) * inv_std


def time_embed(steps_int):
    half_dim = D // 2
    frequency = jnp.exp(-math.log(10000.0) * jnp.arange(half_dim).astype(F32) / half_dim)
    angles = steps_int.astype(F32)[:, None] * frequency[None, :]
    return jnp.concatenate([jnp.cos(angles), jnp.sin(angles)], axis=1)


def adam_update(weight, moment, second, grad, clip_scale):
    scaled = grad * clip_scale
    moment_new = 0.9 * moment + 0.1 * scaled
    second_new = 0.999 * second + 0.001 * scaled * scaled
    rate = 1.5 / math.sqrt(D)
    direction = (
        moment_new / (1.0 - 0.9**STEP) / (jnp.sqrt(second_new / (1.0 - 0.999**STEP)) + 1e-08)
    )
    return (weight - rate * (direction + 0.1 * weight), moment_new, second_new)


def exact_parts(values):
    first = values.astype(BF16)
    rest = values - first.astype(F32)
    second = rest.astype(BF16)
    return (first, second, (rest - second.astype(F32)).astype(BF16))


def mm_split(a, b, dims=NN):
    one, two, three = exact_parts(a)
    return mm(one, b, dims) + mm(two, b, dims) + mm(three, b, dims)


def params(**kw):
    return pltpu.CompilerParams(vmem_limit_bytes=VMEM_BYTES, **kw)


def cost(flops, nbytes):
    return pl.CostEstimate(flops=flops, bytes_accessed=nbytes, transcendentals=0)


def position():
    return (lax.axis_index("wide"), lax.axis_index("narrow"), lax.axis_index("mlp"))


def remote(src, dst, send, recv, device):
    return pltpu.make_async_remote_copy(
        src_ref=src, dst_ref=dst, send_sem=send, recv_sem=recv, device_id=device, device_id_type=MESH
    )


def greet_group(nw, nn, with_mlp):
    w, n, m = position()
    mine = w * nn + n
    groups = nw * nn
    bar = pltpu.get_barrier_semaphore()

    def ask(k, carry):
        other = lax.rem(mine + k, groups)
        pl.semaphore_signal(
            bar, inc=1, device_id=(lax.div(other, nn), lax.rem(other, nn), m), device_id_type=MESH
        )
        return carry

    lax.fori_loop(1, groups, ask, 0)
    if with_mlp:
        pl.semaphore_signal(bar, inc=1, device_id=(w, n, 1 - m), device_id_type=MESH)
    pl.semaphore_wait(bar, groups - 1 + (1 if with_mlp else 0))


def pack_body(att_ref, one_ref, two_ref, perm_ref, out_ref):
    rows = att_ref.shape[0]
    out_ref[:, 0:D] = mm(att_ref[:, 6 * D : 7 * D].astype(BF16), perm_ref[...]).astype(BF16)
    out_ref[:, D:SPACE_AT] = jnp.zeros((rows, SPACE_AT - D), BF16)
    space = att_ref[:, 0 : 3 * D]
    for h in range(HEADS):
        cols = [space[:, p * D + h * HD : p * D + (h + 1) * HD] for p in range(3)]
        cols.append(jnp.zeros((rows, HEADW - 3 * HD), F32))
        at = SPACE_AT + h * HEADW
        out_ref[:, at : at + HEADW] = jnp.concatenate(cols, axis=1).astype(BF16)
    half = one_ref.shape[1]
    out_ref[:, ONE_AT : ONE_AT + half] = one_ref[...].astype(BF16)
    out_ref[:, ONE_AT + half : ONE_AT + 2 * half] = two_ref[...].astype(BF16)


def pack_weights(att, one, two, perm):
    rows, half = one.shape
    return pl.pallas_call(
        pack_body,
        out_shape=jax.ShapeDtypeStruct((rows, ONE_AT + 2 * half), BF16),
        compiler_params=params(),
        name="pack",
    )(att, one, two, perm)


def modul_body(nw, nn, emb_ref, att_ref, pick_ref, cot_ref, sum_ref, emb_out, silu_out, cot_out,
               gath, flat, parts, from_c, from_x, from_z, gs, gr, cs, cr, xs, xr, zs, zr, ys, yr, ls):
    w, n, m = position()
    nlo, nhi, groups = (2, nn // 2, nw * nn)
    c, x = (lax.rem(n, nlo), lax.div(n, nlo))
    half = cot_ref.shape[0]
    width = parts.shape[2]
    slot = (c * nhi + x) * nw + w
    mine = w * nn + n
    greet_group(nw, nn, True)
    rows = pl.ds(m * half, half)
    to_y = remote(cot_ref, cot_out.at[rows], ys, yr, (w, n, 1 - m))
    to_y.start()
    keep = pltpu.make_async_copy(cot_ref, cot_out.at[rows], ls)
    keep.start()
    gath[slot] = emb_ref[...]

    def copy_to(k):
        other = lax.rem(mine + k, groups)
        return remote(gath.at[slot], gath.at[slot], gs.at[k], gr.at[k], (lax.div(other, nn), lax.rem(other, nn), m))

    def send(k, carry):
        copy_to(k).start()
        return carry

    def finish(k, carry):
        copy_to(k).wait()
        return carry

    lax.fori_loop(1, groups, send, 0)
    lax.fori_loop(1, groups, finish, 0)
    picked = mm(gath[...].reshape(groups * 8, D), pick_ref[...]).astype(BF16)
    line = lax.broadcasted_iota(jnp.int32, (2 * groups, 8 * groups), 0)
    col = lax.broadcasted_iota(jnp.int32, (2 * groups, 8 * groups), 1)
    at = (line // 2) * 8 + line % 2
    emb = mm((col == at).astype(BF16), picked).astype(BF16)
    silu = mm((col == at + 2).astype(BF16), picked).astype(BF16)
    emb_out[...] = emb
    silu_out[...] = silu
    flat[:, 0 : 3 * D] = mm(emb, att_ref[:, 3 * D : 6 * D].astype(BF16))
    flat[:, 3 * D : 9 * D] = mm(silu, att_ref[:, 7 * D : 13 * D].astype(BF16))
    for g in range(groups):
        parts[g] = flat[2 * g : 2 * g + 2, :]
    block = nhi * nw
    other_c = (1 - c) * block
    mine_c = c * block
    hop = remote(parts.at[pl.ds(other_c, block)], from_c, cs, cr, (w, x * nlo + 1 - c, m))
    hop.start()
    hop.wait()
    parts[pl.ds(mine_c, block)] = parts[pl.ds(mine_c, block)] + from_c[...]
    hops = []
    for k in range(1, nhi):
        there = lax.rem(x + k, nhi)
        hop = remote(
            parts.at[pl.ds(mine_c + there * nw, nw)], from_x.at[k - 1], xs.at[k - 1], xr.at[k - 1], (w, there * nlo + c, m)
        )
        hop.start()
        hops.append(hop)
    for hop in hops:
        hop.wait()
    first = mine_c + x * nw
    total = parts[pl.ds(first, nw)]
    for k in range(1, nhi):
        total = total + from_x[k - 1]
    parts[pl.ds(first, nw)] = total
    hops = []
    for k in range(1, nw):
        there = lax.rem(w + k, nw)
        hop = remote(parts.at[first + there], from_z.at[k - 1], zs.at[k - 1], zr.at[k - 1], (there, n, m))
        hop.start()
        hops.append(hop)
    for hop in hops:
        hop.wait()
    total = parts[first + w]
    for k in range(1, nw):
        total = total + from_z[k - 1]
    sum_ref[...] = total
    keep.wait()
    to_y.wait()


def modul_exchange(emb_rows, att, pick, cot, nw, nn):
    groups = nw * nn
    nhi = nn // 2
    width = 9 * D
    half = cot.shape[0]
    vmem = pl.BlockSpec(memory_space=pltpu.VMEM)
    dma = pltpu.SemaphoreType.DMA
    return pl.pallas_call(
        partial(modul_body, nw, nn),
        in_specs=[vmem, vmem, vmem, ANY],
        out_specs=[vmem, vmem, vmem, ANY],
        out_shape=[
            jax.ShapeDtypeStruct((2, width), F32),
            jax.ShapeDtypeStruct((2 * groups, att.shape[0]), BF16),
            jax.ShapeDtypeStruct((2 * groups, att.shape[0]), BF16),
            jax.ShapeDtypeStruct((2 * half, D), BF16),
        ],
        scratch_shapes=[
            pltpu.VMEM((groups, 8, D), BF16),
            pltpu.VMEM((2 * groups, width), F32),
            pltpu.VMEM((groups, 2, width), F32),
            pltpu.VMEM((nhi * nw, 2, width), F32),
            pltpu.VMEM((max(nhi - 1, 1), nw, 2, width), F32),
            pltpu.VMEM((max(nw - 1, 1), 2, width), F32),
            dma((groups,)), dma((groups,)), dma, dma,
            dma((max(nhi - 1, 1),)), dma((max(nhi - 1, 1),)),
            dma((max(nw - 1, 1),)), dma((max(nw - 1, 1),)),
            dma, dma, dma,
        ],
        compiler_params=params(collective_id=1, has_side_effects=True),
        cost_estimate=cost(10**8, 3 * 10**7),
        name="modul_exchange",
    )(emb_rows, att, pick, cot)


def bias_body(index_ref, table_ref, bias_ref):
    low = jnp.bitwise_and(index_ref[...], 127)
    high = jnp.right_shift(index_ref[...], 7)
    for part in range(index_ref.shape[1] // 128):
        at = slice(part * 128, (part + 1) * 128)
        lo = low[:, at]
        hi = high[:, at]
        total = jnp.zeros(lo.shape, F32)
        for chunk in range(8):
            row = jnp.broadcast_to(table_ref[0, :, chunk * 128 : (chunk + 1) * 128], lo.shape)
            total = jnp.where(hi == chunk, jnp.take_along_axis(row, lo, axis=1), total)
        bias_ref[0, :, at] = total


def rel_bias(index_t, table_t, seq):
    return pl.pallas_call(
        bias_body,
        grid=(HEADS,),
        in_specs=[
            pl.BlockSpec((seq, seq), lambda h: (0, 0)),
            pl.BlockSpec((1, 1, 1024), lambda h: (h, 0, 0)),
        ],
        out_specs=pl.BlockSpec((1, seq, seq), lambda h: (h, 0, 0)),
        out_shape=jax.ShapeDtypeStruct((HEADS, seq, seq), F32),
        cost_estimate=cost(2 * 10**8, 4 * 10**7),
        name="rel_bias",
    )(index_t, table_t)


def front_body(tok_ref, cot_ref, perm_ref, mod_ref, tok_out, shaped_out, shaped_t, cot_out, branch_out, sums):
    moved = mm(tok_ref[...], perm_ref[...])
    tok_out[...] = moved.astype(BF16)
    normed, _ = norm_stats(moved)
    shaped = normed * (1.0 + mod_ref[0, 1:2]) + mod_ref[0, 0:1]
    shaped_out[...] = shaped.astype(BF16)
    shaped_t[...] = shaped.T.astype(BF16)
    cot = mm(cot_ref[...], perm_ref[...])
    cot_out[...] = cot.astype(BF16)
    branch = (cot * mod_ref[0, 5:6]).astype(BF16)
    branch_out[...] = branch
    sums[0, 0:1] = jnp.sum(branch.astype(F32), axis=0, keepdims=True)
    sums[0, 1:2] = jnp.sum(cot, axis=0, keepdims=True)
    sums[0, 2:8] = jnp.zeros((6, D), F32)


def front(tokens, cot, perm, mod, seq, images):
    rows = seq * images
    tok = pl.BlockSpec((seq, D), lambda n: (n, 0))
    per = pl.BlockSpec((1, 8, D), lambda n: (n, 0, 0))
    return pl.pallas_call(
        front_body,
        grid=(images,),
        in_specs=[tok, tok, pl.BlockSpec((D, D), lambda n: (0, 0)), per],
        out_specs=[tok, tok, pl.BlockSpec((D, seq), lambda n: (0, n)), tok, tok, per],
        out_shape=[
            jax.ShapeDtypeStruct((rows, D), BF16),
            jax.ShapeDtypeStruct((rows, D), BF16),
            jax.ShapeDtypeStruct((D, rows), BF16),
            jax.ShapeDtypeStruct((rows, D), BF16),
            jax.ShapeDtypeStruct((rows, D), BF16),
            jax.ShapeDtypeStruct((images, 8, D), F32),
        ],
        compiler_params=params(),
        cost_estimate=cost(4 * rows * D * D, 10**7),
        name="front",
    )(tokens, cot, perm, mod)


def attend_fwd_body(seq, images, own_ref, shaped_ref, w_ref, time_ref, bias_ref, qkv_ref, out_ref, lse_ref):
    qkv = mm(shaped_ref[...], w_ref[...])
    qkv = jnp.concatenate(
        [qkv[n * seq : (n + 1) * seq] + time_ref[0, n : n + 1] for n in range(images)], axis=0
    ).T
    query, key, value = [qkv[p * HD : (p + 1) * HD].astype(BF16) for p in range(3)]
    qkv_ref[0, 0] = query
    qkv_ref[0, 1] = key
    qkv_ref[0, 2] = value
    for n in range(images):
        at = slice(n * seq, (n + 1) * seq)
        scores = mm(key[:, at], query[:, at], TN) * INV_ROOT + bias_ref[0]
        top = jnp.max(scores, axis=0, keepdims=True)
        weights = jnp.exp(scores - top)
        total = jnp.sum(weights, axis=0, keepdims=True)
        probs = (weights * (1.0 / total)).astype(BF16)
        out_ref[0, :, at] = mm(value[:, at], probs).astype(BF16)
        lse_ref[0, :, at] = top + jnp.log(total)


def attend_fwd(own, shaped, gathered, time_h, bias, seq, images, moved):
    rows = seq * images
    place = (lambda h, own: (own[h], 0, 0)) if moved else (lambda h, own: (h, 0, 0))
    first = SPACE_AT // HEADW
    return pl.pallas_call(
        partial(attend_fwd_body, seq, images),
        grid_spec=pltpu.PrefetchScalarGridSpec(
            num_scalar_prefetch=1,
            grid=(HEADS,),
            in_specs=[
                pl.BlockSpec((rows, D), lambda h, own: (0, 0)),
                pl.BlockSpec((D, HEADW), lambda h, own: (0, first + h)),
                pl.BlockSpec((1, images, HEADW), lambda h, own: (h, 0, 0)),
                pl.BlockSpec((1, seq, seq), lambda h, own: (h, 0, 0)),
            ],
            out_specs=[
                pl.BlockSpec((1, 3, HD, rows), lambda h, own: (h, 0, 0, 0)),
                pl.BlockSpec((1, HD, rows), place),
                pl.BlockSpec((1, 1, rows), lambda h, own: (h, 0, 0)),
            ],
        ),
        out_shape=[
            jax.ShapeDtypeStruct((HEADS, 3, HD, rows), BF16),
            jax.ShapeDtypeStruct((HEADS, HD, rows), BF16),
            jax.ShapeDtypeStruct((HEADS, 1, rows), F32),
        ],
        compiler_params=params(),
        cost_estimate=cost(6 * 10**9, 2 * 10**7),
        name="attend_fwd",
    )(own, shaped, gathered, time_h, bias)


def mid_body(att_ref, w_ref, tok_ref, mod_ref, attn_out, shaped_out):
    attn = mm(att_ref[...], w_ref[...], TN) + mod_ref[0, 6:7]
    attn_out[...] = attn
    mid = tok_ref[...].astype(F32) + mod_ref[0, 2:3] * attn
    normed, _ = norm_stats(mid)
    shaped_out[...] = (normed * (1.0 + mod_ref[0, 4:5]) + mod_ref[0, 3:4]).astype(BF16)


def middle(att, gathered, tok, mod, seq, images):
    rows = seq * images
    row = pl.BlockSpec((seq, D), lambda n: (n, 0))
    return pl.pallas_call(
        mid_body,
        grid=(images,),
        in_specs=[
            pl.BlockSpec((D, seq), lambda n: (0, n)),
            pl.BlockSpec((D, D), lambda n: (0, 0)),
            row,
            pl.BlockSpec((1, 8, D), lambda n: (n, 0, 0)),
        ],
        out_specs=[row, row],
        out_shape=[jax.ShapeDtypeStruct((rows, D), F32), jax.ShapeDtypeStruct((rows, D), BF16)],
        compiler_params=params(),
        cost_estimate=cost(2 * rows * D * D, 10**7),
        name="middle",
    )(att, gathered, tok, mod)


def mlp_body(seq, images, x_ref, gb_ref, one_ref, two_ref, bias_ref, cot_ref,
             dw_ref, branch_ref, back_ref, bias_out, gate_ref, x_t, gb_t, acc):
    step = pl.program_id(0)

    @pl.when(step == 0)
    def _():
        branch_ref[...] = jnp.zeros_like(branch_ref)
        acc[...] = jnp.zeros_like(acc)
        x_t[...] = x_ref[...].T
        gb_t[...] = gb_ref[...].T

    pre = mm(x_ref[...], one_ref[...]) + bias_ref[...]
    root = math.sqrt(2.0 / math.pi)
    square = pre * pre
    bend = jnp.tanh(root * (pre + 0.044715 * (square * pre)))
    rise = 0.5 * (1.0 + bend)
    hidden = (pre * rise).astype(BF16)
    slope = rise + 0.5 * pre * (1.0 - bend * bend) * (root * (1.0 + 3 * 0.044715 * square))
    grad = (mm(gb_ref[...], two_ref[...]) * slope).astype(BF16)
    acc[...] += mm(grad, one_ref[...], NT)
    branch_ref[...] += mm(hidden, two_ref[...], NT)
    dw_ref[:, 0:HEADW] = mm(x_t[...], grad).astype(BF16)
    dw_ref[:, HEADW : 2 * HEADW] = mm(gb_t[...], hidden).astype(BF16)
    bias_out[...] = jnp.sum(grad.astype(F32), axis=0, keepdims=True)

    @pl.when(step == pl.num_programs(0) - 1)
    def _():
        back_ref[...] = acc[...].astype(BF16)
        gate_ref[...] = jnp.zeros_like(gate_ref)
        for n in range(images):
            at = slice(n * seq, (n + 1) * seq)
            gate_ref[n : n + 1] = jnp.sum(
                cot_ref[at].astype(F32) * branch_ref[at], axis=0, keepdims=True
            )


def mlp_block(x, gb, gathered, bias, cot, seq, images):
    rows = seq * images
    half = bias.shape[1]
    tiles = half // HEADW
    one, two = (ONE_AT // HEADW, (ONE_AT + half) // HEADW)
    whole = pl.BlockSpec((rows, D), lambda f: (0, 0))
    return pl.pallas_call(
        partial(mlp_body, seq, images),
        grid=(tiles,),
        in_specs=[
            whole,
            whole,
            pl.BlockSpec((D, HEADW), lambda f: (0, one + f)),
            pl.BlockSpec((D, HEADW), lambda f: (0, two + f)),
            pl.BlockSpec((1, HEADW), lambda f: (0, f)),
            whole,
        ],
        out_specs=[
            pl.BlockSpec((D, 2 * HEADW), lambda f: (0, f)),
            whole,
            whole,
            pl.BlockSpec((1, HEADW), lambda f: (0, f)),
            pl.BlockSpec((8, D), lambda f: (0, 0)),
        ],
        out_shape=[
            jax.ShapeDtypeStruct((D, 2 * half), BF16),
            jax.ShapeDtypeStruct((rows, D), F32),
            jax.ShapeDtypeStruct((rows, D), BF16),
            jax.ShapeDtypeStruct((1, half), F32),
            jax.ShapeDtypeStruct((8, D), F32),
        ],
        scratch_shapes=[pltpu.VMEM((D, rows), BF16), pltpu.VMEM((D, rows), BF16), pltpu.VMEM((rows, D), F32)],
        compiler_params=params(),
        cost_estimate=cost(12 * rows * D * half, 4 * 10**7),
        name="mlp_block",
    )(x, gb, gathered, gathered, bias, cot)


def back_mid_body(own_ref, peer_ref, attn_ref, tok_ref, cot_ref, mod_ref, w_ref,
                  grad_mid, grad_attn, grad_att_t, sums):
    attn = attn_ref[...]
    mid = tok_ref[...].astype(F32) + mod_ref[0, 2:3] * attn
    normed, inv = norm_stats(mid)
    grad = own_ref[...].astype(F32) + peer_ref[...].astype(F32)
    sums[0, 0:1] = jnp.sum(grad, axis=0, keepdims=True)
    sums[0, 1:2] = jnp.sum(grad * normed, axis=0, keepdims=True)
    grad = cot_ref[...].astype(F32) + norm_back(grad * (1.0 + mod_ref[0, 4:5]), normed, inv)
    grad_mid[...] = grad
    sums[0, 2:3] = jnp.sum(grad * attn, axis=0, keepdims=True)
    low = (grad * mod_ref[0, 2:3]).astype(BF16)
    sums[0, 3:4] = jnp.sum(low.astype(F32), axis=0, keepdims=True)
    sums[0, 4:8] = jnp.zeros((4, D), F32)
    grad_attn[:, 0:D] = low
    grad_attn[:, D:SPACE_AT] = jnp.zeros((low.shape[0], SPACE_AT - D), BF16)
    grad_att_t[...] = mm(w_ref[...], low, NT).astype(BF16)


def back_middle(own, peer, attn, tok, cot, mod, gathered, seq, images):
    rows = seq * images
    row = pl.BlockSpec((seq, D), lambda n: (n, 0))
    per = pl.BlockSpec((1, 8, D), lambda n: (n, 0, 0))
    return pl.pallas_call(
        back_mid_body,
        grid=(images,),
        in_specs=[row, row, row, row, row, per, pl.BlockSpec((D, D), lambda n: (0, 0))],
        out_specs=[
            row,
            pl.BlockSpec((seq, SPACE_AT), lambda n: (n, 0)),
            pl.BlockSpec((D, seq), lambda n: (0, n)),
            per,
        ],
        out_shape=[
            jax.ShapeDtypeStruct((rows, D), F32),
            jax.ShapeDtypeStruct((rows, SPACE_AT), BF16),
            jax.ShapeDtypeStruct((D, rows), BF16),
            jax.ShapeDtypeStruct((images, 8, D), F32),
        ],
        compiler_params=params(),
        cost_estimate=cost(2 * rows * D * D, 10**7),
        name="back_middle",
    )(own, peer, attn, tok, cot, mod, gathered)


def attend_bwd_body(seq, images, own, att_ref, ga_ref, shaped_ref, w_ref, qkv_ref, grad_ref, bias_ref, lse_ref,
                    dw_ref, acc_ref, ds_ref, time_ref):
    step = pl.program_id(0)
    first = SPACE_AT // HEADW

    @pl.when(step == 0)
    def _():
        acc_ref[...] = jnp.zeros_like(acc_ref)

    @pl.when(step < first)
    def _():
        dw_ref[...] = mm(att_ref[...], ga_ref[...]).astype(BF16)

    @pl.when(step >= first)
    def _():
        pieces = [[], [], []]
        for n in range(images):
            at = slice(n * seq, (n + 1) * seq)
            query, key, value = [qkv_ref[0, p, :, at] for p in range(3)]
            grad = grad_ref[0, :, at]
            probs = jnp.exp(mm(key, query, TN) * INV_ROOT + (bias_ref[0] - lse_ref[0, :, at]))
            grad_probs = mm(value, grad, TN)
            inner = jnp.sum(probs * grad_probs, axis=0, keepdims=True)
            ds = (probs * (grad_probs - inner)).astype(BF16)
            pieces[0].append(mm(key, ds) * INV_ROOT)
            pieces[1].append(mm(query, ds, NT) * INV_ROOT)
            pieces[2].append(mm(grad, probs.astype(BF16), NT))
            ds_ref[0, :, at] = ds.astype(F32)
        cols = [jnp.concatenate(p, axis=1) for p in pieces]
        cols.append(jnp.zeros((HEADW - 3 * HD, seq * images), F32))
        grad_qkv = jnp.concatenate(cols, axis=0).T.astype(BF16)
        acc_ref[...] += mm(grad_qkv, w_ref[...], NT)
        dw_ref[...] = mm(shaped_ref[...], grad_qkv).astype(BF16)
        wide = grad_qkv.astype(F32)
        for n in range(images):
            time_ref[0, n : n + 1] = jnp.sum(wide[n * seq : (n + 1) * seq], axis=0, keepdims=True)


def attend_bwd(own, att, ga, shaped_t, gathered, qkv, grad, bias, lse, seq, images, moved):
    rows = seq * images
    first = SPACE_AT // HEADW

    def head(s):
        return jnp.maximum(s - first, 0)

    place = (lambda s, own: (own[head(s)], 0, 0)) if moved else (lambda s, own: (head(s), 0, 0))
    return pl.pallas_call(
        partial(attend_bwd_body, seq, images),
        grid_spec=pltpu.PrefetchScalarGridSpec(
            num_scalar_prefetch=1,
            grid=(first + HEADS,),
            in_specs=[
                pl.BlockSpec((D, rows), lambda s, own: (0, 0)),
                pl.BlockSpec((rows, HEADW), lambda s, own: (0, jnp.minimum(s, first - 1))),
                pl.BlockSpec((D, rows), lambda s, own: (0, 0)),
                pl.BlockSpec((D, HEADW), lambda s, own: (0, jnp.maximum(s, first))),
                pl.BlockSpec((1, 3, HD, rows), lambda s, own: (head(s), 0, 0, 0)),
                pl.BlockSpec((1, HD, rows), place),
                pl.BlockSpec((1, seq, seq), lambda s, own: (head(s), 0, 0)),
                pl.BlockSpec((1, 1, rows), lambda s, own: (head(s), 0, 0)),
            ],
            out_specs=[
                pl.BlockSpec((D, HEADW), lambda s, own: (0, s)),
                pl.BlockSpec((rows, D), lambda s, own: (0, 0)),
                pl.BlockSpec((1, seq, rows), lambda s, own: (head(s), 0, 0)),
                pl.BlockSpec((1, images, HEADW), lambda s, own: (head(s), 0, 0)),
            ],
        ),
        out_shape=[
            jax.ShapeDtypeStruct((D, ONE_AT), BF16),
            jax.ShapeDtypeStruct((rows, D), F32),
            jax.ShapeDtypeStruct((HEADS, seq, rows), F32),
            jax.ShapeDtypeStruct((HEADS, images, HEADW), F32),
        ],
        compiler_params=params(),
        cost_estimate=cost(16 * 10**9, 4 * 10**7),
        name="attend_bwd",
    )(own, att, ga, shaped_t, gathered, qkv, grad, bias, lse)


def finish_in_body(acc_ref, tok_ref, mod_ref, mid_ref, perm_ref, out_ref, sums):
    normed, inv = norm_stats(tok_ref[...].astype(F32))
    grad = acc_ref[...]
    sums[0, 0:1] = jnp.sum(grad, axis=0, keepdims=True)
    sums[0, 1:2] = jnp.sum(grad * normed, axis=0, keepdims=True)
    sums[0, 2:8] = jnp.zeros((6, D), F32)
    grad = mid_ref[...] + norm_back(grad * (1.0 + mod_ref[0, 1:2]), normed, inv)
    out_ref[...] = mm_split(grad, perm_ref[...], NT)


def finish_in(acc, tok, mod, mid, perm, seq, images):
    rows = seq * images
    row = pl.BlockSpec((seq, D), lambda n: (n, 0))
    per = pl.BlockSpec((1, 8, D), lambda n: (n, 0, 0))
    return pl.pallas_call(
        finish_in_body,
        grid=(images,),
        in_specs=[row, row, per, row, pl.BlockSpec((D, D), lambda n: (0, 0))],
        out_specs=[row, per],
        out_shape=[jax.ShapeDtypeStruct((rows, D), F32), jax.ShapeDtypeStruct((images, 8, D), F32)],
        compiler_params=params(),
        cost_estimate=cost(6 * rows * D * D, 10**7),
        name="finish_in",
    )(acc, tok, mod, mid, perm)


def share_body(nw, nn, img_ref, small_ref, img_out, small_out, gath, sc, sx, sz,
               zs, zr, xs, xr, cs, cr, tcs, tcr, txs, txr, tzs, tzr):
    w, n, m = position()
    nlo, nhi, groups = (2, nn // 2, nw * nn)
    c, x = (lax.rem(n, nlo), lax.div(n, nlo))
    slot = (c * nhi + x) * nw + w
    greet_group(nw, nn, False)
    gath[slot] = img_ref[...]
    hops = []
    for k in range(1, nw):
        there = lax.rem(w + k, nw)
        hops.append(remote(gath.at[slot], gath.at[slot], zs.at[k - 1], zr.at[k - 1], (there, n, m)))
    sc[c] = small_ref[...]
    small = remote(sc.at[c], sc.at[c], tcs, tcr, (w, x * nlo + 1 - c, m))
    small.start()
    for hop in hops:
        hop.start()
    small.wait()
    sx[x] = sc[0] + sc[1]
    smalls = []
    for k in range(1, nhi):
        there = lax.rem(x + k, nhi)
        smalls.append(remote(sx.at[x], sx.at[x], txs.at[k - 1], txr.at[k - 1], (w, there * nlo + c, m)))
    for hop in smalls:
        hop.start()
    for hop in hops:
        hop.wait()
    own = pl.ds((c * nhi + x) * nw, nw)
    hops = []
    for k in range(1, nhi):
        there = lax.rem(x + k, nhi)
        hops.append(remote(gath.at[own], gath.at[own], xs.at[k - 1], xr.at[k - 1], (w, there * nlo + c, m)))
    for hop in hops:
        hop.start()
    for hop in smalls:
        hop.wait()
    total = sx[0]
    for k in range(1, nhi):
        total = total + sx[k]
    sz[w] = total
    smalls = []
    for k in range(1, nw):
        there = lax.rem(w + k, nw)
        smalls.append(remote(sz.at[w], sz.at[w], tzs.at[k - 1], tzr.at[k - 1], (there, n, m)))
    for hop in smalls:
        hop.start()
    for hop in hops:
        hop.wait()
    own = pl.ds(c * nhi * nw, nhi * nw)
    hop = remote(gath.at[own], gath.at[own], cs, cr, (w, x * nlo + 1 - c, m))
    hop.start()
    for other in smalls:
        other.wait()
    total = sz[0]
    for k in range(1, nw):
        total = total + sz[k]
    small_out[...] = total
    hop.wait()
    for g in range(groups):
        img_out[2 * g : 2 * g + 2, :] = gath[g]


def share(imgs, small, nw, nn):
    groups = nw * nn
    nhi = nn // 2
    rows = small.shape[0]
    width = imgs.shape[1]
    vmem = pl.BlockSpec(memory_space=pltpu.VMEM)
    dma = pltpu.SemaphoreType.DMA
    hi, wi = (max(nhi - 1, 1), max(nw - 1, 1))
    return pl.pallas_call(
        partial(share_body, nw, nn),
        in_specs=[vmem, vmem],
        out_specs=[vmem, vmem],
        out_shape=[
            jax.ShapeDtypeStruct((2 * groups, width), F32),
            jax.ShapeDtypeStruct(small.shape, F32),
        ],
        scratch_shapes=[
            pltpu.VMEM((groups, 2, width), F32),
            pltpu.VMEM((2, rows, 128), F32),
            pltpu.VMEM((nhi, rows, 128), F32),
            pltpu.VMEM((nw, rows, 128), F32),
            dma((wi,)), dma((wi,)), dma((hi,)), dma((hi,)), dma, dma,
            dma, dma, dma((hi,)), dma((hi,)), dma((wi,)), dma((wi,)),
        ],
        compiler_params=params(collective_id=2, has_side_effects=True),
        cost_estimate=cost(10**8, 3 * 10**7),
        name="share",
    )(imgs, small)


def norm_body(nw, nn, nm, bias_rows, att_ref, mlp_ref, img_ref, emb_ref, silu_ref, small_ref, perm_ref,
              att_out, one_out, two_out, ada_out, norm_out, slots, ss, sr):
    w, n, m = position()
    groups = nw * nn
    count = groups * nm
    mine = (w * nn + n) * nm + m
    bar = pltpu.get_barrier_semaphore()

    def who(k):
        other = lax.rem(mine + k, count)
        pair = lax.div(other, nm)
        return (lax.div(pair, nn), lax.rem(pair, nn), lax.rem(other, nm))

    def ask(k, carry):
        pl.semaphore_signal(bar, inc=1, device_id=who(k), device_id_type=MESH)
        return carry

    lax.fori_loop(1, count, ask, 0)
    emb = emb_ref[...]
    silu = silu_ref[...]
    att_sq = jnp.zeros((1, 1), F32)

    def spread(values):
        return [
            jnp.concatenate(
                [values[:, h * HEADW + p * HD : h * HEADW + (p + 1) * HD] for h in range(HEADS)], axis=1
            )
            for p in range(3)
        ]

    def tally(values):
        return jnp.sum(jnp.sum(values * values, axis=0, keepdims=True), axis=1, keepdims=True)

    for p, part in enumerate(spread(att_ref[:, SPACE_AT:].astype(F32))):
        att_out[:, p * D : (p + 1) * D] = part
        att_sq = att_sq + tally(part)
    imgs = exact_parts(img_ref[:, 0 : HEADS * HEADW])
    timed = mm(emb, imgs[0], TN) + mm(emb, imgs[1], TN) + mm(emb, imgs[2], TN)
    for p, part in enumerate(spread(timed)):
        att_out[:, (3 + p) * D : (4 + p) * D] = part
        att_sq = att_sq + tally(part)
    part = mm(att_ref[:, 0:D], perm_ref[...], NT)
    att_out[:, 6 * D : 7 * D] = part
    att_sq = att_sq + tally(part)
    ada = img_ref[:, HEADS * HEADW :]
    ada_sum = jnp.sum(ada, axis=0, keepdims=True)
    ada_out[...] = ada_sum
    imgs = exact_parts(ada)
    part = mm(silu, imgs[0], TN) + mm(silu, imgs[1], TN) + mm(silu, imgs[2], TN)
    att_out[:, 7 * D :] = part
    att_sq = att_sq + tally(part)
    mlp_sq = jnp.zeros((1, 1), F32)
    for f in range(mlp_ref.shape[1] // (2 * HEADW)):
        at = slice(f * HEADW, (f + 1) * HEADW)
        part = mlp_ref[:, 2 * f * HEADW : (2 * f + 1) * HEADW].astype(F32)
        one_out[:, at] = part
        mlp_sq = mlp_sq + tally(part)
        part = mlp_ref[:, (2 * f + 1) * HEADW : (2 * f + 2) * HEADW].astype(F32)
        two_out[:, at] = part
        mlp_sq = mlp_sq + tally(part)
    shared_rows = small_ref.shape[0] - bias_rows
    small_sq = tally(small_ref[0:shared_rows]) + tally(ada_sum)
    bias_sq = tally(small_ref[shared_rows:])
    local = mlp_sq + att_sq / nm + small_sq / count + bias_sq / groups
    slots[mine] = jnp.broadcast_to(local, (8, 128))
    pl.semaphore_wait(bar, count - 1)

    def copy_to(k):
        return remote(slots.at[mine], slots.at[mine], ss.at[k], sr.at[k], who(k))

    def send(k, carry):
        copy_to(k).start()
        return carry

    def finish(k, carry):
        copy_to(k).wait()
        return carry

    lax.fori_loop(1, count, send, 0)
    lax.fori_loop(1, count, finish, 0)
    norm_out[...] = jnp.sqrt(jnp.sum(slots[...], axis=0))


def collect_norm(att, mlp, imgs, emb, silu, small, perm, bias_rows, nw, nn, nm):
    rows = att.shape[0]
    half = mlp.shape[1] // 2
    count = nw * nn * nm
    dma = pltpu.SemaphoreType.DMA
    return pl.pallas_call(
        partial(norm_body, nw, nn, nm, bias_rows),
        out_shape=[
            jax.ShapeDtypeStruct((rows, 13 * D), F32),
            jax.ShapeDtypeStruct((rows, half), F32),
            jax.ShapeDtypeStruct((rows, half), F32),
            jax.ShapeDtypeStruct((1, 6 * D), F32),
            jax.ShapeDtypeStruct((8, 128), F32),
        ],
        scratch_shapes=[pltpu.VMEM((count, 8, 128), F32), dma((count,)), dma((count,))],
        compiler_params=params(collective_id=3, has_side_effects=True),
        cost_estimate=cost(10**8, 10**7),
        name="collect_norm",
    )(att, mlp, imgs, emb, silu, small, perm)


def rel_grad_body(seq, images, step, ds_ref, index_ref, out_ref):
    @pl.when(pl.program_id(0) == 0)
    def _():
        out_ref[...] = jnp.zeros_like(out_ref)

    bucket = lax.broadcasted_iota(jnp.int32, (256, seq), 0)
    for j in range(step):
        index = index_ref[j : j + 1, :]
        low = jnp.bitwise_and(index, 255)
        high = jnp.right_shift(index, 8)
        hot = jnp.where(bucket == low, 1.0, 0.0).astype(BF16)
        total = ds_ref[:, j, :]
        picked = []
        for n in range(images):
            for a in range(4):
                picked.append(jnp.where(high == a, total[:, n * seq : (n + 1) * seq], 0.0))
        sums = mm(jnp.concatenate(picked, axis=0).astype(BF16), hot, NT)
        for n in range(images):
            out_ref[...] += sums[n * 4 * HEADS : (n + 1) * 4 * HEADS]


def rel_grad_sum(ds, index_t, seq, images):
    rows = seq * images
    step = 8
    return pl.pallas_call(
        partial(rel_grad_body, seq, images, step),
        grid=(seq // step,),
        in_specs=[
            pl.BlockSpec((HEADS, step, rows), lambda j: (0, j, 0)),
            pl.BlockSpec((step, seq), lambda j: (j, 0)),
        ],
        out_specs=pl.BlockSpec((4 * HEADS, 256), lambda j: (0, 0)),
        out_shape=jax.ShapeDtypeStruct((4 * HEADS, 256), F32),
        name="rel_grad",
    )(ds, index_t)


def on_device(
    tokens,
    timesteps,
    owners,
    rel_index,
    cotangent,
    att_master,
    att_moment,
    att_second,
    mlp_master,
    mlp_moment,
    mlp_second,
    small_master,
    small_moment,
    small_second,
    bias_master,
    bias_moment,
    bias_second,
):
    groups = owners.shape[0]
    rows_blk = att_master.shape[0]
    half_ff = mlp_master.shape[2]
    images = timesteps.shape[0]
    tok_rows = tokens.shape[0]
    half_rows = cotangent.shape[0]
    seq_len = tok_rows // images
    nw, nn, nm = (lax.axis_size("wide"), lax.axis_size("narrow"), lax.axis_size("mlp"))
    mlp_at = lax.axis_index("mlp")
    mine = lax.axis_index(GRID)
    moved = rows_blk == HD
    swap = [(i, nm - 1 - i) for i in range(nm)]

    place = (owners[:, None] * rows_blk + jnp.arange(rows_blk)[None, :]).reshape(D)
    perm = (place[:, None] == jnp.arange(D)[None, :]).astype(BF16)
    perm_f = perm.astype(F32)
    pick = (place[:, None] == (mine * rows_blk + jnp.arange(rows_blk))[None, :]).astype(BF16)

    packed = pack_weights(att_master, mlp_master[:, 0], mlp_master[:, 1], perm)
    gathered = lax.all_gather(packed, GRID, axis=0, tiled=True)

    time_emb = time_embed(timesteps)
    emb_rows = jnp.concatenate(
        [time_emb, jax.nn.silu(time_emb), jnp.zeros((8 - 2 * images, D), F32)], axis=0
    ).astype(BF16)
    summed, emb_mine, silu_mine, cot_all = modul_exchange(
        emb_rows, att_master, pick, cotangent, nw, nn
    )
    time_part = summed[:, 0 : 3 * D].reshape(images, 3, HEADS, HD).transpose(2, 0, 1, 3)
    time_part = jnp.pad(
        time_part.reshape(HEADS, images, 3 * HD), ((0, 0), (0, 0), (0, HEADW - 3 * HD))
    )
    offset = NREL * HEADS
    table_t = jnp.pad(small_master[0:offset].reshape(NREL, HEADS).T, ((0, 0), (0, 1024 - NREL)))
    b_ada = small_master[offset : offset + 6 * D]
    b_rest = small_master[offset + 6 * D : offset + 8 * D].reshape(1, 2, D)
    modulation = (summed[:, 3 * D :] + b_ada).reshape(images, 6, D)
    mod = jnp.concatenate([modulation, jnp.broadcast_to(b_rest, (images, 2, D))], axis=1)
    mod = mm_exact(mod.reshape(images * 8, D), perm_f).reshape(images, 8, D)
    index_t = rel_index.T
    bias = rel_bias(index_t, table_t.reshape(HEADS, 1, 1024), seq_len)

    tok, shaped, shaped_t, cot, grad_branch, front_sums = front(
        tokens, cot_all, perm, mod, seq_len, images
    )
    qkv, attended, lse = attend_fwd(
        owners, shaped, gathered, time_part, bias, seq_len, images, moved
    )
    attended = attended.reshape(D, tok_rows)
    if not moved:
        attended = mm(perm, attended, TN).astype(BF16)
    attn_out, shaped_two = middle(attended, gathered, tok, mod, seq_len, images)
    mlp_term, branch, back_own, b_one_grad, gate_own = mlp_block(
        shaped_two, grad_branch, gathered, bias_master.reshape(1, half_ff), cot, seq_len, images
    )
    back_peer, gate_peer = (
        lax.ppermute(back_own, "mlp", swap),
        lax.ppermute(gate_own, "mlp", swap),
    )
    first_row = mlp_at * half_rows
    their_row = (nm - 1 - mlp_at) * half_rows
    branch_peer = lax.ppermute(
        lax.dynamic_slice_in_dim(branch, their_row, half_rows, 0).astype(BF16), "mlp", swap
    )
    mlp_part = lax.psum_scatter(mlp_term, GRID, scatter_dimension=0, tiled=True)

    grad_mid, grad_attn, grad_att, mid_sums = back_middle(
        back_own, back_peer, attn_out, tok, cot, mod, gathered, seq_len, images
    )
    if not moved:
        grad_att = mm(perm, grad_att).astype(BF16)
    att_term, acc, ds, time_grad = attend_bwd(
        owners,
        attended,
        grad_attn,
        shaped_t,
        gathered,
        qkv,
        grad_att.reshape(HEADS, HD, tok_rows),
        bias,
        lse,
        seq_len,
        images,
        moved,
    )
    att_part = lax.psum_scatter(att_term, GRID, scatter_dimension=0, tiled=True)
    rel_sum = rel_grad_sum(ds, index_t, seq_len, images)
    input_grad, in_sums = finish_in(acc, tok, mod, grad_mid, perm, seq_len, images)
    gate_two_grad = gate_own[0:images] + gate_peer[0:images] + mod[:, 7] * front_sums[:, 1]
    modul_grad = jnp.stack(
        [
            in_sums[:, 0],
            in_sums[:, 1],
            mid_sums[:, 2],
            mid_sums[:, 0],
            mid_sums[:, 1],
            gate_two_grad,
        ],
        axis=1,
    ).reshape(images * 6, D)
    back = mm_exact(
        jnp.concatenate(
            [
                modul_grad,
                jnp.sum(mid_sums[:, 3], axis=0, keepdims=True),
                jnp.sum(front_sums[:, 0], axis=0, keepdims=True),
            ],
            axis=0,
        ),
        perm_f,
        NT,
    )
    imgs = jnp.concatenate(
        [
            time_grad.transpose(1, 0, 2).reshape(images, HEADS * HEADW),
            back[0 : images * 6].reshape(images, 6 * D),
        ],
        axis=1,
    )
    small = jnp.concatenate(
        [rel_sum.reshape(-1, 128), back[images * 6 :].reshape(-1, 128), b_one_grad.reshape(-1, 128)],
        axis=0,
    )
    bias_rows = half_ff // 128
    imgs_all, small_all = share(imgs, small, nw, nn)

    branch_half = lax.dynamic_slice_in_dim(branch, first_row, half_rows, 0) + branch_peer.astype(F32)
    tok_half = lax.dynamic_slice_in_dim(tok, first_row, half_rows, 0).astype(F32)
    attn_half = lax.dynamic_slice_in_dim(attn_out, first_row, half_rows, 0)
    mod_half = lax.dynamic_index_in_dim(mod, first_row // seq_len, 0, keepdims=False)
    out_phys = tok_half + mod_half[2] * attn_half + mod_half[5] * (branch_half + mod_half[7])
    output = mm(out_phys.astype(BF16), perm, NT).astype(BF16)

    att_grad, one_grad, two_grad, b_ada_grad, norm = collect_norm(
        att_part, mlp_part, imgs_all, emb_mine, silu_mine, small_all, perm, bias_rows, nw, nn, nm
    )
    grad_norm = norm[0, 0]
    clip_scale = jnp.minimum(1.0, 1.0 / (grad_norm + 1e-06))
    mlp_grad = jnp.stack([one_grad, two_grad], axis=1)
    rel_rows = 4 * HEADS * 2
    rel_grad = small_all[0:rel_rows].reshape(4, HEADS, 256).transpose(0, 2, 1).reshape(-1)[0:offset]
    rest_rows = 2 * D // 128
    small_grad = jnp.concatenate(
        [
            rel_grad,
            b_ada_grad.reshape(-1),
            small_all[rel_rows : rel_rows + rest_rows].reshape(-1),
        ]
    )
    bias_grad = small_all[rel_rows + rest_rows :].reshape(-1)
    att_new, att_mom_new, att_sec_new = adam_update(
        att_master, att_moment, att_second, att_grad, clip_scale
    )
    mlp_new, mlp_mom_new, mlp_sec_new = adam_update(
        mlp_master, mlp_moment, mlp_second, mlp_grad, clip_scale
    )
    small_new, small_mom_new, small_sec_new = adam_update(
        small_master, small_moment, small_second, small_grad, clip_scale
    )
    bias_new, bias_mom_new, bias_sec_new = adam_update(
        bias_master, bias_moment, bias_second, bias_grad, clip_scale
    )
    return (
        output,
        input_grad,
        att_new,
        att_mom_new,
        att_sec_new,
        mlp_new,
        mlp_mom_new,
        mlp_sec_new,
        small_new,
        small_mom_new,
        small_sec_new,
        bias_new,
        bias_mom_new,
        bias_sec_new,
        att_new.astype(BF16),
        mlp_new.astype(BF16),
        grad_norm,
    )


def solution(mesh):
    rows = P(GRID, None)
    cube = P(GRID, None, "mlp")
    return jax.shard_map(
        on_device,
        mesh=mesh,
        in_specs=(
            rows,
            P(GRID),
            P(),
            P(),
            P(("wide", "narrow", "mlp"), None),
            rows,
            rows,
            rows,
            cube,
            cube,
            cube,
            P(),
            P(),
            P(),
            P("mlp"),
            P("mlp"),
            P("mlp"),
        ),
        out_specs=(
            P(("wide", "narrow", "mlp"), None),
            rows,
            rows,
            rows,
            rows,
            cube,
            cube,
            cube,
            P(),
            P(),
            P(),
            P("mlp"),
            P("mlp"),
            P("mlp"),
            rows,
            cube,
            P(),
        ),
        check_vma=False,
    )
```

```python
from functools import partial
import math

import jax
import jax.numpy as jnp
from jax import lax
from jax.experimental import pallas as pl
from jax.experimental.pallas import tpu as pltpu
from jax.sharding import PartitionSpec as P

D = 1152
HEADS = 16
HD = 72
NREL = 961
STEP = 10

HIGH = lax.Precision.HIGHEST
F32 = jnp.float32
BF16 = jnp.bfloat16
GRID = ("wide", "narrow")
NN = (((1,), (0,)), ((), ()))
TN = (((0,), (0,)), ((), ()))
NT = (((1,), (1,)), ((), ()))
INV_ROOT = 1.0 / math.sqrt(HD)
MESH = pl.DeviceIdType.MESH
ANY = pl.BlockSpec(memory_space=pl.ANY)
ATT = 4 * D
GROUP = 4
TILE = 768
VMEM_BYTES = 58 * 1024 * 1024


def mm(a, b, dims=NN):
    return lax.dot_general(a, b, dims, preferred_element_type=F32)


def mm_exact(a, b, dims=NN):
    return lax.dot_general(a, b, dims, precision=HIGH, preferred_element_type=F32)


def norm_stats(values):
    center = values - jnp.mean(values, axis=-1, keepdims=True)
    inv_std = lax.rsqrt(jnp.mean(center * center, axis=-1, keepdims=True) + 1e-06)
    return (center * inv_std, inv_std)


def norm_back(grad_normed, normed, inv_std):
    mean_grad = jnp.mean(grad_normed, axis=-1, keepdims=True)
    mean_proj = jnp.mean(grad_normed * normed, axis=-1, keepdims=True)
    return (grad_normed - mean_grad - normed * mean_proj) * inv_std


def time_embed(steps_int):
    half_dim = D // 2
    frequency = jnp.exp(-math.log(10000.0) * jnp.arange(half_dim).astype(F32) / half_dim)
    angles = steps_int.astype(F32)[:, None] * frequency[None, :]
    return jnp.concatenate([jnp.cos(angles), jnp.sin(angles)], axis=1)


def adam_update(weight, moment, second, grad, clip_scale):
    scaled = grad * clip_scale
    moment_new = 0.9 * moment + 0.1 * scaled
    second_new = 0.999 * second + 0.001 * scaled * scaled
    rate = 1.5 / math.sqrt(D)
    direction = (
        moment_new / (1.0 - 0.9**STEP) / (jnp.sqrt(second_new / (1.0 - 0.999**STEP)) + 1e-08)
    )
    return (weight - rate * (direction + 0.1 * weight), moment_new, second_new)


def exact_parts(values):
    first = values.astype(BF16)
    rest = values - first.astype(F32)
    second = rest.astype(BF16)
    return (first, second, (rest - second.astype(F32)).astype(BF16))


def mm_split(a, b, dims=NN):
    one, two, three = exact_parts(a)
    return mm(one, b, dims) + mm(two, b, dims) + mm(three, b, dims)


def params(**kw):
    return pltpu.CompilerParams(vmem_limit_bytes=VMEM_BYTES, **kw)


def cost(flops, nbytes):
    return pl.CostEstimate(flops=flops, bytes_accessed=nbytes, transcendentals=0)


def position():
    return (lax.axis_index("wide"), lax.axis_index("narrow"), lax.axis_index("mlp"))


def remote(src, dst, send, recv, device):
    return pltpu.make_async_remote_copy(
        src_ref=src, dst_ref=dst, send_sem=send, recv_sem=recv, device_id=device, device_id_type=MESH
    )


def greet_group(nw, nn, with_mlp):
    w, n, m = position()
    mine = w * nn + n
    groups = nw * nn
    bar = pltpu.get_barrier_semaphore()

    def ask(k, carry):
        other = lax.rem(mine + k, groups)
        pl.semaphore_signal(
            bar, inc=1, device_id=(lax.div(other, nn), lax.rem(other, nn), m), device_id_type=MESH
        )
        return carry

    lax.fori_loop(1, groups, ask, 0)
    if with_mlp:
        pl.semaphore_signal(bar, inc=1, device_id=(w, n, 1 - m), device_id_type=MESH)
    pl.semaphore_wait(bar, groups - 1 + (1 if with_mlp else 0))


def pack_body(owners_ref, att_ref, mlp_ref, out_ref, perm_ref):
    rows = att_ref.shape[0]
    half = mlp_ref.shape[2]
    line = lax.broadcasted_iota(jnp.int32, (D, 128), 0)
    block = line // rows
    place = line - block * rows
    for b in range(owners_ref.shape[0]):
        place = place + jnp.where(block == b, owners_ref[b] * rows, 0)
    col = lax.broadcasted_iota(jnp.int32, (D, 128), 1)
    for j in range(D // 128):
        perm_ref[:, j * 128 : (j + 1) * 128] = jnp.where(place == col + j * 128, 1.0, 0.0).astype(BF16)
    out_ref[:, 0 : 3 * D] = att_ref[:, 0 : 3 * D].astype(BF16)
    out_ref[:, 3 * D : ATT] = mm(att_ref[:, 6 * D : 7 * D].astype(BF16), perm_ref[...]).astype(BF16)
    out_ref[:, ATT : ATT + half] = mlp_ref[:, 0, :].astype(BF16)
    out_ref[:, ATT + half : ATT + 2 * half] = mlp_ref[:, 1, :].astype(BF16)


def pack_weights(owners, att, mlp):
    rows, _, half = mlp.shape
    vmem = pl.BlockSpec(memory_space=pltpu.VMEM)
    return pl.pallas_call(
        pack_body,
        grid=(1,),
        in_specs=[
            pl.BlockSpec(memory_space=pltpu.SMEM),
            pl.BlockSpec((rows, 7 * D), lambda s: (0, 0)),
            pl.BlockSpec((rows, 2, half), lambda s: (0, 0, 0)),
        ],
        out_specs=[vmem, vmem],
        out_shape=[
            jax.ShapeDtypeStruct((rows, ATT + 2 * half), BF16),
            jax.ShapeDtypeStruct((D, D), BF16),
        ],
        compiler_params=params(),
        name="pack",
    )(owners, att, mlp)


def modul_body(nw, nn, emb_ref, att_ref, pick_ref, cot_ref, sum_ref, emb_out, silu_out, cot_out,
               gath, flat, parts, from_c, from_x, from_z, gs, gr, cs, cr, xs, xr, zs, zr, ys, yr, ls):
    w, n, m = position()
    nlo, nhi, groups = (2, nn // 2, nw * nn)
    c, x = (lax.rem(n, nlo), lax.div(n, nlo))
    half = cot_ref.shape[0]
    width = parts.shape[2]
    slot = (c * nhi + x) * nw + w
    mine = w * nn + n
    greet_group(nw, nn, True)
    rows = pl.ds(m * half, half)
    to_y = remote(cot_ref, cot_out.at[rows], ys, yr, (w, n, 1 - m))
    to_y.start()
    keep = pltpu.make_async_copy(cot_ref, cot_out.at[rows], ls)
    keep.start()
    gath[slot] = emb_ref[...]

    def copy_to(k):
        other = lax.rem(mine + k, groups)
        return remote(gath.at[slot], gath.at[slot], gs.at[k], gr.at[k], (lax.div(other, nn), lax.rem(other, nn), m))

    def send(k, carry):
        copy_to(k).start()
        return carry

    def finish(k, carry):
        copy_to(k).wait()
        return carry

    lax.fori_loop(1, groups, send, 0)
    lax.fori_loop(1, groups, finish, 0)
    picked = mm(gath[...].reshape(groups * 8, D), pick_ref[...]).astype(BF16)
    line = lax.broadcasted_iota(jnp.int32, (2 * groups, 8 * groups), 0)
    col = lax.broadcasted_iota(jnp.int32, (2 * groups, 8 * groups), 1)
    at = (line // 2) * 8 + line % 2
    emb = mm((col == at).astype(BF16), picked).astype(BF16)
    silu = mm((col == at + 2).astype(BF16), picked).astype(BF16)
    emb_out[...] = emb
    silu_out[...] = silu
    flat[:, 0 : 3 * D] = mm(emb, att_ref[:, 3 * D : 6 * D].astype(BF16))
    flat[:, 3 * D : 9 * D] = mm(silu, att_ref[:, 7 * D : 13 * D].astype(BF16))
    for g in range(groups):
        parts[g] = flat[2 * g : 2 * g + 2, :]
    block = nhi * nw
    other_c = (1 - c) * block
    mine_c = c * block
    hop = remote(parts.at[pl.ds(other_c, block)], from_c, cs, cr, (w, x * nlo + 1 - c, m))
    hop.start()
    hop.wait()
    parts[pl.ds(mine_c, block)] = parts[pl.ds(mine_c, block)] + from_c[...]
    hops = []
    for k in range(1, nhi):
        there = lax.rem(x + k, nhi)
        hop = remote(
            parts.at[pl.ds(mine_c + there * nw, nw)], from_x.at[k - 1], xs.at[k - 1], xr.at[k - 1], (w, there * nlo + c, m)
        )
        hop.start()
        hops.append(hop)
    for hop in hops:
        hop.wait()
    first = mine_c + x * nw
    total = parts[pl.ds(first, nw)]
    for k in range(1, nhi):
        total = total + from_x[k - 1]
    parts[pl.ds(first, nw)] = total
    hops = []
    for k in range(1, nw):
        there = lax.rem(w + k, nw)
        hop = remote(parts.at[first + there], from_z.at[k - 1], zs.at[k - 1], zr.at[k - 1], (there, n, m))
        hop.start()
        hops.append(hop)
    for hop in hops:
        hop.wait()
    total = parts[first + w]
    for k in range(1, nw):
        total = total + from_z[k - 1]
    sum_ref[...] = total
    keep.wait()
    to_y.wait()


def modul_exchange(emb_rows, att, pick, cot, nw, nn):
    groups = nw * nn
    nhi = nn // 2
    width = 9 * D
    half = cot.shape[0]
    vmem = pl.BlockSpec(memory_space=pltpu.VMEM)
    dma = pltpu.SemaphoreType.DMA
    return pl.pallas_call(
        partial(modul_body, nw, nn),
        in_specs=[vmem, vmem, vmem, ANY],
        out_specs=[vmem, vmem, vmem, ANY],
        out_shape=[
            jax.ShapeDtypeStruct((2, width), F32),
            jax.ShapeDtypeStruct((2 * groups, att.shape[0]), BF16),
            jax.ShapeDtypeStruct((2 * groups, att.shape[0]), BF16),
            jax.ShapeDtypeStruct((2 * half, D), BF16),
        ],
        scratch_shapes=[
            pltpu.VMEM((groups, 8, D), BF16),
            pltpu.VMEM((2 * groups, width), F32),
            pltpu.VMEM((groups, 2, width), F32),
            pltpu.VMEM((nhi * nw, 2, width), F32),
            pltpu.VMEM((max(nhi - 1, 1), nw, 2, width), F32),
            pltpu.VMEM((max(nw - 1, 1), 2, width), F32),
            dma((groups,)), dma((groups,)), dma, dma,
            dma((max(nhi - 1, 1),)), dma((max(nhi - 1, 1),)),
            dma((max(nw - 1, 1),)), dma((max(nw - 1, 1),)),
            dma, dma, dma,
        ],
        compiler_params=params(collective_id=1, has_side_effects=True),
        cost_estimate=cost(10**8, 3 * 10**7),
        name="modul_exchange",
    )(emb_rows, att, pick, cot)


def bias_body(index_ref, table_ref, bias_ref):
    low = jnp.bitwise_and(index_ref[...], 127)
    high = jnp.right_shift(index_ref[...], 7)
    for part in range(index_ref.shape[1] // 128):
        at = slice(part * 128, (part + 1) * 128)
        lo = low[:, at]
        hi = high[:, at]
        total = jnp.zeros(lo.shape, F32)
        for chunk in range(8):
            row = jnp.broadcast_to(table_ref[0, :, chunk * 128 : (chunk + 1) * 128], lo.shape)
            total = jnp.where(hi == chunk, jnp.take_along_axis(row, lo, axis=1), total)
        bias_ref[0, :, at] = total


def rel_bias(index_t, table_t, seq):
    return pl.pallas_call(
        bias_body,
        grid=(HEADS,),
        in_specs=[
            pl.BlockSpec((seq, seq), lambda h: (0, 0)),
            pl.BlockSpec((1, 1, 1024), lambda h: (h, 0, 0)),
        ],
        out_specs=pl.BlockSpec((1, seq, seq), lambda h: (h, 0, 0)),
        out_shape=jax.ShapeDtypeStruct((HEADS, seq, seq), F32),
        cost_estimate=cost(2 * 10**8, 4 * 10**7),
        name="rel_bias",
    )(index_t, table_t)


def front_body(tok_ref, cot_ref, perm_ref, mod_ref, tok_out, shaped_out, shaped_t, cot_out, branch_out, sums):
    moved = mm(tok_ref[...], perm_ref[...])
    tok_out[...] = moved.astype(BF16)
    normed, _ = norm_stats(moved)
    shaped = normed * (1.0 + mod_ref[0, 1:2]) + mod_ref[0, 0:1]
    shaped_out[...] = shaped.astype(BF16)
    shaped_t[...] = shaped.T.astype(BF16)
    cot = mm(cot_ref[...], perm_ref[...])
    cot_out[...] = cot.astype(BF16)
    branch = (cot * mod_ref[0, 5:6]).astype(BF16)
    branch_out[...] = branch
    sums[0, 0:1] = jnp.sum(branch.astype(F32), axis=0, keepdims=True)
    sums[0, 1:2] = jnp.sum(cot, axis=0, keepdims=True)
    sums[0, 2:8] = jnp.zeros((6, D), F32)


def front(tokens, cot, perm, mod, seq, images):
    rows = seq * images
    tok = pl.BlockSpec((seq, D), lambda n: (n, 0))
    per = pl.BlockSpec((1, 8, D), lambda n: (n, 0, 0))
    return pl.pallas_call(
        front_body,
        grid=(images,),
        in_specs=[tok, tok, pl.BlockSpec((D, D), lambda n: (0, 0)), per],
        out_specs=[tok, tok, pl.BlockSpec((D, seq), lambda n: (0, n)), tok, tok, per],
        out_shape=[
            jax.ShapeDtypeStruct((rows, D), BF16),
            jax.ShapeDtypeStruct((rows, D), BF16),
            jax.ShapeDtypeStruct((D, rows), BF16),
            jax.ShapeDtypeStruct((rows, D), BF16),
            jax.ShapeDtypeStruct((rows, D), BF16),
            jax.ShapeDtypeStruct((images, 8, D), F32),
        ],
        compiler_params=params(),
        cost_estimate=cost(4 * rows * D * D, 10**7),
        name="front",
    )(tokens, cot, perm, mod)


def attend_fwd_body(seq, images, own, shaped_ref, w_ref, time_ref, bias_ref, qkv_ref, out_ref, lse_ref):
    step = pl.program_id(0)

    @pl.when(step < 3)
    def _():
        made = mm(shaped_ref[...], w_ref[...])
        made = jnp.concatenate(
            [made[n * seq : (n + 1) * seq] + time_ref[n : n + 1] for n in range(images)], axis=0
        )
        qkv_ref[step] = made.T.reshape(HEADS, HD, seq * images).astype(BF16)

    @pl.when(step >= 3)
    def _():
        for j in range(GROUP):
            h = (step - 3) * GROUP + j
            query, key, value = [qkv_ref[p, h] for p in range(3)]
            place = own[h]
            for n in range(images):
                at = slice(n * seq, (n + 1) * seq)
                scores = mm(key[:, at], query[:, at], TN) * INV_ROOT + bias_ref[j]
                top = jnp.max(scores, axis=0, keepdims=True)
                weights = jnp.exp(scores - top)
                total = jnp.sum(weights, axis=0, keepdims=True)
                probs = (weights * (1.0 / total)).astype(BF16)
                out_ref[place, :, at] = mm(value[:, at], probs).astype(BF16)
                lse_ref[j, :, at] = top + jnp.log(total)


def attend_fwd(own, shaped, gathered, time_part, bias, seq, images):
    rows = seq * images

    def part(s):
        return jnp.minimum(s, 2)

    def group(s):
        return jnp.maximum(s - 3, 0)

    return pl.pallas_call(
        partial(attend_fwd_body, seq, images),
        grid_spec=pltpu.PrefetchScalarGridSpec(
            num_scalar_prefetch=1,
            grid=(3 + HEADS // GROUP,),
            in_specs=[
                pl.BlockSpec((rows, D), lambda s, own: (0, 0)),
                pl.BlockSpec((D, D), lambda s, own: (0, part(s))),
                pl.BlockSpec((images, D), lambda s, own: (0, part(s))),
                pl.BlockSpec((GROUP, seq, seq), lambda s, own: (group(s), 0, 0)),
            ],
            out_specs=[
                pl.BlockSpec((3, HEADS, HD, rows), lambda s, own: (0, 0, 0, 0)),
                pl.BlockSpec((HEADS, HD, rows), lambda s, own: (0, 0, 0)),
                pl.BlockSpec((GROUP, 1, rows), lambda s, own: (group(s), 0, 0)),
            ],
        ),
        out_shape=[
            jax.ShapeDtypeStruct((3, HEADS, HD, rows), BF16),
            jax.ShapeDtypeStruct((HEADS, HD, rows), BF16),
            jax.ShapeDtypeStruct((HEADS, 1, rows), F32),
        ],
        compiler_params=params(),
        cost_estimate=cost(6 * 10**9, 2 * 10**7),
        name="attend_fwd",
    )(own, shaped, gathered, time_part, bias)


def mid_body(att_ref, w_ref, tok_ref, mod_ref, attn_out, shaped_out):
    attn = mm(att_ref[...], w_ref[...], TN) + mod_ref[0, 6:7]
    attn_out[...] = attn
    mid = tok_ref[...].astype(F32) + mod_ref[0, 2:3] * attn
    normed, _ = norm_stats(mid)
    shaped_out[...] = (normed * (1.0 + mod_ref[0, 4:5]) + mod_ref[0, 3:4]).astype(BF16)


def middle(att, gathered, tok, mod, seq, images):
    rows = seq * images
    row = pl.BlockSpec((seq, D), lambda n: (n, 0))
    return pl.pallas_call(
        mid_body,
        grid=(images,),
        in_specs=[
            pl.BlockSpec((D, seq), lambda n: (0, n)),
            pl.BlockSpec((D, D), lambda n: (0, 3)),
            row,
            pl.BlockSpec((1, 8, D), lambda n: (n, 0, 0)),
        ],
        out_specs=[row, row],
        out_shape=[jax.ShapeDtypeStruct((rows, D), F32), jax.ShapeDtypeStruct((rows, D), BF16)],
        compiler_params=params(),
        cost_estimate=cost(2 * rows * D * D, 10**7),
        name="middle",
    )(att, gathered, tok, mod)


def hidden_body(x_ref, gb_ref, one_ref, two_ref, bias_ref, hidden_ref, grad_ref, back_ref, bias_out, acc):
    step = pl.program_id(0)
    pre = mm(x_ref[...], one_ref[...]) + bias_ref[...]
    root = math.sqrt(2.0 / math.pi)
    square = pre * pre
    bend = jnp.tanh(root * (pre + 0.044715 * (square * pre)))
    rise = 0.5 * (1.0 + bend)
    hidden_ref[...] = (pre * rise).astype(BF16)
    slope = rise + 0.5 * pre * (1.0 - bend * bend) * (root * (1.0 + 3 * 0.044715 * square))
    grad = (mm(gb_ref[...], two_ref[...]) * slope).astype(BF16)
    grad_ref[...] = grad
    bias_out[...] = jnp.sum(grad.astype(F32), axis=0, keepdims=True)
    back = mm(grad, one_ref[...], NT)

    @pl.when(step == 0)
    def _():
        acc[...] = back

    @pl.when(step > 0)
    def _():
        acc[...] += back

    @pl.when(step == pl.num_programs(0) - 1)
    def _():
        back_ref[...] = acc[...].astype(BF16)


def hidden_block(n, x, gb, gathered, bias, seq):
    half = bias.shape[1]
    one, two = (ATT // TILE, (ATT + half) // TILE)
    image = pl.BlockSpec((seq, D), lambda f: (n, 0))
    made = pl.BlockSpec((seq, TILE), lambda f: (0, f))
    return pl.pallas_call(
        hidden_body,
        grid=(half // TILE,),
        in_specs=[
            image,
            image,
            pl.BlockSpec((D, TILE), lambda f: (0, one + f)),
            pl.BlockSpec((D, TILE), lambda f: (0, two + f)),
            pl.BlockSpec((1, TILE), lambda f: (0, f)),
        ],
        out_specs=[
            made,
            made,
            pl.BlockSpec((seq, D), lambda f: (0, 0)),
            pl.BlockSpec((1, TILE), lambda f: (0, f)),
        ],
        out_shape=[
            jax.ShapeDtypeStruct((seq, half), BF16),
            jax.ShapeDtypeStruct((seq, half), BF16),
            jax.ShapeDtypeStruct((seq, D), BF16),
            jax.ShapeDtypeStruct((1, half), F32),
        ],
        scratch_shapes=[pltpu.VMEM((seq, D), F32)],
        compiler_params=params(),
        cost_estimate=cost(6 * seq * D * half, 2 * 10**7),
        name="hidden_block",
    )(x, gb, gathered, gathered, bias)


def weight_body(seq, at_mlp, x_ref, gb_ref, two_ref, hid_a, hid_b, grad_a, grad_b, cot_ref,
                dw_ref, branch_ref, send_ref, gate_ref, x_t, gb_t):
    step = pl.program_id(0)

    @pl.when(step == 0)
    def _():
        x_t[...] = x_ref[...].T
        gb_t[...] = gb_ref[...].T

    hidden = jnp.concatenate([hid_a[...], hid_b[...]], axis=0)
    grad = jnp.concatenate([grad_a[...], grad_b[...]], axis=0)
    dw_ref[:, 0:TILE] = mm(x_t[...], grad).astype(BF16)
    dw_ref[:, TILE : 2 * TILE] = mm(gb_t[...], hidden).astype(BF16)
    branch = mm(hidden, two_ref[...], NT)

    @pl.when(step == 0)
    def _():
        branch_ref[...] = branch

    @pl.when(step > 0)
    def _():
        branch_ref[...] += branch

    @pl.when(step == pl.num_programs(0) - 1)
    def _():
        gate_ref[...] = jnp.zeros_like(gate_ref)
        for n in range(2):
            at = slice(n * seq, (n + 1) * seq)
            gate_ref[n : n + 1] = jnp.sum(
                cot_ref[at].astype(F32) * branch_ref[at], axis=0, keepdims=True
            )
        theirs = 1 - at_mlp[0]
        send_ref[...] = branch_ref[pl.ds(pl.multiple_of(theirs * seq, seq), seq)].astype(BF16)


def weight_block(at_mlp, x, gb, gathered, hiddens, grads, cot, seq):
    half = hiddens[0].shape[1]
    rows = 2 * seq
    two = (ATT + half) // TILE
    whole = pl.BlockSpec((rows, D), lambda f, at: (0, 0))
    made = pl.BlockSpec((seq, TILE), lambda f, at: (0, f))
    return pl.pallas_call(
        partial(weight_body, seq),
        grid_spec=pltpu.PrefetchScalarGridSpec(
            num_scalar_prefetch=1,
            grid=(half // TILE,),
            in_specs=[
                whole,
                whole,
                pl.BlockSpec((D, TILE), lambda f, at: (0, two + f)),
                made,
                made,
                made,
                made,
                whole,
            ],
            out_specs=[
                pl.BlockSpec((D, 2 * TILE), lambda f, at: (0, f)),
                whole,
                pl.BlockSpec((seq, D), lambda f, at: (0, 0)),
                pl.BlockSpec((8, D), lambda f, at: (0, 0)),
            ],
            scratch_shapes=[pltpu.VMEM((D, rows), BF16), pltpu.VMEM((D, rows), BF16)],
        ),
        out_shape=[
            jax.ShapeDtypeStruct((D, 2 * half), BF16),
            jax.ShapeDtypeStruct((rows, D), F32),
            jax.ShapeDtypeStruct((seq, D), BF16),
            jax.ShapeDtypeStruct((8, D), F32),
        ],
        compiler_params=params(),
        cost_estimate=cost(6 * rows * D * half, 3 * 10**7),
        name="weight_block",
    )(at_mlp, x, gb, gathered, hiddens[0], hiddens[1], grads[0], grads[1], cot)


def back_mid_body(own_a, own_b, peer_a, peer_b, attn_ref, tok_ref, cot_ref, mod_ref, w_ref,
                  grad_mid, grad_attn, grad_att_t, sums):
    attn = attn_ref[...]
    mid = tok_ref[...].astype(F32) + mod_ref[0, 2:3] * attn
    normed, inv = norm_stats(mid)
    first = pl.program_id(0) == 0
    grad = jnp.where(first, own_a[...], own_b[...]).astype(F32)
    grad = grad + jnp.where(first, peer_a[...], peer_b[...]).astype(F32)
    sums[0, 0:1] = jnp.sum(grad, axis=0, keepdims=True)
    sums[0, 1:2] = jnp.sum(grad * normed, axis=0, keepdims=True)
    grad = cot_ref[...].astype(F32) + norm_back(grad * (1.0 + mod_ref[0, 4:5]), normed, inv)
    grad_mid[...] = grad
    sums[0, 2:3] = jnp.sum(grad * attn, axis=0, keepdims=True)
    low = (grad * mod_ref[0, 2:3]).astype(BF16)
    sums[0, 3:4] = jnp.sum(low.astype(F32), axis=0, keepdims=True)
    sums[0, 4:8] = jnp.zeros((4, D), F32)
    grad_attn[...] = low
    grad_att_t[...] = mm(w_ref[...], low, NT).astype(BF16)


def back_middle(owns, peers, attn, tok, cot, mod, gathered, seq, images):
    rows = seq * images
    row = pl.BlockSpec((seq, D), lambda n: (n, 0))
    per = pl.BlockSpec((1, 8, D), lambda n: (n, 0, 0))
    one = pl.BlockSpec((seq, D), lambda n: (0, 0))
    return pl.pallas_call(
        back_mid_body,
        grid=(images,),
        in_specs=[one, one, one, one, row, row, row, per, pl.BlockSpec((D, D), lambda n: (0, 3))],
        out_specs=[
            row,
            row,
            pl.BlockSpec((D, seq), lambda n: (0, n)),
            per,
        ],
        out_shape=[
            jax.ShapeDtypeStruct((rows, D), F32),
            jax.ShapeDtypeStruct((rows, D), BF16),
            jax.ShapeDtypeStruct((D, rows), BF16),
            jax.ShapeDtypeStruct((images, 8, D), F32),
        ],
        compiler_params=params(),
        cost_estimate=cost(2 * rows * D * D, 10**7),
        name="back_middle",
    )(owns[0], owns[1], peers[0], peers[1], attn, tok, cot, mod, gathered)


def attend_bwd_body(seq, images, own, att_ref, ga_ref, shaped_ref, w_ref, qkv_ref, grad_ref, bias_ref, lse_ref,
                    dw_ref, acc_ref, ds_ref, time_ref, made):
    step = pl.program_id(0)
    groups = HEADS // GROUP
    rows = seq * images

    @pl.when(step < groups)
    def _():
        for j in range(GROUP):
            h = step * GROUP + j
            place = own[h]
            ds_sum = jnp.zeros((seq, seq), F32)
            for n in range(images):
                at = slice(n * seq, (n + 1) * seq)
                query, key, value = [qkv_ref[p, j, :, at] for p in range(3)]
                grad = grad_ref[place, :, at]
                probs = jnp.exp(mm(key, query, TN) * INV_ROOT + (bias_ref[j] - lse_ref[j, :, at]))
                grad_probs = mm(value, grad, TN)
                inner = jnp.sum(probs * grad_probs, axis=0, keepdims=True)
                ds = (probs * (grad_probs - inner)).astype(BF16)
                made[0, h, :, at] = mm(key, ds) * INV_ROOT
                made[1, h, :, at] = mm(query, ds, NT) * INV_ROOT
                made[2, h, :, at] = mm(grad, probs.astype(BF16), NT)
                ds_sum = ds_sum + ds.astype(F32)
            ds_ref[j] = ds_sum

    @pl.when((step >= groups) & (step < groups + 3))
    def _():
        p = step - groups
        across = made[p].reshape(D, rows)
        upright = across.T.astype(BF16)
        back = mm(upright, w_ref[...], NT)

        @pl.when(p == 0)
        def _():
            acc_ref[...] = back

        @pl.when(p > 0)
        def _():
            acc_ref[...] += back

        dw_ref[...] = mm(shaped_ref[...], across.astype(BF16), NT).astype(BF16)
        wide = upright.astype(F32)
        for n in range(images):
            time_ref[n : n + 1] = jnp.sum(wide[n * seq : (n + 1) * seq], axis=0, keepdims=True)

    @pl.when(step == groups + 3)
    def _():
        dw_ref[...] = mm(att_ref[...], ga_ref[...]).astype(BF16)


def attend_bwd(own, att, ga, shaped_t, gathered, qkv, grad, bias, lse, seq, images):
    rows = seq * images
    groups = HEADS // GROUP

    def group(s):
        return jnp.minimum(s, groups - 1)

    def part(s):
        return jnp.clip(s - groups, 0, 2)

    return pl.pallas_call(
        partial(attend_bwd_body, seq, images),
        grid_spec=pltpu.PrefetchScalarGridSpec(
            num_scalar_prefetch=1,
            grid=(groups + 4,),
            in_specs=[
                pl.BlockSpec((D, rows), lambda s, own: (0, 0)),
                pl.BlockSpec((rows, D), lambda s, own: (0, 0)),
                pl.BlockSpec((D, rows), lambda s, own: (0, 0)),
                pl.BlockSpec((D, D), lambda s, own: (0, part(s))),
                pl.BlockSpec((3, GROUP, HD, rows), lambda s, own: (0, group(s), 0, 0)),
                pl.BlockSpec((HEADS, HD, rows), lambda s, own: (0, 0, 0)),
                pl.BlockSpec((GROUP, seq, seq), lambda s, own: (group(s), 0, 0)),
                pl.BlockSpec((GROUP, 1, rows), lambda s, own: (group(s), 0, 0)),
            ],
            out_specs=[
                pl.BlockSpec((D, D), lambda s, own: (0, jnp.clip(s - groups, 0, 3))),
                pl.BlockSpec((rows, D), lambda s, own: (0, 0)),
                pl.BlockSpec((GROUP, seq, seq), lambda s, own: (group(s), 0, 0)),
                pl.BlockSpec((images, D), lambda s, own: (0, part(s))),
            ],
            scratch_shapes=[pltpu.VMEM((3, HEADS, HD, rows), F32)],
        ),
        out_shape=[
            jax.ShapeDtypeStruct((D, ATT), BF16),
            jax.ShapeDtypeStruct((rows, D), F32),
            jax.ShapeDtypeStruct((HEADS, seq, seq), F32),
            jax.ShapeDtypeStruct((images, 3 * D), F32),
        ],
        compiler_params=params(),
        cost_estimate=cost(16 * 10**9, 4 * 10**7),
        name="attend_bwd",
    )(own, att, ga, shaped_t, gathered, qkv, grad, bias, lse)


def finish_in_body(acc_ref, tok_ref, mod_ref, mid_ref, perm_ref, out_ref, sums):
    normed, inv = norm_stats(tok_ref[...].astype(F32))
    grad = acc_ref[...]
    sums[0, 0:1] = jnp.sum(grad, axis=0, keepdims=True)
    sums[0, 1:2] = jnp.sum(grad * normed, axis=0, keepdims=True)
    sums[0, 2:8] = jnp.zeros((6, D), F32)
    grad = mid_ref[...] + norm_back(grad * (1.0 + mod_ref[0, 1:2]), normed, inv)
    out_ref[...] = mm_split(grad, perm_ref[...], NT)


def finish_in(acc, tok, mod, mid, perm, seq, images):
    rows = seq * images
    row = pl.BlockSpec((seq, D), lambda n: (n, 0))
    per = pl.BlockSpec((1, 8, D), lambda n: (n, 0, 0))
    return pl.pallas_call(
        finish_in_body,
        grid=(images,),
        in_specs=[row, row, per, row, pl.BlockSpec((D, D), lambda n: (0, 0))],
        out_specs=[row, per],
        out_shape=[jax.ShapeDtypeStruct((rows, D), F32), jax.ShapeDtypeStruct((images, 8, D), F32)],
        compiler_params=params(),
        cost_estimate=cost(6 * rows * D * D, 10**7),
        name="finish_in",
    )(acc, tok, mod, mid, perm)


CHUNKS = 3


def collect_body(nw, nn, nm, term_ref, img_ref, small_ref, out_ref, img_out, small_out,
                 own, from_c, one, from_x, two, from_z, gath, sc, sx, sz,
                 ls, cs, cr, xs, xr, zs, zr, ys, yr, ics, icr, ixs, ixr, izs, izr, tcs, tcr, txs, txr, tzs, tzr):
    w, n, m = position()
    nlo, nhi, groups = (2, nn // 2, nw * nn)
    c, x = (lax.rem(n, nlo), lax.div(n, nlo))
    slot = (c * nhi + x) * nw + w
    part = out_ref.shape[1] // nm
    width = part // CHUNKS
    sibling = (w, x * nlo + 1 - c, m)
    twin = (w, n, 1 - m)

    def along_x(k):
        there = lax.rem(x + k, nhi)
        return (there, (w, there * nlo + c, m))

    def along_z(k):
        there = lax.rem(w + k, nw)
        return (there, (there, n, m))

    greet_group(nw, nn, True)

    def cols(k):
        return pl.ds(pl.multiple_of(m * part + k * width, 128), width)

    def load(k):
        return pltpu.make_async_copy(term_ref.at[:, :, c, :, cols(k)], own.at[k], ls.at[k])

    def hop_c(k):
        return remote(term_ref.at[:, :, 1 - c, :, cols(k)], from_c.at[k], cs.at[k], cr.at[k], sibling)

    def hop_x(k, d):
        there, device = along_x(d)
        return remote(one.at[k, d - 1], from_x.at[k, d - 1], xs.at[k, d - 1], xr.at[k, d - 1], device)

    def hop_z(k, d):
        there, device = along_z(d)
        return remote(two.at[k, d - 1], from_z.at[k, d - 1], zs.at[k, d - 1], zr.at[k, d - 1], device)

    def hop_y(k):
        return remote(out_ref.at[:, cols(k)], out_ref.at[:, cols(k)], ys.at[k], yr.at[k], twin)

    for k in range(CHUNKS):
        hop_c(k).start()
        load(k).start()

    gath[slot] = img_ref[...]
    img_z = []
    for d in range(1, nw):
        there, device = along_z(d)
        img_z.append(remote(gath.at[slot], gath.at[slot], izs.at[d - 1], izr.at[d - 1], device))
    mine_x = pl.ds((c * nhi + x) * nw, nw)
    img_x = []
    for d in range(1, nhi):
        there, device = along_x(d)
        img_x.append(remote(gath.at[mine_x], gath.at[mine_x], ixs.at[d - 1], ixr.at[d - 1], device))
    mine_c = pl.ds(c * nhi * nw, nhi * nw)
    img_c = remote(gath.at[mine_c], gath.at[mine_c], ics, icr, sibling)
    sc[c] = small_ref[...]
    small_c = remote(sc.at[c], sc.at[c], tcs, tcr, sibling)
    small_x = []
    for d in range(1, nhi):
        there, device = along_x(d)
        small_x.append(remote(sx.at[x], sx.at[x], txs.at[d - 1], txr.at[d - 1], device))
    small_z = []
    for d in range(1, nw):
        there, device = along_z(d)
        small_z.append(remote(sz.at[w], sz.at[w], tzs.at[d - 1], tzr.at[d - 1], device))

    small_c.start()
    for hop in img_z:
        hop.start()

    def pair(k, zi, xi):
        return own[k, zi, xi].astype(F32) + from_c[k, zi, xi].astype(F32)

    def stage_a(k):
        hop_c(k).wait()
        load(k).wait()
        for d in range(1, nhi):
            there, _ = along_x(d)
            for zi in range(nw):
                one[k, d - 1, zi] = pair(k, zi, there).astype(BF16)
            hop_x(k, d).start()

    def chain(k, zi):
        total = pair(k, zi, x)
        for d in range(1, nhi):
            total = total + from_x[k, d - 1, zi].astype(F32)
        return total

    def stage_b(k):
        for d in range(1, nhi):
            hop_x(k, d).wait()
        for d in range(1, nw):
            there, _ = along_z(d)
            two[k, d - 1] = chain(k, there).astype(BF16)
            hop_z(k, d).start()

    def stage_c(k):
        for d in range(1, nw):
            hop_z(k, d).wait()
        total = chain(k, w)
        for d in range(1, nw):
            total = total + from_z[k, d - 1].astype(F32)
        out_ref[:, cols(k)] = total.astype(BF16)
        hop_y(k).start()

    stage_a(0)
    small_c.wait()
    sx[x] = sc[0] + sc[1]
    for hop in small_x:
        hop.start()
    stage_a(1)
    for hop in img_z:
        hop.wait()
    for hop in img_x:
        hop.start()
    stage_a(2)
    stage_b(0)
    for hop in small_x:
        hop.wait()
    total = sx[0]
    for k in range(1, nhi):
        total = total + sx[k]
    sz[w] = total
    for hop in small_z:
        hop.start()
    stage_b(1)
    stage_c(0)
    for hop in img_x:
        hop.wait()
    img_c.start()
    stage_b(2)
    stage_c(1)
    for hop in small_z:
        hop.wait()
    total = sz[0]
    for k in range(1, nw):
        total = total + sz[k]
    small_out[...] = total
    img_c.wait()
    for g in range(groups):
        img_out[2 * g : 2 * g + 2, :] = gath[g]
    stage_c(2)
    for k in range(CHUNKS):
        hop_y(k).wait()


def collect(term, imgs, small, nw, nn, nm):
    groups = nw * nn
    nhi = nn // 2
    rows = small.shape[0]
    img_width = imgs.shape[1]
    blk, cols = (term.shape[0] // groups, term.shape[1])
    width = cols // nm // CHUNKS
    vmem = pl.BlockSpec(memory_space=pltpu.VMEM)
    dma = pltpu.SemaphoreType.DMA
    hi, wi = (max(nhi - 1, 1), max(nw - 1, 1))
    many = dma((CHUNKS,))
    return pl.pallas_call(
        partial(collect_body, nw, nn, nm),
        in_specs=[ANY, vmem, vmem],
        out_specs=[vmem, vmem, vmem],
        out_shape=[
            jax.ShapeDtypeStruct((blk, cols), BF16),
            jax.ShapeDtypeStruct((2 * groups, img_width), F32),
            jax.ShapeDtypeStruct(small.shape, F32),
        ],
        scratch_shapes=[
            pltpu.VMEM((CHUNKS, nw, nhi, blk, width), BF16),
            pltpu.VMEM((CHUNKS, nw, nhi, blk, width), BF16),
            pltpu.VMEM((CHUNKS, hi, nw, blk, width), BF16),
            pltpu.VMEM((CHUNKS, hi, nw, blk, width), BF16),
            pltpu.VMEM((CHUNKS, wi, blk, width), BF16),
            pltpu.VMEM((CHUNKS, wi, blk, width), BF16),
            pltpu.VMEM((groups, 2, img_width), F32),
            pltpu.VMEM((2, rows, 128), F32),
            pltpu.VMEM((nhi, rows, 128), F32),
            pltpu.VMEM((nw, rows, 128), F32),
            many, many, many, dma((CHUNKS, hi)), dma((CHUNKS, hi)), dma((CHUNKS, wi)), dma((CHUNKS, wi)), many, many,
            dma, dma, dma((hi,)), dma((hi,)), dma((wi,)), dma((wi,)),
            dma, dma, dma((hi,)), dma((hi,)), dma((wi,)), dma((wi,)),
        ],
        compiler_params=params(collective_id=2, has_side_effects=True),
        cost_estimate=cost(10**8, 3 * 10**7),
        name="collect",
    )(term.reshape(nw, nhi, 2, blk, cols), imgs, small)


def norm_body(nw, nn, nm, bias_rows, att_ref, mlp_ref, img_ref, emb_ref, silu_ref, small_ref, perm_ref,
              att_out, mlp_out, ada_out, norm_out, slots, ss, sr):
    w, n, m = position()
    groups = nw * nn
    count = groups * nm
    mine = (w * nn + n) * nm + m
    bar = pltpu.get_barrier_semaphore()

    def who(k):
        other = lax.rem(mine + k, count)
        pair = lax.div(other, nm)
        return (lax.div(pair, nn), lax.rem(pair, nn), lax.rem(other, nm))

    def ask(k, carry):
        pl.semaphore_signal(bar, inc=1, device_id=who(k), device_id_type=MESH)
        return carry

    lax.fori_loop(1, count, ask, 0)
    emb = emb_ref[...]
    silu = silu_ref[...]
    att_sq = jnp.zeros((1, 1), F32)

    def tally(values):
        return jnp.sum(jnp.sum(values * values, axis=0, keepdims=True), axis=1, keepdims=True)

    part = att_ref[:, 0 : 3 * D].astype(F32)
    att_out[:, 0 : 3 * D] = part
    att_sq = att_sq + tally(part)
    imgs = exact_parts(img_ref[:, 0 : 3 * D])
    part = mm(emb, imgs[0], TN) + mm(emb, imgs[1], TN) + mm(emb, imgs[2], TN)
    att_out[:, 3 * D : 6 * D] = part
    att_sq = att_sq + tally(part)
    part = mm(att_ref[:, 3 * D :], perm_ref[...], NT)
    att_out[:, 6 * D : 7 * D] = part
    att_sq = att_sq + tally(part)
    ada = img_ref[:, 3 * D :]
    ada_sum = jnp.sum(ada, axis=0, keepdims=True)
    ada_out[...] = ada_sum
    imgs = exact_parts(ada)
    part = mm(silu, imgs[0], TN) + mm(silu, imgs[1], TN) + mm(silu, imgs[2], TN)
    att_out[:, 7 * D :] = part
    att_sq = att_sq + tally(part)
    mlp_sq = jnp.zeros((1, 1), F32)
    for f in range(mlp_ref.shape[1] // (2 * TILE)):
        at = slice(f * TILE, (f + 1) * TILE)
        part = mlp_ref[:, 2 * f * TILE : (2 * f + 1) * TILE].astype(F32)
        mlp_out[:, 0, at] = part
        mlp_sq = mlp_sq + tally(part)
        part = mlp_ref[:, (2 * f + 1) * TILE : (2 * f + 2) * TILE].astype(F32)
        mlp_out[:, 1, at] = part
        mlp_sq = mlp_sq + tally(part)
    shared_rows = small_ref.shape[0] - bias_rows
    small_sq = tally(small_ref[0:shared_rows]) + tally(ada_sum)
    bias_sq = tally(small_ref[shared_rows:])
    local = mlp_sq + att_sq / nm + small_sq / count + bias_sq / groups
    slots[mine] = jnp.broadcast_to(local, (8, 128))
    pl.semaphore_wait(bar, count - 1)

    def copy_to(k):
        return remote(slots.at[mine], slots.at[mine], ss.at[k], sr.at[k], who(k))

    def send(k, carry):
        copy_to(k).start()
        return carry

    def finish(k, carry):
        copy_to(k).wait()
        return carry

    lax.fori_loop(1, count, send, 0)
    lax.fori_loop(1, count, finish, 0)
    norm_out[...] = jnp.sqrt(jnp.sum(slots[...], axis=0))


def output_body(at_mlp, branch_ref, peer_ref, tok_ref, attn_ref, mod_ref, perm_ref, out_ref):
    branch = branch_ref[...] + peer_ref[...].astype(F32) + mod_ref[0, 7:8]
    mid = tok_ref[...].astype(F32) + mod_ref[0, 2:3] * attn_ref[...]
    out = (mid + mod_ref[0, 5:6] * branch).astype(BF16)
    out_ref[...] = mm(out, perm_ref[...], NT).astype(BF16)


def make_output(at_mlp, branch, peer, tok, attn, mod, perm, seq):
    mine = pl.BlockSpec((seq, D), lambda s, at: (at[0], 0))
    zero = pl.BlockSpec((seq, D), lambda s, at: (0, 0))
    return pl.pallas_call(
        output_body,
        grid_spec=pltpu.PrefetchScalarGridSpec(
            num_scalar_prefetch=1,
            grid=(1,),
            in_specs=[
                mine,
                zero,
                mine,
                mine,
                pl.BlockSpec((1, 8, D), lambda s, at: (at[0], 0, 0)),
                pl.BlockSpec((D, D), lambda s, at: (0, 0)),
            ],
            out_specs=zero,
        ),
        out_shape=jax.ShapeDtypeStruct((seq, D), BF16),
        compiler_params=params(),
        cost_estimate=cost(2 * seq * D * D, 10**7),
        name="make_output",
    )(at_mlp, branch, peer, tok, attn, mod, perm)


def collect_norm(att, mlp, imgs, emb, silu, small, perm, bias_rows, nw, nn, nm):
    rows = att.shape[0]
    half = mlp.shape[1] // 2
    count = nw * nn * nm
    dma = pltpu.SemaphoreType.DMA
    return pl.pallas_call(
        partial(norm_body, nw, nn, nm, bias_rows),
        out_shape=[
            jax.ShapeDtypeStruct((rows, 13 * D), F32),
            jax.ShapeDtypeStruct((rows, 2, half), F32),
            jax.ShapeDtypeStruct((1, 6 * D), F32),
            jax.ShapeDtypeStruct((8, 128), F32),
        ],
        scratch_shapes=[pltpu.VMEM((count, 8, 128), F32), dma((count,)), dma((count,))],
        compiler_params=params(collective_id=3, has_side_effects=True),
        cost_estimate=cost(10**8, 10**7),
        name="collect_norm",
    )(att, mlp, imgs, emb, silu, small, perm)


def rel_grad_body(step, ds_ref, index_ref, out_ref):
    @pl.when(pl.program_id(0) == 0)
    def _():
        out_ref[...] = jnp.zeros_like(out_ref)

    index = index_ref[0]
    low = jnp.bitwise_and(index, 255)
    high = jnp.right_shift(index, 8)
    bucket = lax.broadcasted_iota(jnp.int32, (256, index.shape[1]), 0)
    hot = jnp.where(bucket == low, 1.0, 0.0).astype(BF16)
    turned = jnp.swapaxes(ds_ref[...], 0, 1)
    total = jnp.concatenate([turned[j] for j in range(step)], axis=1)
    picked = jnp.concatenate([jnp.where(high == a, total, 0.0) for a in range(4)], axis=0)
    out_ref[...] += mm(picked.astype(BF16), hot, NT)


def rel_grad_sum(ds, index_t, seq):
    step = 32
    return pl.pallas_call(
        partial(rel_grad_body, step),
        grid=(seq // step,),
        in_specs=[
            pl.BlockSpec((HEADS, step, seq), lambda j: (0, j, 0)),
            pl.BlockSpec((1, 1, step * seq), lambda j: (j, 0, 0)),
        ],
        out_specs=pl.BlockSpec((4 * HEADS, 256), lambda j: (0, 0)),
        out_shape=jax.ShapeDtypeStruct((4 * HEADS, 256), F32),
        compiler_params=params(),
        cost_estimate=cost(3 * 10**9, 10**7),
        name="rel_grad",
    )(ds, index_t.reshape(seq // step, 1, step * seq))


def on_device(
    tokens,
    timesteps,
    owners,
    rel_index,
    cotangent,
    att_master,
    att_moment,
    att_second,
    mlp_master,
    mlp_moment,
    mlp_second,
    small_master,
    small_moment,
    small_second,
    bias_master,
    bias_moment,
    bias_second,
):
    groups = owners.shape[0]
    rows_blk = att_master.shape[0]
    half_ff = mlp_master.shape[2]
    images = timesteps.shape[0]
    tok_rows = tokens.shape[0]
    half_rows = cotangent.shape[0]
    seq_len = tok_rows // images
    nw, nn, nm = (lax.axis_size("wide"), lax.axis_size("narrow"), lax.axis_size("mlp"))
    mlp_at = lax.axis_index("mlp")
    mine = lax.axis_index(GRID)
    moved = rows_blk == HD
    swap = [(i, nm - 1 - i) for i in range(nm)]

    place = (owners[:, None] * rows_blk + jnp.arange(rows_blk)[None, :]).reshape(D)
    pick = (place[:, None] == (mine * rows_blk + jnp.arange(rows_blk))[None, :]).astype(BF16)

    packed, perm = pack_weights(owners, att_master, mlp_master)
    perm_f = perm.astype(F32)
    gathered = lax.all_gather(packed, GRID, axis=0, tiled=True)

    time_emb = time_embed(timesteps)
    emb_rows = jnp.concatenate(
        [time_emb, jax.nn.silu(time_emb), jnp.zeros((8 - 2 * images, D), F32)], axis=0
    ).astype(BF16)
    summed, emb_mine, silu_mine, cot_all = modul_exchange(
        emb_rows, att_master, pick, cotangent, nw, nn
    )
    time_part = summed[:, 0 : 3 * D]
    offset = NREL * HEADS
    table_t = jnp.pad(small_master[0:offset].reshape(NREL, HEADS).T, ((0, 0), (0, 1024 - NREL)))
    b_ada = small_master[offset : offset + 6 * D]
    b_rest = small_master[offset + 6 * D : offset + 8 * D].reshape(1, 2, D)
    modulation = (summed[:, 3 * D :] + b_ada).reshape(images, 6, D)
    mod = jnp.concatenate([modulation, jnp.broadcast_to(b_rest, (images, 2, D))], axis=1)
    mod = mm_exact(mod.reshape(images * 8, D), perm_f).reshape(images, 8, D)
    index_t = rel_index.T
    bias = rel_bias(index_t, table_t.reshape(HEADS, 1, 1024), seq_len)

    tok, shaped, shaped_t, cot, grad_branch, front_sums = front(
        tokens, cot_all, perm, mod, seq_len, images
    )
    heads_at = owners if moved else jnp.arange(HEADS, dtype=jnp.int32)
    qkv, attended, lse = attend_fwd(heads_at, shaped, gathered, time_part, bias, seq_len, images)
    attended = attended.reshape(D, tok_rows)
    if not moved:
        attended = mm(perm, attended, TN).astype(BF16)
    attn_out, shaped_two = middle(attended, gathered, tok, mod, seq_len, images)
    made = []
    for n in range(images):
        made.append(
            hidden_block(n, shaped_two, grad_branch, gathered, bias_master.reshape(1, half_ff), seq_len)
        )
    owns = [part[2] for part in made]
    peers = [lax.ppermute(part, "mlp", swap) for part in owns]
    b_one_grad = made[0][3] + made[1][3]
    at_mlp = mlp_at.astype(jnp.int32).reshape(1)
    mlp_term, branch, branch_send, gate_own = weight_block(
        at_mlp,
        shaped_two,
        grad_branch,
        gathered,
        [part[0] for part in made],
        [part[1] for part in made],
        cot,
        seq_len,
    )
    mlp_part = lax.psum_scatter(mlp_term, GRID, scatter_dimension=0, tiled=True)

    grad_mid, grad_attn, grad_att, mid_sums = back_middle(
        owns, peers, attn_out, tok, cot, mod, gathered, seq_len, images
    )
    branch_send, gate_send, _ = lax.optimization_barrier((branch_send, gate_own, mid_sums))
    branch_peer = lax.ppermute(branch_send, "mlp", swap)
    gate_peer = lax.ppermute(gate_send, "mlp", swap)
    if not moved:
        grad_att = mm(perm, grad_att).astype(BF16)
    att_term, acc, ds, time_grad = attend_bwd(
        heads_at,
        attended,
        grad_attn,
        shaped_t,
        gathered,
        qkv,
        grad_att.reshape(HEADS, HD, tok_rows),
        bias,
        lse,
        seq_len,
        images,
    )
    rel_sum = rel_grad_sum(ds, index_t, seq_len)
    input_grad, in_sums = finish_in(acc, tok, mod, grad_mid, perm, seq_len, images)
    gate_two_grad = gate_own[0:images] + gate_peer[0:images] + mod[:, 7] * front_sums[:, 1]
    modul_grad = jnp.stack(
        [
            in_sums[:, 0],
            in_sums[:, 1],
            mid_sums[:, 2],
            mid_sums[:, 0],
            mid_sums[:, 1],
            gate_two_grad,
        ],
        axis=1,
    ).reshape(images * 6, D)
    back = mm_exact(
        jnp.concatenate(
            [
                modul_grad,
                jnp.sum(mid_sums[:, 3], axis=0, keepdims=True),
                jnp.sum(front_sums[:, 0], axis=0, keepdims=True),
            ],
            axis=0,
        ),
        perm_f,
        NT,
    )
    imgs = jnp.concatenate(
        [
            time_grad,
            back[0 : images * 6].reshape(images, 6 * D),
        ],
        axis=1,
    )
    small = jnp.concatenate(
        [rel_sum.reshape(-1, 128), back[images * 6 :].reshape(-1, 128), b_one_grad.reshape(-1, 128)],
        axis=0,
    )
    bias_rows = half_ff // 128
    att_part, imgs_all, small_all = collect(att_term, imgs, small, nw, nn, nm)

    output = make_output(at_mlp, branch, branch_peer, tok, attn_out, mod, perm, seq_len)

    att_grad, mlp_grad, b_ada_grad, norm = collect_norm(
        att_part, mlp_part, imgs_all, emb_mine, silu_mine, small_all, perm, bias_rows, nw, nn, nm
    )
    grad_norm = norm[0, 0]
    clip_scale = jnp.minimum(1.0, 1.0 / (grad_norm + 1e-06))
    rel_rows = 4 * HEADS * 2
    rel_grad = small_all[0:rel_rows].reshape(4, HEADS, 256).transpose(0, 2, 1).reshape(-1)[0:offset]
    rest_rows = 2 * D // 128
    small_grad = jnp.concatenate(
        [
            rel_grad,
            b_ada_grad.reshape(-1),
            small_all[rel_rows : rel_rows + rest_rows].reshape(-1),
        ]
    )
    bias_grad = small_all[rel_rows + rest_rows :].reshape(-1)
    att_new, att_mom_new, att_sec_new = adam_update(
        att_master, att_moment, att_second, att_grad, clip_scale
    )
    mlp_new, mlp_mom_new, mlp_sec_new = adam_update(
        mlp_master, mlp_moment, mlp_second, mlp_grad, clip_scale
    )
    small_new, small_mom_new, small_sec_new = adam_update(
        small_master, small_moment, small_second, small_grad, clip_scale
    )
    bias_new, bias_mom_new, bias_sec_new = adam_update(
        bias_master, bias_moment, bias_second, bias_grad, clip_scale
    )
    return (
        output,
        input_grad,
        att_new,
        att_mom_new,
        att_sec_new,
        mlp_new,
        mlp_mom_new,
        mlp_sec_new,
        small_new,
        small_mom_new,
        small_sec_new,
        bias_new,
        bias_mom_new,
        bias_sec_new,
        att_new.astype(BF16),
        mlp_new.astype(BF16),
        grad_norm,
    )


def solution(mesh):
    rows = P(GRID, None)
    cube = P(GRID, None, "mlp")
    return jax.shard_map(
        on_device,
        mesh=mesh,
        in_specs=(
            rows,
            P(GRID),
            P(),
            P(),
            P(("wide", "narrow", "mlp"), None),
            rows,
            rows,
            rows,
            cube,
            cube,
            cube,
            P(),
            P(),
            P(),
            P("mlp"),
            P("mlp"),
            P("mlp"),
        ),
        out_specs=(
            P(("wide", "narrow", "mlp"), None),
            rows,
            rows,
            rows,
            rows,
            cube,
            cube,
            cube,
            P(),
            P(),
            P(),
            P("mlp"),
            P("mlp"),
            P("mlp"),
            rows,
            cube,
            P(),
        ),
        check_vma=False,
    )
```

```python
from functools import partial
import math

import jax
import jax.numpy as jnp
from jax import lax
from jax.experimental import pallas as pl
from jax.experimental.pallas import tpu as pltpu
from jax.sharding import PartitionSpec as P

D = 1152
HEADS = 16
HD = 72
NREL = 961
STEP = 10

HIGH = lax.Precision.HIGHEST
F32 = jnp.float32
BF16 = jnp.bfloat16
GRID = ("wide", "narrow")
NN = (((1,), (0,)), ((), ()))
TN = (((0,), (0,)), ((), ()))
NT = (((1,), (1,)), ((), ()))
INV_ROOT = 1.0 / math.sqrt(HD)
MESH = pl.DeviceIdType.MESH
ANY = pl.BlockSpec(memory_space=pl.ANY)
ATT = 4 * D
GROUP = 4
TILE = 768
VMEM_BYTES = 63 * 1024 * 1024


def mm(a, b, dims=NN):
    return lax.dot_general(a, b, dims, preferred_element_type=F32)


def mm_exact(a, b, dims=NN):
    return lax.dot_general(a, b, dims, precision=HIGH, preferred_element_type=F32)


def norm_stats(values):
    center = values - jnp.mean(values, axis=-1, keepdims=True)
    inv_std = lax.rsqrt(jnp.mean(center * center, axis=-1, keepdims=True) + 1e-06)
    return (center * inv_std, inv_std)


def norm_back(grad_normed, normed, inv_std):
    mean_grad = jnp.mean(grad_normed, axis=-1, keepdims=True)
    mean_proj = jnp.mean(grad_normed * normed, axis=-1, keepdims=True)
    return (grad_normed - mean_grad - normed * mean_proj) * inv_std


def time_embed(steps_int):
    half_dim = D // 2
    frequency = jnp.exp(-math.log(10000.0) * jnp.arange(half_dim).astype(F32) / half_dim)
    angles = steps_int.astype(F32)[:, None] * frequency[None, :]
    return jnp.concatenate([jnp.cos(angles), jnp.sin(angles)], axis=1)


def adam_update(weight, moment, second, grad, clip_scale):
    scaled = grad * clip_scale
    moment_new = 0.9 * moment + 0.1 * scaled
    second_new = 0.999 * second + 0.001 * scaled * scaled
    rate = 1.5 / math.sqrt(D)
    direction = (
        moment_new / (1.0 - 0.9**STEP) / (jnp.sqrt(second_new / (1.0 - 0.999**STEP)) + 1e-08)
    )
    return (weight - rate * (direction + 0.1 * weight), moment_new, second_new)


def exact_parts(values):
    first = values.astype(BF16)
    rest = values - first.astype(F32)
    second = rest.astype(BF16)
    return (first, second, (rest - second.astype(F32)).astype(BF16))


def mm_split(a, b, dims=NN):
    one, two, three = exact_parts(a)
    return mm(one, b, dims) + mm(two, b, dims) + mm(three, b, dims)


def params(**kw):
    return pltpu.CompilerParams(vmem_limit_bytes=VMEM_BYTES, **kw)


def cost(flops, nbytes):
    return pl.CostEstimate(flops=flops, bytes_accessed=nbytes, transcendentals=0)


def position():
    return (lax.axis_index("wide"), lax.axis_index("narrow"), lax.axis_index("mlp"))


def remote(src, dst, send, recv, device):
    return pltpu.make_async_remote_copy(
        src_ref=src, dst_ref=dst, send_sem=send, recv_sem=recv, device_id=device, device_id_type=MESH
    )


def greet_group(nw, nn, with_mlp):
    w, n, m = position()
    mine = w * nn + n
    groups = nw * nn
    bar = pltpu.get_barrier_semaphore()

    def ask(k, carry):
        other = lax.rem(mine + k, groups)
        pl.semaphore_signal(
            bar, inc=1, device_id=(lax.div(other, nn), lax.rem(other, nn), m), device_id_type=MESH
        )
        return carry

    lax.fori_loop(1, groups, ask, 0)
    if with_mlp:
        pl.semaphore_signal(bar, inc=1, device_id=(w, n, 1 - m), device_id_type=MESH)
    pl.semaphore_wait(bar, groups - 1 + (1 if with_mlp else 0))


def pack_body(owners_ref, att_ref, mlp_ref, out_ref, perm_ref):
    rows = att_ref.shape[0]
    half = mlp_ref.shape[2]
    line = lax.broadcasted_iota(jnp.int32, (D, 128), 0)
    block = line // rows
    place = line - block * rows
    for b in range(owners_ref.shape[0]):
        place = place + jnp.where(block == b, owners_ref[b] * rows, 0)
    col = lax.broadcasted_iota(jnp.int32, (D, 128), 1)
    for j in range(D // 128):
        perm_ref[:, j * 128 : (j + 1) * 128] = jnp.where(place == col + j * 128, 1.0, 0.0).astype(BF16)
    out_ref[:, 0 : 3 * D] = att_ref[:, 0 : 3 * D].astype(BF16)
    out_ref[:, 3 * D : ATT] = mm(att_ref[:, 6 * D : 7 * D].astype(BF16), perm_ref[...]).astype(BF16)
    out_ref[:, ATT : ATT + half] = mlp_ref[:, 0, :].astype(BF16)
    out_ref[:, ATT + half : ATT + 2 * half] = mlp_ref[:, 1, :].astype(BF16)


def pack_weights(owners, att, mlp):
    rows, _, half = mlp.shape
    vmem = pl.BlockSpec(memory_space=pltpu.VMEM)
    return pl.pallas_call(
        pack_body,
        grid=(1,),
        in_specs=[
            pl.BlockSpec(memory_space=pltpu.SMEM),
            pl.BlockSpec((rows, 7 * D), lambda s: (0, 0)),
            pl.BlockSpec((rows, 2, half), lambda s: (0, 0, 0)),
        ],
        out_specs=[vmem, vmem],
        out_shape=[
            jax.ShapeDtypeStruct((rows, ATT + 2 * half), BF16),
            jax.ShapeDtypeStruct((D, D), BF16),
        ],
        compiler_params=params(),
        name="pack",
    )(owners, att, mlp)


def modul_body(nw, nn, emb_ref, att_ref, pick_ref, cot_ref, sum_ref, emb_out, silu_out, cot_out,
               gath, flat, parts, from_c, from_x, from_z, gs, gr, cs, cr, xs, xr, zs, zr, ys, yr, ls):
    w, n, m = position()
    nlo, nhi, groups = (2, nn // 2, nw * nn)
    c, x = (lax.rem(n, nlo), lax.div(n, nlo))
    half = cot_ref.shape[0]
    width = parts.shape[2]
    slot = (c * nhi + x) * nw + w
    mine = w * nn + n
    greet_group(nw, nn, True)
    rows = pl.ds(m * half, half)
    to_y = remote(cot_ref, cot_out.at[rows], ys, yr, (w, n, 1 - m))
    to_y.start()
    keep = pltpu.make_async_copy(cot_ref, cot_out.at[rows], ls)
    keep.start()
    gath[slot] = emb_ref[...]

    def copy_to(k):
        other = lax.rem(mine + k, groups)
        return remote(gath.at[slot], gath.at[slot], gs.at[k], gr.at[k], (lax.div(other, nn), lax.rem(other, nn), m))

    def send(k, carry):
        copy_to(k).start()
        return carry

    def finish(k, carry):
        copy_to(k).wait()
        return carry

    lax.fori_loop(1, groups, send, 0)
    lax.fori_loop(1, groups, finish, 0)
    picked = mm(gath[...].reshape(groups * 8, D), pick_ref[...]).astype(BF16)
    line = lax.broadcasted_iota(jnp.int32, (2 * groups, 8 * groups), 0)
    col = lax.broadcasted_iota(jnp.int32, (2 * groups, 8 * groups), 1)
    at = (line // 2) * 8 + line % 2
    emb = mm((col == at).astype(BF16), picked).astype(BF16)
    silu = mm((col == at + 2).astype(BF16), picked).astype(BF16)
    emb_out[...] = emb
    silu_out[...] = silu
    flat[:, 0 : 3 * D] = mm(emb, att_ref[:, 3 * D : 6 * D].astype(BF16))
    flat[:, 3 * D : 9 * D] = mm(silu, att_ref[:, 7 * D : 13 * D].astype(BF16))
    for g in range(groups):
        parts[g] = flat[2 * g : 2 * g + 2, :]
    block = nhi * nw
    other_c = (1 - c) * block
    mine_c = c * block
    hop = remote(parts.at[pl.ds(other_c, block)], from_c, cs, cr, (w, x * nlo + 1 - c, m))
    hop.start()
    hop.wait()
    parts[pl.ds(mine_c, block)] = parts[pl.ds(mine_c, block)] + from_c[...]
    hops = []
    for k in range(1, nhi):
        there = lax.rem(x + k, nhi)
        hop = remote(
            parts.at[pl.ds(mine_c + there * nw, nw)], from_x.at[k - 1], xs.at[k - 1], xr.at[k - 1], (w, there * nlo + c, m)
        )
        hop.start()
        hops.append(hop)
    for hop in hops:
        hop.wait()
    first = mine_c + x * nw
    total = parts[pl.ds(first, nw)]
    for k in range(1, nhi):
        total = total + from_x[k - 1]
    parts[pl.ds(first, nw)] = total
    hops = []
    for k in range(1, nw):
        there = lax.rem(w + k, nw)
        hop = remote(parts.at[first + there], from_z.at[k - 1], zs.at[k - 1], zr.at[k - 1], (there, n, m))
        hop.start()
        hops.append(hop)
    for hop in hops:
        hop.wait()
    total = parts[first + w]
    for k in range(1, nw):
        total = total + from_z[k - 1]
    sum_ref[...] = total
    keep.wait()
    to_y.wait()


def modul_exchange(emb_rows, att, pick, cot, nw, nn):
    groups = nw * nn
    nhi = nn // 2
    width = 9 * D
    half = cot.shape[0]
    vmem = pl.BlockSpec(memory_space=pltpu.VMEM)
    dma = pltpu.SemaphoreType.DMA
    return pl.pallas_call(
        partial(modul_body, nw, nn),
        in_specs=[vmem, vmem, vmem, ANY],
        out_specs=[vmem, vmem, vmem, ANY],
        out_shape=[
            jax.ShapeDtypeStruct((2, width), F32),
            jax.ShapeDtypeStruct((2 * groups, att.shape[0]), BF16),
            jax.ShapeDtypeStruct((2 * groups, att.shape[0]), BF16),
            jax.ShapeDtypeStruct((2 * half, D), BF16),
        ],
        scratch_shapes=[
            pltpu.VMEM((groups, 8, D), BF16),
            pltpu.VMEM((2 * groups, width), F32),
            pltpu.VMEM((groups, 2, width), F32),
            pltpu.VMEM((nhi * nw, 2, width), F32),
            pltpu.VMEM((max(nhi - 1, 1), nw, 2, width), F32),
            pltpu.VMEM((max(nw - 1, 1), 2, width), F32),
            dma((groups,)), dma((groups,)), dma, dma,
            dma((max(nhi - 1, 1),)), dma((max(nhi - 1, 1),)),
            dma((max(nw - 1, 1),)), dma((max(nw - 1, 1),)),
            dma, dma, dma,
        ],
        compiler_params=params(collective_id=1, has_side_effects=True),
        cost_estimate=cost(10**8, 3 * 10**7),
        name="modul_exchange",
    )(emb_rows, att, pick, cot)


def bias_body(index_ref, table_ref, bias_ref):
    low = jnp.bitwise_and(index_ref[...], 127)
    high = jnp.right_shift(index_ref[...], 7)
    for part in range(index_ref.shape[1] // 128):
        at = slice(part * 128, (part + 1) * 128)
        lo = low[:, at]
        hi = high[:, at]
        total = jnp.zeros(lo.shape, F32)
        for chunk in range(8):
            row = jnp.broadcast_to(table_ref[0, :, chunk * 128 : (chunk + 1) * 128], lo.shape)
            total = jnp.where(hi == chunk, jnp.take_along_axis(row, lo, axis=1), total)
        bias_ref[0, :, at] = total


def rel_bias(index_t, table_t, seq):
    return pl.pallas_call(
        bias_body,
        grid=(HEADS,),
        in_specs=[
            pl.BlockSpec((seq, seq), lambda h: (0, 0)),
            pl.BlockSpec((1, 1, 1024), lambda h: (h, 0, 0)),
        ],
        out_specs=pl.BlockSpec((1, seq, seq), lambda h: (h, 0, 0)),
        out_shape=jax.ShapeDtypeStruct((HEADS, seq, seq), F32),
        cost_estimate=cost(2 * 10**8, 4 * 10**7),
        name="rel_bias",
    )(index_t, table_t)


def front_body(tok_ref, cot_ref, perm_ref, mod_ref, tok_out, shaped_out, shaped_t, cot_out, branch_out, sums):
    moved = mm(tok_ref[...], perm_ref[...])
    tok_out[...] = moved.astype(BF16)
    normed, _ = norm_stats(moved)
    shaped = normed * (1.0 + mod_ref[0, 1:2]) + mod_ref[0, 0:1]
    shaped_out[...] = shaped.astype(BF16)
    shaped_t[...] = shaped.T.astype(BF16)
    cot = mm(cot_ref[...], perm_ref[...])
    cot_out[...] = cot.astype(BF16)
    branch = (cot * mod_ref[0, 5:6]).astype(BF16)
    branch_out[...] = branch
    sums[0, 0:1] = jnp.sum(branch.astype(F32), axis=0, keepdims=True)
    sums[0, 1:2] = jnp.sum(cot, axis=0, keepdims=True)
    sums[0, 2:8] = jnp.zeros((6, D), F32)


def front(tokens, cot, perm, mod, seq, images):
    rows = seq * images
    tok = pl.BlockSpec((seq, D), lambda n: (n, 0))
    per = pl.BlockSpec((1, 8, D), lambda n: (n, 0, 0))
    return pl.pallas_call(
        front_body,
        grid=(images,),
        in_specs=[tok, tok, pl.BlockSpec((D, D), lambda n: (0, 0)), per],
        out_specs=[tok, tok, pl.BlockSpec((D, seq), lambda n: (0, n)), tok, tok, per],
        out_shape=[
            jax.ShapeDtypeStruct((rows, D), BF16),
            jax.ShapeDtypeStruct((rows, D), BF16),
            jax.ShapeDtypeStruct((D, rows), BF16),
            jax.ShapeDtypeStruct((rows, D), BF16),
            jax.ShapeDtypeStruct((rows, D), BF16),
            jax.ShapeDtypeStruct((images, 8, D), F32),
        ],
        compiler_params=params(),
        cost_estimate=cost(4 * rows * D * D, 10**7),
        name="front",
    )(tokens, cot, perm, mod)


def attend_fwd_body(seq, images, own, shaped_ref, w_ref, time_ref, bias_ref, qkv_ref, out_ref, lse_ref):
    step = pl.program_id(0)

    @pl.when(step < 3)
    def _():
        made = mm(shaped_ref[...], w_ref[...])
        made = jnp.concatenate(
            [made[n * seq : (n + 1) * seq] + time_ref[n : n + 1] for n in range(images)], axis=0
        )
        qkv_ref[step] = made.T.reshape(HEADS, HD, seq * images).astype(BF16)

    @pl.when(step >= 3)
    def _():
        for j in range(GROUP):
            h = (step - 3) * GROUP + j
            query, key, value = [qkv_ref[p, h] for p in range(3)]
            place = own[h]
            for n in range(images):
                at = slice(n * seq, (n + 1) * seq)
                scores = mm(key[:, at], query[:, at], TN) * INV_ROOT + bias_ref[j]
                top = jnp.max(scores, axis=0, keepdims=True)
                weights = jnp.exp(scores - top)
                total = jnp.sum(weights, axis=0, keepdims=True)
                probs = (weights * (1.0 / total)).astype(BF16)
                out_ref[place, :, at] = mm(value[:, at], probs).astype(BF16)
                lse_ref[j, :, at] = top + jnp.log(total)


def attend_fwd(own, shaped, gathered, time_part, bias, seq, images):
    rows = seq * images

    def part(s):
        return jnp.minimum(s, 2)

    def group(s):
        return jnp.maximum(s - 3, 0)

    return pl.pallas_call(
        partial(attend_fwd_body, seq, images),
        grid_spec=pltpu.PrefetchScalarGridSpec(
            num_scalar_prefetch=1,
            grid=(3 + HEADS // GROUP,),
            in_specs=[
                pl.BlockSpec((rows, D), lambda s, own: (0, 0)),
                pl.BlockSpec((D, D), lambda s, own: (0, part(s))),
                pl.BlockSpec((images, D), lambda s, own: (0, part(s))),
                pl.BlockSpec((GROUP, seq, seq), lambda s, own: (group(s), 0, 0)),
            ],
            out_specs=[
                pl.BlockSpec((3, HEADS, HD, rows), lambda s, own: (0, 0, 0, 0)),
                pl.BlockSpec((HEADS, HD, rows), lambda s, own: (0, 0, 0)),
                pl.BlockSpec((GROUP, 1, rows), lambda s, own: (group(s), 0, 0)),
            ],
        ),
        out_shape=[
            jax.ShapeDtypeStruct((3, HEADS, HD, rows), BF16),
            jax.ShapeDtypeStruct((HEADS, HD, rows), BF16),
            jax.ShapeDtypeStruct((HEADS, 1, rows), F32),
        ],
        compiler_params=params(),
        cost_estimate=cost(6 * 10**9, 2 * 10**7),
        name="attend_fwd",
    )(own, shaped, gathered, time_part, bias)


def mid_body(att_ref, w_ref, tok_ref, mod_ref, attn_out, shaped_out):
    attn = mm(att_ref[...], w_ref[...], TN) + mod_ref[0, 6:7]
    attn_out[...] = attn
    mid = tok_ref[...].astype(F32) + mod_ref[0, 2:3] * attn
    normed, _ = norm_stats(mid)
    shaped_out[...] = (normed * (1.0 + mod_ref[0, 4:5]) + mod_ref[0, 3:4]).astype(BF16)


def middle(att, gathered, tok, mod, seq, images):
    rows = seq * images
    row = pl.BlockSpec((seq, D), lambda n: (n, 0))
    return pl.pallas_call(
        mid_body,
        grid=(images,),
        in_specs=[
            pl.BlockSpec((D, seq), lambda n: (0, n)),
            pl.BlockSpec((D, D), lambda n: (0, 3)),
            row,
            pl.BlockSpec((1, 8, D), lambda n: (n, 0, 0)),
        ],
        out_specs=[row, row],
        out_shape=[jax.ShapeDtypeStruct((rows, D), F32), jax.ShapeDtypeStruct((rows, D), BF16)],
        compiler_params=params(),
        cost_estimate=cost(2 * rows * D * D, 10**7),
        name="middle",
    )(att, gathered, tok, mod)


def once(shape, index):
    return pl.BlockSpec(shape, index, pipeline_mode=pl.Buffered(1))


def mlp_body(nw, nn, seq, tiles, direct, x_ref, gb_ref, one_ref, two_ref, bias_ref, cot_ref,
             term_ref, mine_ref, send_ref, gate_ref, bias_out, own_ref, peer_ref, *rest):
    if direct:
        first_ref, hidden, grads, x_t, gb_t, acc, branch_ref, peer_in, ts, tr, made, from_c, red, from_x, cs, cr, xs, xr = rest
    else:
        hidden, grads, x_t, gb_t, acc, branch_ref, peer_in, ts, tr = rest
    step = pl.program_id(0)
    w, n, m = position()
    nlo, nhi = (2, nn // 2)
    c, x = (lax.rem(n, nlo), lax.div(n, nlo))
    groups = nw * nn
    blk = D // groups
    sibling = (w, x * nlo + 1 - c, m)
    twin = (w, n, 1 - m)

    def to_twin(i):
        return remote(own_ref.at[i], peer_in.at[i], ts.at[i], tr.at[i], twin)

    def to_sibling(k):
        return remote(made.at[k, :, :, 1 - c], from_c.at[k], cs.at[k], cr.at[k], sibling)

    def along_x(d):
        there = lax.rem(x + d, nhi)
        return (there, (w, there * nlo + c, m))

    def hop_x(k, d):
        there, device = along_x(d)
        return remote(red.at[k, :, there], from_x.at[k, d - 1], xs.at[k, d - 1], xr.at[k, d - 1], device)

    @pl.when(step == 0)
    def _():
        bar = pltpu.get_barrier_semaphore()
        friends = [twin]
        if direct:
            friends = [twin, sibling] + [along_x(d)[1] for d in range(1, nhi)]
        for device in friends:
            pl.semaphore_signal(bar, inc=1, device_id=device, device_id_type=MESH)
        x_t[...] = x_ref[...].T
        gb_t[...] = gb_ref[...].T
        pl.semaphore_wait(bar, len(friends))

    for image in range(2):

        @pl.when((step >= image * tiles) & (step < (image + 1) * tiles))
        def _():
            f = step - image * tiles
            at = slice(image * seq, (image + 1) * seq)
            pre = mm(x_ref[at], one_ref[...]) + bias_ref[...]
            root = math.sqrt(2.0 / math.pi)
            square = pre * pre
            bend = jnp.tanh(root * (pre + 0.044715 * (square * pre)))
            rise = 0.5 * (1.0 + bend)
            hidden[f, at] = (pre * rise).astype(BF16)
            slope = rise + 0.5 * pre * (1.0 - bend * bend) * (root * (1.0 + 3 * 0.044715 * square))
            grad = (mm(gb_ref[at], two_ref[...]) * slope).astype(BF16)
            grads[f, at] = grad
            back = mm(grad, one_ref[...], NT)

            @pl.when(f == 0)
            def _():
                acc[...] = back

            @pl.when(f > 0)
            def _():
                acc[...] += back

            @pl.when(f == tiles - 1)
            def _():
                own_ref[image] = acc[...].astype(BF16)
                to_twin(image).start()

    def place(k, values):
        made[k] = values.reshape(nw, nhi, nlo, blk, TILE).astype(BF16)

    def combine(k):
        to_sibling(k).wait()
        return (made[k, :, :, c].astype(F32) + from_c[k].astype(F32)).astype(BF16)

    for f in range(tiles):

        @pl.when(step == 2 * tiles + f)
        def _():
            one_grad = mm(x_t[...], grads[f])
            two_grad = mm(gb_t[...], hidden[f])
            if direct:
                place(2 * f, one_grad)
                to_sibling(2 * f).start()
                place(2 * f + 1, two_grad)
                to_sibling(2 * f + 1).start()
            else:
                term_ref[:, 0:TILE] = one_grad.astype(BF16)
                term_ref[:, TILE : 2 * TILE] = two_grad.astype(BF16)
            bias_out[...] = jnp.sum(grads[f].astype(F32), axis=0, keepdims=True)
            branch = mm(hidden[f], two_ref[...], NT)
            branch_ref[...] = branch if f == 0 else branch_ref[...] + branch
            if direct and f == 0:
                for k in range(2):
                    red[k] = combine(k)
                    for d in range(1, nhi):
                        hop_x(k, d).start()

        if direct and f > 0:

            @pl.when(step == 2 * tiles + f + 1)
            def _():
                for half in range(2):
                    term_ref[:, :, :, half * TILE : (half + 1) * TILE] = combine(2 * f + half)

    @pl.when(step == 3 * tiles)
    def _():
        gate_ref[...] = jnp.zeros_like(gate_ref)
        for image in range(2):
            at = slice(image * seq, (image + 1) * seq)
            gate_ref[image : image + 1] = jnp.sum(
                cot_ref[at].astype(F32) * branch_ref[at], axis=0, keepdims=True
            )
        send_ref[...] = branch_ref[pl.ds(pl.multiple_of((1 - m) * seq, seq), seq)].astype(BF16)
        mine_ref[...] = branch_ref[pl.ds(pl.multiple_of(m * seq, seq), seq)]
        to_twin(0).wait()
        to_twin(1).wait()
        peer_ref[...] = peer_in[...]
        if direct:
            for k in range(2):
                for d in range(1, nhi):
                    hop_x(k, d).wait()
                total = red[k, :, x].astype(F32)
                for d in range(1, nhi):
                    total = total + from_x[k, d - 1].astype(F32)
                first_ref[:, :, k * TILE : (k + 1) * TILE] = total.astype(BF16)


def mlp_core(x, gb, gathered, bias, cot, seq, nw, nn):
    half = bias.shape[1]
    rows = 2 * seq
    tiles = half // TILE
    nhi = nn // 2
    blk = D // (nw * nn)
    one, two = (ATT // TILE, (ATT + half) // TILE)
    whole = once((rows, D), lambda s: (0, 0))
    vmem = pl.BlockSpec(memory_space=pltpu.VMEM)
    dma = pltpu.SemaphoreType.DMA

    def weight(s):
        return jnp.where(s < 3 * tiles, lax.rem(s, tiles), tiles - 1)

    def behind(s):
        return jnp.clip(s - 2 * tiles - 2, 0, tiles - 2)

    direct = blk % 8 == 0
    hi = max(nhi - 1, 1)
    if direct:
        term_spec = pl.BlockSpec((nw, nhi, blk, 2 * TILE), lambda s: (0, 0, 0, behind(s)))
        term_shape = jax.ShapeDtypeStruct((nw, nhi, blk, 2 * half - 2 * TILE), BF16)
    else:
        term_spec = pl.BlockSpec((D, 2 * TILE), lambda s: (0, jnp.clip(s - 2 * tiles, 0, tiles - 1)))
        term_shape = jax.ShapeDtypeStruct((D, 2 * half), BF16)
    return pl.pallas_call(
        partial(mlp_body, nw, nn, seq, tiles, direct),
        grid=(3 * tiles + 1,),
        in_specs=[
            whole,
            whole,
            pl.BlockSpec((D, TILE), lambda s: (0, one + jnp.where(s < 2 * tiles, lax.rem(s, tiles), tiles - 1))),
            pl.BlockSpec((D, TILE), lambda s: (0, two + weight(s))),
            pl.BlockSpec((1, TILE), lambda s: (0, weight(s))),
            whole,
        ],
        out_specs=[
            term_spec,
            vmem,
            vmem,
            vmem,
            pl.BlockSpec((1, TILE), lambda s: (0, jnp.clip(s - 2 * tiles, 0, tiles - 1))),
            vmem,
            vmem,
        ]
        + ([vmem] if direct else []),
        out_shape=[
            term_shape,
            jax.ShapeDtypeStruct((seq, D), F32),
            jax.ShapeDtypeStruct((seq, D), BF16),
            jax.ShapeDtypeStruct((8, D), F32),
            jax.ShapeDtypeStruct((1, half), F32),
            jax.ShapeDtypeStruct((2, seq, D), BF16),
            jax.ShapeDtypeStruct((2, seq, D), BF16),
        ]
        + ([jax.ShapeDtypeStruct((nw, blk, 2 * TILE), BF16)] if direct else []),
        scratch_shapes=[
            pltpu.VMEM((tiles, rows, TILE), BF16),
            pltpu.VMEM((tiles, rows, TILE), BF16),
            pltpu.VMEM((D, rows), BF16),
            pltpu.VMEM((D, rows), BF16),
            pltpu.VMEM((seq, D), F32),
            pltpu.VMEM((rows, D), F32),
            pltpu.VMEM((2, seq, D), BF16),
            dma((2,)),
            dma((2,)),
        ]
        + (
            [
                pltpu.VMEM((2 * tiles, nw, nhi, 2, blk, TILE), BF16),
                pltpu.VMEM((2 * tiles, nw, nhi, blk, TILE), BF16),
                pltpu.VMEM((2, nw, nhi, blk, TILE), BF16),
                pltpu.VMEM((2, hi, nw, blk, TILE), BF16),
                dma((2 * tiles,)),
                dma((2 * tiles,)),
                dma((2, hi)),
                dma((2, hi)),
            ]
            if direct
            else []
        ),
        compiler_params=params(collective_id=4, has_side_effects=True),
        cost_estimate=cost(12 * rows * D * half, 4 * 10**7),
        name="mlp_core",
    )(x, gb, gathered, gathered, bias, cot)


REL_ROWS = 32
REL_SUB = 16


def back_body(nw, nn, seq, images, moved, direct, own, att_ref, shaped_ref, w_ref, qkv_ref, bias_ref, lse_ref,
              index_ref, tok_ref, mod_ref, perm_ref, back_own, back_peer, attn_ref, cot_ref, mine_ref,
              send_ref, gate_ref, *rest):
    if direct:
        term_ref, first_ref = rest[:2]
        rest = rest[2:]
    dw_ref, time_ref, rel_ref, in_ref, sums, mid_sums, out_ref, gate_out = rest[:8]
    rest = rest[8:]
    if direct:
        part_ref = rest[0]
        rest = rest[1:]
    made, acc, ds_all, mid, ga, ga_t, keep, keep_mod, branch_in, gate_in, yb, yc, ybr, ycr = rest[:14]
    if direct:
        held, from_x, two, from_z, ls, xs, xr, zs, zr = rest[14:]
    step = pl.program_id(0)
    groups = HEADS // GROUP
    rows = seq * images
    att_at = images
    part_at = att_at + groups
    rel_at = part_at + 4
    end_at = rel_at + seq // REL_ROWS
    last = end_at + images
    w, n, m = position()
    nlo, nhi = (2, nn // 2)
    c, x = (lax.rem(n, nlo), lax.div(n, nlo))
    twin = (w, n, 1 - m)

    def along_x(d):
        there = lax.rem(x + d, nhi)
        return (there, (w, there * nlo + c, m))

    def along_z(d):
        there = lax.rem(w + d, nw)
        return (there, (there, n, m))

    def swap_branch():
        return remote(send_ref, branch_in, yb, ybr, twin)

    def swap_gate():
        return remote(gate_ref, gate_in, yc, ycr, twin)

    if direct:
        chunks = part_ref.shape[1] // TILE

        def load(k):
            return pltpu.make_async_copy(
                term_ref.at[:, x, :, pl.ds((k - 2) * TILE, TILE)], held.at[k - 2], ls.at[k - 2]
            )

        def hop_x(k, d):
            there, device = along_x(d)
            return remote(
                term_ref.at[:, there, :, pl.ds((k - 2) * TILE, TILE)],
                from_x.at[k - 2, d - 1], xs.at[k - 2, d - 1], xr.at[k - 2, d - 1], device,
            )

        def hop_z(k, d):
            there, device = along_z(d)
            return remote(two.at[k, d - 1], from_z.at[k, d - 1], zs.at[k, d - 1], zr.at[k, d - 1], device)

        def chain(k, zi):
            if k < 2:
                return first_ref[zi, :, k * TILE : (k + 1) * TILE].astype(F32)
            total = held[k - 2, zi].astype(F32)
            for d in range(1, nhi):
                total = total + from_x[k - 2, d - 1, zi].astype(F32)
            return total

        def stage_x(k):
            if k >= 2:
                load(k).wait()
                for d in range(1, nhi):
                    hop_x(k, d).wait()
            for d in range(1, nw):
                there, _ = along_z(d)
                two[k, d - 1] = chain(k, there).astype(BF16)
                hop_z(k, d).start()

        def stage_z(k):
            for d in range(1, nw):
                hop_z(k, d).wait()
            total = chain(k, w)
            for d in range(1, nw):
                total = total + from_z[k, d - 1].astype(F32)
            part_ref[:, k * TILE : (k + 1) * TILE] = total.astype(BF16)

    @pl.when(step == 0)
    def _():
        greet_group(nw, nn, True)
        if direct:
            for k in range(2, chunks):
                for d in range(1, nhi):
                    hop_x(k, d).start()
                load(k).start()
            stage_x(0)
            stage_x(1)
        swap_branch().start()
        swap_gate().start()

    for image in range(images):

        @pl.when(step == image)
        def _():
            at = slice(image * seq, (image + 1) * seq)
            attn = attn_ref[...]
            value = tok_ref[...].astype(F32) + mod_ref[0, 2:3] * attn

            @pl.when(m == image)
            def _():
                keep[...] = value
                keep_mod[...] = mod_ref[0]

            normed, inv = norm_stats(value)
            grad = back_own[0].astype(F32) + back_peer[0].astype(F32)
            mid_sums[0, 0:1] = jnp.sum(grad, axis=0, keepdims=True)
            mid_sums[0, 1:2] = jnp.sum(grad * normed, axis=0, keepdims=True)
            grad = cot_ref[...].astype(F32) + norm_back(grad * (1.0 + mod_ref[0, 4:5]), normed, inv)
            mid[at] = grad
            mid_sums[0, 2:3] = jnp.sum(grad * attn, axis=0, keepdims=True)
            low = (grad * mod_ref[0, 2:3]).astype(BF16)
            mid_sums[0, 3:4] = jnp.sum(low.astype(F32), axis=0, keepdims=True)
            mid_sums[0, 4:8] = jnp.zeros((4, D), F32)
            ga[at] = low
            turned = mm(w_ref[...], low, NT)
            if not moved:
                turned = mm(perm_ref[...], turned.astype(BF16))
            ga_t[:, :, at] = turned.reshape(HEADS, HD, seq).astype(BF16)

    @pl.when((step >= att_at) & (step < part_at))
    def _():
        for j in range(GROUP):
            h = (step - att_at) * GROUP + j
            place = own[h]
            ds_sum = jnp.zeros((seq, seq), F32)
            for image in range(images):
                at = slice(image * seq, (image + 1) * seq)
                query, key, value = [qkv_ref[p, j, :, at] for p in range(3)]
                grad = ga_t[place, :, at]
                probs = jnp.exp(mm(key, query, TN) * INV_ROOT + (bias_ref[j] - lse_ref[j, :, at]))
                grad_probs = mm(value, grad, TN)
                inner = jnp.sum(probs * grad_probs, axis=0, keepdims=True)
                ds = (probs * (grad_probs - inner)).astype(BF16)
                made[0, h, :, at] = (mm(key, ds) * INV_ROOT).astype(BF16)
                made[1, h, :, at] = (mm(query, ds, NT) * INV_ROOT).astype(BF16)
                made[2, h, :, at] = mm(grad, probs.astype(BF16), NT).astype(BF16)
                ds_sum = ds_sum + ds.astype(F32)
            ds_all[h] = ds_sum

    @pl.when((step >= part_at) & (step < part_at + 3))
    def _():
        p = step - part_at
        across = made[p].astype(F32).reshape(D, rows)
        upright = across.T.astype(BF16)
        back = mm(upright, w_ref[...], NT)

        @pl.when(p == 0)
        def _():
            acc[...] = back

        @pl.when(p > 0)
        def _():
            acc[...] += back

        dw_ref[...] = mm(shaped_ref[...], across.astype(BF16), NT).astype(BF16)
        wide = upright.astype(F32)
        for image in range(images):
            time_ref[image : image + 1] = jnp.sum(
                wide[image * seq : (image + 1) * seq], axis=0, keepdims=True
            )

    @pl.when(step == part_at + 3)
    def _():
        dw_ref[...] = mm(att_ref[...], ga[...]).astype(BF16)
        rel_ref[...] = jnp.zeros_like(rel_ref)

    @pl.when((step >= rel_at) & (step < end_at))
    def _():
        size = REL_SUB * seq
        bucket = lax.broadcasted_iota(jnp.int32, (256, size), 0)
        for part in range(REL_ROWS // REL_SUB):
            index = index_ref[0][:, part * size : (part + 1) * size]
            low = jnp.bitwise_and(index, 255)
            high = jnp.right_shift(index, 8)
            hot = jnp.where(bucket == low, 1.0, 0.0).astype(BF16)
            start = pl.multiple_of((step - rel_at) * REL_ROWS + part * REL_SUB, REL_SUB)
            turned = jnp.swapaxes(ds_all[:, pl.ds(start, REL_SUB), :], 0, 1)
            total = jnp.concatenate([turned[j] for j in range(REL_SUB)], axis=1)
            picked = jnp.concatenate([jnp.where(high == a, total, 0.0) for a in range(4)], axis=0)
            rel_ref[...] += mm(picked.astype(BF16), hot, NT)

    @pl.when((step >= end_at) & (step < last))
    def _():
        normed, inv = norm_stats(tok_ref[...].astype(F32))
        at = pl.ds(pl.multiple_of((step - end_at) * seq, seq), seq)
        grad = acc[at]
        sums[0, 0:1] = jnp.sum(grad, axis=0, keepdims=True)
        sums[0, 1:2] = jnp.sum(grad * normed, axis=0, keepdims=True)
        sums[0, 2:8] = jnp.zeros((6, D), F32)
        grad = mid[at] + norm_back(grad * (1.0 + mod_ref[0, 1:2]), normed, inv)
        in_ref[...] = mm_split(grad, perm_ref[...], NT)

    @pl.when(step == last)
    def _():
        swap_branch().wait()
        swap_gate().wait()
        gate_out[...] = gate_in[...]
        branch = mine_ref[...] + branch_in[...].astype(F32) + keep_mod[7:8]
        out = (keep[...] + keep_mod[5:6] * branch).astype(BF16)
        out_ref[...] = mm(out, perm_ref[...], NT).astype(BF16)

    if direct:
        spread = [0, 0, 2, 4, 6, part_at + 3]
        after = [4, 5, 7, rel_at + 1, rel_at + 5, last]
        for k in range(2, chunks):

            @pl.when(step == spread[min(k, 5)])
            def _(k=k):
                stage_x(k)

        for k in range(chunks):

            @pl.when(step == after[min(k, 5)])
            def _(k=k):
                stage_z(k)


def back_core(own, att, shaped_t, gathered, qkv, bias, lse, index_t, tok, mod, perm, back_own, back_peer,
              attn, cot, mine, send, gate, reduced, seq, images, nw, nn, moved):
    rows = seq * images
    groups = HEADS // GROUP
    att_at = images
    part_at = att_at + groups
    rel_at = part_at + 4
    end_at = rel_at + seq // REL_ROWS
    last = end_at + images
    nhi = nn // 2
    direct = len(reduced) == 2
    hi, wi = (max(nhi - 1, 1), max(nw - 1, 1))
    vmem = pl.BlockSpec(memory_space=pltpu.VMEM)
    dma = pltpu.SemaphoreType.DMA

    def group(s):
        return jnp.clip(s - att_at, 0, groups - 1)

    def part(s):
        return jnp.clip(s - part_at, 0, 2)

    def early(s):
        return jnp.minimum(s, images - 1)

    def both(s):
        return jnp.where(s < images, s, jnp.clip(s - end_at, 0, images - 1))

    def late(s):
        return jnp.clip(s - end_at, 0, images - 1)

    per = pl.BlockSpec((1, 8, D), lambda s, own: (both(s), 0, 0))
    swapped = once((1, seq, D), lambda s, own: (early(s), 0, 0))
    extra_in, extra_out, extra_shape, extra_scratch = ([], [], [], [])
    if direct:
        blk, cols = reduced[0].shape[2:]
        cols = cols + 2 * TILE
        chunks = cols // TILE
        extra_in = [ANY, once((nw, blk, 2 * TILE), lambda s, own: (0, 0, 0))]
        extra_out = [vmem]
        extra_shape = [jax.ShapeDtypeStruct((blk, cols), BF16)]
        extra_scratch = [
            pltpu.VMEM((chunks - 2, nw, blk, TILE), BF16),
            pltpu.VMEM((chunks - 2, hi, nw, blk, TILE), BF16),
            pltpu.VMEM((chunks, wi, blk, TILE), BF16),
            pltpu.VMEM((chunks, wi, blk, TILE), BF16),
            dma((chunks - 2,)),
            dma((chunks - 2, hi)),
            dma((chunks - 2, hi)),
            dma((chunks, wi)),
            dma((chunks, wi)),
        ]
    return pl.pallas_call(
        partial(back_body, nw, nn, seq, images, moved, direct),
        grid_spec=pltpu.PrefetchScalarGridSpec(
            num_scalar_prefetch=1,
            grid=(last + 1,),
            in_specs=[
                once((D, rows), lambda s, own: (0, 0)),
                once((D, rows), lambda s, own: (0, 0)),
                pl.BlockSpec((D, D), lambda s, own: (0, jnp.where(s < images, 3, part(s)))),
                pl.BlockSpec((3, GROUP, HD, rows), lambda s, own: (0, group(s), 0, 0)),
                pl.BlockSpec((GROUP, seq, seq), lambda s, own: (group(s), 0, 0)),
                pl.BlockSpec((GROUP, 1, rows), lambda s, own: (group(s), 0, 0)),
                pl.BlockSpec(
                    (1, 1, REL_ROWS * seq), lambda s, own: (jnp.clip(s - rel_at, 0, seq // REL_ROWS - 1), 0, 0)
                ),
                pl.BlockSpec((seq, D), lambda s, own: (both(s), 0)),
                per,
                once((D, D), lambda s, own: (0, 0)),
                swapped,
                swapped,
                once((seq, D), lambda s, own: (early(s), 0)),
                once((seq, D), lambda s, own: (early(s), 0)),
                once((seq, D), lambda s, own: (0, 0)),
                ANY,
                ANY,
            ]
            + extra_in,
            out_specs=[
                pl.BlockSpec((D, D), lambda s, own: (0, jnp.clip(s - part_at, 0, 3))),
                pl.BlockSpec((images, D), lambda s, own: (0, part(s))),
                pl.BlockSpec((4 * HEADS, 256), lambda s, own: (0, 0)),
                pl.BlockSpec((seq, D), lambda s, own: (late(s), 0)),
                pl.BlockSpec((1, 8, D), lambda s, own: (late(s), 0, 0)),
                pl.BlockSpec((1, 8, D), lambda s, own: (early(s), 0, 0)),
                vmem,
                vmem,
            ]
            + extra_out,
            scratch_shapes=[
                pltpu.VMEM((3, HEADS, HD, rows), BF16),
                pltpu.VMEM((rows, D), F32),
                pltpu.VMEM((HEADS, seq, seq), F32),
                pltpu.VMEM((rows, D), F32),
                pltpu.VMEM((rows, D), BF16),
                pltpu.VMEM((HEADS, HD, rows), BF16),
                pltpu.VMEM((seq, D), F32),
                pltpu.VMEM((8, D), F32),
                pltpu.VMEM((seq, D), BF16),
                pltpu.VMEM((8, D), F32),
                dma,
                dma,
                dma,
                dma,
            ]
            + extra_scratch,
        ),
        out_shape=[
            jax.ShapeDtypeStruct((D, ATT), BF16),
            jax.ShapeDtypeStruct((images, 3 * D), F32),
            jax.ShapeDtypeStruct((4 * HEADS, 256), F32),
            jax.ShapeDtypeStruct((rows, D), F32),
            jax.ShapeDtypeStruct((images, 8, D), F32),
            jax.ShapeDtypeStruct((images, 8, D), F32),
            jax.ShapeDtypeStruct((seq, D), BF16),
            jax.ShapeDtypeStruct((8, D), F32),
        ]
        + extra_shape,
        compiler_params=params(collective_id=5, has_side_effects=True),
        cost_estimate=cost(30 * 10**9, 8 * 10**7),
        name="back_core",
    )(
        own, att, shaped_t, gathered, qkv, bias, lse,
        index_t.reshape(seq // REL_ROWS, 1, REL_ROWS * seq), tok, mod, perm, back_own, back_peer,
        attn, cot, mine, send, gate, *reduced,
    )


CHUNKS = 3


def collect_body(nw, nn, nm, term_ref, img_ref, small_ref, out_ref, img_out, small_out,
                 own, from_c, one, from_x, two, from_z, gath, sc, sx, sz,
                 ls, cs, cr, xs, xr, zs, zr, ys, yr, ics, icr, ixs, ixr, izs, izr, tcs, tcr, txs, txr, tzs, tzr):
    w, n, m = position()
    nlo, nhi, groups = (2, nn // 2, nw * nn)
    c, x = (lax.rem(n, nlo), lax.div(n, nlo))
    slot = (c * nhi + x) * nw + w
    part = out_ref.shape[1] // nm
    width = part // CHUNKS
    sibling = (w, x * nlo + 1 - c, m)
    twin = (w, n, 1 - m)

    def along_x(k):
        there = lax.rem(x + k, nhi)
        return (there, (w, there * nlo + c, m))

    def along_z(k):
        there = lax.rem(w + k, nw)
        return (there, (there, n, m))

    greet_group(nw, nn, True)

    def cols(k):
        return pl.ds(pl.multiple_of(m * part + k * width, 128), width)

    def load(k):
        return pltpu.make_async_copy(term_ref.at[:, :, c, :, cols(k)], own.at[k], ls.at[k])

    def hop_c(k):
        return remote(term_ref.at[:, :, 1 - c, :, cols(k)], from_c.at[k], cs.at[k], cr.at[k], sibling)

    def hop_x(k, d):
        there, device = along_x(d)
        return remote(one.at[k, d - 1], from_x.at[k, d - 1], xs.at[k, d - 1], xr.at[k, d - 1], device)

    def hop_z(k, d):
        there, device = along_z(d)
        return remote(two.at[k, d - 1], from_z.at[k, d - 1], zs.at[k, d - 1], zr.at[k, d - 1], device)

    def hop_y(k):
        return remote(out_ref.at[:, cols(k)], out_ref.at[:, cols(k)], ys.at[k], yr.at[k], twin)

    for k in range(CHUNKS):
        hop_c(k).start()
        load(k).start()

    gath[slot] = img_ref[...]
    img_z = []
    for d in range(1, nw):
        there, device = along_z(d)
        img_z.append(remote(gath.at[slot], gath.at[slot], izs.at[d - 1], izr.at[d - 1], device))
    mine_x = pl.ds((c * nhi + x) * nw, nw)
    img_x = []
    for d in range(1, nhi):
        there, device = along_x(d)
        img_x.append(remote(gath.at[mine_x], gath.at[mine_x], ixs.at[d - 1], ixr.at[d - 1], device))
    mine_c = pl.ds(c * nhi * nw, nhi * nw)
    img_c = remote(gath.at[mine_c], gath.at[mine_c], ics, icr, sibling)
    sc[c] = small_ref[...]
    small_c = remote(sc.at[c], sc.at[c], tcs, tcr, sibling)
    small_x = []
    for d in range(1, nhi):
        there, device = along_x(d)
        small_x.append(remote(sx.at[x], sx.at[x], txs.at[d - 1], txr.at[d - 1], device))
    small_z = []
    for d in range(1, nw):
        there, device = along_z(d)
        small_z.append(remote(sz.at[w], sz.at[w], tzs.at[d - 1], tzr.at[d - 1], device))

    small_c.start()
    for hop in img_z:
        hop.start()

    def pair(k, zi, xi):
        return own[k, zi, xi].astype(F32) + from_c[k, zi, xi].astype(F32)

    def stage_a(k):
        hop_c(k).wait()
        load(k).wait()
        for d in range(1, nhi):
            there, _ = along_x(d)
            for zi in range(nw):
                one[k, d - 1, zi] = pair(k, zi, there).astype(BF16)
            hop_x(k, d).start()

    def chain(k, zi):
        total = pair(k, zi, x)
        for d in range(1, nhi):
            total = total + from_x[k, d - 1, zi].astype(F32)
        return total

    def stage_b(k):
        for d in range(1, nhi):
            hop_x(k, d).wait()
        for d in range(1, nw):
            there, _ = along_z(d)
            two[k, d - 1] = chain(k, there).astype(BF16)
            hop_z(k, d).start()

    def stage_c(k):
        for d in range(1, nw):
            hop_z(k, d).wait()
        total = chain(k, w)
        for d in range(1, nw):
            total = total + from_z[k, d - 1].astype(F32)
        out_ref[:, cols(k)] = total.astype(BF16)
        hop_y(k).start()

    stage_a(0)
    small_c.wait()
    sx[x] = sc[0] + sc[1]
    for hop in small_x:
        hop.start()
    stage_a(1)
    for hop in img_z:
        hop.wait()
    for hop in img_x:
        hop.start()
    stage_a(2)
    stage_b(0)
    for hop in small_x:
        hop.wait()
    total = sx[0]
    for k in range(1, nhi):
        total = total + sx[k]
    sz[w] = total
    for hop in small_z:
        hop.start()
    stage_b(1)
    stage_c(0)
    for hop in img_x:
        hop.wait()
    img_c.start()
    stage_b(2)
    stage_c(1)
    for hop in small_z:
        hop.wait()
    total = sz[0]
    for k in range(1, nw):
        total = total + sz[k]
    small_out[...] = total
    img_c.wait()
    for g in range(groups):
        img_out[2 * g : 2 * g + 2, :] = gath[g]
    stage_c(2)
    for k in range(CHUNKS):
        hop_y(k).wait()


def collect(term, imgs, small, nw, nn, nm):
    groups = nw * nn
    nhi = nn // 2
    rows = small.shape[0]
    img_width = imgs.shape[1]
    blk, cols = (term.shape[0] // groups, term.shape[1])
    width = cols // nm // CHUNKS
    vmem = pl.BlockSpec(memory_space=pltpu.VMEM)
    dma = pltpu.SemaphoreType.DMA
    hi, wi = (max(nhi - 1, 1), max(nw - 1, 1))
    many = dma((CHUNKS,))
    return pl.pallas_call(
        partial(collect_body, nw, nn, nm),
        in_specs=[ANY, vmem, vmem],
        out_specs=[vmem, vmem, vmem],
        out_shape=[
            jax.ShapeDtypeStruct((blk, cols), BF16),
            jax.ShapeDtypeStruct((2 * groups, img_width), F32),
            jax.ShapeDtypeStruct(small.shape, F32),
        ],
        scratch_shapes=[
            pltpu.VMEM((CHUNKS, nw, nhi, blk, width), BF16),
            pltpu.VMEM((CHUNKS, nw, nhi, blk, width), BF16),
            pltpu.VMEM((CHUNKS, hi, nw, blk, width), BF16),
            pltpu.VMEM((CHUNKS, hi, nw, blk, width), BF16),
            pltpu.VMEM((CHUNKS, wi, blk, width), BF16),
            pltpu.VMEM((CHUNKS, wi, blk, width), BF16),
            pltpu.VMEM((groups, 2, img_width), F32),
            pltpu.VMEM((2, rows, 128), F32),
            pltpu.VMEM((nhi, rows, 128), F32),
            pltpu.VMEM((nw, rows, 128), F32),
            many, many, many, dma((CHUNKS, hi)), dma((CHUNKS, hi)), dma((CHUNKS, wi)), dma((CHUNKS, wi)), many, many,
            dma, dma, dma((hi,)), dma((hi,)), dma((wi,)), dma((wi,)),
            dma, dma, dma((hi,)), dma((hi,)), dma((wi,)), dma((wi,)),
        ],
        compiler_params=params(collective_id=2, has_side_effects=True),
        cost_estimate=cost(10**8, 3 * 10**7),
        name="collect",
    )(term.reshape(nw, nhi, 2, blk, cols), imgs, small)


def norm_body(nw, nn, nm, bias_rows, att_ref, mlp_ref, img_ref, emb_ref, silu_ref, small_ref, perm_ref,
              att_out, mlp_out, ada_out, norm_out, slots, ss, sr):
    w, n, m = position()
    groups = nw * nn
    count = groups * nm
    mine = (w * nn + n) * nm + m
    bar = pltpu.get_barrier_semaphore()

    def who(k):
        other = lax.rem(mine + k, count)
        pair = lax.div(other, nm)
        return (lax.div(pair, nn), lax.rem(pair, nn), lax.rem(other, nm))

    def ask(k, carry):
        pl.semaphore_signal(bar, inc=1, device_id=who(k), device_id_type=MESH)
        return carry

    lax.fori_loop(1, count, ask, 0)
    emb = emb_ref[...]
    silu = silu_ref[...]
    att_sq = jnp.zeros((1, 1), F32)

    def tally(values):
        return jnp.sum(jnp.sum(values * values, axis=0, keepdims=True), axis=1, keepdims=True)

    part = att_ref[:, 0 : 3 * D].astype(F32)
    att_out[:, 0 : 3 * D] = part
    att_sq = att_sq + tally(part)
    imgs = exact_parts(img_ref[:, 0 : 3 * D])
    part = mm(emb, imgs[0], TN) + mm(emb, imgs[1], TN) + mm(emb, imgs[2], TN)
    att_out[:, 3 * D : 6 * D] = part
    att_sq = att_sq + tally(part)
    part = mm(att_ref[:, 3 * D :], perm_ref[...], NT)
    att_out[:, 6 * D : 7 * D] = part
    att_sq = att_sq + tally(part)
    ada = img_ref[:, 3 * D :]
    ada_sum = jnp.sum(ada, axis=0, keepdims=True)
    ada_out[...] = ada_sum
    imgs = exact_parts(ada)
    part = mm(silu, imgs[0], TN) + mm(silu, imgs[1], TN) + mm(silu, imgs[2], TN)
    att_out[:, 7 * D :] = part
    att_sq = att_sq + tally(part)
    mlp_sq = jnp.zeros((1, 1), F32)
    for f in range(mlp_ref.shape[1] // (2 * TILE)):
        at = slice(f * TILE, (f + 1) * TILE)
        part = mlp_ref[:, 2 * f * TILE : (2 * f + 1) * TILE].astype(F32)
        mlp_out[:, 0, at] = part
        mlp_sq = mlp_sq + tally(part)
        part = mlp_ref[:, (2 * f + 1) * TILE : (2 * f + 2) * TILE].astype(F32)
        mlp_out[:, 1, at] = part
        mlp_sq = mlp_sq + tally(part)
    shared_rows = small_ref.shape[0] - bias_rows
    small_sq = tally(small_ref[0:shared_rows]) + tally(ada_sum)
    bias_sq = tally(small_ref[shared_rows:])
    local = mlp_sq + att_sq / nm + small_sq / count + bias_sq / groups
    slots[mine] = jnp.broadcast_to(local, (8, 128))
    pl.semaphore_wait(bar, count - 1)

    def copy_to(k):
        return remote(slots.at[mine], slots.at[mine], ss.at[k], sr.at[k], who(k))

    def send(k, carry):
        copy_to(k).start()
        return carry

    def finish(k, carry):
        copy_to(k).wait()
        return carry

    lax.fori_loop(1, count, send, 0)
    lax.fori_loop(1, count, finish, 0)
    norm_out[...] = jnp.sqrt(jnp.sum(slots[...], axis=0))


def collect_norm(att, mlp, imgs, emb, silu, small, perm, bias_rows, nw, nn, nm):
    rows = att.shape[0]
    half = mlp.shape[1] // 2
    count = nw * nn * nm
    dma = pltpu.SemaphoreType.DMA
    return pl.pallas_call(
        partial(norm_body, nw, nn, nm, bias_rows),
        out_shape=[
            jax.ShapeDtypeStruct((rows, 13 * D), F32),
            jax.ShapeDtypeStruct((rows, 2, half), F32),
            jax.ShapeDtypeStruct((1, 6 * D), F32),
            jax.ShapeDtypeStruct((8, 128), F32),
        ],
        scratch_shapes=[pltpu.VMEM((count, 8, 128), F32), dma((count,)), dma((count,))],
        compiler_params=params(collective_id=3, has_side_effects=True),
        cost_estimate=cost(10**8, 10**7),
        name="collect_norm",
    )(att, mlp, imgs, emb, silu, small, perm)


def on_device(
    tokens,
    timesteps,
    owners,
    rel_index,
    cotangent,
    att_master,
    att_moment,
    att_second,
    mlp_master,
    mlp_moment,
    mlp_second,
    small_master,
    small_moment,
    small_second,
    bias_master,
    bias_moment,
    bias_second,
):
    groups = owners.shape[0]
    rows_blk = att_master.shape[0]
    half_ff = mlp_master.shape[2]
    images = timesteps.shape[0]
    tok_rows = tokens.shape[0]
    half_rows = cotangent.shape[0]
    seq_len = tok_rows // images
    nw, nn, nm = (lax.axis_size("wide"), lax.axis_size("narrow"), lax.axis_size("mlp"))
    mlp_at = lax.axis_index("mlp")
    mine = lax.axis_index(GRID)
    moved = rows_blk == HD
    swap = [(i, nm - 1 - i) for i in range(nm)]

    place = (owners[:, None] * rows_blk + jnp.arange(rows_blk)[None, :]).reshape(D)
    pick = (place[:, None] == (mine * rows_blk + jnp.arange(rows_blk))[None, :]).astype(BF16)

    packed, perm = pack_weights(owners, att_master, mlp_master)
    perm_f = perm.astype(F32)
    gathered = lax.all_gather(packed, GRID, axis=0, tiled=True)

    time_emb = time_embed(timesteps)
    emb_rows = jnp.concatenate(
        [time_emb, jax.nn.silu(time_emb), jnp.zeros((8 - 2 * images, D), F32)], axis=0
    ).astype(BF16)
    summed, emb_mine, silu_mine, cot_all = modul_exchange(
        emb_rows, att_master, pick, cotangent, nw, nn
    )
    time_part = summed[:, 0 : 3 * D]
    offset = NREL * HEADS
    table_t = jnp.pad(small_master[0:offset].reshape(NREL, HEADS).T, ((0, 0), (0, 1024 - NREL)))
    b_ada = small_master[offset : offset + 6 * D]
    b_rest = small_master[offset + 6 * D : offset + 8 * D].reshape(1, 2, D)
    modulation = (summed[:, 3 * D :] + b_ada).reshape(images, 6, D)
    mod = jnp.concatenate([modulation, jnp.broadcast_to(b_rest, (images, 2, D))], axis=1)
    mod = mm_exact(mod.reshape(images * 8, D), perm_f).reshape(images, 8, D)
    index_t = rel_index.T
    bias = rel_bias(index_t, table_t.reshape(HEADS, 1, 1024), seq_len)

    tok, shaped, shaped_t, cot, grad_branch, front_sums = front(
        tokens, cot_all, perm, mod, seq_len, images
    )
    heads_at = owners if moved else jnp.arange(HEADS, dtype=jnp.int32)
    qkv, attended, lse = attend_fwd(heads_at, shaped, gathered, time_part, bias, seq_len, images)
    attended = attended.reshape(D, tok_rows)
    if not moved:
        attended = mm(perm, attended, TN).astype(BF16)
    attn_out, shaped_two = middle(attended, gathered, tok, mod, seq_len, images)
    made = mlp_core(
        shaped_two, grad_branch, gathered, bias_master.reshape(1, half_ff), cot, seq_len, nw, nn
    )
    mlp_term, branch_mine, branch_send, gate_own, b_one_grad, back_own, back_peer = made[:7]
    reduced = (mlp_term, made[7]) if len(made) == 8 else ()

    done = back_core(
        heads_at,
        attended,
        shaped_t,
        gathered,
        qkv,
        bias,
        lse,
        index_t,
        tok,
        mod,
        perm,
        back_own,
        back_peer,
        attn_out,
        cot,
        branch_mine,
        branch_send,
        gate_own,
        reduced,
        seq_len,
        images,
        nw,
        nn,
        moved,
    )
    att_term, time_grad, rel_sum, input_grad, in_sums, mid_sums, output, gate_peer = done[:8]
    if len(done) == 9:
        mlp_part = done[8]
    else:
        mlp_part = lax.psum_scatter(mlp_term, GRID, scatter_dimension=0, tiled=True)
    gate_two_grad = gate_own[0:images] + gate_peer[0:images] + mod[:, 7] * front_sums[:, 1]
    modul_grad = jnp.stack(
        [
            in_sums[:, 0],
            in_sums[:, 1],
            mid_sums[:, 2],
            mid_sums[:, 0],
            mid_sums[:, 1],
            gate_two_grad,
        ],
        axis=1,
    ).reshape(images * 6, D)
    back = mm_exact(
        jnp.concatenate(
            [
                modul_grad,
                jnp.sum(mid_sums[:, 3], axis=0, keepdims=True),
                jnp.sum(front_sums[:, 0], axis=0, keepdims=True),
            ],
            axis=0,
        ),
        perm_f,
        NT,
    )
    imgs = jnp.concatenate(
        [
            time_grad,
            back[0 : images * 6].reshape(images, 6 * D),
        ],
        axis=1,
    )
    small = jnp.concatenate(
        [rel_sum.reshape(-1, 128), back[images * 6 :].reshape(-1, 128), b_one_grad.reshape(-1, 128)],
        axis=0,
    )
    bias_rows = half_ff // 128
    att_part, imgs_all, small_all = collect(att_term, imgs, small, nw, nn, nm)

    att_grad, mlp_grad, b_ada_grad, norm = collect_norm(
        att_part, mlp_part, imgs_all, emb_mine, silu_mine, small_all, perm, bias_rows, nw, nn, nm
    )
    grad_norm = norm[0, 0]
    clip_scale = jnp.minimum(1.0, 1.0 / (grad_norm + 1e-06))
    rel_rows = 4 * HEADS * 2
    rel_grad = small_all[0:rel_rows].reshape(4, HEADS, 256).transpose(0, 2, 1).reshape(-1)[0:offset]
    rest_rows = 2 * D // 128
    small_grad = jnp.concatenate(
        [
            rel_grad,
            b_ada_grad.reshape(-1),
            small_all[rel_rows : rel_rows + rest_rows].reshape(-1),
        ]
    )
    bias_grad = small_all[rel_rows + rest_rows :].reshape(-1)
    att_new, att_mom_new, att_sec_new = adam_update(
        att_master, att_moment, att_second, att_grad, clip_scale
    )
    mlp_new, mlp_mom_new, mlp_sec_new = adam_update(
        mlp_master, mlp_moment, mlp_second, mlp_grad, clip_scale
    )
    small_new, small_mom_new, small_sec_new = adam_update(
        small_master, small_moment, small_second, small_grad, clip_scale
    )
    bias_new, bias_mom_new, bias_sec_new = adam_update(
        bias_master, bias_moment, bias_second, bias_grad, clip_scale
    )
    return (
        output,
        input_grad,
        att_new,
        att_mom_new,
        att_sec_new,
        mlp_new,
        mlp_mom_new,
        mlp_sec_new,
        small_new,
        small_mom_new,
        small_sec_new,
        bias_new,
        bias_mom_new,
        bias_sec_new,
        att_new.astype(BF16),
        mlp_new.astype(BF16),
        grad_norm,
    )


def solution(mesh):
    rows = P(GRID, None)
    cube = P(GRID, None, "mlp")
    return jax.shard_map(
        on_device,
        mesh=mesh,
        in_specs=(
            rows,
            P(GRID),
            P(),
            P(),
            P(("wide", "narrow", "mlp"), None),
            rows,
            rows,
            rows,
            cube,
            cube,
            cube,
            P(),
            P(),
            P(),
            P("mlp"),
            P("mlp"),
            P("mlp"),
        ),
        out_specs=(
            P(("wide", "narrow", "mlp"), None),
            rows,
            rows,
            rows,
            rows,
            cube,
            cube,
            cube,
            P(),
            P(),
            P(),
            P("mlp"),
            P("mlp"),
            P("mlp"),
            rows,
            cube,
            P(),
        ),
        check_vma=False,
    )
```

```python
from functools import partial
import math

import jax
import jax.numpy as jnp
from jax import lax
from jax.experimental import pallas as pl
from jax.experimental.pallas import tpu as pltpu
from jax.sharding import PartitionSpec as P

D = 1152
HEADS = 16
HD = 72
NREL = 961
STEP = 10

HIGH = lax.Precision.HIGHEST
F32 = jnp.float32
BF16 = jnp.bfloat16
GRID = ("wide", "narrow")
NN = (((1,), (0,)), ((), ()))
TN = (((0,), (0,)), ((), ()))
NT = (((1,), (1,)), ((), ()))
INV_ROOT = 1.0 / math.sqrt(HD)
MESH = pl.DeviceIdType.MESH
ANY = pl.BlockSpec(memory_space=pl.ANY)
ATT = 4 * D
GROUP = 4
TILE = 768
VMEM_BYTES = 63 * 1024 * 1024


def mm(a, b, dims=NN):
    return lax.dot_general(a, b, dims, preferred_element_type=F32)


def mm_exact(a, b, dims=NN):
    return lax.dot_general(a, b, dims, precision=HIGH, preferred_element_type=F32)


def norm_stats(values):
    center = values - jnp.mean(values, axis=-1, keepdims=True)
    inv_std = lax.rsqrt(jnp.mean(center * center, axis=-1, keepdims=True) + 1e-06)
    return (center * inv_std, inv_std)


def norm_back(grad_normed, normed, inv_std):
    mean_grad = jnp.mean(grad_normed, axis=-1, keepdims=True)
    mean_proj = jnp.mean(grad_normed * normed, axis=-1, keepdims=True)
    return (grad_normed - mean_grad - normed * mean_proj) * inv_std


def time_embed(steps_int):
    half_dim = D // 2
    frequency = jnp.exp(-math.log(10000.0) * jnp.arange(half_dim).astype(F32) / half_dim)
    angles = steps_int.astype(F32)[:, None] * frequency[None, :]
    return jnp.concatenate([jnp.cos(angles), jnp.sin(angles)], axis=1)


def adam_update(weight, moment, second, grad, clip_scale):
    scaled = grad * clip_scale
    moment_new = 0.9 * moment + 0.1 * scaled
    second_new = 0.999 * second + 0.001 * scaled * scaled
    rate = 1.5 / math.sqrt(D)
    direction = (
        moment_new / (1.0 - 0.9**STEP) / (jnp.sqrt(second_new / (1.0 - 0.999**STEP)) + 1e-08)
    )
    return (weight - rate * (direction + 0.1 * weight), moment_new, second_new)


def exact_parts(values):
    first = values.astype(BF16)
    rest = values - first.astype(F32)
    second = rest.astype(BF16)
    return (first, second, (rest - second.astype(F32)).astype(BF16))


def mm_split(a, b, dims=NN):
    one, two, three = exact_parts(a)
    return mm(one, b, dims) + mm(two, b, dims) + mm(three, b, dims)


def params(**kw):
    return pltpu.CompilerParams(vmem_limit_bytes=VMEM_BYTES, **kw)


def cost(flops, nbytes):
    return pl.CostEstimate(flops=flops, bytes_accessed=nbytes, transcendentals=0)


def position():
    return (lax.axis_index("wide"), lax.axis_index("narrow"), lax.axis_index("mlp"))


def remote(src, dst, send, recv, device):
    return pltpu.make_async_remote_copy(
        src_ref=src, dst_ref=dst, send_sem=send, recv_sem=recv, device_id=device, device_id_type=MESH
    )


def greet_group(nw, nn, with_mlp):
    w, n, m = position()
    mine = w * nn + n
    groups = nw * nn
    bar = pltpu.get_barrier_semaphore()

    def ask(k, carry):
        other = lax.rem(mine + k, groups)
        pl.semaphore_signal(
            bar, inc=1, device_id=(lax.div(other, nn), lax.rem(other, nn), m), device_id_type=MESH
        )
        return carry

    lax.fori_loop(1, groups, ask, 0)
    if with_mlp:
        pl.semaphore_signal(bar, inc=1, device_id=(w, n, 1 - m), device_id_type=MESH)
    pl.semaphore_wait(bar, groups - 1 + (1 if with_mlp else 0))


def pack_body(owners_ref, att_ref, mlp_ref, out_ref, perm_ref):
    rows = att_ref.shape[0]
    half = mlp_ref.shape[2]
    line = lax.broadcasted_iota(jnp.int32, (D, 128), 0)
    block = line // rows
    place = line - block * rows
    for b in range(owners_ref.shape[0]):
        place = place + jnp.where(block == b, owners_ref[b] * rows, 0)
    col = lax.broadcasted_iota(jnp.int32, (D, 128), 1)
    for j in range(D // 128):
        perm_ref[:, j * 128 : (j + 1) * 128] = jnp.where(place == col + j * 128, 1.0, 0.0).astype(BF16)
    out_ref[:, 0 : 3 * D] = att_ref[:, 0 : 3 * D].astype(BF16)
    out_ref[:, 3 * D : ATT] = mm(att_ref[:, 6 * D : 7 * D].astype(BF16), perm_ref[...]).astype(BF16)
    out_ref[:, ATT : ATT + half] = mlp_ref[:, 0, :].astype(BF16)
    out_ref[:, ATT + half : ATT + 2 * half] = mlp_ref[:, 1, :].astype(BF16)


def pack_weights(owners, att, mlp):
    rows, _, half = mlp.shape
    vmem = pl.BlockSpec(memory_space=pltpu.VMEM)
    return pl.pallas_call(
        pack_body,
        grid=(1,),
        in_specs=[
            pl.BlockSpec(memory_space=pltpu.SMEM),
            pl.BlockSpec((rows, 7 * D), lambda s: (0, 0)),
            pl.BlockSpec((rows, 2, half), lambda s: (0, 0, 0)),
        ],
        out_specs=[vmem, vmem],
        out_shape=[
            jax.ShapeDtypeStruct((rows, ATT + 2 * half), BF16),
            jax.ShapeDtypeStruct((D, D), BF16),
        ],
        compiler_params=params(),
        name="pack",
    )(owners, att, mlp)


def modul_body(nw, nn, emb_ref, att_ref, pick_ref, cot_ref, sum_ref, emb_out, silu_out, cot_out,
               gath, flat, parts, from_c, from_x, from_z, gs, gr, cs, cr, xs, xr, zs, zr, ys, yr, ls):
    w, n, m = position()
    nlo, nhi, groups = (2, nn // 2, nw * nn)
    c, x = (lax.rem(n, nlo), lax.div(n, nlo))
    half = cot_ref.shape[0]
    width = parts.shape[2]
    slot = (c * nhi + x) * nw + w
    mine = w * nn + n
    greet_group(nw, nn, True)
    rows = pl.ds(m * half, half)
    to_y = remote(cot_ref, cot_out.at[rows], ys, yr, (w, n, 1 - m))
    to_y.start()
    keep = pltpu.make_async_copy(cot_ref, cot_out.at[rows], ls)
    keep.start()
    gath[slot] = emb_ref[...]

    def copy_to(k):
        other = lax.rem(mine + k, groups)
        return remote(gath.at[slot], gath.at[slot], gs.at[k], gr.at[k], (lax.div(other, nn), lax.rem(other, nn), m))

    def send(k, carry):
        copy_to(k).start()
        return carry

    def finish(k, carry):
        copy_to(k).wait()
        return carry

    lax.fori_loop(1, groups, send, 0)
    lax.fori_loop(1, groups, finish, 0)
    picked = mm(gath[...].reshape(groups * 8, D), pick_ref[...]).astype(BF16)
    line = lax.broadcasted_iota(jnp.int32, (2 * groups, 8 * groups), 0)
    col = lax.broadcasted_iota(jnp.int32, (2 * groups, 8 * groups), 1)
    at = (line // 2) * 8 + line % 2
    emb = mm((col == at).astype(BF16), picked).astype(BF16)
    silu = mm((col == at + 2).astype(BF16), picked).astype(BF16)
    emb_out[...] = emb
    silu_out[...] = silu
    flat[:, 0 : 3 * D] = mm(emb, att_ref[:, 3 * D : 6 * D].astype(BF16))
    flat[:, 3 * D : 9 * D] = mm(silu, att_ref[:, 7 * D : 13 * D].astype(BF16))
    for g in range(groups):
        parts[g] = flat[2 * g : 2 * g + 2, :]
    block = nhi * nw
    other_c = (1 - c) * block
    mine_c = c * block
    hop = remote(parts.at[pl.ds(other_c, block)], from_c, cs, cr, (w, x * nlo + 1 - c, m))
    hop.start()
    hop.wait()
    parts[pl.ds(mine_c, block)] = parts[pl.ds(mine_c, block)] + from_c[...]
    hops = []
    for k in range(1, nhi):
        there = lax.rem(x + k, nhi)
        hop = remote(
            parts.at[pl.ds(mine_c + there * nw, nw)], from_x.at[k - 1], xs.at[k - 1], xr.at[k - 1], (w, there * nlo + c, m)
        )
        hop.start()
        hops.append(hop)
    for hop in hops:
        hop.wait()
    first = mine_c + x * nw
    total = parts[pl.ds(first, nw)]
    for k in range(1, nhi):
        total = total + from_x[k - 1]
    parts[pl.ds(first, nw)] = total
    hops = []
    for k in range(1, nw):
        there = lax.rem(w + k, nw)
        hop = remote(parts.at[first + there], from_z.at[k - 1], zs.at[k - 1], zr.at[k - 1], (there, n, m))
        hop.start()
        hops.append(hop)
    for hop in hops:
        hop.wait()
    total = parts[first + w]
    for k in range(1, nw):
        total = total + from_z[k - 1]
    sum_ref[...] = total
    keep.wait()
    to_y.wait()


def modul_exchange(emb_rows, att, pick, cot, nw, nn):
    groups = nw * nn
    nhi = nn // 2
    width = 9 * D
    half = cot.shape[0]
    vmem = pl.BlockSpec(memory_space=pltpu.VMEM)
    dma = pltpu.SemaphoreType.DMA
    return pl.pallas_call(
        partial(modul_body, nw, nn),
        in_specs=[vmem, vmem, vmem, ANY],
        out_specs=[vmem, vmem, vmem, ANY],
        out_shape=[
            jax.ShapeDtypeStruct((2, width), F32),
            jax.ShapeDtypeStruct((2 * groups, att.shape[0]), BF16),
            jax.ShapeDtypeStruct((2 * groups, att.shape[0]), BF16),
            jax.ShapeDtypeStruct((2 * half, D), BF16),
        ],
        scratch_shapes=[
            pltpu.VMEM((groups, 8, D), BF16),
            pltpu.VMEM((2 * groups, width), F32),
            pltpu.VMEM((groups, 2, width), F32),
            pltpu.VMEM((nhi * nw, 2, width), F32),
            pltpu.VMEM((max(nhi - 1, 1), nw, 2, width), F32),
            pltpu.VMEM((max(nw - 1, 1), 2, width), F32),
            dma((groups,)), dma((groups,)), dma, dma,
            dma((max(nhi - 1, 1),)), dma((max(nhi - 1, 1),)),
            dma((max(nw - 1, 1),)), dma((max(nw - 1, 1),)),
            dma, dma, dma,
        ],
        compiler_params=params(collective_id=1, has_side_effects=True),
        cost_estimate=cost(10**8, 3 * 10**7),
        name="modul_exchange",
    )(emb_rows, att, pick, cot)


def bias_body(index_ref, table_ref, bias_ref):
    low = jnp.bitwise_and(index_ref[...], 127)
    high = jnp.right_shift(index_ref[...], 7)
    for part in range(index_ref.shape[1] // 128):
        at = slice(part * 128, (part + 1) * 128)
        lo = low[:, at]
        hi = high[:, at]
        total = jnp.zeros(lo.shape, F32)
        for chunk in range(8):
            row = jnp.broadcast_to(table_ref[0, :, chunk * 128 : (chunk + 1) * 128], lo.shape)
            total = jnp.where(hi == chunk, jnp.take_along_axis(row, lo, axis=1), total)
        bias_ref[0, :, at] = total


def rel_bias(index_t, table_t, seq):
    return pl.pallas_call(
        bias_body,
        grid=(HEADS,),
        in_specs=[
            pl.BlockSpec((seq, seq), lambda h: (0, 0)),
            pl.BlockSpec((1, 1, 1024), lambda h: (h, 0, 0)),
        ],
        out_specs=pl.BlockSpec((1, seq, seq), lambda h: (h, 0, 0)),
        out_shape=jax.ShapeDtypeStruct((HEADS, seq, seq), F32),
        cost_estimate=cost(2 * 10**8, 4 * 10**7),
        name="rel_bias",
    )(index_t, table_t)


def front_body(tok_ref, cot_ref, perm_ref, mod_ref, tok_out, shaped_out, shaped_t, cot_out, branch_out, sums):
    moved = mm(tok_ref[...], perm_ref[...])
    tok_out[...] = moved.astype(BF16)
    normed, _ = norm_stats(moved)
    shaped = normed * (1.0 + mod_ref[0, 1:2]) + mod_ref[0, 0:1]
    shaped_out[...] = shaped.astype(BF16)
    shaped_t[...] = shaped.T.astype(BF16)
    cot = mm(cot_ref[...], perm_ref[...])
    cot_out[...] = cot.astype(BF16)
    branch = (cot * mod_ref[0, 5:6]).astype(BF16)
    branch_out[...] = branch
    sums[0, 0:1] = jnp.sum(branch.astype(F32), axis=0, keepdims=True)
    sums[0, 1:2] = jnp.sum(cot, axis=0, keepdims=True)
    sums[0, 2:8] = jnp.zeros((6, D), F32)


def front(tokens, cot, perm, mod, seq, images):
    rows = seq * images
    tok = pl.BlockSpec((seq, D), lambda n: (n, 0))
    per = pl.BlockSpec((1, 8, D), lambda n: (n, 0, 0))
    return pl.pallas_call(
        front_body,
        grid=(images,),
        in_specs=[tok, tok, pl.BlockSpec((D, D), lambda n: (0, 0)), per],
        out_specs=[tok, tok, pl.BlockSpec((D, seq), lambda n: (0, n)), tok, tok, per],
        out_shape=[
            jax.ShapeDtypeStruct((rows, D), BF16),
            jax.ShapeDtypeStruct((rows, D), BF16),
            jax.ShapeDtypeStruct((D, rows), BF16),
            jax.ShapeDtypeStruct((rows, D), BF16),
            jax.ShapeDtypeStruct((rows, D), BF16),
            jax.ShapeDtypeStruct((images, 8, D), F32),
        ],
        compiler_params=params(),
        cost_estimate=cost(4 * rows * D * D, 10**7),
        name="front",
    )(tokens, cot, perm, mod)


def attend_fwd_body(seq, images, own, shaped_ref, w_ref, time_ref, bias_ref, qkv_ref, out_ref, lse_ref):
    step = pl.program_id(0)

    @pl.when(step < 3)
    def _():
        made = mm(shaped_ref[...], w_ref[...])
        made = jnp.concatenate(
            [made[n * seq : (n + 1) * seq] + time_ref[n : n + 1] for n in range(images)], axis=0
        )
        qkv_ref[step] = made.T.reshape(HEADS, HD, seq * images).astype(BF16)

    @pl.when(step >= 3)
    def _():
        for j in range(GROUP):
            h = (step - 3) * GROUP + j
            query, key, value = [qkv_ref[p, h] for p in range(3)]
            place = own[h]
            for n in range(images):
                at = slice(n * seq, (n + 1) * seq)
                scores = mm(key[:, at], query[:, at], TN) * INV_ROOT + bias_ref[j]
                top = jnp.max(scores, axis=0, keepdims=True)
                weights = jnp.exp(scores - top)
                total = jnp.sum(weights, axis=0, keepdims=True)
                probs = (weights * (1.0 / total)).astype(BF16)
                out_ref[place, :, at] = mm(value[:, at], probs).astype(BF16)
                lse_ref[j, :, at] = top + jnp.log(total)


def attend_fwd(own, shaped, gathered, time_part, bias, seq, images):
    rows = seq * images

    def part(s):
        return jnp.minimum(s, 2)

    def group(s):
        return jnp.maximum(s - 3, 0)

    return pl.pallas_call(
        partial(attend_fwd_body, seq, images),
        grid_spec=pltpu.PrefetchScalarGridSpec(
            num_scalar_prefetch=1,
            grid=(3 + HEADS // GROUP,),
            in_specs=[
                pl.BlockSpec((rows, D), lambda s, own: (0, 0)),
                pl.BlockSpec((D, D), lambda s, own: (0, part(s))),
                pl.BlockSpec((images, D), lambda s, own: (0, part(s))),
                pl.BlockSpec((GROUP, seq, seq), lambda s, own: (group(s), 0, 0)),
            ],
            out_specs=[
                pl.BlockSpec((3, HEADS, HD, rows), lambda s, own: (0, 0, 0, 0)),
                pl.BlockSpec((HEADS, HD, rows), lambda s, own: (0, 0, 0)),
                pl.BlockSpec((GROUP, 1, rows), lambda s, own: (group(s), 0, 0)),
            ],
        ),
        out_shape=[
            jax.ShapeDtypeStruct((3, HEADS, HD, rows), BF16),
            jax.ShapeDtypeStruct((HEADS, HD, rows), BF16),
            jax.ShapeDtypeStruct((HEADS, 1, rows), F32),
        ],
        compiler_params=params(),
        cost_estimate=cost(6 * 10**9, 2 * 10**7),
        name="attend_fwd",
    )(own, shaped, gathered, time_part, bias)


def mid_body(att_ref, w_ref, tok_ref, mod_ref, attn_out, shaped_out):
    attn = mm(att_ref[...], w_ref[...], TN) + mod_ref[0, 6:7]
    attn_out[...] = attn
    mid = tok_ref[...].astype(F32) + mod_ref[0, 2:3] * attn
    normed, _ = norm_stats(mid)
    shaped_out[...] = (normed * (1.0 + mod_ref[0, 4:5]) + mod_ref[0, 3:4]).astype(BF16)


def middle(att, gathered, tok, mod, seq, images):
    rows = seq * images
    row = pl.BlockSpec((seq, D), lambda n: (n, 0))
    return pl.pallas_call(
        mid_body,
        grid=(images,),
        in_specs=[
            pl.BlockSpec((D, seq), lambda n: (0, n)),
            pl.BlockSpec((D, D), lambda n: (0, 3)),
            row,
            pl.BlockSpec((1, 8, D), lambda n: (n, 0, 0)),
        ],
        out_specs=[row, row],
        out_shape=[jax.ShapeDtypeStruct((rows, D), F32), jax.ShapeDtypeStruct((rows, D), BF16)],
        compiler_params=params(),
        cost_estimate=cost(2 * rows * D * D, 10**7),
        name="middle",
    )(att, gathered, tok, mod)


def once(shape, index):
    return pl.BlockSpec(shape, index, pipeline_mode=pl.Buffered(1))


def mlp_body(nw, nn, seq, tiles, direct, x_ref, gb_ref, one_ref, two_ref, bias_ref, cot_ref,
             term_ref, mine_ref, send_ref, gate_ref, bias_out, own_ref, peer_ref, *rest):
    if direct:
        first_ref, hidden, grads, x_t, gb_t, acc, branch_ref, peer_in, ts, tr, made, from_c, red, from_x, cs, cr, xs, xr = rest
    else:
        hidden, grads, x_t, gb_t, acc, branch_ref, peer_in, ts, tr = rest
    step = pl.program_id(0)
    w, n, m = position()
    nlo, nhi = (2, nn // 2)
    c, x = (lax.rem(n, nlo), lax.div(n, nlo))
    groups = nw * nn
    blk = D // groups
    sibling = (w, x * nlo + 1 - c, m)
    twin = (w, n, 1 - m)

    def to_twin(i):
        return remote(own_ref.at[i], peer_in.at[i], ts.at[i], tr.at[i], twin)

    def to_sibling(k):
        return remote(made.at[k, :, :, 1 - c], from_c.at[k], cs.at[k], cr.at[k], sibling)

    def along_x(d):
        there = lax.rem(x + d, nhi)
        return (there, (w, there * nlo + c, m))

    def hop_x(k, d):
        there, device = along_x(d)
        return remote(red.at[k, :, there], from_x.at[k, d - 1], xs.at[k, d - 1], xr.at[k, d - 1], device)

    @pl.when(step == 0)
    def _():
        bar = pltpu.get_barrier_semaphore()
        friends = [twin]
        if direct:
            friends = [twin, sibling] + [along_x(d)[1] for d in range(1, nhi)]
        for device in friends:
            pl.semaphore_signal(bar, inc=1, device_id=device, device_id_type=MESH)
        x_t[...] = x_ref[...].T
        gb_t[...] = gb_ref[...].T
        pl.semaphore_wait(bar, len(friends))

    for image in range(2):

        @pl.when((step >= image * tiles) & (step < (image + 1) * tiles))
        def _():
            f = step - image * tiles
            at = slice(image * seq, (image + 1) * seq)
            pre = mm(x_ref[at], one_ref[...]) + bias_ref[...]
            root = math.sqrt(2.0 / math.pi)
            square = pre * pre
            bend = jnp.tanh(root * (pre + 0.044715 * (square * pre)))
            rise = 0.5 * (1.0 + bend)
            hidden[f, at] = (pre * rise).astype(BF16)
            slope = rise + 0.5 * pre * (1.0 - bend * bend) * (root * (1.0 + 3 * 0.044715 * square))
            grad = (mm(gb_ref[at], two_ref[...]) * slope).astype(BF16)
            grads[f, at] = grad
            back = mm(grad, one_ref[...], NT)

            @pl.when(f == 0)
            def _():
                acc[...] = back

            @pl.when(f > 0)
            def _():
                acc[...] += back

            @pl.when(f == tiles - 1)
            def _():
                own_ref[image] = acc[...].astype(BF16)
                to_twin(image).start()

    def place(k, values):
        made[k] = values.reshape(nw, nhi, nlo, blk, TILE).astype(BF16)

    def combine(k):
        to_sibling(k).wait()
        return made[k, :, :, c] + from_c[k]

    for f in range(tiles):

        @pl.when(step == 2 * tiles + f)
        def _():
            one_grad = mm(x_t[...], grads[f])
            two_grad = mm(gb_t[...], hidden[f])
            if direct:
                place(2 * f, one_grad)
                to_sibling(2 * f).start()
                place(2 * f + 1, two_grad)
                to_sibling(2 * f + 1).start()
            else:
                term_ref[:, 0:TILE] = one_grad.astype(BF16)
                term_ref[:, TILE : 2 * TILE] = two_grad.astype(BF16)
            bias_out[...] = jnp.sum(grads[f].astype(F32), axis=0, keepdims=True)
            branch = mm(hidden[f], two_ref[...], NT)
            branch_ref[...] = branch if f == 0 else branch_ref[...] + branch
            if direct and f == 0:
                for k in range(2):
                    red[k] = combine(k)
                    for d in range(1, nhi):
                        hop_x(k, d).start()

        if direct and f > 0:

            @pl.when(step == 2 * tiles + f + 1)
            def _():
                for half in range(2):
                    term_ref[:, :, :, half * TILE : (half + 1) * TILE] = combine(2 * f + half)

    @pl.when(step == 3 * tiles)
    def _():
        gate_ref[...] = jnp.zeros_like(gate_ref)
        for image in range(2):
            at = slice(image * seq, (image + 1) * seq)
            gate_ref[image : image + 1] = jnp.sum(
                cot_ref[at].astype(F32) * branch_ref[at], axis=0, keepdims=True
            )
        send_ref[...] = branch_ref[pl.ds(pl.multiple_of((1 - m) * seq, seq), seq)].astype(BF16)
        mine_ref[...] = branch_ref[pl.ds(pl.multiple_of(m * seq, seq), seq)]
        to_twin(0).wait()
        to_twin(1).wait()
        peer_ref[...] = peer_in[...]
        if direct:
            for k in range(2):
                for d in range(1, nhi):
                    hop_x(k, d).wait()
                total = red[k, :, x]
                for d in range(1, nhi):
                    total = total + from_x[k, d - 1]
                first_ref[:, :, k * TILE : (k + 1) * TILE] = total


def mlp_core(x, gb, gathered, bias, cot, seq, nw, nn):
    half = bias.shape[1]
    rows = 2 * seq
    tiles = half // TILE
    nhi = nn // 2
    blk = D // (nw * nn)
    one, two = (ATT // TILE, (ATT + half) // TILE)
    whole = once((rows, D), lambda s: (0, 0))
    vmem = pl.BlockSpec(memory_space=pltpu.VMEM)
    dma = pltpu.SemaphoreType.DMA

    def weight(s):
        return jnp.where(s < 3 * tiles, lax.rem(s, tiles), tiles - 1)

    def behind(s):
        return jnp.clip(s - 2 * tiles - 2, 0, tiles - 2)

    direct = blk % 8 == 0
    hi = max(nhi - 1, 1)
    if direct:
        term_spec = pl.BlockSpec((nw, nhi, blk, 2 * TILE), lambda s: (0, 0, 0, behind(s)))
        term_shape = jax.ShapeDtypeStruct((nw, nhi, blk, 2 * half - 2 * TILE), BF16)
    else:
        term_spec = pl.BlockSpec((D, 2 * TILE), lambda s: (0, jnp.clip(s - 2 * tiles, 0, tiles - 1)))
        term_shape = jax.ShapeDtypeStruct((D, 2 * half), BF16)
    return pl.pallas_call(
        partial(mlp_body, nw, nn, seq, tiles, direct),
        grid=(3 * tiles + 1,),
        in_specs=[
            whole,
            whole,
            pl.BlockSpec((D, TILE), lambda s: (0, one + jnp.where(s < 2 * tiles, lax.rem(s, tiles), tiles - 1))),
            pl.BlockSpec((D, TILE), lambda s: (0, two + weight(s))),
            pl.BlockSpec((1, TILE), lambda s: (0, weight(s))),
            whole,
        ],
        out_specs=[
            term_spec,
            vmem,
            vmem,
            vmem,
            pl.BlockSpec((1, TILE), lambda s: (0, jnp.clip(s - 2 * tiles, 0, tiles - 1))),
            vmem,
            vmem,
        ]
        + ([vmem] if direct else []),
        out_shape=[
            term_shape,
            jax.ShapeDtypeStruct((seq, D), F32),
            jax.ShapeDtypeStruct((seq, D), BF16),
            jax.ShapeDtypeStruct((8, D), F32),
            jax.ShapeDtypeStruct((1, half), F32),
            jax.ShapeDtypeStruct((2, seq, D), BF16),
            jax.ShapeDtypeStruct((2, seq, D), BF16),
        ]
        + ([jax.ShapeDtypeStruct((nw, blk, 2 * TILE), BF16)] if direct else []),
        scratch_shapes=[
            pltpu.VMEM((tiles, rows, TILE), BF16),
            pltpu.VMEM((tiles, rows, TILE), BF16),
            pltpu.VMEM((D, rows), BF16),
            pltpu.VMEM((D, rows), BF16),
            pltpu.VMEM((seq, D), F32),
            pltpu.VMEM((rows, D), F32),
            pltpu.VMEM((2, seq, D), BF16),
            dma((2,)),
            dma((2,)),
        ]
        + (
            [
                pltpu.VMEM((2 * tiles, nw, nhi, 2, blk, TILE), BF16),
                pltpu.VMEM((2 * tiles, nw, nhi, blk, TILE), BF16),
                pltpu.VMEM((2, nw, nhi, blk, TILE), BF16),
                pltpu.VMEM((2, hi, nw, blk, TILE), BF16),
                dma((2 * tiles,)),
                dma((2 * tiles,)),
                dma((2, hi)),
                dma((2, hi)),
            ]
            if direct
            else []
        ),
        compiler_params=params(collective_id=4, has_side_effects=True),
        cost_estimate=cost(12 * rows * D * half, 4 * 10**7),
        name="mlp_core",
    )(x, gb, gathered, gathered, bias, cot)


REL_ROWS = 32
BUCKETS = 128


def back_body(nw, nn, seq, images, moved, direct, own, att_ref, shaped_ref, w_ref, qkv_ref, bias_ref, lse_ref,
              index_ref, tok_ref, mod_ref, perm_ref, back_own, back_peer, attn_ref, cot_ref, send_ref, gate_ref, *rest):
    if direct:
        term_ref, first_ref = rest[:2]
        rest = rest[2:]
    time_ref, rel_ref, in_ref, sums, mid_sums, keep, keep_mod, branch_out, gate_out = rest[:9]
    rest = rest[9:]
    if direct:
        part_ref, done_ref, half_ref = rest[:3]
        rest = rest[3:]
    else:
        dw_ref = rest[0]
        rest = rest[1:]
    made, ga, ga_t, branch_in, gate_in, acc, ds_all, mid, yb, yc, ybr, ycr = rest[:12]
    if direct:
        held, from_x, two, from_z, ls, xs, xr, zs, zr, dwt, att_c, att_red, att_x, att_two, att_z, acs, acr, axs, axr, azs, azr = rest[12:]
    step = pl.program_id(0)
    groups = HEADS // GROUP
    rows = seq * images
    att_at = images + 1
    part_at = att_at + groups
    rel_at = part_at + 3
    end_at = rel_at + seq // REL_ROWS
    last = end_at + images - 1
    w, n, m = position()
    nlo, nhi = (2, nn // 2)
    c, x = (lax.rem(n, nlo), lax.div(n, nlo))
    twin = (w, n, 1 - m)

    def along_x(d):
        there = lax.rem(x + d, nhi)
        return (there, (w, there * nlo + c, m))

    def along_z(d):
        there = lax.rem(w + d, nw)
        return (there, (there, n, m))

    def swap_branch():
        return remote(send_ref, branch_in, yb, ybr, twin)

    def swap_gate():
        return remote(gate_ref, gate_in, yc, ycr, twin)

    if direct:
        chunks = part_ref.shape[1] // TILE

        def load(k):
            return pltpu.make_async_copy(
                term_ref.at[:, x, :, pl.ds((k - 2) * TILE, TILE)], held.at[k - 2], ls.at[k - 2]
            )

        def hop_x(k, d):
            there, device = along_x(d)
            return remote(
                term_ref.at[:, there, :, pl.ds((k - 2) * TILE, TILE)],
                from_x.at[k - 2, d - 1], xs.at[k - 2, d - 1], xr.at[k - 2, d - 1], device,
            )

        def hop_z(k, d):
            there, device = along_z(d)
            return remote(two.at[k, d - 1], from_z.at[k, d - 1], zs.at[k, d - 1], zr.at[k, d - 1], device)

        def chain(k, zi):
            if k < 2:
                return first_ref[zi, :, k * TILE : (k + 1) * TILE]
            total = held[k - 2, zi]
            for d in range(1, nhi):
                total = total + from_x[k - 2, d - 1, zi]
            return total

        def start_x(k):
            for d in range(1, nhi):
                hop_x(k, d).start()

        def stage_x(k):
            if k >= 2:
                load(k).wait()
                for d in range(1, nhi):
                    hop_x(k, d).wait()
            for d in range(1, nw):
                there, _ = along_z(d)
                two[k, d - 1] = chain(k, there)
                hop_z(k, d).start()

        def stage_z(k):
            for d in range(1, nw):
                hop_z(k, d).wait()
            total = chain(k, w).astype(F32)
            for d in range(1, nw):
                total = total + from_z[k, d - 1].astype(F32)
            part_ref[:, k * TILE : (k + 1) * TILE] = total.astype(BF16)

        sibling = (w, x * nlo + 1 - c, m)

        def att_hop_c(i):
            return remote(dwt.at[i, :, :, 1 - c], att_c.at[i], acs.at[i], acr.at[i], sibling)

        def att_hop_x(i, d):
            there, device = along_x(d)
            return remote(att_red.at[i, :, there], att_x.at[i, d - 1], axs.at[i, d - 1], axr.at[i, d - 1], device)

        def att_place(i, values):
            dwt[i] = values.reshape(nw, nhi, nlo, -1, D).astype(BF16)
            att_hop_c(i).start()

        def att_combine(i):
            att_hop_c(i).wait()
            att_red[i] = dwt[i, :, :, c] + att_c[i]
            for d in range(1, nhi):
                att_hop_x(i, d).start()

        def att_hop_z(d):
            there, device = along_z(d)
            return remote(att_two.at[d - 1], att_z.at[d - 1], azs.at[d - 1], azr.at[d - 1], device)

        def att_chain(i, zi):
            total = att_red[i, zi, x]
            for d in range(1, nhi):
                total = total + att_x[i, d - 1, zi]
            return total

        def att_spread(i):
            for d in range(1, nhi):
                att_hop_x(i, d).wait()
            for d in range(1, nw):
                there, _ = along_z(d)
                att_two[d - 1] = att_chain(i, there)
                att_hop_z(d).start()

        def att_finish(i, j):
            for d in range(1, nw):
                att_hop_z(d).wait()
            total = att_chain(i, w).astype(F32)
            for d in range(1, nw):
                total = total + att_z[d - 1].astype(F32)
            done_ref[...] = total.astype(BF16)
            for d in range(1, nhi):
                att_hop_x(j, d).wait()
            total = att_red[j, :, x]
            for d in range(1, nhi):
                total = total + att_x[j, d - 1]
            half_ref[...] = total

    @pl.when(step == 0)
    def _():
        greet_group(nw, nn, True)
        if direct:
            for k in range(2, chunks):
                load(k).start()
            start_x(2)
            stage_x(0)
            stage_x(1)
        swap_branch().start()
        swap_gate().start()

    for image in range(images):

        @pl.when(step == image)
        def _():
            at = slice(image * seq, (image + 1) * seq)
            attn = attn_ref[...]
            value = tok_ref[...].astype(F32) + mod_ref[0, 2:3] * attn

            @pl.when(m == image)
            def _():
                keep[...] = value
                keep_mod[...] = mod_ref[0]

            normed, inv = norm_stats(value)
            grad = back_own[0].astype(F32) + back_peer[0].astype(F32)
            mid_sums[0, 0:1] = jnp.sum(grad, axis=0, keepdims=True)
            mid_sums[0, 1:2] = jnp.sum(grad * normed, axis=0, keepdims=True)
            grad = cot_ref[...].astype(F32) + norm_back(grad * (1.0 + mod_ref[0, 4:5]), normed, inv)
            mid[at] = grad
            mid_sums[0, 2:3] = jnp.sum(grad * attn, axis=0, keepdims=True)
            low = (grad * mod_ref[0, 2:3]).astype(BF16)
            mid_sums[0, 3:4] = jnp.sum(low.astype(F32), axis=0, keepdims=True)
            mid_sums[0, 4:8] = jnp.zeros((4, D), F32)
            ga[at] = low
            turned = mm(w_ref[...], low, NT)
            if not moved:
                turned = mm(perm_ref[...], turned.astype(BF16))
            ga_t[:, :, at] = turned.reshape(HEADS, HD, seq).astype(BF16)

    @pl.when((step >= att_at) & (step < part_at))
    def _():
        for j in range(GROUP):
            h = (step - att_at) * GROUP + j
            place = own[h]
            ds_sum = jnp.zeros((seq, seq), F32)
            for image in range(images):
                at = slice(image * seq, (image + 1) * seq)
                query, key, value = [qkv_ref[p, j, :, at] for p in range(3)]
                grad = ga_t[place, :, at]
                probs = jnp.exp(mm(key, query, TN) * INV_ROOT + (bias_ref[j] - lse_ref[j, :, at]))
                grad_probs = mm(value, grad, TN)
                inner = jnp.sum(probs * grad_probs, axis=0, keepdims=True)
                ds = (probs * (grad_probs - inner)).astype(BF16)
                made[0, h, :, at] = (mm(key, ds) * INV_ROOT).astype(BF16)
                made[1, h, :, at] = (mm(query, ds, NT) * INV_ROOT).astype(BF16)
                made[2, h, :, at] = mm(grad, probs.astype(BF16), NT).astype(BF16)
                ds_sum = ds_sum + ds.astype(F32)
            ds_all[h] = ds_sum

    @pl.when((step >= part_at) & (step < part_at + 3))
    def _():
        p = step - part_at
        across = made[p].astype(F32).reshape(D, rows)
        upright = across.T.astype(BF16)
        back = mm(upright, w_ref[...], NT)

        @pl.when(p == 0)
        def _():
            acc[...] = back

        @pl.when(p > 0)
        def _():
            acc[...] += back

        if direct:
            for q in range(3):

                @pl.when((p == q) & (m == (0 if q == 2 else 1)))
                def _(q=q):
                    att_place(q % 2, mm(shaped_ref[...], across.astype(BF16), NT))
        else:
            dw_ref[...] = mm(shaped_ref[...], across.astype(BF16), NT).astype(BF16)
        wide = upright.astype(F32)
        for image in range(images):
            time_ref[image : image + 1] = jnp.sum(
                wide[image * seq : (image + 1) * seq], axis=0, keepdims=True
            )

    @pl.when((step >= rel_at) & (step < end_at))
    def _():
        index = index_ref[0]
        low = jnp.bitwise_and(index, BUCKETS - 1)
        high = jnp.right_shift(index, 7)
        bucket = lax.broadcasted_iota(jnp.int32, (BUCKETS, index.shape[1]), 0)
        hot = jnp.where(bucket == low, 1.0, 0.0).astype(BF16)
        start = pl.multiple_of((step - rel_at) * REL_ROWS, REL_ROWS)
        turned = jnp.swapaxes(ds_all[:, pl.ds(start, REL_ROWS), :], 0, 1)
        total = jnp.concatenate([turned[j] for j in range(REL_ROWS)], axis=1)
        picked = jnp.concatenate([jnp.where(high == a, total, 0.0) for a in range(1024 // BUCKETS)], axis=0)
        found = mm(picked.astype(BF16), hot, NT)

        @pl.when(step == rel_at)
        def _():
            rel_ref[...] = found

        @pl.when(step > rel_at)
        def _():
            rel_ref[...] += found

    @pl.when(step >= end_at)
    def _():
        normed, inv = norm_stats(tok_ref[...].astype(F32))
        at = pl.ds(pl.multiple_of((step - end_at) * seq, seq), seq)
        grad = acc[at]
        sums[0, 0:1] = jnp.sum(grad, axis=0, keepdims=True)
        sums[0, 1:2] = jnp.sum(grad * normed, axis=0, keepdims=True)
        sums[0, 2:8] = jnp.zeros((6, D), F32)
        grad = mid[at] + norm_back(grad * (1.0 + mod_ref[0, 1:2]), normed, inv)
        in_ref[...] = mm_split(grad, perm_ref[...], NT)

    if direct:

        @pl.when((step == images) & (m == 0))
        def _():
            att_place(1, mm(att_ref[...], ga[...]))

        @pl.when((step == part_at + 1) & (m == 0))
        def _():
            att_combine(1)

        @pl.when((step == part_at + 1) & (m == 1))
        def _():
            att_combine(0)

        @pl.when((step == rel_at + 4) & (m == 1))
        def _():
            att_combine(1)

        @pl.when((step == rel_at + 4) & (m == 0))
        def _():
            att_combine(0)

        spread = [0, 0, 3, 5, 8, 9]
        begin = [0, 0, 0, 1, 3, 5]
        after = [5, 6, 9, end_at, last, last]

        for i in range(2):

            @pl.when((step == end_at - 1) & (m == 1 - i))
            def _(i=i):
                att_spread(i)

        for k in range(2, chunks):

            @pl.when(step == spread[min(k, 5)])
            def _(k=k):
                stage_x(k)

        for k in range(3, chunks):

            @pl.when(step == begin[min(k, 5)])
            def _(k=k):
                start_x(k)

        for k in range(chunks):

            @pl.when(step == after[min(k, 5)])
            def _(k=k):
                stage_z(k)
    else:

        @pl.when(step == images)
        def _():
            dw_ref[...] = mm(att_ref[...], ga[...]).astype(BF16)

    @pl.when(step == last)
    def _():
        swap_branch().wait()
        swap_gate().wait()
        branch_out[...] = branch_in[...]
        gate_out[...] = gate_in[...]

    if direct:
        for i in range(2):

            @pl.when((step == last) & (m == 1 - i))
            def _(i=i):
                att_finish(i, 1 - i)


def back_core(own, att, shaped_t, gathered, qkv, bias, lse, index_t, tok, mod, perm, back_own, back_peer,
              attn, cot, send, gate, reduced, seq, images, nw, nn, moved):
    rows = seq * images
    groups = HEADS // GROUP
    att_at = images + 1
    part_at = att_at + groups
    rel_at = part_at + 3
    end_at = rel_at + seq // REL_ROWS
    last = end_at + images - 1
    nhi = nn // 2
    direct = len(reduced) == 2
    hi, wi = (max(nhi - 1, 1), max(nw - 1, 1))
    vmem = pl.BlockSpec(memory_space=pltpu.VMEM)
    dma = pltpu.SemaphoreType.DMA

    def group(s):
        return jnp.clip(s - att_at, 0, groups - 1)

    def part(s):
        return jnp.clip(s - part_at, 0, 2)

    def early(s):
        return jnp.minimum(s, images - 1)

    def both(s):
        return jnp.where(s < images, s, jnp.clip(s - end_at, 0, images - 1))

    def late(s):
        return jnp.clip(s - end_at, 0, images - 1)

    per = pl.BlockSpec((1, 8, D), lambda s, own: (both(s), 0, 0))
    swapped = once((1, seq, D), lambda s, own: (early(s), 0, 0))
    extra_in, extra_out, extra_shape, extra_scratch = ([], [], [], [])
    if direct:
        blk, cols = reduced[0].shape[2:]
        cols = cols + 2 * TILE
        chunks = cols // TILE
        extra_in = [ANY, once((nw, blk, 2 * TILE), lambda s, own: (0, 0, 0))]
        extra_out = [vmem, vmem, vmem]
        extra_shape = [
            jax.ShapeDtypeStruct((blk, cols), BF16),
            jax.ShapeDtypeStruct((blk, D), BF16),
            jax.ShapeDtypeStruct((nw, blk, D), BF16),
        ]
        extra_scratch = [
            pltpu.VMEM((chunks - 2, nw, blk, TILE), BF16),
            pltpu.VMEM((chunks - 2, hi, nw, blk, TILE), BF16),
            pltpu.VMEM((chunks, wi, blk, TILE), BF16),
            pltpu.VMEM((chunks, wi, blk, TILE), BF16),
            dma((chunks - 2,)),
            dma((chunks - 2, hi)),
            dma((chunks - 2, hi)),
            dma((chunks, wi)),
            dma((chunks, wi)),
            pltpu.VMEM((2, nw, nhi, 2, blk, D), BF16),
            pltpu.VMEM((2, nw, nhi, blk, D), BF16),
            pltpu.VMEM((2, nw, nhi, blk, D), BF16),
            pltpu.VMEM((2, hi, nw, blk, D), BF16),
            pltpu.VMEM((wi, blk, D), BF16),
            pltpu.VMEM((wi, blk, D), BF16),
            dma((2,)),
            dma((2,)),
            dma((2, hi)),
            dma((2, hi)),
            dma((wi,)),
            dma((wi,)),
        ]
    else:
        extra_out = [
            pl.BlockSpec((D, D), lambda s, own: (0, jnp.where(s < part_at, 3, jnp.clip(s - part_at, 0, 2))))
        ]
        extra_shape = [jax.ShapeDtypeStruct((D, ATT), BF16)]
    return pl.pallas_call(
        partial(back_body, nw, nn, seq, images, moved, direct),
        grid_spec=pltpu.PrefetchScalarGridSpec(
            num_scalar_prefetch=1,
            grid=(last + 1,),
            in_specs=[
                once((D, rows), lambda s, own: (0, 0)),
                once((D, rows), lambda s, own: (0, 0)),
                pl.BlockSpec((D, D), lambda s, own: (0, jnp.where(s < images, 3, part(s)))),
                pl.BlockSpec((3, GROUP, HD, rows), lambda s, own: (0, group(s), 0, 0)),
                pl.BlockSpec((GROUP, seq, seq), lambda s, own: (group(s), 0, 0)),
                pl.BlockSpec((GROUP, 1, rows), lambda s, own: (group(s), 0, 0)),
                pl.BlockSpec(
                    (1, 1, REL_ROWS * seq), lambda s, own: (jnp.clip(s - rel_at, 0, seq // REL_ROWS - 1), 0, 0)
                ),
                once((seq, D), lambda s, own: (both(s), 0)),
                per,
                once((D, D), lambda s, own: (0, 0)),
                swapped,
                swapped,
                once((seq, D), lambda s, own: (early(s), 0)),
                once((seq, D), lambda s, own: (early(s), 0)),
                ANY,
                ANY,
            ]
            + extra_in,
            out_specs=[
                pl.BlockSpec((images, D), lambda s, own: (0, part(s))),
                vmem,
                pl.BlockSpec((seq, D), lambda s, own: (late(s), 0)),
                pl.BlockSpec((1, 8, D), lambda s, own: (late(s), 0, 0)),
                pl.BlockSpec((1, 8, D), lambda s, own: (early(s), 0, 0)),
                vmem,
                vmem,
                vmem,
                vmem,
            ]
            + extra_out,
            scratch_shapes=[
                pltpu.VMEM((3, HEADS, HD, rows), BF16),
                pltpu.VMEM((rows, D), BF16),
                pltpu.VMEM((HEADS, HD, rows), BF16),
                pltpu.VMEM((seq, D), BF16),
                pltpu.VMEM((8, D), F32),
                pltpu.VMEM((rows, D), F32),
                pltpu.VMEM((HEADS, seq, seq), F32),
                pltpu.VMEM((rows, D), F32),
                dma,
                dma,
                dma,
                dma,
            ]
            + extra_scratch,
        ),
        out_shape=[
            jax.ShapeDtypeStruct((images, 3 * D), F32),
            jax.ShapeDtypeStruct((HEADS * 1024 // BUCKETS, BUCKETS), F32),
            jax.ShapeDtypeStruct((rows, D), F32),
            jax.ShapeDtypeStruct((images, 8, D), F32),
            jax.ShapeDtypeStruct((images, 8, D), F32),
            jax.ShapeDtypeStruct((seq, D), F32),
            jax.ShapeDtypeStruct((8, D), F32),
            jax.ShapeDtypeStruct((seq, D), BF16),
            jax.ShapeDtypeStruct((8, D), F32),
        ]
        + extra_shape,
        compiler_params=params(collective_id=5, has_side_effects=True),
        cost_estimate=cost(30 * 10**9, 8 * 10**7),
        name="back_core",
    )(
        own, att, shaped_t, gathered, qkv, bias, lse,
        index_t.reshape(seq // REL_ROWS, 1, REL_ROWS * seq), tok, mod, perm, back_own, back_peer, attn, cot,
        send, gate, *reduced,
    )


CHUNKS = 3


def collect_body(nw, nn, nm, seq, images, direct, shared_rows, red_ref, time_ref, mid_sums, front_sums, in_sums, gate_own,
                 gate_peer, b_one_ref, rel_ref, mod_ref, keep_mod, perm_ref, *rest):
    if direct:
        done_ref, mlp_ref, emb_ref, silu_ref = rest[:4]
        rest = rest[4:]
    keep_hbm, mine_hbm, branch_hbm = rest[:3]
    rest = rest[3:]
    if direct:
        att_out, mlp_out, ada_out, norm_out = rest[:4]
        small_out, final_ref, out_ref, img_out, slots, ss, sr = rest[4:11]
        rest = rest[11:]
    else:
        img_out, small_out, final_ref = rest[:3]
        rest = rest[3:]
    (from_z, gath, sc, sx, sz, keep, mine, branch,
     zs, zr, ys, yr, ics, icr, ixs, ixr, izs, izr, tcs, tcr, txs, txr, tzs, tzr, ms) = rest
    w, n, m = position()
    nlo, nhi, groups = (2, nn // 2, nw * nn)
    c, x = (lax.rem(n, nlo), lax.div(n, nlo))
    slot = (c * nhi + x) * nw + w
    width = D // CHUNKS
    first_at = pl.multiple_of((1 - m) * 3 * D, 128)
    later_at = (1 - m) * 2 * D + m * D
    sibling = (w, x * nlo + 1 - c, m)
    twin = (w, n, 1 - m)

    def along_x(k):
        there = lax.rem(x + k, nhi)
        return (there, (w, there * nlo + c, m))

    def along_z(k):
        there = lax.rem(w + k, nw)
        return (there, (there, n, m))

    if direct:
        greet_all(nw, nn, nm)
    else:
        greet_group(nw, nn, True)

    def cols(k):
        return pl.ds(pl.multiple_of(later_at + k * width, 128), width)

    def hop_z(k, d):
        there, device = along_z(d)
        return remote(
            red_ref.at[there, :, pl.ds(k * width, width)], from_z.at[k, d - 1], zs.at[k, d - 1], zr.at[k, d - 1], device
        )

    def start_z(k):
        if direct:
            for d in range(1, nw):
                hop_z(k, d).start()

    def hop_y(k):
        at = pl.ds(first_at, D) if k == CHUNKS else cols(k)
        return remote(out_ref.at[:, at], out_ref.at[:, at], ys.at[k], yr.at[k], twin)

    places = ((keep_hbm, keep), (mine_hbm, mine), (branch_hbm, branch))
    loads = [pltpu.make_async_copy(a, b, ms.at[i]) for i, (a, b) in enumerate(places)]
    for copy in loads:
        copy.start()

    def image_rows():
        rows = []
        for i in range(images):
            gate_two = gate_own[i : i + 1] + gate_peer[i : i + 1] + mod_ref[i, 7:8] * front_sums[i, 1:2]
            rows += [
                in_sums[i, 0:1], in_sums[i, 1:2], mid_sums[i, 2:3], mid_sums[i, 0:1], mid_sums[i, 1:2], gate_two,
            ]
        rows.append(mid_sums[0, 3:4] + mid_sums[1, 3:4])
        rows.append(front_sums[0, 0:1] + front_sums[1, 0:1])
        rows.append(jnp.zeros((16 - len(rows), D), F32))
        parts = jnp.concatenate(exact_parts(jnp.concatenate(rows, axis=0)), axis=0)
        thrice = mm(parts, perm_ref[...], NT)
        back = thrice[0:16] + thrice[16:32] + thrice[32:48]
        gath[slot, :, 0 : 3 * D] = time_ref[...]
        for i in range(images):
            for q in range(6):
                gath[slot, i : i + 1, (3 + q) * D : (4 + q) * D] = back[i * 6 + q : i * 6 + q + 1]
        return back

    def small_rows(back):
        mine_small = sc.at[c]
        count = rel_ref.shape[0]
        mine_small[0:count] = rel_ref[...]
        mine_small[count:] = jnp.zeros((SMALL_ROWS - count, 128), F32)
        at = count
        for row in (back[images * 6 : images * 6 + 1], back[images * 6 + 1 : images * 6 + 2], b_one_ref[...]):
            for j in range(row.shape[1] // 128):
                mine_small[at : at + 1] = row[:, j * 128 : (j + 1) * 128]
                at += 1

    img_z = []
    for d in range(1, nw):
        there, device = along_z(d)
        img_z.append(remote(gath.at[slot], gath.at[slot], izs.at[d - 1], izr.at[d - 1], device))
    mine_x = pl.ds((c * nhi + x) * nw, nw)
    img_x = []
    for d in range(1, nhi):
        there, device = along_x(d)
        img_x.append(remote(gath.at[mine_x], gath.at[mine_x], ixs.at[d - 1], ixr.at[d - 1], device))
    mine_c = pl.ds(c * nhi * nw, nhi * nw)
    img_c = remote(gath.at[mine_c], gath.at[mine_c], ics, icr, sibling)
    small_c = remote(sc.at[c], sc.at[c], tcs, tcr, sibling)
    small_x = []
    for d in range(1, nhi):
        there, device = along_x(d)
        small_x.append(remote(sx.at[x], sx.at[x], txs.at[d - 1], txr.at[d - 1], device))
    small_z = []
    for d in range(1, nw):
        there, device = along_z(d)
        small_z.append(remote(sz.at[w], sz.at[w], tzs.at[d - 1], tzr.at[d - 1], device))

    def stage_c(k):
        if not direct:
            return
        for d in range(1, nw):
            hop_z(k, d).wait()
        total = red_ref[w, :, k * width : (k + 1) * width].astype(F32)
        for d in range(1, nw):
            total = total + from_z[k, d - 1].astype(F32)
        out_ref[:, cols(k)] = total.astype(BF16)
        hop_y(k).start()

    back = image_rows()
    for hop in img_z:
        hop.start()
    small_rows(back)
    small_c.start()
    if direct:
        out_ref[:, pl.ds(first_at, D)] = done_ref[...]
        hop_y(CHUNKS).start()
        mlp_sq = mlp_rows(mlp_ref, mlp_out)
    small_c.wait()
    sx[x] = sc[0] + sc[1]
    for hop in small_x:
        hop.start()
    for hop in img_z:
        hop.wait()
    for hop in img_x:
        hop.start()
    start_z(0)
    for hop in small_x:
        hop.wait()
    total = sx[0]
    for k in range(1, nhi):
        total = total + sx[k]
    sz[w] = total
    for hop in small_z:
        hop.start()
    start_z(1)
    for copy in loads:
        copy.wait()
    summed = mine[...] + branch[...].astype(F32) + keep_mod[7:8]
    final = (keep[...] + keep_mod[5:6] * summed).astype(BF16)
    final_ref[...] = mm(final, perm_ref[...], NT).astype(BF16)
    for hop in img_x:
        hop.wait()
    img_c.start()
    start_z(2)
    stage_c(0)
    img_c.wait()
    for g in range(groups):
        img_out[2 * g : 2 * g + 2, :] = gath[g]
    if direct:
        att_sq = image_weights(img_out, emb_ref, silu_ref, att_out, ada_out)
    for hop in small_z:
        hop.wait()
    total = sz[0]
    for k in range(1, nw):
        total = total + sz[k]
    small_out[...] = total
    stage_c(1)
    stage_c(2)
    if direct:
        for k in range(CHUNKS + 1):
            hop_y(k).wait()
        att_sq = att_sq + space_rows(out_ref, perm_ref, att_out)
        norm_of(att_sq, mlp_sq, small_out, ada_out, shared_rows, norm_out, slots, ss, sr, nw, nn, nm)


SMALL_ROWS = 168


def collect(red, time_grad, mid_sums, front_sums, in_sums, gate_own, gate_peer, b_one, rel, mod, keep_mod, perm,
            keep, mine, branch, extra, seq, images, shared_rows, nw, nn, nm):
    groups = nw * nn
    count = groups * nm
    nhi = nn // 2
    img_width = 9 * D
    direct = len(extra) > 0
    blk = D // groups
    half = b_one.shape[1]
    width = D // CHUNKS
    vmem = pl.BlockSpec(memory_space=pltpu.VMEM)
    dma = pltpu.SemaphoreType.DMA
    hi, wi = (max(nhi - 1, 1), max(nw - 1, 1))
    many = dma((CHUNKS + 1,))
    small = jax.ShapeDtypeStruct((SMALL_ROWS, 128), F32)
    final = jax.ShapeDtypeStruct((seq, D), BF16)
    if direct:
        out_shape = [
            jax.ShapeDtypeStruct((blk, 13 * D), F32),
            jax.ShapeDtypeStruct((blk, 2, half), F32),
            jax.ShapeDtypeStruct((1, 6 * D), F32),
            jax.ShapeDtypeStruct((8, 128), F32),
            small,
            final,
        ]
        ahead = [
            pltpu.VMEM((blk, ATT), BF16),
            pltpu.VMEM((2 * groups, img_width), F32),
            pltpu.VMEM((count, 8, 128), F32),
            dma((count,)),
            dma((count,)),
        ]
    else:
        out_shape = [jax.ShapeDtypeStruct((2 * groups, img_width), F32), small, final]
        ahead = []
    return pl.pallas_call(
        partial(collect_body, nw, nn, nm, seq, images, direct, shared_rows),
        in_specs=[vmem] * (12 + len(extra)) + [ANY] * 3,
        out_specs=[vmem] * len(out_shape),
        out_shape=out_shape,
        scratch_shapes=ahead
        + [
            pltpu.VMEM((CHUNKS, wi, blk, width), BF16),
            pltpu.VMEM((groups, 2, img_width), F32),
            pltpu.VMEM((2, SMALL_ROWS, 128), F32),
            pltpu.VMEM((nhi, SMALL_ROWS, 128), F32),
            pltpu.VMEM((nw, SMALL_ROWS, 128), F32),
            pltpu.VMEM((seq, D), F32),
            pltpu.VMEM((seq, D), F32),
            pltpu.VMEM((seq, D), BF16),
            dma((CHUNKS, wi)), dma((CHUNKS, wi)), many, many,
            dma, dma, dma((hi,)), dma((hi,)), dma((wi,)), dma((wi,)),
            dma, dma, dma((hi,)), dma((hi,)), dma((wi,)), dma((wi,)),
            dma((3,)),
        ],
        compiler_params=params(collective_id=2, has_side_effects=True),
        cost_estimate=cost(10**9, 3 * 10**7),
        name="collect",
    )(
        red, time_grad, mid_sums, front_sums, in_sums, gate_own, gate_peer, b_one, rel, mod, keep_mod, perm,
        *extra, keep, mine, branch,
    )


def who_is(k, nw, nn, nm):
    w, n, m = position()
    count = nw * nn * nm
    other = lax.rem((w * nn + n) * nm + m + k, count)
    pair = lax.div(other, nm)
    return (lax.div(pair, nn), lax.rem(pair, nn), lax.rem(other, nm))


def greet_all(nw, nn, nm):
    bar = pltpu.get_barrier_semaphore()
    count = nw * nn * nm

    def ask(k, carry):
        pl.semaphore_signal(bar, inc=1, device_id=who_is(k, nw, nn, nm), device_id_type=MESH)
        return carry

    lax.fori_loop(1, count, ask, 0)
    pl.semaphore_wait(bar, count - 1)


def tally(values):
    return jnp.sum(jnp.sum(values * values, axis=0, keepdims=True), axis=1, keepdims=True)


def mlp_rows(mlp_ref, mlp_out):
    total = jnp.zeros((1, 1), F32)
    for f in range(mlp_ref.shape[1] // (2 * TILE)):
        at = slice(f * TILE, (f + 1) * TILE)
        for half in range(2):
            part = mlp_ref[:, (2 * f + half) * TILE : (2 * f + half + 1) * TILE].astype(F32)
            mlp_out[:, half, at] = part
            total = total + tally(part)
    return total


def image_weights(img_ref, emb_ref, silu_ref, att_out, ada_out):
    emb = emb_ref[...]
    silu = silu_ref[...]
    imgs = exact_parts(img_ref[:, 0 : 3 * D])
    part = mm(emb, imgs[0], TN) + mm(emb, imgs[1], TN) + mm(emb, imgs[2], TN)
    att_out[:, 3 * D : 6 * D] = part
    total = tally(part)
    ada = img_ref[:, 3 * D :]
    ada_out[...] = jnp.sum(ada, axis=0, keepdims=True)
    imgs = exact_parts(ada)
    part = mm(silu, imgs[0], TN) + mm(silu, imgs[1], TN) + mm(silu, imgs[2], TN)
    att_out[:, 7 * D :] = part
    return total + tally(part)


def space_rows(att_ref, perm_ref, att_out):
    part = att_ref[:, 0 : 3 * D].astype(F32)
    att_out[:, 0 : 3 * D] = part
    total = tally(part)
    part = mm(att_ref[:, 3 * D :], perm_ref[...], NT)
    att_out[:, 6 * D : 7 * D] = part
    return total + tally(part)


def norm_of(att_sq, mlp_sq, small_ref, ada_out, shared_rows, norm_out, slots, ss, sr, nw, nn, nm):
    w, n, m = position()
    groups = nw * nn
    count = groups * nm
    mine = (w * nn + n) * nm + m
    small_sq = tally(small_ref[0:shared_rows]) + tally(ada_out[...])
    bias_sq = tally(small_ref[shared_rows:])
    local = mlp_sq + att_sq / nm + small_sq / count + bias_sq / groups
    slots[mine] = jnp.broadcast_to(local, (8, 128))

    def copy_to(k):
        return remote(slots.at[mine], slots.at[mine], ss.at[k], sr.at[k], who_is(k, nw, nn, nm))

    def send(k, carry):
        copy_to(k).start()
        return carry

    def finish(k, carry):
        copy_to(k).wait()
        return carry

    lax.fori_loop(1, count, send, 0)
    lax.fori_loop(1, count, finish, 0)
    norm_out[...] = jnp.sqrt(jnp.sum(slots[...], axis=0))


def norm_body(nw, nn, nm, shared_rows, att_ref, mlp_ref, img_ref, emb_ref, silu_ref, small_ref, perm_ref,
              att_out, mlp_out, ada_out, norm_out, slots, ss, sr):
    greet_all(nw, nn, nm)
    mlp_sq = mlp_rows(mlp_ref, mlp_out)
    att_sq = image_weights(img_ref, emb_ref, silu_ref, att_out, ada_out)
    att_sq = att_sq + space_rows(att_ref, perm_ref, att_out)
    norm_of(att_sq, mlp_sq, small_ref, ada_out, shared_rows, norm_out, slots, ss, sr, nw, nn, nm)


def collect_norm(att, mlp, imgs, emb, silu, small, perm, shared_rows, nw, nn, nm):
    rows = att.shape[0]
    half = mlp.shape[1] // 2
    count = nw * nn * nm
    dma = pltpu.SemaphoreType.DMA
    return pl.pallas_call(
        partial(norm_body, nw, nn, nm, shared_rows),
        out_shape=[
            jax.ShapeDtypeStruct((rows, 13 * D), F32),
            jax.ShapeDtypeStruct((rows, 2, half), F32),
            jax.ShapeDtypeStruct((1, 6 * D), F32),
            jax.ShapeDtypeStruct((8, 128), F32),
        ],
        scratch_shapes=[pltpu.VMEM((count, 8, 128), F32), dma((count,)), dma((count,))],
        compiler_params=params(collective_id=3, has_side_effects=True),
        cost_estimate=cost(10**8, 10**7),
        name="collect_norm",
    )(att, mlp, imgs, emb, silu, small, perm)


def on_device(
    tokens,
    timesteps,
    owners,
    rel_index,
    cotangent,
    att_master,
    att_moment,
    att_second,
    mlp_master,
    mlp_moment,
    mlp_second,
    small_master,
    small_moment,
    small_second,
    bias_master,
    bias_moment,
    bias_second,
):
    groups = owners.shape[0]
    rows_blk = att_master.shape[0]
    half_ff = mlp_master.shape[2]
    images = timesteps.shape[0]
    tok_rows = tokens.shape[0]
    half_rows = cotangent.shape[0]
    seq_len = tok_rows // images
    nw, nn, nm = (lax.axis_size("wide"), lax.axis_size("narrow"), lax.axis_size("mlp"))
    mlp_at = lax.axis_index("mlp")
    mine = lax.axis_index(GRID)
    moved = rows_blk == HD
    swap = [(i, nm - 1 - i) for i in range(nm)]

    place = (owners[:, None] * rows_blk + jnp.arange(rows_blk)[None, :]).reshape(D)
    pick = (place[:, None] == (mine * rows_blk + jnp.arange(rows_blk))[None, :]).astype(BF16)

    packed, perm = pack_weights(owners, att_master, mlp_master)
    perm_f = perm.astype(F32)
    gathered = lax.all_gather(packed, GRID, axis=0, tiled=True)

    time_emb = time_embed(timesteps)
    emb_rows = jnp.concatenate(
        [time_emb, jax.nn.silu(time_emb), jnp.zeros((8 - 2 * images, D), F32)], axis=0
    ).astype(BF16)
    summed, emb_mine, silu_mine, cot_all = modul_exchange(
        emb_rows, att_master, pick, cotangent, nw, nn
    )
    time_part = summed[:, 0 : 3 * D]
    offset = NREL * HEADS
    table_t = jnp.pad(small_master[0:offset].reshape(NREL, HEADS).T, ((0, 0), (0, 1024 - NREL)))
    b_ada = small_master[offset : offset + 6 * D]
    b_rest = small_master[offset + 6 * D : offset + 8 * D].reshape(1, 2, D)
    modulation = (summed[:, 3 * D :] + b_ada).reshape(images, 6, D)
    mod = jnp.concatenate([modulation, jnp.broadcast_to(b_rest, (images, 2, D))], axis=1)
    mod = mm_exact(mod.reshape(images * 8, D), perm_f).reshape(images, 8, D)
    index_t = rel_index.T
    bias = rel_bias(index_t, table_t.reshape(HEADS, 1, 1024), seq_len)

    tok, shaped, shaped_t, cot, grad_branch, front_sums = front(
        tokens, cot_all, perm, mod, seq_len, images
    )
    heads_at = owners if moved else jnp.arange(HEADS, dtype=jnp.int32)
    qkv, attended, lse = attend_fwd(heads_at, shaped, gathered, time_part, bias, seq_len, images)
    attended = attended.reshape(D, tok_rows)
    if not moved:
        attended = mm(perm, attended, TN).astype(BF16)
    attn_out, shaped_two = middle(attended, gathered, tok, mod, seq_len, images)
    made = mlp_core(
        shaped_two, grad_branch, gathered, bias_master.reshape(1, half_ff), cot, seq_len, nw, nn
    )
    mlp_term, branch_mine, branch_send, gate_own, b_one_grad, back_own, back_peer = made[:7]
    reduced = (mlp_term, made[7]) if len(made) == 8 else ()

    done = back_core(
        heads_at,
        attended,
        shaped_t,
        gathered,
        qkv,
        bias,
        lse,
        index_t,
        tok,
        mod,
        perm,
        back_own,
        back_peer,
        attn_out,
        cot,
        branch_send,
        gate_own,
        reduced,
        seq_len,
        images,
        nw,
        nn,
        moved,
    )
    time_grad, rel_sum, input_grad, in_sums, mid_sums, keep, keep_mod, branch_peer, gate_peer = done[:9]
    rel_rows = HEADS * 1024 // BUCKETS
    shared_rows = rel_rows + 2 * D // 128
    direct = len(done) == 12
    if direct:
        mlp_part, part_done, red = done[9:]
        extra = (part_done, mlp_part, emb_mine, silu_mine)
    else:
        mlp_part = lax.psum_scatter(mlp_term, GRID, scatter_dimension=0, tiled=True)
        red = jnp.zeros((1, 1, 1), BF16)
        extra = ()
    shared = collect(
        red, time_grad, mid_sums, front_sums, in_sums, gate_own, gate_peer, b_one_grad, rel_sum, mod, keep_mod, perm,
        keep, branch_mine, branch_peer, extra, seq_len, images, shared_rows, nw, nn, nm,
    )
    if direct:
        att_grad, mlp_grad, b_ada_grad, norm, small_all, output = shared
    else:
        imgs_all, small_all, output = shared
        att_part = lax.psum_scatter(done[9], GRID, scatter_dimension=0, tiled=True)
        att_grad, mlp_grad, b_ada_grad, norm = collect_norm(
            att_part, mlp_part, imgs_all, emb_mine, silu_mine, small_all, perm, shared_rows, nw, nn, nm
        )

    grad_norm = norm[0, 0]
    clip_scale = jnp.minimum(1.0, 1.0 / (grad_norm + 1e-06))
    rel_grad = small_all[0:rel_rows].reshape(-1, HEADS, BUCKETS).transpose(0, 2, 1).reshape(-1)[0:offset]
    small_grad = jnp.concatenate(
        [rel_grad, b_ada_grad.reshape(-1), small_all[rel_rows:shared_rows].reshape(-1)]
    )
    bias_grad = small_all[shared_rows : shared_rows + half_ff // 128].reshape(-1)
    att_new, att_mom_new, att_sec_new = adam_update(
        att_master, att_moment, att_second, att_grad, clip_scale
    )
    mlp_new, mlp_mom_new, mlp_sec_new = adam_update(
        mlp_master, mlp_moment, mlp_second, mlp_grad, clip_scale
    )
    small_new, small_mom_new, small_sec_new = adam_update(
        small_master, small_moment, small_second, small_grad, clip_scale
    )
    bias_new, bias_mom_new, bias_sec_new = adam_update(
        bias_master, bias_moment, bias_second, bias_grad, clip_scale
    )
    return (
        output,
        input_grad,
        att_new,
        att_mom_new,
        att_sec_new,
        mlp_new,
        mlp_mom_new,
        mlp_sec_new,
        small_new,
        small_mom_new,
        small_sec_new,
        bias_new,
        bias_mom_new,
        bias_sec_new,
        att_new.astype(BF16),
        mlp_new.astype(BF16),
        grad_norm,
    )


def solution(mesh):
    rows = P(GRID, None)
    cube = P(GRID, None, "mlp")
    return jax.shard_map(
        on_device,
        mesh=mesh,
        in_specs=(
            rows,
            P(GRID),
            P(),
            P(),
            P(("wide", "narrow", "mlp"), None),
            rows,
            rows,
            rows,
            cube,
            cube,
            cube,
            P(),
            P(),
            P(),
            P("mlp"),
            P("mlp"),
            P("mlp"),
        ),
        out_specs=(
            P(("wide", "narrow", "mlp"), None),
            rows,
            rows,
            rows,
            rows,
            cube,
            cube,
            cube,
            P(),
            P(),
            P(),
            P("mlp"),
            P("mlp"),
            P("mlp"),
            rows,
            cube,
            P(),
        ),
        check_vma=False,
    )
```

```python
from functools import partial
import math

import jax
import jax.numpy as jnp
from jax import lax
from jax.experimental import pallas as pl
from jax.experimental.pallas import tpu as pltpu
from jax.sharding import PartitionSpec as P

D = 1152
HEADS = 16
HD = 72
NREL = 961
STEP = 10

HIGH = lax.Precision.HIGHEST
F32 = jnp.float32
BF16 = jnp.bfloat16
GRID = ("wide", "narrow")
NN = (((1,), (0,)), ((), ()))
TN = (((0,), (0,)), ((), ()))
NT = (((1,), (1,)), ((), ()))
INV_ROOT = 1.0 / math.sqrt(HD)
MESH = pl.DeviceIdType.MESH
ANY = pl.BlockSpec(memory_space=pl.ANY)
ATT = 4 * D
GROUP = 4
TILE = 768
VMEM_BYTES = 63 * 1024 * 1024


def mm(a, b, dims=NN):
    return lax.dot_general(a, b, dims, preferred_element_type=F32)


def mm_exact(a, b, dims=NN):
    return lax.dot_general(a, b, dims, precision=HIGH, preferred_element_type=F32)


def norm_stats(values):
    center = values - jnp.mean(values, axis=-1, keepdims=True)
    inv_std = lax.rsqrt(jnp.mean(center * center, axis=-1, keepdims=True) + 1e-06)
    return (center * inv_std, inv_std)


def norm_back(grad_normed, normed, inv_std):
    mean_grad = jnp.mean(grad_normed, axis=-1, keepdims=True)
    mean_proj = jnp.mean(grad_normed * normed, axis=-1, keepdims=True)
    return (grad_normed - mean_grad - normed * mean_proj) * inv_std


def time_embed(steps_int):
    half_dim = D // 2
    frequency = jnp.exp(-math.log(10000.0) * jnp.arange(half_dim).astype(F32) / half_dim)
    angles = steps_int.astype(F32)[:, None] * frequency[None, :]
    return jnp.concatenate([jnp.cos(angles), jnp.sin(angles)], axis=1)


def adam_update(weight, moment, second, grad, clip_scale):
    scaled = grad * clip_scale
    moment_new = 0.9 * moment + 0.1 * scaled
    second_new = 0.999 * second + 0.001 * scaled * scaled
    rate = 1.5 / math.sqrt(D)
    direction = (
        moment_new / (1.0 - 0.9**STEP) / (jnp.sqrt(second_new / (1.0 - 0.999**STEP)) + 1e-08)
    )
    return (weight - rate * (direction + 0.1 * weight), moment_new, second_new)


def exact_parts(values):
    first = values.astype(BF16)
    rest = values - first.astype(F32)
    second = rest.astype(BF16)
    return (first, second, (rest - second.astype(F32)).astype(BF16))


def mm_split(a, b, dims=NN):
    one, two, three = exact_parts(a)
    return mm(one, b, dims) + mm(two, b, dims) + mm(three, b, dims)


def params(**kw):
    return pltpu.CompilerParams(vmem_limit_bytes=VMEM_BYTES, **kw)


def cost(flops, nbytes):
    return pl.CostEstimate(flops=flops, bytes_accessed=nbytes, transcendentals=0)


def position():
    return (lax.axis_index("wide"), lax.axis_index("narrow"), lax.axis_index("mlp"))


def remote(src, dst, send, recv, device):
    return pltpu.make_async_remote_copy(
        src_ref=src, dst_ref=dst, send_sem=send, recv_sem=recv, device_id=device, device_id_type=MESH
    )


def greet_group(nw, nn, with_mlp):
    w, n, m = position()
    mine = w * nn + n
    groups = nw * nn
    bar = pltpu.get_barrier_semaphore()

    def ask(k, carry):
        other = lax.rem(mine + k, groups)
        pl.semaphore_signal(
            bar, inc=1, device_id=(lax.div(other, nn), lax.rem(other, nn), m), device_id_type=MESH
        )
        return carry

    lax.fori_loop(1, groups, ask, 0)
    if with_mlp:
        pl.semaphore_signal(bar, inc=1, device_id=(w, n, 1 - m), device_id_type=MESH)
    pl.semaphore_wait(bar, groups - 1 + (1 if with_mlp else 0))


def pack_body(owners_ref, att_ref, mlp_ref, out_ref, perm_ref):
    rows = att_ref.shape[0]
    half = mlp_ref.shape[2]
    line = lax.broadcasted_iota(jnp.int32, (D, 128), 0)
    move = jnp.zeros((D, 128), jnp.int32) + owners_ref[0] * rows
    for b in range(1, owners_ref.shape[0]):
        move = jnp.where(line >= b * rows, (owners_ref[b] - b) * rows, move)
    place = line + move
    col = lax.broadcasted_iota(jnp.int32, (D, 128), 1)
    for j in range(D // 128):
        perm_ref[:, j * 128 : (j + 1) * 128] = jnp.where(place == col + j * 128, 1.0, 0.0).astype(BF16)
    out_ref[:, 0 : 3 * D] = att_ref[:, 0 : 3 * D].astype(BF16)
    out_ref[:, 3 * D : ATT] = mm(att_ref[:, 6 * D : 7 * D].astype(BF16), perm_ref[...]).astype(BF16)
    out_ref[:, ATT : ATT + half] = mlp_ref[:, 0, :].astype(BF16)
    out_ref[:, ATT + half : ATT + 2 * half] = mlp_ref[:, 1, :].astype(BF16)


def pack_weights(owners, att, mlp):
    rows, _, half = mlp.shape
    vmem = pl.BlockSpec(memory_space=pltpu.VMEM)
    return pl.pallas_call(
        pack_body,
        grid=(1,),
        in_specs=[
            pl.BlockSpec(memory_space=pltpu.SMEM),
            pl.BlockSpec((rows, 7 * D), lambda s: (0, 0)),
            pl.BlockSpec((rows, 2, half), lambda s: (0, 0, 0)),
        ],
        out_specs=[vmem, vmem],
        out_shape=[
            jax.ShapeDtypeStruct((rows, ATT + 2 * half), BF16),
            jax.ShapeDtypeStruct((D, D), BF16),
        ],
        compiler_params=params(),
        name="pack",
    )(owners, att, mlp)


def modul_body(nw, nn, emb_ref, att_ref, pick_ref, cot_ref, sum_ref, emb_out, silu_out, cot_out,
               gath, flat, parts, from_c, from_x, from_z, gs, gr, cs, cr, xs, xr, zs, zr, ys, yr, ls):
    w, n, m = position()
    nlo, nhi, groups = (2, nn // 2, nw * nn)
    c, x = (lax.rem(n, nlo), lax.div(n, nlo))
    half = cot_ref.shape[0]
    width = parts.shape[2]
    slot = (c * nhi + x) * nw + w
    mine = w * nn + n
    greet_group(nw, nn, True)
    rows = pl.ds(m * half, half)
    to_y = remote(cot_ref, cot_out.at[rows], ys, yr, (w, n, 1 - m))
    to_y.start()
    keep = pltpu.make_async_copy(cot_ref, cot_out.at[rows], ls)
    keep.start()
    gath[slot] = emb_ref[...]

    def copy_to(k):
        other = lax.rem(mine + k, groups)
        return remote(gath.at[slot], gath.at[slot], gs.at[k], gr.at[k], (lax.div(other, nn), lax.rem(other, nn), m))

    def send(k, carry):
        copy_to(k).start()
        return carry

    def finish(k, carry):
        copy_to(k).wait()
        return carry

    lax.fori_loop(1, groups, send, 0)
    lax.fori_loop(1, groups, finish, 0)
    picked = mm(gath[...].reshape(groups * 8, D), pick_ref[...]).astype(BF16)
    line = lax.broadcasted_iota(jnp.int32, (2 * groups, 8 * groups), 0)
    col = lax.broadcasted_iota(jnp.int32, (2 * groups, 8 * groups), 1)
    at = (line // 2) * 8 + line % 2
    emb = mm((col == at).astype(BF16), picked).astype(BF16)
    silu = mm((col == at + 2).astype(BF16), picked).astype(BF16)
    emb_out[...] = emb
    silu_out[...] = silu
    flat[:, 0 : 3 * D] = mm(emb, att_ref[:, 3 * D : 6 * D].astype(BF16))
    flat[:, 3 * D : 9 * D] = mm(silu, att_ref[:, 7 * D : 13 * D].astype(BF16))
    for g in range(groups):
        parts[g] = flat[2 * g : 2 * g + 2, :]
    block = nhi * nw
    other_c = (1 - c) * block
    mine_c = c * block
    hop = remote(parts.at[pl.ds(other_c, block)], from_c, cs, cr, (w, x * nlo + 1 - c, m))
    hop.start()
    hop.wait()
    parts[pl.ds(mine_c, block)] = parts[pl.ds(mine_c, block)] + from_c[...]
    hops = []
    for k in range(1, nhi):
        there = lax.rem(x + k, nhi)
        hop = remote(
            parts.at[pl.ds(mine_c + there * nw, nw)], from_x.at[k - 1], xs.at[k - 1], xr.at[k - 1], (w, there * nlo + c, m)
        )
        hop.start()
        hops.append(hop)
    for hop in hops:
        hop.wait()
    first = mine_c + x * nw
    total = parts[pl.ds(first, nw)]
    for k in range(1, nhi):
        total = total + from_x[k - 1]
    parts[pl.ds(first, nw)] = total
    hops = []
    for k in range(1, nw):
        there = lax.rem(w + k, nw)
        hop = remote(parts.at[first + there], from_z.at[k - 1], zs.at[k - 1], zr.at[k - 1], (there, n, m))
        hop.start()
        hops.append(hop)
    for hop in hops:
        hop.wait()
    total = parts[first + w]
    for k in range(1, nw):
        total = total + from_z[k - 1]
    sum_ref[...] = total
    keep.wait()
    to_y.wait()


def modul_exchange(emb_rows, att, pick, cot, nw, nn):
    groups = nw * nn
    nhi = nn // 2
    width = 9 * D
    half = cot.shape[0]
    vmem = pl.BlockSpec(memory_space=pltpu.VMEM)
    dma = pltpu.SemaphoreType.DMA
    return pl.pallas_call(
        partial(modul_body, nw, nn),
        in_specs=[vmem, vmem, vmem, ANY],
        out_specs=[vmem, vmem, vmem, ANY],
        out_shape=[
            jax.ShapeDtypeStruct((2, width), F32),
            jax.ShapeDtypeStruct((2 * groups, att.shape[0]), BF16),
            jax.ShapeDtypeStruct((2 * groups, att.shape[0]), BF16),
            jax.ShapeDtypeStruct((2 * half, D), BF16),
        ],
        scratch_shapes=[
            pltpu.VMEM((groups, 8, D), BF16),
            pltpu.VMEM((2 * groups, width), F32),
            pltpu.VMEM((groups, 2, width), F32),
            pltpu.VMEM((nhi * nw, 2, width), F32),
            pltpu.VMEM((max(nhi - 1, 1), nw, 2, width), F32),
            pltpu.VMEM((max(nw - 1, 1), 2, width), F32),
            dma((groups,)), dma((groups,)), dma, dma,
            dma((max(nhi - 1, 1),)), dma((max(nhi - 1, 1),)),
            dma((max(nw - 1, 1),)), dma((max(nw - 1, 1),)),
            dma, dma, dma,
        ],
        compiler_params=params(collective_id=1, has_side_effects=True),
        cost_estimate=cost(10**8, 3 * 10**7),
        name="modul_exchange",
    )(emb_rows, att, pick, cot)


def bias_body(index_ref, table_ref, bias_ref):
    low = jnp.bitwise_and(index_ref[...], 127)
    high = jnp.right_shift(index_ref[...], 7)
    for part in range(index_ref.shape[1] // 128):
        at = slice(part * 128, (part + 1) * 128)
        lo = low[:, at]
        hi = high[:, at]
        total = jnp.zeros(lo.shape, F32)
        for chunk in range(8):
            row = jnp.broadcast_to(table_ref[0, :, chunk * 128 : (chunk + 1) * 128], lo.shape)
            total = jnp.where(hi == chunk, jnp.take_along_axis(row, lo, axis=1), total)
        bias_ref[0, :, at] = total


def rel_bias(index_t, table_t, seq):
    return pl.pallas_call(
        bias_body,
        grid=(HEADS,),
        in_specs=[
            pl.BlockSpec((seq, seq), lambda h: (0, 0)),
            pl.BlockSpec((1, 1, 1024), lambda h: (h, 0, 0)),
        ],
        out_specs=pl.BlockSpec((1, seq, seq), lambda h: (h, 0, 0)),
        out_shape=jax.ShapeDtypeStruct((HEADS, seq, seq), F32),
        cost_estimate=cost(2 * 10**8, 4 * 10**7),
        name="rel_bias",
    )(index_t, table_t)


def front_body(tok_ref, cot_ref, perm_ref, mod_ref, tok_out, shaped_out, shaped_t, cot_out, branch_out, sums):
    moved = mm(tok_ref[...], perm_ref[...])
    tok_out[...] = moved.astype(BF16)
    normed, _ = norm_stats(moved)
    shaped = normed * (1.0 + mod_ref[0, 1:2]) + mod_ref[0, 0:1]
    shaped_out[...] = shaped.astype(BF16)
    shaped_t[...] = shaped.T.astype(BF16)
    cot = mm(cot_ref[...], perm_ref[...])
    cot_out[...] = cot.astype(BF16)
    branch = (cot * mod_ref[0, 5:6]).astype(BF16)
    branch_out[...] = branch
    sums[0, 0:1] = jnp.sum(branch.astype(F32), axis=0, keepdims=True)
    sums[0, 1:2] = jnp.sum(cot, axis=0, keepdims=True)
    sums[0, 2:8] = jnp.zeros((6, D), F32)


def front(tokens, cot, perm, mod, seq, images):
    rows = seq * images
    tok = pl.BlockSpec((seq, D), lambda n: (n, 0))
    per = pl.BlockSpec((1, 8, D), lambda n: (n, 0, 0))
    return pl.pallas_call(
        front_body,
        grid=(images,),
        in_specs=[tok, tok, pl.BlockSpec((D, D), lambda n: (0, 0)), per],
        out_specs=[tok, tok, pl.BlockSpec((D, seq), lambda n: (0, n)), tok, tok, per],
        out_shape=[
            jax.ShapeDtypeStruct((rows, D), BF16),
            jax.ShapeDtypeStruct((rows, D), BF16),
            jax.ShapeDtypeStruct((D, rows), BF16),
            jax.ShapeDtypeStruct((rows, D), BF16),
            jax.ShapeDtypeStruct((rows, D), BF16),
            jax.ShapeDtypeStruct((images, 8, D), F32),
        ],
        compiler_params=params(),
        cost_estimate=cost(4 * rows * D * D, 10**7),
        name="front",
    )(tokens, cot, perm, mod)


def attend_fwd_body(seq, images, own, shaped_ref, w_ref, time_ref, bias_ref, qkv_ref, out_ref, lse_ref):
    step = pl.program_id(0)

    @pl.when(step < 3)
    def _():
        made = mm(shaped_ref[...], w_ref[...])
        made = jnp.concatenate(
            [made[n * seq : (n + 1) * seq] + time_ref[n : n + 1] for n in range(images)], axis=0
        )
        qkv_ref[step] = made.T.reshape(HEADS, HD, seq * images).astype(BF16)

    @pl.when(step >= 3)
    def _():
        for j in range(GROUP):
            h = (step - 3) * GROUP + j
            query, key, value = [qkv_ref[p, h] for p in range(3)]
            place = own[h]
            for n in range(images):
                at = slice(n * seq, (n + 1) * seq)
                scores = mm(key[:, at], query[:, at], TN) * INV_ROOT + bias_ref[j]
                top = jnp.max(scores, axis=0, keepdims=True)
                weights = jnp.exp(scores - top)
                total = jnp.sum(weights, axis=0, keepdims=True)
                probs = (weights * (1.0 / total)).astype(BF16)
                out_ref[place, :, at] = mm(value[:, at], probs).astype(BF16)
                lse_ref[j, :, at] = top + jnp.log(total)


def attend_fwd(own, shaped, gathered, time_part, bias, seq, images):
    rows = seq * images

    def part(s):
        return jnp.minimum(s, 2)

    def group(s):
        return jnp.maximum(s - 3, 0)

    return pl.pallas_call(
        partial(attend_fwd_body, seq, images),
        grid_spec=pltpu.PrefetchScalarGridSpec(
            num_scalar_prefetch=1,
            grid=(3 + HEADS // GROUP,),
            in_specs=[
                pl.BlockSpec((rows, D), lambda s, own: (0, 0)),
                pl.BlockSpec((D, D), lambda s, own: (0, part(s))),
                pl.BlockSpec((images, D), lambda s, own: (0, part(s))),
                pl.BlockSpec((GROUP, seq, seq), lambda s, own: (group(s), 0, 0)),
            ],
            out_specs=[
                pl.BlockSpec((3, HEADS, HD, rows), lambda s, own: (0, 0, 0, 0)),
                pl.BlockSpec((HEADS, HD, rows), lambda s, own: (0, 0, 0)),
                pl.BlockSpec((GROUP, 1, rows), lambda s, own: (group(s), 0, 0)),
            ],
        ),
        out_shape=[
            jax.ShapeDtypeStruct((3, HEADS, HD, rows), BF16),
            jax.ShapeDtypeStruct((HEADS, HD, rows), BF16),
            jax.ShapeDtypeStruct((HEADS, 1, rows), F32),
        ],
        compiler_params=params(),
        cost_estimate=cost(6 * 10**9, 2 * 10**7),
        name="attend_fwd",
    )(own, shaped, gathered, time_part, bias)


def mid_body(att_ref, w_ref, tok_ref, mod_ref, attn_out, shaped_out):
    attn = mm(att_ref[...], w_ref[...], TN) + mod_ref[0, 6:7]
    attn_out[...] = attn
    mid = tok_ref[...].astype(F32) + mod_ref[0, 2:3] * attn
    normed, _ = norm_stats(mid)
    shaped_out[...] = (normed * (1.0 + mod_ref[0, 4:5]) + mod_ref[0, 3:4]).astype(BF16)


def middle(att, gathered, tok, mod, seq, images):
    rows = seq * images
    row = pl.BlockSpec((seq, D), lambda n: (n, 0))
    return pl.pallas_call(
        mid_body,
        grid=(images,),
        in_specs=[
            pl.BlockSpec((D, seq), lambda n: (0, n)),
            pl.BlockSpec((D, D), lambda n: (0, 3)),
            row,
            pl.BlockSpec((1, 8, D), lambda n: (n, 0, 0)),
        ],
        out_specs=[row, row],
        out_shape=[jax.ShapeDtypeStruct((rows, D), F32), jax.ShapeDtypeStruct((rows, D), BF16)],
        compiler_params=params(),
        cost_estimate=cost(2 * rows * D * D, 10**7),
        name="middle",
    )(att, gathered, tok, mod)


def once(shape, index):
    return pl.BlockSpec(shape, index, pipeline_mode=pl.Buffered(1))


def mlp_body(nw, nn, seq, tiles, direct, x_ref, gb_ref, one_ref, two_ref, bias_ref, cot_ref,
             term_ref, mine_ref, send_ref, gate_ref, bias_out, own_ref, peer_ref, *rest):
    if direct:
        first_ref, hidden, grads, x_t, gb_t, acc, branch_ref, peer_in, ts, tr, made, from_c, red, from_x, cs, cr, xs, xr = rest
    else:
        hidden, grads, x_t, gb_t, acc, branch_ref, peer_in, ts, tr = rest
    step = pl.program_id(0)
    w, n, m = position()
    nlo, nhi = (2, nn // 2)
    c, x = (lax.rem(n, nlo), lax.div(n, nlo))
    groups = nw * nn
    blk = D // groups
    sibling = (w, x * nlo + 1 - c, m)
    twin = (w, n, 1 - m)

    def to_twin(i):
        return remote(own_ref.at[i], peer_in.at[i], ts.at[i], tr.at[i], twin)

    def to_sibling(k):
        return remote(made.at[k, :, :, 1 - c], from_c.at[k], cs.at[k], cr.at[k], sibling)

    def along_x(d):
        there = lax.rem(x + d, nhi)
        return (there, (w, there * nlo + c, m))

    def hop_x(k, d):
        there, device = along_x(d)
        return remote(red.at[k, :, there], from_x.at[k, d - 1], xs.at[k, d - 1], xr.at[k, d - 1], device)

    @pl.when(step == 0)
    def _():
        bar = pltpu.get_barrier_semaphore()
        friends = [twin]
        if direct:
            friends = [twin, sibling] + [along_x(d)[1] for d in range(1, nhi)]
        for device in friends:
            pl.semaphore_signal(bar, inc=1, device_id=device, device_id_type=MESH)
        x_t[...] = x_ref[...].T
        gb_t[...] = gb_ref[...].T
        pl.semaphore_wait(bar, len(friends))

    if tiles > 0:

        @pl.when(step < 2 * tiles)
        def _():
            image = lax.div(step, tiles)
            f = step - image * tiles
            at = pl.ds(pl.multiple_of(image * seq, seq), seq)
            pre = mm(x_ref[at], one_ref[...]) + bias_ref[...]
            root = math.sqrt(2.0 / math.pi)
            square = pre * pre
            bend = jnp.tanh(root * (pre + 0.044715 * (square * pre)))
            rise = 0.5 * (1.0 + bend)
            hidden[f, at] = (pre * rise).astype(BF16)
            slope = rise + 0.5 * pre * (1.0 - bend * bend) * (root * (1.0 + 3 * 0.044715 * square))
            grad = (mm(gb_ref[at], two_ref[...]) * slope).astype(BF16)
            grads[f, at] = grad
            back = mm(grad, one_ref[...], NT)

            @pl.when(f == 0)
            def _():
                acc[...] = back

            @pl.when(f > 0)
            def _():
                acc[...] += back

            @pl.when(f == tiles - 1)
            def _():
                own_ref[image] = acc[...].astype(BF16)
                to_twin(image).start()

    def place(k, values):
        made[k] = values.reshape(nw, nhi, nlo, blk, TILE).astype(BF16)

    def combine(k):
        to_sibling(k).wait()
        return made[k, :, :, c] + from_c[k]

    @pl.when((step >= 2 * tiles) & (step < 3 * tiles))
    def _():
        f = step - 2 * tiles
        one_grad = mm(x_t[...], grads[f])
        two_grad = mm(gb_t[...], hidden[f])
        if direct:
            place(2 * f, one_grad)
            to_sibling(2 * f).start()
            place(2 * f + 1, two_grad)
            to_sibling(2 * f + 1).start()
        else:
            term_ref[:, 0:TILE] = one_grad.astype(BF16)
            term_ref[:, TILE : 2 * TILE] = two_grad.astype(BF16)
        bias_out[...] = jnp.sum(grads[f].astype(F32), axis=0, keepdims=True)
        branch = mm(hidden[f], two_ref[...], NT)

        @pl.when(f == 0)
        def _():
            branch_ref[...] = branch
            if direct:
                for k in range(2):
                    red[k] = combine(k)
                    for d in range(1, nhi):
                        hop_x(k, d).start()

        @pl.when(f > 0)
        def _():
            branch_ref[...] += branch

    if direct:

        @pl.when(step >= 2 * tiles + 2)
        def _():
            f = step - 2 * tiles - 1
            for half in range(2):
                term_ref[:, :, :, half * TILE : (half + 1) * TILE] = combine(2 * f + half)

    @pl.when(step == 3 * tiles)
    def _():
        gate_ref[...] = jnp.zeros_like(gate_ref)
        for image in range(2):
            at = slice(image * seq, (image + 1) * seq)
            gate_ref[image : image + 1] = jnp.sum(
                cot_ref[at].astype(F32) * branch_ref[at], axis=0, keepdims=True
            )
        send_ref[...] = branch_ref[pl.ds(pl.multiple_of((1 - m) * seq, seq), seq)].astype(BF16)
        mine_ref[...] = branch_ref[pl.ds(pl.multiple_of(m * seq, seq), seq)]
        to_twin(0).wait()
        to_twin(1).wait()
        peer_ref[...] = peer_in[...]
        if direct:
            for k in range(2):
                for d in range(1, nhi):
                    hop_x(k, d).wait()
                total = red[k, :, x]
                for d in range(1, nhi):
                    total = total + from_x[k, d - 1]
                first_ref[:, :, k * TILE : (k + 1) * TILE] = total


def mlp_core(x, gb, gathered, bias, cot, seq, nw, nn):
    half = bias.shape[1]
    rows = 2 * seq
    tiles = half // TILE
    nhi = nn // 2
    blk = D // (nw * nn)
    one, two = (ATT // TILE, (ATT + half) // TILE)
    whole = once((rows, D), lambda s: (0, 0))
    vmem = pl.BlockSpec(memory_space=pltpu.VMEM)
    dma = pltpu.SemaphoreType.DMA

    def weight(s):
        return jnp.where(s < 3 * tiles, lax.rem(s, tiles), tiles - 1)

    def behind(s):
        return jnp.clip(s - 2 * tiles - 2, 0, tiles - 2)

    direct = blk % 8 == 0
    hi = max(nhi - 1, 1)
    if direct:
        term_spec = pl.BlockSpec((nw, nhi, blk, 2 * TILE), lambda s: (0, 0, 0, behind(s)))
        term_shape = jax.ShapeDtypeStruct((nw, nhi, blk, 2 * half - 2 * TILE), BF16)
    else:
        term_spec = pl.BlockSpec((D, 2 * TILE), lambda s: (0, jnp.clip(s - 2 * tiles, 0, tiles - 1)))
        term_shape = jax.ShapeDtypeStruct((D, 2 * half), BF16)
    return pl.pallas_call(
        partial(mlp_body, nw, nn, seq, tiles, direct),
        grid=(3 * tiles + 1,),
        in_specs=[
            whole,
            whole,
            pl.BlockSpec((D, TILE), lambda s: (0, one + jnp.where(s < 2 * tiles, lax.rem(s, tiles), tiles - 1))),
            pl.BlockSpec((D, TILE), lambda s: (0, two + weight(s))),
            pl.BlockSpec((1, TILE), lambda s: (0, weight(s))),
            whole,
        ],
        out_specs=[
            term_spec,
            vmem,
            vmem,
            vmem,
            pl.BlockSpec((1, TILE), lambda s: (0, jnp.clip(s - 2 * tiles, 0, tiles - 1))),
            vmem,
            vmem,
        ]
        + ([vmem] if direct else []),
        out_shape=[
            term_shape,
            jax.ShapeDtypeStruct((seq, D), F32),
            jax.ShapeDtypeStruct((seq, D), BF16),
            jax.ShapeDtypeStruct((8, D), F32),
            jax.ShapeDtypeStruct((1, half), F32),
            jax.ShapeDtypeStruct((2, seq, D), BF16),
            jax.ShapeDtypeStruct((2, seq, D), BF16),
        ]
        + ([jax.ShapeDtypeStruct((nw, blk, 2 * TILE), BF16)] if direct else []),
        scratch_shapes=[
            pltpu.VMEM((tiles, rows, TILE), BF16),
            pltpu.VMEM((tiles, rows, TILE), BF16),
            pltpu.VMEM((D, rows), BF16),
            pltpu.VMEM((D, rows), BF16),
            pltpu.VMEM((seq, D), F32),
            pltpu.VMEM((rows, D), F32),
            pltpu.VMEM((2, seq, D), BF16),
            dma((2,)),
            dma((2,)),
        ]
        + (
            [
                pltpu.VMEM((2 * tiles, nw, nhi, 2, blk, TILE), BF16),
                pltpu.VMEM((2 * tiles, nw, nhi, blk, TILE), BF16),
                pltpu.VMEM((2, nw, nhi, blk, TILE), BF16),
                pltpu.VMEM((2, hi, nw, blk, TILE), BF16),
                dma((2 * tiles,)),
                dma((2 * tiles,)),
                dma((2, hi)),
                dma((2, hi)),
            ]
            if direct
            else []
        ),
        compiler_params=params(collective_id=4, has_side_effects=True),
        cost_estimate=cost(12 * rows * D * half, 4 * 10**7),
        name="mlp_core",
    )(x, gb, gathered, gathered, bias, cot)


REL_ROWS = 32
BUCKETS = 128


def back_body(nw, nn, seq, images, moved, direct, own, att_ref, shaped_ref, w_ref, qkv_ref, bias_ref, lse_ref,
              index_ref, tok_ref, mod_ref, perm_ref, back_own, back_peer, attn_ref, cot_ref, front_sums, gate_mine, send_ref, gate_ref, *rest):
    if direct:
        term_ref, first_ref = rest[:2]
        rest = rest[2:]
    time_ref, rel_ref, in_ref, rows_out, keep, keep_mod, branch_out = rest[:7]
    rest = rest[7:]
    if direct:
        part_ref, done_ref, half_ref = rest[:3]
        rest = rest[3:]
    else:
        dw_ref = rest[0]
        rest = rest[1:]
    made, ga, ga_t, branch_in, gate_in, acc, ds_all, mid, line, yb, yc, ybr, ycr = rest[:13]
    if direct:
        held, from_x, two, from_z, ls, xs, xr, zs, zr, dwt, att_c, att_red, att_x, att_two, att_z, acs, acr, axs, axr, azs, azr = rest[13:]
    step = pl.program_id(0)
    groups = HEADS // GROUP
    rows = seq * images
    att_at = images + 1
    part_at = att_at + groups
    rel_at = part_at + 3
    end_at = rel_at + seq // REL_ROWS
    last = end_at + images - 1
    w, n, m = position()
    nlo, nhi = (2, nn // 2)
    c, x = (lax.rem(n, nlo), lax.div(n, nlo))
    twin = (w, n, 1 - m)

    def along_x(d):
        there = lax.rem(x + d, nhi)
        return (there, (w, there * nlo + c, m))

    def along_z(d):
        there = lax.rem(w + d, nw)
        return (there, (there, n, m))

    def swap_branch():
        return remote(send_ref, branch_in, yb, ybr, twin)

    def swap_gate():
        return remote(gate_ref, gate_in, yc, ycr, twin)

    if direct:
        chunks = part_ref.shape[1] // TILE

        def load(k):
            return pltpu.make_async_copy(
                term_ref.at[:, x, :, pl.ds(pl.multiple_of((k - 2) * TILE, 128), TILE)], held.at[k - 2], ls.at[k - 2]
            )

        def hop_x(k, d):
            there, device = along_x(d)
            return remote(
                term_ref.at[:, there, :, pl.ds(pl.multiple_of((k - 2) * TILE, 128), TILE)],
                from_x.at[k - 2, d - 1], xs.at[k - 2, d - 1], xr.at[k - 2, d - 1], device,
            )

        def hop_z(k, d):
            there, device = along_z(d)
            return remote(two.at[k, d - 1], from_z.at[k, d - 1], zs.at[k, d - 1], zr.at[k, d - 1], device)

        def chain(k, zi):
            total = held[k - 2, zi]
            for d in range(1, nhi):
                total = total + from_x[k - 2, d - 1, zi]
            return total

        def start_x(k):
            for d in range(1, nhi):
                hop_x(k, d).start()

        def span(k):
            return pl.ds(pl.multiple_of(k * TILE, 128), TILE)

        def stage_x(k):
            load(k).wait()
            for d in range(1, nhi):
                hop_x(k, d).wait()
            for d in range(1, nw):
                there, _ = along_z(d)
                two[k, d - 1] = chain(k, there)
                hop_z(k, d).start()

        def finish_z(k, total):
            for d in range(1, nw):
                hop_z(k, d).wait()
            total = total.astype(F32)
            for d in range(1, nw):
                total = total + from_z[k, d - 1].astype(F32)
            part_ref[:, span(k)] = total.astype(BF16)

        sibling = (w, x * nlo + 1 - c, m)

        def att_hop_c(i):
            return remote(dwt.at[i, :, :, 1 - c], att_c.at[i], acs.at[i], acr.at[i], sibling)

        def att_hop_x(i, d):
            there, device = along_x(d)
            return remote(att_red.at[i, :, there], att_x.at[i, d - 1], axs.at[i, d - 1], axr.at[i, d - 1], device)

        def att_place(i, values):
            dwt[i] = values.reshape(nw, nhi, nlo, -1, D).astype(BF16)
            att_hop_c(i).start()

        def att_combine(i):
            att_hop_c(i).wait()
            att_red[i] = dwt[i, :, :, c] + att_c[i]
            for d in range(1, nhi):
                att_hop_x(i, d).start()

        def att_hop_z(d):
            there, device = along_z(d)
            return remote(att_two.at[d - 1], att_z.at[d - 1], azs.at[d - 1], azr.at[d - 1], device)

        def att_chain(i, zi):
            total = att_red[i, zi, x]
            for d in range(1, nhi):
                total = total + att_x[i, d - 1, zi]
            return total

        def att_spread(i):
            for d in range(1, nhi):
                att_hop_x(i, d).wait()
            for d in range(1, nw):
                there, _ = along_z(d)
                att_two[d - 1] = att_chain(i, there)
                att_hop_z(d).start()

        def att_finish(i, j):
            for d in range(1, nw):
                att_hop_z(d).wait()
            total = att_chain(i, w).astype(F32)
            for d in range(1, nw):
                total = total + att_z[d - 1].astype(F32)
            done_ref[...] = total.astype(BF16)
            for d in range(1, nhi):
                att_hop_x(j, d).wait()
            total = att_red[j, :, x]
            for d in range(1, nhi):
                total = total + att_x[j, d - 1]
            half_ref[...] = total

    @pl.when(step == 0)
    def _():
        greet_group(nw, nn, True)
        if direct:
            for k in range(2, chunks):
                load(k).start()
            start_x(2)
            for k in range(2):
                for d in range(1, nw):
                    there, _ = along_z(d)
                    two[k, d - 1] = first_ref[there, :, k * TILE : (k + 1) * TILE]
                    hop_z(k, d).start()
        swap_branch().start()
        swap_gate().start()

    @pl.when(step < images)
    def _():
        at = pl.ds(pl.multiple_of(step * seq, seq), seq)
        attn = attn_ref[...]
        value = tok_ref[...].astype(F32) + mod_ref[0, 2:3] * attn

        @pl.when(m == step)
        def _():
            keep[...] = value
            keep_mod[...] = mod_ref[0]

        normed, inv = norm_stats(value)
        grad = back_own[0].astype(F32) + back_peer[0].astype(F32)
        line[pl.ds(step * 6 + 3, 1)] = jnp.sum(grad, axis=0, keepdims=True)
        line[pl.ds(step * 6 + 4, 1)] = jnp.sum(grad * normed, axis=0, keepdims=True)
        grad = cot_ref[...].astype(F32) + norm_back(grad * (1.0 + mod_ref[0, 4:5]), normed, inv)
        mid[at] = grad
        line[pl.ds(step * 6 + 2, 1)] = jnp.sum(grad * attn, axis=0, keepdims=True)
        low = (grad * mod_ref[0, 2:3]).astype(BF16)
        out_sum = jnp.sum(low.astype(F32), axis=0, keepdims=True)
        at_row = slice(6 * images, 6 * images + 1)

        @pl.when(step == 0)
        def _():
            line[at_row] = out_sum

        @pl.when(step > 0)
        def _():
            line[at_row] += out_sum

        ga[at] = low
        turned = mm(w_ref[...], low, NT)
        if not moved:
            turned = mm(perm_ref[...], turned.astype(BF16))
        ga_t[:, :, at] = turned.reshape(HEADS, HD, seq).astype(BF16)

    @pl.when((step >= att_at) & (step < part_at))
    def _():
        for j in range(GROUP):
            h = (step - att_at) * GROUP + j
            place = own[h]
            ds_sum = jnp.zeros((seq, seq), F32)
            for image in range(images):
                at = slice(image * seq, (image + 1) * seq)
                query, key, value = [qkv_ref[p, j, :, at] for p in range(3)]
                grad = ga_t[place, :, at]
                probs = jnp.exp(mm(key, query, TN) * INV_ROOT + (bias_ref[j] - lse_ref[j, :, at]))
                grad_probs = mm(value, grad, TN)
                inner = jnp.sum(probs * grad_probs, axis=0, keepdims=True)
                ds = (probs * (grad_probs - inner)).astype(BF16)
                made[0, h, :, at] = (mm(key, ds) * INV_ROOT).astype(BF16)
                made[1, h, :, at] = (mm(query, ds, NT) * INV_ROOT).astype(BF16)
                made[2, h, :, at] = mm(grad, probs.astype(BF16), NT).astype(BF16)
                ds_sum = ds_sum + ds.astype(F32)
            ds_all[h] = ds_sum.astype(BF16)

    @pl.when((step >= part_at) & (step < part_at + 3))
    def _():
        p = step - part_at
        across = made[p].astype(F32).reshape(D, rows)
        upright = across.T.astype(BF16)
        back = mm(upright, w_ref[...], NT)

        @pl.when(p == 0)
        def _():
            acc[...] = back

        @pl.when(p > 0)
        def _():
            acc[...] += back

        if direct:


            @pl.when((p == 2) == (m == 0))
            def _():
                att_place(lax.rem(p, 2), mm(shaped_ref[...], across.astype(BF16), NT))
        else:
            dw_ref[...] = mm(shaped_ref[...], across.astype(BF16), NT).astype(BF16)
        wide = upright.astype(F32)
        for image in range(images):
            time_ref[image : image + 1] = jnp.sum(
                wide[image * seq : (image + 1) * seq], axis=0, keepdims=True
            )

    @pl.when((step >= rel_at) & (step < end_at))
    def _():
        index = index_ref[0]
        low = jnp.bitwise_and(index, BUCKETS - 1)
        high = jnp.right_shift(index, 7)
        bucket = lax.broadcasted_iota(jnp.int32, (BUCKETS, index.shape[1]), 0)
        hot = jnp.where(bucket == low, 1.0, 0.0).astype(BF16)
        start = pl.multiple_of((step - rel_at) * REL_ROWS, REL_ROWS)
        turned = jnp.swapaxes(ds_all[:, pl.ds(start, REL_ROWS), :].astype(F32), 0, 1)
        total = jnp.concatenate([turned[j] for j in range(REL_ROWS)], axis=1)
        picked = jnp.concatenate([jnp.where(high == a, total, 0.0) for a in range(1024 // BUCKETS)], axis=0)
        found = mm(picked.astype(BF16), hot, NT)

        @pl.when(step == rel_at)
        def _():
            rel_ref[...] = found

        @pl.when(step > rel_at)
        def _():
            rel_ref[...] += found

    @pl.when(step >= end_at)
    def _():
        image = step - end_at
        normed, inv = norm_stats(tok_ref[...].astype(F32))
        at = pl.ds(pl.multiple_of(image * seq, seq), seq)
        grad = acc[at]
        line[pl.ds(image * 6, 1)] = jnp.sum(grad, axis=0, keepdims=True)
        line[pl.ds(image * 6 + 1, 1)] = jnp.sum(grad * normed, axis=0, keepdims=True)
        grad = mid[at] + norm_back(grad * (1.0 + mod_ref[0, 1:2]), normed, inv)
        in_ref[...] = mm_split(grad, perm_ref[...], NT)

    @pl.when(step == last)
    def _():
        swap_branch().wait()
        swap_gate().wait()
        branch_out[...] = branch_in[...]
        two_sum = front_sums[0, 0:1]
        for image in range(images):
            gate_two = gate_mine[image : image + 1] + gate_in[image : image + 1]
            line[image * 6 + 5 : image * 6 + 6] = gate_two + mod_ref[0, 7:8] * front_sums[image, 1:2]
            if image > 0:
                two_sum = two_sum + front_sums[image, 0:1]
        line[6 * images + 1 : 6 * images + 2] = two_sum
        line[6 * images + 2 : 16] = jnp.zeros((14 - 6 * images, D), F32)
        thrice = mm(jnp.concatenate(exact_parts(line[...]), axis=0), perm_ref[...], NT)
        rows_out[...] = thrice[0:16] + thrice[16:32] + thrice[32:48]

    if direct:

        @pl.when((step == images) & (m == 0))
        def _():
            att_place(1, mm(att_ref[...], ga[...]))

        @pl.when((step == part_at + 1) | (step == rel_at + 4))
        def _():
            att_combine(jnp.where(step == part_at + 1, 1 - m, m))

        @pl.when((step == 3) | (step == 5) | (step == 8) | (step == 9))
        def _():
            stage_x(2 + (step >= 5).astype(jnp.int32) + (step >= 8).astype(jnp.int32) + (step >= 9).astype(jnp.int32))

        @pl.when((step == 1) | (step == 3) | (step == 5))
        def _():
            start_x(3 + (step >= 3).astype(jnp.int32) + (step >= 5).astype(jnp.int32))

        @pl.when((step == 5) | (step == 6))
        def _():
            k = step - 5
            finish_z(k, first_ref[w, :, span(k)])

        @pl.when(step == end_at - 1)
        def _():
            att_spread(1 - m)

        @pl.when(step >= end_at)
        def _():
            for half in range(2):
                k = 2 + 2 * (step - end_at) + half
                finish_z(k, chain(k, w))

    else:

        @pl.when(step == images)
        def _():
            dw_ref[...] = mm(att_ref[...], ga[...]).astype(BF16)

    if direct:

        @pl.when(step == last)
        def _():
            att_finish(1 - m, m)


def back_core(own, att, shaped_t, gathered, qkv, bias, lse, index_t, tok, mod, perm, back_own, back_peer,
              attn, cot, front_sums, send, gate, reduced, seq, images, nw, nn, moved):
    rows = seq * images
    groups = HEADS // GROUP
    att_at = images + 1
    part_at = att_at + groups
    rel_at = part_at + 3
    end_at = rel_at + seq // REL_ROWS
    last = end_at + images - 1
    nhi = nn // 2
    direct = len(reduced) == 2
    hi, wi = (max(nhi - 1, 1), max(nw - 1, 1))
    vmem = pl.BlockSpec(memory_space=pltpu.VMEM)
    dma = pltpu.SemaphoreType.DMA

    def group(s):
        return jnp.clip(s - att_at, 0, groups - 1)

    def part(s):
        return jnp.clip(s - part_at, 0, 2)

    def early(s):
        return jnp.minimum(s, images - 1)

    def both(s):
        return jnp.where(s < images, s, jnp.clip(s - end_at, 0, images - 1))

    def late(s):
        return jnp.clip(s - end_at, 0, images - 1)

    per = pl.BlockSpec((1, 8, D), lambda s, own: (both(s), 0, 0))
    swapped = once((1, seq, D), lambda s, own: (early(s), 0, 0))
    extra_in, extra_out, extra_shape, extra_scratch = ([], [], [], [])
    if direct:
        blk, cols = reduced[0].shape[2:]
        cols = cols + 2 * TILE
        chunks = cols // TILE
        extra_in = [ANY, once((nw, blk, 2 * TILE), lambda s, own: (0, 0, 0))]
        extra_out = [vmem, vmem, vmem]
        extra_shape = [
            jax.ShapeDtypeStruct((blk, cols), BF16),
            jax.ShapeDtypeStruct((blk, D), BF16),
            jax.ShapeDtypeStruct((nw, blk, D), BF16),
        ]
        extra_scratch = [
            pltpu.VMEM((chunks - 2, nw, blk, TILE), BF16),
            pltpu.VMEM((chunks - 2, hi, nw, blk, TILE), BF16),
            pltpu.VMEM((chunks, wi, blk, TILE), BF16),
            pltpu.VMEM((chunks, wi, blk, TILE), BF16),
            dma((chunks - 2,)),
            dma((chunks - 2, hi)),
            dma((chunks - 2, hi)),
            dma((chunks, wi)),
            dma((chunks, wi)),
            pltpu.VMEM((2, nw, nhi, 2, blk, D), BF16),
            pltpu.VMEM((2, nw, nhi, blk, D), BF16),
            pltpu.VMEM((2, nw, nhi, blk, D), BF16),
            pltpu.VMEM((2, hi, nw, blk, D), BF16),
            pltpu.VMEM((wi, blk, D), BF16),
            pltpu.VMEM((wi, blk, D), BF16),
            dma((2,)),
            dma((2,)),
            dma((2, hi)),
            dma((2, hi)),
            dma((wi,)),
            dma((wi,)),
        ]
    else:
        extra_out = [
            pl.BlockSpec((D, D), lambda s, own: (0, jnp.where(s < part_at, 3, jnp.clip(s - part_at, 0, 2))))
        ]
        extra_shape = [jax.ShapeDtypeStruct((D, ATT), BF16)]
    return pl.pallas_call(
        partial(back_body, nw, nn, seq, images, moved, direct),
        grid_spec=pltpu.PrefetchScalarGridSpec(
            num_scalar_prefetch=1,
            grid=(last + 1,),
            in_specs=[
                once((D, rows), lambda s, own: (0, 0)),
                once((D, rows), lambda s, own: (0, 0)),
                once((D, D), lambda s, own: (0, jnp.where(s < images, 3, part(s)))),
                pl.BlockSpec((3, GROUP, HD, rows), lambda s, own: (0, group(s), 0, 0)),
                pl.BlockSpec((GROUP, seq, seq), lambda s, own: (group(s), 0, 0)),
                pl.BlockSpec((GROUP, 1, rows), lambda s, own: (group(s), 0, 0)),
                pl.BlockSpec(
                    (1, 1, REL_ROWS * seq), lambda s, own: (jnp.clip(s - rel_at, 0, seq // REL_ROWS - 1), 0, 0)
                ),
                once((seq, D), lambda s, own: (both(s), 0)),
                per,
                once((D, D), lambda s, own: (0, 0)),
                swapped,
                swapped,
                once((seq, D), lambda s, own: (early(s), 0)),
                once((seq, D), lambda s, own: (early(s), 0)),
                once((images, 8, D), lambda s, own: (0, 0, 0)),
                once((8, D), lambda s, own: (0, 0)),
                ANY,
                ANY,
            ]
            + extra_in,
            out_specs=[
                pl.BlockSpec((images, D), lambda s, own: (0, part(s))),
                vmem,
                pl.BlockSpec((seq, D), lambda s, own: (late(s), 0)),
                vmem,
                vmem,
                vmem,
                vmem,
            ]
            + extra_out,
            scratch_shapes=[
                pltpu.VMEM((3, HEADS, HD, rows), BF16),
                pltpu.VMEM((rows, D), BF16),
                pltpu.VMEM((HEADS, HD, rows), BF16),
                pltpu.VMEM((seq, D), BF16),
                pltpu.VMEM((8, D), F32),
                pltpu.VMEM((rows, D), F32),
                pltpu.VMEM((HEADS, seq, seq), BF16),
                pltpu.VMEM((rows, D), F32),
                pltpu.VMEM((16, D), F32),
                dma,
                dma,
                dma,
                dma,
            ]
            + extra_scratch,
        ),
        out_shape=[
            jax.ShapeDtypeStruct((images, 3 * D), F32),
            jax.ShapeDtypeStruct((HEADS * 1024 // BUCKETS, BUCKETS), F32),
            jax.ShapeDtypeStruct((rows, D), F32),
            jax.ShapeDtypeStruct((16, D), F32),
            jax.ShapeDtypeStruct((seq, D), F32),
            jax.ShapeDtypeStruct((8, D), F32),
            jax.ShapeDtypeStruct((seq, D), BF16),
        ]
        + extra_shape,
        compiler_params=params(collective_id=5, has_side_effects=True),
        cost_estimate=cost(30 * 10**9, 8 * 10**7),
        name="back_core",
    )(
        own, att, shaped_t, gathered, qkv, bias, lse,
        index_t.reshape(seq // REL_ROWS, 1, REL_ROWS * seq), tok, mod, perm, back_own, back_peer, attn, cot,
        front_sums, gate, send, gate, *reduced,
    )


CHUNKS = 3


def collect_body(nw, nn, nm, seq, images, direct, shared_rows, red_ref, time_ref, rows_ref, b_one_ref, rel_ref, keep_mod, perm_ref, *rest):
    if direct:
        done_ref, mlp_ref, emb_ref, silu_ref = rest[:4]
        rest = rest[4:]
    keep_hbm, mine_hbm, branch_hbm = rest[:3]
    rest = rest[3:]
    if direct:
        att_out, mlp_out, ada_out, norm_out = rest[:4]
        small_out, final_ref, out_ref, img_out, slots, ss, sr = rest[4:11]
        rest = rest[11:]
    else:
        img_out, small_out, final_ref = rest[:3]
        rest = rest[3:]
    (from_z, gath, sc, sx, sz, keep, mine, branch,
     zs, zr, ys, yr, ics, icr, ixs, ixr, izs, izr, tcs, tcr, txs, txr, tzs, tzr, ms) = rest
    w, n, m = position()
    nlo, nhi, groups = (2, nn // 2, nw * nn)
    c, x = (lax.rem(n, nlo), lax.div(n, nlo))
    slot = (c * nhi + x) * nw + w
    width = D // CHUNKS
    first_at = pl.multiple_of((1 - m) * 3 * D, 128)
    later_at = (1 - m) * 2 * D + m * D
    sibling = (w, x * nlo + 1 - c, m)
    twin = (w, n, 1 - m)

    def along_x(k):
        there = lax.rem(x + k, nhi)
        return (there, (w, there * nlo + c, m))

    def along_z(k):
        there = lax.rem(w + k, nw)
        return (there, (there, n, m))

    if direct:
        ask_all(nw, nn, nm)
    else:
        greet_group(nw, nn, True)

    def cols(k):
        return pl.ds(pl.multiple_of(later_at + k * width, 128), width)

    def hop_z(k, d):
        there, device = along_z(d)
        return remote(
            red_ref.at[there, :, pl.ds(k * width, width)], from_z.at[k, d - 1], zs.at[k, d - 1], zr.at[k, d - 1], device
        )

    def start_z(k):
        if direct:
            for d in range(1, nw):
                hop_z(k, d).start()

    def hop_y(k):
        at = pl.ds(first_at, D) if k == CHUNKS else cols(k)
        return remote(out_ref.at[:, at], out_ref.at[:, at], ys.at[k], yr.at[k], twin)

    places = ((keep_hbm, keep), (mine_hbm, mine), (branch_hbm, branch))
    loads = [pltpu.make_async_copy(a, b, ms.at[i]) for i, (a, b) in enumerate(places)]
    for copy in loads:
        copy.start()

    def image_rows():
        back = rows_ref[...]
        gath[slot, :, 0 : 3 * D] = time_ref[...]
        for i in range(images):
            for q in range(6):
                gath[slot, i : i + 1, (3 + q) * D : (4 + q) * D] = back[i * 6 + q : i * 6 + q + 1]
        return back

    def small_rows(back):
        mine_small = sc.at[c]
        count = rel_ref.shape[0]
        mine_small[0:count] = rel_ref[...]
        mine_small[count:] = jnp.zeros((SMALL_ROWS - count, 128), F32)
        at = count
        for row in (back[images * 6 : images * 6 + 1], back[images * 6 + 1 : images * 6 + 2], b_one_ref[...]):
            for j in range(row.shape[1] // 128):
                mine_small[at : at + 1] = row[:, j * 128 : (j + 1) * 128]
                at += 1

    img_z = []
    for d in range(1, nw):
        there, device = along_z(d)
        img_z.append(remote(gath.at[slot], gath.at[slot], izs.at[d - 1], izr.at[d - 1], device))
    mine_x = pl.ds((c * nhi + x) * nw, nw)
    img_x = []
    for d in range(1, nhi):
        there, device = along_x(d)
        img_x.append(remote(gath.at[mine_x], gath.at[mine_x], ixs.at[d - 1], ixr.at[d - 1], device))
    mine_c = pl.ds(c * nhi * nw, nhi * nw)
    img_c = remote(gath.at[mine_c], gath.at[mine_c], ics, icr, sibling)
    small_c = remote(sc.at[c], sc.at[c], tcs, tcr, sibling)
    small_x = []
    for d in range(1, nhi):
        there, device = along_x(d)
        small_x.append(remote(sx.at[x], sx.at[x], txs.at[d - 1], txr.at[d - 1], device))
    small_z = []
    for d in range(1, nw):
        there, device = along_z(d)
        small_z.append(remote(sz.at[w], sz.at[w], tzs.at[d - 1], tzr.at[d - 1], device))

    def stage_c(k):
        if not direct:
            return
        for d in range(1, nw):
            hop_z(k, d).wait()
        total = red_ref[w, :, k * width : (k + 1) * width].astype(F32)
        for d in range(1, nw):
            total = total + from_z[k, d - 1].astype(F32)
        out_ref[:, cols(k)] = total.astype(BF16)
        hop_y(k).start()

    back = image_rows()
    small_rows(back)
    if direct:
        pl.semaphore_wait(pltpu.get_barrier_semaphore(), groups * nm - 1)
    for hop in img_z:
        hop.start()
    small_c.start()
    if direct:
        out_ref[:, pl.ds(first_at, D)] = done_ref[...]
        hop_y(CHUNKS).start()
        mlp_sq = mlp_rows(mlp_ref, mlp_out)
    small_c.wait()
    sx[x] = sc[0] + sc[1]
    for hop in small_x:
        hop.start()
    for hop in img_z:
        hop.wait()
    for hop in img_x:
        hop.start()
    start_z(0)
    start_z(1)
    for hop in small_x:
        hop.wait()
    total = sx[0]
    for k in range(1, nhi):
        total = total + sx[k]
    sz[w] = total
    for hop in small_z:
        hop.start()
    start_z(2)
    for copy in loads:
        copy.wait()
    summed = mine[...] + branch[...].astype(F32) + keep_mod[7:8]
    final = (keep[...] + keep_mod[5:6] * summed).astype(BF16)
    final_ref[...] = mm(final, perm_ref[...], NT).astype(BF16)
    stage_c(0)
    for hop in img_x:
        hop.wait()
    img_c.start()
    if direct:
        hop_y(CHUNKS).wait()
        att_sq = space_rows(out_ref, perm_ref, att_out, True, False)
    stage_c(1)
    img_c.wait()
    for g in range(groups):
        img_out[2 * g : 2 * g + 2, :] = gath[g]
    if direct:
        att_sq = att_sq + image_weights(img_out, emb_ref, silu_ref, att_out, ada_out)
    stage_c(2)
    for hop in small_z:
        hop.wait()
    total = sz[0]
    for k in range(1, nw):
        total = total + sz[k]
    small_out[...] = total
    if direct:
        for k in range(CHUNKS):
            hop_y(k).wait()
        att_sq = att_sq + space_rows(out_ref, perm_ref, att_out, False, True)
        norm_of(att_sq, mlp_sq, small_out, ada_out, shared_rows, norm_out, slots, ss, sr, nw, nn, nm)


SMALL_ROWS = 168


def collect(red, time_grad, line, b_one, rel, keep_mod, perm, keep, mine, branch, extra, seq, images, shared_rows, nw, nn, nm):
    groups = nw * nn
    count = groups * nm
    nhi = nn // 2
    img_width = 9 * D
    direct = len(extra) > 0
    blk = D // groups
    half = b_one.shape[1]
    width = D // CHUNKS
    vmem = pl.BlockSpec(memory_space=pltpu.VMEM)
    dma = pltpu.SemaphoreType.DMA
    hi, wi = (max(nhi - 1, 1), max(nw - 1, 1))
    many = dma((CHUNKS + 1,))
    small = jax.ShapeDtypeStruct((SMALL_ROWS, 128), F32)
    final = jax.ShapeDtypeStruct((seq, D), BF16)
    if direct:
        out_shape = [
            jax.ShapeDtypeStruct((blk, 13 * D), F32),
            jax.ShapeDtypeStruct((blk, 2, half), F32),
            jax.ShapeDtypeStruct((1, 6 * D), F32),
            jax.ShapeDtypeStruct((8, 128), F32),
            small,
            final,
        ]
        ahead = [
            pltpu.VMEM((blk, ATT), BF16),
            pltpu.VMEM((2 * groups, img_width), F32),
            pltpu.VMEM((count, 8, 128), F32),
            dma((count,)),
            dma((count,)),
        ]
    else:
        out_shape = [jax.ShapeDtypeStruct((2 * groups, img_width), F32), small, final]
        ahead = []
    return pl.pallas_call(
        partial(collect_body, nw, nn, nm, seq, images, direct, shared_rows),
        in_specs=[vmem] * (7 + len(extra)) + [ANY] * 3,
        out_specs=[vmem] * len(out_shape),
        out_shape=out_shape,
        scratch_shapes=ahead
        + [
            pltpu.VMEM((CHUNKS, wi, blk, width), BF16),
            pltpu.VMEM((groups, 2, img_width), F32),
            pltpu.VMEM((2, SMALL_ROWS, 128), F32),
            pltpu.VMEM((nhi, SMALL_ROWS, 128), F32),
            pltpu.VMEM((nw, SMALL_ROWS, 128), F32),
            pltpu.VMEM((seq, D), F32),
            pltpu.VMEM((seq, D), F32),
            pltpu.VMEM((seq, D), BF16),
            dma((CHUNKS, wi)), dma((CHUNKS, wi)), many, many,
            dma, dma, dma((hi,)), dma((hi,)), dma((wi,)), dma((wi,)),
            dma, dma, dma((hi,)), dma((hi,)), dma((wi,)), dma((wi,)),
            dma((3,)),
        ],
        compiler_params=params(collective_id=2, has_side_effects=True),
        cost_estimate=cost(10**9, 3 * 10**7),
        name="collect",
    )(
        red, time_grad, line, b_one, rel, keep_mod, perm, *extra, keep, mine, branch,
    )


def who_is(k, nw, nn, nm):
    w, n, m = position()
    count = nw * nn * nm
    other = lax.rem((w * nn + n) * nm + m + k, count)
    pair = lax.div(other, nm)
    return (lax.div(pair, nn), lax.rem(pair, nn), lax.rem(other, nm))


def ask_all(nw, nn, nm):
    bar = pltpu.get_barrier_semaphore()
    count = nw * nn * nm

    def ask(k, carry):
        pl.semaphore_signal(bar, inc=1, device_id=who_is(k, nw, nn, nm), device_id_type=MESH)
        return carry

    lax.fori_loop(1, count, ask, 0)


def greet_all(nw, nn, nm):
    ask_all(nw, nn, nm)
    pl.semaphore_wait(pltpu.get_barrier_semaphore(), nw * nn * nm - 1)


def tally(values):
    return jnp.sum(jnp.sum(values * values, axis=0, keepdims=True), axis=1, keepdims=True)


def mlp_rows(mlp_ref, mlp_out):
    total = jnp.zeros((1, 1), F32)
    for f in range(mlp_ref.shape[1] // (2 * TILE)):
        at = slice(f * TILE, (f + 1) * TILE)
        for half in range(2):
            part = mlp_ref[:, (2 * f + half) * TILE : (2 * f + half + 1) * TILE].astype(F32)
            mlp_out[:, half, at] = part
            total = total + tally(part)
    return total


def image_weights(img_ref, emb_ref, silu_ref, att_out, ada_out):
    def product(rows, values):
        return mm(jnp.concatenate([rows] * 3, axis=0), jnp.concatenate(exact_parts(values), axis=0), TN)

    part = product(emb_ref[...], img_ref[:, 0 : 3 * D])
    att_out[:, 3 * D : 6 * D] = part
    total = tally(part)
    ada = img_ref[:, 3 * D :]
    ada_out[...] = jnp.sum(ada, axis=0, keepdims=True)
    part = product(silu_ref[...], ada)
    att_out[:, 7 * D :] = part
    return total + tally(part)


def space_rows(att_ref, perm_ref, att_out, early, late):
    total = jnp.zeros((1, 1), F32)
    if early:
        part = att_ref[:, 0:D].astype(F32)
        att_out[:, 0:D] = part
        total = total + tally(part)
        part = mm(att_ref[:, 3 * D :], perm_ref[...], NT)
        att_out[:, 6 * D : 7 * D] = part
        total = total + tally(part)
    if late:
        part = att_ref[:, D : 3 * D].astype(F32)
        att_out[:, D : 3 * D] = part
        total = total + tally(part)
    return total


def norm_of(att_sq, mlp_sq, small_ref, ada_out, shared_rows, norm_out, slots, ss, sr, nw, nn, nm):
    w, n, m = position()
    groups = nw * nn
    count = groups * nm
    mine = (w * nn + n) * nm + m
    small_sq = tally(small_ref[0:shared_rows]) + tally(ada_out[...])
    bias_sq = tally(small_ref[shared_rows:])
    local = mlp_sq + att_sq / nm + small_sq / count + bias_sq / groups
    slots[mine] = jnp.broadcast_to(local, (8, 128))

    def copy_to(k):
        return remote(slots.at[mine], slots.at[mine], ss.at[k], sr.at[k], who_is(k, nw, nn, nm))

    def send(k, carry):
        copy_to(k).start()
        return carry

    def finish(k, carry):
        copy_to(k).wait()
        return carry

    lax.fori_loop(1, count, send, 0)
    lax.fori_loop(1, count, finish, 0)
    norm_out[...] = jnp.sqrt(jnp.sum(slots[...], axis=0))


def norm_body(nw, nn, nm, shared_rows, att_ref, mlp_ref, img_ref, emb_ref, silu_ref, small_ref, perm_ref,
              att_out, mlp_out, ada_out, norm_out, slots, ss, sr):
    greet_all(nw, nn, nm)
    mlp_sq = mlp_rows(mlp_ref, mlp_out)
    att_sq = image_weights(img_ref, emb_ref, silu_ref, att_out, ada_out)
    att_sq = att_sq + space_rows(att_ref, perm_ref, att_out, True, True)
    norm_of(att_sq, mlp_sq, small_ref, ada_out, shared_rows, norm_out, slots, ss, sr, nw, nn, nm)


def collect_norm(att, mlp, imgs, emb, silu, small, perm, shared_rows, nw, nn, nm):
    rows = att.shape[0]
    half = mlp.shape[1] // 2
    count = nw * nn * nm
    dma = pltpu.SemaphoreType.DMA
    return pl.pallas_call(
        partial(norm_body, nw, nn, nm, shared_rows),
        out_shape=[
            jax.ShapeDtypeStruct((rows, 13 * D), F32),
            jax.ShapeDtypeStruct((rows, 2, half), F32),
            jax.ShapeDtypeStruct((1, 6 * D), F32),
            jax.ShapeDtypeStruct((8, 128), F32),
        ],
        scratch_shapes=[pltpu.VMEM((count, 8, 128), F32), dma((count,)), dma((count,))],
        compiler_params=params(collective_id=3, has_side_effects=True),
        cost_estimate=cost(10**8, 10**7),
        name="collect_norm",
    )(att, mlp, imgs, emb, silu, small, perm)


def on_device(
    tokens,
    timesteps,
    owners,
    rel_index,
    cotangent,
    att_master,
    att_moment,
    att_second,
    mlp_master,
    mlp_moment,
    mlp_second,
    small_master,
    small_moment,
    small_second,
    bias_master,
    bias_moment,
    bias_second,
):
    groups = owners.shape[0]
    rows_blk = att_master.shape[0]
    half_ff = mlp_master.shape[2]
    images = timesteps.shape[0]
    tok_rows = tokens.shape[0]
    half_rows = cotangent.shape[0]
    seq_len = tok_rows // images
    nw, nn, nm = (lax.axis_size("wide"), lax.axis_size("narrow"), lax.axis_size("mlp"))
    mlp_at = lax.axis_index("mlp")
    mine = lax.axis_index(GRID)
    moved = rows_blk == HD
    swap = [(i, nm - 1 - i) for i in range(nm)]

    place = (owners[:, None] * rows_blk + jnp.arange(rows_blk)[None, :]).reshape(D)
    pick = (place[:, None] == (mine * rows_blk + jnp.arange(rows_blk))[None, :]).astype(BF16)

    packed, perm = pack_weights(owners, att_master, mlp_master)
    perm_f = perm.astype(F32)
    gathered = lax.all_gather(packed, GRID, axis=0, tiled=True)

    time_emb = time_embed(timesteps)
    emb_rows = jnp.concatenate(
        [time_emb, jax.nn.silu(time_emb), jnp.zeros((8 - 2 * images, D), F32)], axis=0
    ).astype(BF16)
    summed, emb_mine, silu_mine, cot_all = modul_exchange(
        emb_rows, att_master, pick, cotangent, nw, nn
    )
    time_part = summed[:, 0 : 3 * D]
    offset = NREL * HEADS
    table_t = jnp.pad(small_master[0:offset].reshape(NREL, HEADS).T, ((0, 0), (0, 1024 - NREL)))
    b_ada = small_master[offset : offset + 6 * D]
    b_rest = small_master[offset + 6 * D : offset + 8 * D].reshape(1, 2, D)
    modulation = (summed[:, 3 * D :] + b_ada).reshape(images, 6, D)
    mod = jnp.concatenate([modulation, jnp.broadcast_to(b_rest, (images, 2, D))], axis=1)
    mod = mm_exact(mod.reshape(images * 8, D), perm_f).reshape(images, 8, D)
    index_t = rel_index.T
    bias = rel_bias(index_t, table_t.reshape(HEADS, 1, 1024), seq_len)

    tok, shaped, shaped_t, cot, grad_branch, front_sums = front(
        tokens, cot_all, perm, mod, seq_len, images
    )
    heads_at = owners if moved else jnp.arange(HEADS, dtype=jnp.int32)
    qkv, attended, lse = attend_fwd(heads_at, shaped, gathered, time_part, bias, seq_len, images)
    attended = attended.reshape(D, tok_rows)
    if not moved:
        attended = mm(perm, attended, TN).astype(BF16)
    attn_out, shaped_two = middle(attended, gathered, tok, mod, seq_len, images)
    made = mlp_core(
        shaped_two, grad_branch, gathered, bias_master.reshape(1, half_ff), cot, seq_len, nw, nn
    )
    mlp_term, branch_mine, branch_send, gate_own, b_one_grad, back_own, back_peer = made[:7]
    reduced = (mlp_term, made[7]) if len(made) == 8 else ()

    done = back_core(
        heads_at,
        attended,
        shaped_t,
        gathered,
        qkv,
        bias,
        lse,
        index_t,
        tok,
        mod,
        perm,
        back_own,
        back_peer,
        attn_out,
        cot,
        front_sums,
        branch_send,
        gate_own,
        reduced,
        seq_len,
        images,
        nw,
        nn,
        moved,
    )
    time_grad, rel_sum, input_grad, line, keep, keep_mod, branch_peer = done[:7]
    rel_rows = HEADS * 1024 // BUCKETS
    shared_rows = rel_rows + 2 * D // 128
    direct = len(done) == 10
    if direct:
        mlp_part, part_done, red = done[7:]
        extra = (part_done, mlp_part, emb_mine, silu_mine)
    else:
        mlp_part = lax.psum_scatter(mlp_term, GRID, scatter_dimension=0, tiled=True)
        red = jnp.zeros((1, 1, 1), BF16)
        extra = ()
    shared = collect(
        red, time_grad, line, b_one_grad, rel_sum, keep_mod, perm, keep, branch_mine, branch_peer, extra, seq_len, images, shared_rows, nw, nn, nm,
    )
    if direct:
        att_grad, mlp_grad, b_ada_grad, norm, small_all, output = shared
    else:
        imgs_all, small_all, output = shared
        att_part = lax.psum_scatter(done[7], GRID, scatter_dimension=0, tiled=True)
        att_grad, mlp_grad, b_ada_grad, norm = collect_norm(
            att_part, mlp_part, imgs_all, emb_mine, silu_mine, small_all, perm, shared_rows, nw, nn, nm
        )

    grad_norm = norm[0, 0]
    clip_scale = jnp.minimum(1.0, 1.0 / (grad_norm + 1e-06))
    rel_grad = small_all[0:rel_rows].reshape(-1, HEADS, BUCKETS).transpose(0, 2, 1).reshape(-1)[0:offset]
    small_grad = jnp.concatenate(
        [rel_grad, b_ada_grad.reshape(-1), small_all[rel_rows:shared_rows].reshape(-1)]
    )
    bias_grad = small_all[shared_rows : shared_rows + half_ff // 128].reshape(-1)
    att_new, att_mom_new, att_sec_new = adam_update(
        att_master, att_moment, att_second, att_grad, clip_scale
    )
    mlp_new, mlp_mom_new, mlp_sec_new = adam_update(
        mlp_master, mlp_moment, mlp_second, mlp_grad, clip_scale
    )
    small_new, small_mom_new, small_sec_new = adam_update(
        small_master, small_moment, small_second, small_grad, clip_scale
    )
    bias_new, bias_mom_new, bias_sec_new = adam_update(
        bias_master, bias_moment, bias_second, bias_grad, clip_scale
    )
    return (
        output,
        input_grad,
        att_new,
        att_mom_new,
        att_sec_new,
        mlp_new,
        mlp_mom_new,
        mlp_sec_new,
        small_new,
        small_mom_new,
        small_sec_new,
        bias_new,
        bias_mom_new,
        bias_sec_new,
        att_new.astype(BF16),
        mlp_new.astype(BF16),
        grad_norm,
    )


def solution(mesh):
    rows = P(GRID, None)
    cube = P(GRID, None, "mlp")
    return jax.shard_map(
        on_device,
        mesh=mesh,
        in_specs=(
            rows,
            P(GRID),
            P(),
            P(),
            P(("wide", "narrow", "mlp"), None),
            rows,
            rows,
            rows,
            cube,
            cube,
            cube,
            P(),
            P(),
            P(),
            P("mlp"),
            P("mlp"),
            P("mlp"),
        ),
        out_specs=(
            P(("wide", "narrow", "mlp"), None),
            rows,
            rows,
            rows,
            rows,
            cube,
            cube,
            cube,
            P(),
            P(),
            P(),
            P("mlp"),
            P("mlp"),
            P("mlp"),
            rows,
            cube,
            P(),
        ),
        check_vma=False,
    )
```

```python
from functools import partial
import math

import jax
import jax.numpy as jnp
from jax import lax
from jax.experimental import pallas as pl
from jax.experimental.pallas import tpu as pltpu
from jax.sharding import PartitionSpec as P

D = 1152
HEADS = 16
HD = 72
NREL = 961
STEP = 10

HIGH = lax.Precision.HIGHEST
F32 = jnp.float32
BF16 = jnp.bfloat16
GRID = ("wide", "narrow")
NN = (((1,), (0,)), ((), ()))
TN = (((0,), (0,)), ((), ()))
NT = (((1,), (1,)), ((), ()))
INV_ROOT = 1.0 / math.sqrt(HD)
MESH = pl.DeviceIdType.MESH
ANY = pl.BlockSpec(memory_space=pl.ANY)
ATT = 4 * D
GROUP = 4
TILE = 768
VMEM_BYTES = 63 * 1024 * 1024


def mm(a, b, dims=NN):
    return lax.dot_general(a, b, dims, preferred_element_type=F32)


def mm_exact(a, b, dims=NN):
    return lax.dot_general(a, b, dims, precision=HIGH, preferred_element_type=F32)


def norm_stats(values):
    center = values - jnp.mean(values, axis=-1, keepdims=True)
    inv_std = lax.rsqrt(jnp.mean(center * center, axis=-1, keepdims=True) + 1e-06)
    return (center * inv_std, inv_std)


def norm_back(grad_normed, normed, inv_std):
    mean_grad = jnp.mean(grad_normed, axis=-1, keepdims=True)
    mean_proj = jnp.mean(grad_normed * normed, axis=-1, keepdims=True)
    return (grad_normed - mean_grad - normed * mean_proj) * inv_std


def time_embed(steps_int):
    half_dim = D // 2
    frequency = jnp.exp(-math.log(10000.0) * jnp.arange(half_dim).astype(F32) / half_dim)
    angles = steps_int.astype(F32)[:, None] * frequency[None, :]
    return jnp.concatenate([jnp.cos(angles), jnp.sin(angles)], axis=1)


def adam_update(weight, moment, second, grad, clip_scale):
    scaled = grad * clip_scale
    moment_new = 0.9 * moment + 0.1 * scaled
    second_new = 0.999 * second + 0.001 * scaled * scaled
    rate = 1.5 / math.sqrt(D)
    direction = (
        moment_new / (1.0 - 0.9**STEP) / (jnp.sqrt(second_new / (1.0 - 0.999**STEP)) + 1e-08)
    )
    return (weight - rate * (direction + 0.1 * weight), moment_new, second_new)


def exact_parts(values):
    first = values.astype(BF16)
    rest = values - first.astype(F32)
    second = rest.astype(BF16)
    return (first, second, (rest - second.astype(F32)).astype(BF16))


def mm_split(a, b, dims=NN):
    one, two, three = exact_parts(a)
    return mm(one, b, dims) + mm(two, b, dims) + mm(three, b, dims)


def params(**kw):
    return pltpu.CompilerParams(vmem_limit_bytes=VMEM_BYTES, **kw)


def cost(flops, nbytes):
    return pl.CostEstimate(flops=flops, bytes_accessed=nbytes, transcendentals=0)


def position():
    return (lax.axis_index("wide"), lax.axis_index("narrow"), lax.axis_index("mlp"))


def remote(src, dst, send, recv, device):
    return pltpu.make_async_remote_copy(
        src_ref=src, dst_ref=dst, send_sem=send, recv_sem=recv, device_id=device, device_id_type=MESH
    )


def greet_group(nw, nn, with_mlp):
    w, n, m = position()
    mine = w * nn + n
    groups = nw * nn
    bar = pltpu.get_barrier_semaphore()

    def ask(k, carry):
        other = lax.rem(mine + k, groups)
        pl.semaphore_signal(
            bar, inc=1, device_id=(lax.div(other, nn), lax.rem(other, nn), m), device_id_type=MESH
        )
        return carry

    lax.fori_loop(1, groups, ask, 0)
    if with_mlp:
        pl.semaphore_signal(bar, inc=1, device_id=(w, n, 1 - m), device_id_type=MESH)
    pl.semaphore_wait(bar, groups - 1 + (1 if with_mlp else 0))


def pack_body(owners_ref, att_ref, mlp_ref, out_ref, perm_ref):
    rows = att_ref.shape[0]
    half = mlp_ref.shape[2]
    line = lax.broadcasted_iota(jnp.int32, (D, 128), 0)
    move = jnp.zeros((D, 128), jnp.int32) + owners_ref[0] * rows
    for b in range(1, owners_ref.shape[0]):
        move = jnp.where(line >= b * rows, (owners_ref[b] - b) * rows, move)
    place = line + move
    col = lax.broadcasted_iota(jnp.int32, (D, 128), 1)
    for j in range(D // 128):
        perm_ref[:, j * 128 : (j + 1) * 128] = jnp.where(place == col + j * 128, 1.0, 0.0).astype(BF16)
    out_ref[:, 0 : 3 * D] = att_ref[:, 0 : 3 * D].astype(BF16)
    out_ref[:, 3 * D : ATT] = mm(att_ref[:, 6 * D : 7 * D].astype(BF16), perm_ref[...]).astype(BF16)
    out_ref[:, ATT : ATT + half] = mlp_ref[:, 0, :].astype(BF16)
    out_ref[:, ATT + half : ATT + 2 * half] = mlp_ref[:, 1, :].astype(BF16)


def pack_weights(owners, att, mlp):
    rows, _, half = mlp.shape
    vmem = pl.BlockSpec(memory_space=pltpu.VMEM)
    return pl.pallas_call(
        pack_body,
        grid=(1,),
        in_specs=[
            pl.BlockSpec(memory_space=pltpu.SMEM),
            pl.BlockSpec((rows, 7 * D), lambda s: (0, 0)),
            pl.BlockSpec((rows, 2, half), lambda s: (0, 0, 0)),
        ],
        out_specs=[vmem, vmem],
        out_shape=[
            jax.ShapeDtypeStruct((rows, ATT + 2 * half), BF16),
            jax.ShapeDtypeStruct((D, D), BF16),
        ],
        compiler_params=params(),
        name="pack",
    )(owners, att, mlp)


def modul_body(nw, nn, emb_ref, att_ref, pick_ref, cot_ref, sum_ref, emb_out, silu_out, cot_out,
               gath, flat, parts, from_c, from_x, from_z, gs, gr, cs, cr, xs, xr, zs, zr, ys, yr, ls):
    w, n, m = position()
    nlo, nhi, groups = (2, nn // 2, nw * nn)
    c, x = (lax.rem(n, nlo), lax.div(n, nlo))
    half = cot_ref.shape[0]
    width = parts.shape[2]
    slot = (c * nhi + x) * nw + w
    mine = w * nn + n
    greet_group(nw, nn, True)
    rows = pl.ds(m * half, half)
    to_y = remote(cot_ref, cot_out.at[rows], ys, yr, (w, n, 1 - m))
    to_y.start()
    keep = pltpu.make_async_copy(cot_ref, cot_out.at[rows], ls)
    keep.start()
    gath[slot] = emb_ref[...]

    def copy_to(k):
        other = lax.rem(mine + k, groups)
        return remote(gath.at[slot], gath.at[slot], gs.at[k], gr.at[k], (lax.div(other, nn), lax.rem(other, nn), m))

    def send(k, carry):
        copy_to(k).start()
        return carry

    def finish(k, carry):
        copy_to(k).wait()
        return carry

    lax.fori_loop(1, groups, send, 0)
    lax.fori_loop(1, groups, finish, 0)
    picked = mm(gath[...].reshape(groups * 8, D), pick_ref[...]).astype(BF16)
    line = lax.broadcasted_iota(jnp.int32, (2 * groups, 8 * groups), 0)
    col = lax.broadcasted_iota(jnp.int32, (2 * groups, 8 * groups), 1)
    at = (line // 2) * 8 + line % 2
    emb = mm((col == at).astype(BF16), picked).astype(BF16)
    silu = mm((col == at + 2).astype(BF16), picked).astype(BF16)
    emb_out[...] = emb
    silu_out[...] = silu
    flat[:, 0 : 3 * D] = mm(emb, att_ref[:, 3 * D : 6 * D].astype(BF16))
    flat[:, 3 * D : 9 * D] = mm(silu, att_ref[:, 7 * D : 13 * D].astype(BF16))
    for g in range(groups):
        parts[g] = flat[2 * g : 2 * g + 2, :]
    block = nhi * nw
    other_c = (1 - c) * block
    mine_c = c * block
    hop = remote(parts.at[pl.ds(other_c, block)], from_c, cs, cr, (w, x * nlo + 1 - c, m))
    hop.start()
    hop.wait()
    parts[pl.ds(mine_c, block)] = parts[pl.ds(mine_c, block)] + from_c[...]
    hops = []
    for k in range(1, nhi):
        there = lax.rem(x + k, nhi)
        hop = remote(
            parts.at[pl.ds(mine_c + there * nw, nw)], from_x.at[k - 1], xs.at[k - 1], xr.at[k - 1], (w, there * nlo + c, m)
        )
        hop.start()
        hops.append(hop)
    for hop in hops:
        hop.wait()
    first = mine_c + x * nw
    total = parts[pl.ds(first, nw)]
    for k in range(1, nhi):
        total = total + from_x[k - 1]
    parts[pl.ds(first, nw)] = total
    hops = []
    for k in range(1, nw):
        there = lax.rem(w + k, nw)
        hop = remote(parts.at[first + there], from_z.at[k - 1], zs.at[k - 1], zr.at[k - 1], (there, n, m))
        hop.start()
        hops.append(hop)
    for hop in hops:
        hop.wait()
    total = parts[first + w]
    for k in range(1, nw):
        total = total + from_z[k - 1]
    sum_ref[...] = total
    keep.wait()
    to_y.wait()


def modul_exchange(emb_rows, att, pick, cot, nw, nn):
    groups = nw * nn
    nhi = nn // 2
    width = 9 * D
    half = cot.shape[0]
    vmem = pl.BlockSpec(memory_space=pltpu.VMEM)
    dma = pltpu.SemaphoreType.DMA
    return pl.pallas_call(
        partial(modul_body, nw, nn),
        in_specs=[vmem, vmem, vmem, ANY],
        out_specs=[vmem, vmem, vmem, ANY],
        out_shape=[
            jax.ShapeDtypeStruct((2, width), F32),
            jax.ShapeDtypeStruct((2 * groups, att.shape[0]), BF16),
            jax.ShapeDtypeStruct((2 * groups, att.shape[0]), BF16),
            jax.ShapeDtypeStruct((2 * half, D), BF16),
        ],
        scratch_shapes=[
            pltpu.VMEM((groups, 8, D), BF16),
            pltpu.VMEM((2 * groups, width), F32),
            pltpu.VMEM((groups, 2, width), F32),
            pltpu.VMEM((nhi * nw, 2, width), F32),
            pltpu.VMEM((max(nhi - 1, 1), nw, 2, width), F32),
            pltpu.VMEM((max(nw - 1, 1), 2, width), F32),
            dma((groups,)), dma((groups,)), dma, dma,
            dma((max(nhi - 1, 1),)), dma((max(nhi - 1, 1),)),
            dma((max(nw - 1, 1),)), dma((max(nw - 1, 1),)),
            dma, dma, dma,
        ],
        compiler_params=params(collective_id=1, has_side_effects=True),
        cost_estimate=cost(10**8, 3 * 10**7),
        name="modul_exchange",
    )(emb_rows, att, pick, cot)


def bias_body(index_ref, table_ref, bias_ref):
    low = jnp.bitwise_and(index_ref[...], 127)
    high = jnp.right_shift(index_ref[...], 7)
    for part in range(index_ref.shape[1] // 128):
        at = slice(part * 128, (part + 1) * 128)
        lo = low[:, at]
        hi = high[:, at]
        total = jnp.zeros(lo.shape, F32)
        for chunk in range(8):
            row = jnp.broadcast_to(table_ref[0, :, chunk * 128 : (chunk + 1) * 128], lo.shape)
            total = jnp.where(hi == chunk, jnp.take_along_axis(row, lo, axis=1), total)
        bias_ref[0, :, at] = total


def rel_bias(index_t, table_t, seq):
    return pl.pallas_call(
        bias_body,
        grid=(HEADS,),
        in_specs=[
            pl.BlockSpec((seq, seq), lambda h: (0, 0)),
            pl.BlockSpec((1, 1, 1024), lambda h: (h, 0, 0)),
        ],
        out_specs=pl.BlockSpec((1, seq, seq), lambda h: (h, 0, 0)),
        out_shape=jax.ShapeDtypeStruct((HEADS, seq, seq), F32),
        cost_estimate=cost(2 * 10**8, 4 * 10**7),
        name="rel_bias",
    )(index_t, table_t)


def front_body(tok_ref, cot_ref, perm_ref, mod_ref, tok_out, shaped_out, shaped_t, cot_out, branch_out, sums):
    moved = mm(tok_ref[...], perm_ref[...])
    tok_out[...] = moved.astype(BF16)
    normed, _ = norm_stats(moved)
    shaped = normed * (1.0 + mod_ref[0, 1:2]) + mod_ref[0, 0:1]
    shaped_out[...] = shaped.astype(BF16)
    shaped_t[...] = shaped.T.astype(BF16)
    cot = mm(cot_ref[...], perm_ref[...])
    cot_out[...] = cot.astype(BF16)
    branch = (cot * mod_ref[0, 5:6]).astype(BF16)
    branch_out[...] = branch
    sums[0, 0:1] = jnp.sum(branch.astype(F32), axis=0, keepdims=True)
    sums[0, 1:2] = jnp.sum(cot, axis=0, keepdims=True)
    sums[0, 2:8] = jnp.zeros((6, D), F32)


def front(tokens, cot, perm, mod, seq, images):
    rows = seq * images
    tok = pl.BlockSpec((seq, D), lambda n: (n, 0))
    per = pl.BlockSpec((1, 8, D), lambda n: (n, 0, 0))
    return pl.pallas_call(
        front_body,
        grid=(images,),
        in_specs=[tok, tok, pl.BlockSpec((D, D), lambda n: (0, 0)), per],
        out_specs=[tok, tok, pl.BlockSpec((D, seq), lambda n: (0, n)), tok, tok, per],
        out_shape=[
            jax.ShapeDtypeStruct((rows, D), BF16),
            jax.ShapeDtypeStruct((rows, D), BF16),
            jax.ShapeDtypeStruct((D, rows), BF16),
            jax.ShapeDtypeStruct((rows, D), BF16),
            jax.ShapeDtypeStruct((rows, D), BF16),
            jax.ShapeDtypeStruct((images, 8, D), F32),
        ],
        compiler_params=params(),
        cost_estimate=cost(4 * rows * D * D, 10**7),
        name="front",
    )(tokens, cot, perm, mod)


def attend_fwd_body(seq, images, own, shaped_ref, w_ref, time_ref, bias_ref, qkv_ref, out_ref, lse_ref):
    step = pl.program_id(0)

    @pl.when(step < 3)
    def _():
        made = mm(shaped_ref[...], w_ref[...])
        made = jnp.concatenate(
            [made[n * seq : (n + 1) * seq] + time_ref[n : n + 1] for n in range(images)], axis=0
        )
        qkv_ref[step] = made.T.reshape(HEADS, HD, seq * images).astype(BF16)

    @pl.when(step >= 3)
    def _():
        for j in range(GROUP):
            h = (step - 3) * GROUP + j
            query, key, value = [qkv_ref[p, h] for p in range(3)]
            place = own[h]
            for n in range(images):
                at = slice(n * seq, (n + 1) * seq)
                scores = mm(key[:, at], query[:, at], TN) * INV_ROOT + bias_ref[j]
                top = jnp.max(scores, axis=0, keepdims=True)
                weights = jnp.exp(scores - top)
                total = jnp.sum(weights, axis=0, keepdims=True)
                probs = (weights * (1.0 / total)).astype(BF16)
                out_ref[place, :, at] = mm(value[:, at], probs).astype(BF16)
                lse_ref[j, :, at] = top + jnp.log(total)


def attend_fwd(own, shaped, gathered, time_part, bias, seq, images):
    rows = seq * images

    def part(s):
        return jnp.minimum(s, 2)

    def group(s):
        return jnp.maximum(s - 3, 0)

    return pl.pallas_call(
        partial(attend_fwd_body, seq, images),
        grid_spec=pltpu.PrefetchScalarGridSpec(
            num_scalar_prefetch=1,
            grid=(3 + HEADS // GROUP,),
            in_specs=[
                pl.BlockSpec((rows, D), lambda s, own: (0, 0)),
                pl.BlockSpec((D, D), lambda s, own: (0, part(s))),
                pl.BlockSpec((images, D), lambda s, own: (0, part(s))),
                pl.BlockSpec((GROUP, seq, seq), lambda s, own: (group(s), 0, 0)),
            ],
            out_specs=[
                pl.BlockSpec((3, HEADS, HD, rows), lambda s, own: (0, 0, 0, 0)),
                pl.BlockSpec((HEADS, HD, rows), lambda s, own: (0, 0, 0)),
                pl.BlockSpec((GROUP, 1, rows), lambda s, own: (group(s), 0, 0)),
            ],
        ),
        out_shape=[
            jax.ShapeDtypeStruct((3, HEADS, HD, rows), BF16),
            jax.ShapeDtypeStruct((HEADS, HD, rows), BF16),
            jax.ShapeDtypeStruct((HEADS, 1, rows), F32),
        ],
        compiler_params=params(),
        cost_estimate=cost(6 * 10**9, 2 * 10**7),
        name="attend_fwd",
    )(own, shaped, gathered, time_part, bias)


def mid_body(att_ref, w_ref, tok_ref, mod_ref, attn_out, shaped_out):
    attn = mm(att_ref[...], w_ref[...], TN) + mod_ref[0, 6:7]
    attn_out[...] = attn
    mid = tok_ref[...].astype(F32) + mod_ref[0, 2:3] * attn
    normed, _ = norm_stats(mid)
    shaped_out[...] = (normed * (1.0 + mod_ref[0, 4:5]) + mod_ref[0, 3:4]).astype(BF16)


def middle(att, gathered, tok, mod, seq, images):
    rows = seq * images
    row = pl.BlockSpec((seq, D), lambda n: (n, 0))
    return pl.pallas_call(
        mid_body,
        grid=(images,),
        in_specs=[
            pl.BlockSpec((D, seq), lambda n: (0, n)),
            pl.BlockSpec((D, D), lambda n: (0, 3)),
            row,
            pl.BlockSpec((1, 8, D), lambda n: (n, 0, 0)),
        ],
        out_specs=[row, row],
        out_shape=[jax.ShapeDtypeStruct((rows, D), F32), jax.ShapeDtypeStruct((rows, D), BF16)],
        compiler_params=params(),
        cost_estimate=cost(2 * rows * D * D, 10**7),
        name="middle",
    )(att, gathered, tok, mod)


def once(shape, index):
    return pl.BlockSpec(shape, index, pipeline_mode=pl.Buffered(1))


def mlp_body(nw, nn, seq, tiles, direct, x_ref, gb_ref, one_ref, two_ref, bias_ref, cot_ref,
             term_ref, mine_ref, send_ref, gate_ref, bias_out, own_ref, peer_ref, *rest):
    if direct:
        first_ref, hidden, grads, x_t, gb_t, acc, branch_ref, peer_in, ts, tr, made, from_c, red, from_x, cs, cr, xs, xr = rest
    else:
        hidden, grads, x_t, gb_t, acc, branch_ref, peer_in, ts, tr = rest
    step = pl.program_id(0)
    w, n, m = position()
    nlo, nhi = (2, nn // 2)
    c, x = (lax.rem(n, nlo), lax.div(n, nlo))
    groups = nw * nn
    blk = D // groups
    sibling = (w, x * nlo + 1 - c, m)
    twin = (w, n, 1 - m)

    def to_twin(i):
        return remote(own_ref.at[i], peer_in.at[i], ts.at[i], tr.at[i], twin)

    def to_sibling(k):
        return remote(made.at[k, :, :, 1 - c], from_c.at[k], cs.at[k], cr.at[k], sibling)

    def along_x(d):
        there = lax.rem(x + d, nhi)
        return (there, (w, there * nlo + c, m))

    def hop_x(k, d):
        there, device = along_x(d)
        return remote(red.at[k, :, there], from_x.at[k, d - 1], xs.at[k, d - 1], xr.at[k, d - 1], device)

    @pl.when(step == 0)
    def _():
        bar = pltpu.get_barrier_semaphore()
        friends = [twin]
        if direct:
            friends = [twin, sibling] + [along_x(d)[1] for d in range(1, nhi)]
        for device in friends:
            pl.semaphore_signal(bar, inc=1, device_id=device, device_id_type=MESH)
        x_t[...] = x_ref[...].T
        gb_t[...] = gb_ref[...].T
        pl.semaphore_wait(bar, len(friends))

    if tiles > 0:

        @pl.when(step < 2 * tiles)
        def _():
            image = lax.div(step, tiles)
            f = step - image * tiles
            at = pl.ds(pl.multiple_of(image * seq, seq), seq)
            pre = mm(x_ref[at], one_ref[...]) + bias_ref[...]
            root = math.sqrt(2.0 / math.pi)
            square = pre * pre
            bend = jnp.tanh(root * (pre + 0.044715 * (square * pre)))
            rise = 0.5 * (1.0 + bend)
            hidden[f, at] = (pre * rise).astype(BF16)
            slope = rise + 0.5 * pre * (1.0 - bend * bend) * (root * (1.0 + 3 * 0.044715 * square))
            grad = (mm(gb_ref[at], two_ref[...]) * slope).astype(BF16)
            grads[f, at] = grad
            back = mm(grad, one_ref[...], NT)

            @pl.when(f == 0)
            def _():
                acc[...] = back

            @pl.when(f > 0)
            def _():
                acc[...] += back

            @pl.when(f == tiles - 1)
            def _():
                own_ref[image] = acc[...].astype(BF16)
                to_twin(image).start()

    def place(k, values):
        made[k] = values.reshape(nw, nhi, nlo, blk, TILE).astype(BF16)

    def combine(k):
        to_sibling(k).wait()
        return made[k, :, :, c] + from_c[k]

    @pl.when((step >= 2 * tiles) & (step < 3 * tiles))
    def _():
        f = step - 2 * tiles
        one_grad = mm(x_t[...], grads[f])
        two_grad = mm(gb_t[...], hidden[f])
        if direct:
            place(2 * f, one_grad)
            to_sibling(2 * f).start()
            place(2 * f + 1, two_grad)
            to_sibling(2 * f + 1).start()
        else:
            term_ref[:, 0:TILE] = one_grad.astype(BF16)
            term_ref[:, TILE : 2 * TILE] = two_grad.astype(BF16)
        bias_out[...] = jnp.sum(grads[f].astype(F32), axis=0, keepdims=True)
        branch = mm(hidden[f], two_ref[...], NT)

        @pl.when(f == 0)
        def _():
            branch_ref[...] = branch
            if direct:
                for k in range(2):
                    red[k] = combine(k)
                    for d in range(1, nhi):
                        hop_x(k, d).start()

        @pl.when(f > 0)
        def _():
            branch_ref[...] += branch

    if direct:

        @pl.when(step >= 2 * tiles + 2)
        def _():
            f = step - 2 * tiles - 1
            for half in range(2):
                term_ref[:, :, :, half * TILE : (half + 1) * TILE] = combine(2 * f + half)

    @pl.when(step == 3 * tiles)
    def _():
        gate_ref[...] = jnp.zeros_like(gate_ref)
        for image in range(2):
            at = slice(image * seq, (image + 1) * seq)
            gate_ref[image : image + 1] = jnp.sum(
                cot_ref[at].astype(F32) * branch_ref[at], axis=0, keepdims=True
            )
        send_ref[...] = branch_ref[pl.ds(pl.multiple_of((1 - m) * seq, seq), seq)].astype(BF16)
        mine_ref[...] = branch_ref[pl.ds(pl.multiple_of(m * seq, seq), seq)]
        to_twin(0).wait()
        to_twin(1).wait()
        peer_ref[...] = peer_in[...]
        if direct:
            for k in range(2):
                for d in range(1, nhi):
                    hop_x(k, d).wait()
                total = red[k, :, x]
                for d in range(1, nhi):
                    total = total + from_x[k, d - 1]
                first_ref[:, :, k * TILE : (k + 1) * TILE] = total


def mlp_core(x, gb, gathered, bias, cot, seq, nw, nn):
    half = bias.shape[1]
    rows = 2 * seq
    tiles = half // TILE
    nhi = nn // 2
    blk = D // (nw * nn)
    one, two = (ATT // TILE, (ATT + half) // TILE)
    whole = once((rows, D), lambda s: (0, 0))
    vmem = pl.BlockSpec(memory_space=pltpu.VMEM)
    dma = pltpu.SemaphoreType.DMA

    def weight(s):
        return jnp.where(s < 3 * tiles, lax.rem(s, tiles), tiles - 1)

    def behind(s):
        return jnp.clip(s - 2 * tiles - 2, 0, tiles - 2)

    direct = blk % 8 == 0
    hi = max(nhi - 1, 1)
    if direct:
        term_spec = pl.BlockSpec((nw, nhi, blk, 2 * TILE), lambda s: (0, 0, 0, behind(s)))
        term_shape = jax.ShapeDtypeStruct((nw, nhi, blk, 2 * half - 2 * TILE), BF16)
    else:
        term_spec = pl.BlockSpec((D, 2 * TILE), lambda s: (0, jnp.clip(s - 2 * tiles, 0, tiles - 1)))
        term_shape = jax.ShapeDtypeStruct((D, 2 * half), BF16)
    return pl.pallas_call(
        partial(mlp_body, nw, nn, seq, tiles, direct),
        grid=(3 * tiles + 1,),
        in_specs=[
            whole,
            whole,
            pl.BlockSpec((D, TILE), lambda s: (0, one + jnp.where(s < 2 * tiles, lax.rem(s, tiles), tiles - 1))),
            pl.BlockSpec((D, TILE), lambda s: (0, two + weight(s))),
            pl.BlockSpec((1, TILE), lambda s: (0, weight(s))),
            whole,
        ],
        out_specs=[
            term_spec,
            vmem,
            vmem,
            vmem,
            pl.BlockSpec((1, TILE), lambda s: (0, jnp.clip(s - 2 * tiles, 0, tiles - 1))),
            vmem,
            vmem,
        ]
        + ([vmem] if direct else []),
        out_shape=[
            term_shape,
            jax.ShapeDtypeStruct((seq, D), F32),
            jax.ShapeDtypeStruct((seq, D), BF16),
            jax.ShapeDtypeStruct((8, D), F32),
            jax.ShapeDtypeStruct((1, half), F32),
            jax.ShapeDtypeStruct((2, seq, D), BF16),
            jax.ShapeDtypeStruct((2, seq, D), BF16),
        ]
        + ([jax.ShapeDtypeStruct((nw, blk, 2 * TILE), BF16)] if direct else []),
        scratch_shapes=[
            pltpu.VMEM((tiles, rows, TILE), BF16),
            pltpu.VMEM((tiles, rows, TILE), BF16),
            pltpu.VMEM((D, rows), BF16),
            pltpu.VMEM((D, rows), BF16),
            pltpu.VMEM((seq, D), F32),
            pltpu.VMEM((rows, D), F32),
            pltpu.VMEM((2, seq, D), BF16),
            dma((2,)),
            dma((2,)),
        ]
        + (
            [
                pltpu.VMEM((2 * tiles, nw, nhi, 2, blk, TILE), BF16),
                pltpu.VMEM((2 * tiles, nw, nhi, blk, TILE), BF16),
                pltpu.VMEM((2, nw, nhi, blk, TILE), BF16),
                pltpu.VMEM((2, hi, nw, blk, TILE), BF16),
                dma((2 * tiles,)),
                dma((2 * tiles,)),
                dma((2, hi)),
                dma((2, hi)),
            ]
            if direct
            else []
        ),
        compiler_params=params(collective_id=4, has_side_effects=True),
        cost_estimate=cost(12 * rows * D * half, 4 * 10**7),
        name="mlp_core",
    )(x, gb, gathered, gathered, bias, cot)


REL_ROWS = 32
BUCKETS = 128


def back_body(nw, nn, seq, images, moved, direct, own, att_ref, shaped_ref, w_ref, qkv_ref, bias_ref, lse_ref,
              index_ref, tok_ref, mod_ref, perm_ref, back_own, back_peer, attn_ref, cot_ref, front_sums, gate_mine, send_ref, gate_ref, *rest):
    if direct:
        term_ref, first_ref = rest[:2]
        rest = rest[2:]
    time_ref, rel_ref, in_ref, rows_out, keep, keep_mod, branch_out = rest[:7]
    rest = rest[7:]
    if direct:
        part_ref, done_ref, half_ref = rest[:3]
        rest = rest[3:]
    else:
        dw_ref = rest[0]
        rest = rest[1:]
    made, ga, ga_t, branch_in, gate_in, acc, ds_all, mid, line, yb, yc, ybr, ycr = rest[:13]
    if direct:
        held, from_x, two, from_z, ls, xs, xr, zs, zr, dwt, att_c, att_red, att_x, att_two, att_z, acs, acr, axs, axr, azs, azr = rest[13:]
    step = pl.program_id(0)
    groups = HEADS // GROUP
    rows = seq * images
    att_at = images + 1
    part_at = att_at + groups
    rel_at = part_at + 3
    end_at = rel_at + seq // REL_ROWS
    last = end_at + images - 1
    w, n, m = position()
    nlo, nhi = (2, nn // 2)
    c, x = (lax.rem(n, nlo), lax.div(n, nlo))
    twin = (w, n, 1 - m)

    def along_x(d):
        there = lax.rem(x + d, nhi)
        return (there, (w, there * nlo + c, m))

    def along_z(d):
        there = lax.rem(w + d, nw)
        return (there, (there, n, m))

    def swap_branch():
        return remote(send_ref, branch_in, yb, ybr, twin)

    def swap_gate():
        return remote(gate_ref, gate_in, yc, ycr, twin)

    if direct:
        chunks = part_ref.shape[1] // TILE

        def load(k):
            return pltpu.make_async_copy(
                term_ref.at[:, x, :, pl.ds(pl.multiple_of((k - 2) * TILE, 128), TILE)], held.at[k - 2], ls.at[k - 2]
            )

        def hop_x(k, d):
            there, device = along_x(d)
            return remote(
                term_ref.at[:, there, :, pl.ds(pl.multiple_of((k - 2) * TILE, 128), TILE)],
                from_x.at[k - 2, d - 1], xs.at[k - 2, d - 1], xr.at[k - 2, d - 1], device,
            )

        def hop_z(k, d):
            there, device = along_z(d)
            return remote(two.at[k, d - 1], from_z.at[k, d - 1], zs.at[k, d - 1], zr.at[k, d - 1], device)

        def chain(k, zi):
            total = held[k - 2, zi]
            for d in range(1, nhi):
                total = total + from_x[k - 2, d - 1, zi]
            return total

        def start_x(k):
            for d in range(1, nhi):
                hop_x(k, d).start()

        def span(k):
            return pl.ds(pl.multiple_of(k * TILE, 128), TILE)

        def stage_x(k):
            load(k).wait()
            for d in range(1, nhi):
                hop_x(k, d).wait()
            for d in range(1, nw):
                there, _ = along_z(d)
                two[k, d - 1] = chain(k, there)
                hop_z(k, d).start()

        def finish_z(k, total):
            for d in range(1, nw):
                hop_z(k, d).wait()
            total = total.astype(F32)
            for d in range(1, nw):
                total = total + from_z[k, d - 1].astype(F32)
            part_ref[:, span(k)] = total.astype(BF16)

        sibling = (w, x * nlo + 1 - c, m)

        def att_hop_c(i):
            return remote(dwt.at[i, :, :, 1 - c], att_c.at[i], acs.at[i], acr.at[i], sibling)

        def att_hop_x(i, d):
            there, device = along_x(d)
            return remote(att_red.at[i, :, there], att_x.at[i, d - 1], axs.at[i, d - 1], axr.at[i, d - 1], device)

        def att_place(i, values):
            dwt[i] = values.reshape(nw, nhi, nlo, -1, D).astype(BF16)
            att_hop_c(i).start()

        def att_combine(i):
            att_hop_c(i).wait()
            att_red[i] = dwt[i, :, :, c] + att_c[i]
            for d in range(1, nhi):
                att_hop_x(i, d).start()

        def att_hop_z(d):
            there, device = along_z(d)
            return remote(att_two.at[d - 1], att_z.at[d - 1], azs.at[d - 1], azr.at[d - 1], device)

        def att_chain(i, zi):
            total = att_red[i, zi, x]
            for d in range(1, nhi):
                total = total + att_x[i, d - 1, zi]
            return total

        def att_spread(i):
            for d in range(1, nhi):
                att_hop_x(i, d).wait()
            for d in range(1, nw):
                there, _ = along_z(d)
                att_two[d - 1] = att_chain(i, there)
                att_hop_z(d).start()

        def att_finish(i, j):
            for d in range(1, nw):
                att_hop_z(d).wait()
            total = att_chain(i, w).astype(F32)
            for d in range(1, nw):
                total = total + att_z[d - 1].astype(F32)
            done_ref[...] = total.astype(BF16)
            for d in range(1, nhi):
                att_hop_x(j, d).wait()
            total = att_red[j, :, x]
            for d in range(1, nhi):
                total = total + att_x[j, d - 1]
            half_ref[...] = total

    @pl.when(step == 0)
    def _():
        greet_group(nw, nn, True)
        if direct:
            for k in range(2, chunks):
                load(k).start()
            start_x(2)
            for k in range(2):
                for d in range(1, nw):
                    there, _ = along_z(d)
                    two[k, d - 1] = first_ref[there, :, k * TILE : (k + 1) * TILE]
                    hop_z(k, d).start()
        swap_branch().start()
        swap_gate().start()

    @pl.when(step < images)
    def _():
        at = pl.ds(pl.multiple_of(step * seq, seq), seq)
        attn = attn_ref[...]
        value = tok_ref[...].astype(F32) + mod_ref[0, 2:3] * attn

        @pl.when(m == step)
        def _():
            keep[...] = value
            keep_mod[...] = mod_ref[0]

        normed, inv = norm_stats(value)
        grad = back_own[0].astype(F32) + back_peer[0].astype(F32)
        line[pl.ds(step * 6 + 3, 1)] = jnp.sum(grad, axis=0, keepdims=True)
        line[pl.ds(step * 6 + 4, 1)] = jnp.sum(grad * normed, axis=0, keepdims=True)
        grad = cot_ref[...].astype(F32) + norm_back(grad * (1.0 + mod_ref[0, 4:5]), normed, inv)
        mid[at] = grad
        line[pl.ds(step * 6 + 2, 1)] = jnp.sum(grad * attn, axis=0, keepdims=True)
        low = (grad * mod_ref[0, 2:3]).astype(BF16)
        out_sum = jnp.sum(low.astype(F32), axis=0, keepdims=True)
        at_row = slice(6 * images, 6 * images + 1)

        @pl.when(step == 0)
        def _():
            line[at_row] = out_sum

        @pl.when(step > 0)
        def _():
            line[at_row] += out_sum

        ga[at] = low
        turned = mm(w_ref[...], low, NT)
        if not moved:
            turned = mm(perm_ref[...], turned.astype(BF16))
        ga_t[:, :, at] = turned.reshape(HEADS, HD, seq).astype(BF16)

    @pl.when((step >= att_at) & (step < part_at))
    def _():
        for j in range(GROUP):
            h = (step - att_at) * GROUP + j
            place = own[h]
            ds_sum = jnp.zeros((seq, seq), F32)
            for image in range(images):
                at = slice(image * seq, (image + 1) * seq)
                query, key, value = [qkv_ref[p, j, :, at] for p in range(3)]
                grad = ga_t[place, :, at]
                probs = jnp.exp(mm(key, query, TN) * INV_ROOT + (bias_ref[j] - lse_ref[j, :, at]))
                grad_probs = mm(value, grad, TN)
                inner = jnp.sum(probs * grad_probs, axis=0, keepdims=True)
                ds = (probs * (grad_probs - inner)).astype(BF16)
                made[0, h, :, at] = (mm(key, ds) * INV_ROOT).astype(BF16)
                made[1, h, :, at] = (mm(query, ds, NT) * INV_ROOT).astype(BF16)
                made[2, h, :, at] = mm(grad, probs.astype(BF16), NT).astype(BF16)
                ds_sum = ds_sum + ds.astype(F32)
            ds_all[h] = ds_sum.astype(BF16)

    @pl.when((step >= part_at) & (step < part_at + 3))
    def _():
        p = step - part_at
        across = made[p].astype(F32).reshape(D, rows)
        upright = across.T.astype(BF16)
        back = mm(upright, w_ref[...], NT)

        @pl.when(p == 0)
        def _():
            acc[...] = back

        @pl.when(p > 0)
        def _():
            acc[...] += back

        if direct:


            @pl.when((p == 2) == (m == 0))
            def _():
                att_place(lax.rem(p, 2), mm(shaped_ref[...], across.astype(BF16), NT))
        else:
            dw_ref[...] = mm(shaped_ref[...], across.astype(BF16), NT).astype(BF16)
        wide = upright.astype(F32)
        for image in range(images):
            time_ref[image : image + 1] = jnp.sum(
                wide[image * seq : (image + 1) * seq], axis=0, keepdims=True
            )

    @pl.when((step >= rel_at) & (step < end_at))
    def _():
        index = index_ref[0]
        low = jnp.bitwise_and(index, BUCKETS - 1)
        high = jnp.right_shift(index, 7)
        bucket = lax.broadcasted_iota(jnp.int32, (BUCKETS, index.shape[1]), 0)
        hot = jnp.where(bucket == low, 1.0, 0.0).astype(BF16)
        start = pl.multiple_of((step - rel_at) * REL_ROWS, REL_ROWS)
        turned = jnp.swapaxes(ds_all[:, pl.ds(start, REL_ROWS), :].astype(F32), 0, 1)
        total = jnp.concatenate([turned[j] for j in range(REL_ROWS)], axis=1)
        picked = jnp.concatenate([jnp.where(high == a, total, 0.0) for a in range(1024 // BUCKETS)], axis=0)
        found = mm(picked.astype(BF16), hot, NT)

        @pl.when(step == rel_at)
        def _():
            rel_ref[...] = found

        @pl.when(step > rel_at)
        def _():
            rel_ref[...] += found

    @pl.when(step >= end_at)
    def _():
        image = step - end_at
        normed, inv = norm_stats(tok_ref[...].astype(F32))
        at = pl.ds(pl.multiple_of(image * seq, seq), seq)
        grad = acc[at]
        line[pl.ds(image * 6, 1)] = jnp.sum(grad, axis=0, keepdims=True)
        line[pl.ds(image * 6 + 1, 1)] = jnp.sum(grad * normed, axis=0, keepdims=True)
        grad = mid[at] + norm_back(grad * (1.0 + mod_ref[0, 1:2]), normed, inv)
        in_ref[...] = mm_split(grad, perm_ref[...], NT)

    @pl.when(step == last)
    def _():
        swap_branch().wait()
        swap_gate().wait()
        branch_out[...] = branch_in[...]
        two_sum = front_sums[0, 0:1]
        for image in range(images):
            gate_two = gate_mine[image : image + 1] + gate_in[image : image + 1]
            line[image * 6 + 5 : image * 6 + 6] = gate_two + mod_ref[0, 7:8] * front_sums[image, 1:2]
            if image > 0:
                two_sum = two_sum + front_sums[image, 0:1]
        line[6 * images + 1 : 6 * images + 2] = two_sum
        line[6 * images + 2 : 16] = jnp.zeros((14 - 6 * images, D), F32)
        thrice = mm(jnp.concatenate(exact_parts(line[...]), axis=0), perm_ref[...], NT)
        rows_out[...] = thrice[0:16] + thrice[16:32] + thrice[32:48]

    if direct:

        @pl.when((step == images) & (m == 0))
        def _():
            att_place(1, mm(att_ref[...], ga[...]))

        @pl.when((step == part_at + 1) | (step == rel_at + 4))
        def _():
            att_combine(jnp.where(step == part_at + 1, 1 - m, m))

        @pl.when((step == 3) | (step == 5) | (step == 8) | (step == 9))
        def _():
            stage_x(2 + (step >= 5).astype(jnp.int32) + (step >= 8).astype(jnp.int32) + (step >= 9).astype(jnp.int32))

        @pl.when((step == 1) | (step == 3) | (step == 5))
        def _():
            start_x(3 + (step >= 3).astype(jnp.int32) + (step >= 5).astype(jnp.int32))

        @pl.when((step == 5) | (step == 6))
        def _():
            k = step - 5
            finish_z(k, first_ref[w, :, span(k)])

        @pl.when(step == end_at - 1)
        def _():
            att_spread(1 - m)

        @pl.when(step >= end_at)
        def _():
            for half in range(2):
                k = 2 + 2 * (step - end_at) + half
                finish_z(k, chain(k, w))

    else:

        @pl.when(step == images)
        def _():
            dw_ref[...] = mm(att_ref[...], ga[...]).astype(BF16)

    if direct:

        @pl.when(step == last)
        def _():
            att_finish(1 - m, m)


def back_core(own, att, shaped_t, gathered, qkv, bias, lse, index_t, tok, mod, perm, back_own, back_peer,
              attn, cot, front_sums, send, gate, reduced, seq, images, nw, nn, moved):
    rows = seq * images
    groups = HEADS // GROUP
    att_at = images + 1
    part_at = att_at + groups
    rel_at = part_at + 3
    end_at = rel_at + seq // REL_ROWS
    last = end_at + images - 1
    nhi = nn // 2
    direct = len(reduced) == 2
    hi, wi = (max(nhi - 1, 1), max(nw - 1, 1))
    vmem = pl.BlockSpec(memory_space=pltpu.VMEM)
    dma = pltpu.SemaphoreType.DMA

    def group(s):
        return jnp.clip(s - att_at, 0, groups - 1)

    def part(s):
        return jnp.clip(s - part_at, 0, 2)

    def early(s):
        return jnp.minimum(s, images - 1)

    def both(s):
        return jnp.where(s < images, s, jnp.clip(s - end_at, 0, images - 1))

    def late(s):
        return jnp.clip(s - end_at, 0, images - 1)

    per = pl.BlockSpec((1, 8, D), lambda s, own: (both(s), 0, 0))
    swapped = once((1, seq, D), lambda s, own: (early(s), 0, 0))
    extra_in, extra_out, extra_shape, extra_scratch = ([], [], [], [])
    if direct:
        blk, cols = reduced[0].shape[2:]
        cols = cols + 2 * TILE
        chunks = cols // TILE
        extra_in = [ANY, once((nw, blk, 2 * TILE), lambda s, own: (0, 0, 0))]
        extra_out = [vmem, vmem, vmem]
        extra_shape = [
            jax.ShapeDtypeStruct((blk, cols), BF16),
            jax.ShapeDtypeStruct((blk, D), BF16),
            jax.ShapeDtypeStruct((nw, blk, D), BF16),
        ]
        extra_scratch = [
            pltpu.VMEM((chunks - 2, nw, blk, TILE), BF16),
            pltpu.VMEM((chunks - 2, hi, nw, blk, TILE), BF16),
            pltpu.VMEM((chunks, wi, blk, TILE), BF16),
            pltpu.VMEM((chunks, wi, blk, TILE), BF16),
            dma((chunks - 2,)),
            dma((chunks - 2, hi)),
            dma((chunks - 2, hi)),
            dma((chunks, wi)),
            dma((chunks, wi)),
            pltpu.VMEM((2, nw, nhi, 2, blk, D), BF16),
            pltpu.VMEM((2, nw, nhi, blk, D), BF16),
            pltpu.VMEM((2, nw, nhi, blk, D), BF16),
            pltpu.VMEM((2, hi, nw, blk, D), BF16),
            pltpu.VMEM((wi, blk, D), BF16),
            pltpu.VMEM((wi, blk, D), BF16),
            dma((2,)),
            dma((2,)),
            dma((2, hi)),
            dma((2, hi)),
            dma((wi,)),
            dma((wi,)),
        ]
    else:
        extra_out = [
            pl.BlockSpec((D, D), lambda s, own: (0, jnp.where(s < part_at, 3, jnp.clip(s - part_at, 0, 2))))
        ]
        extra_shape = [jax.ShapeDtypeStruct((D, ATT), BF16)]
    return pl.pallas_call(
        partial(back_body, nw, nn, seq, images, moved, direct),
        grid_spec=pltpu.PrefetchScalarGridSpec(
            num_scalar_prefetch=1,
            grid=(last + 1,),
            in_specs=[
                once((D, rows), lambda s, own: (0, 0)),
                once((D, rows), lambda s, own: (0, 0)),
                once((D, D), lambda s, own: (0, jnp.where(s < images, 3, part(s)))),
                pl.BlockSpec((3, GROUP, HD, rows), lambda s, own: (0, group(s), 0, 0)),
                pl.BlockSpec((GROUP, seq, seq), lambda s, own: (group(s), 0, 0)),
                pl.BlockSpec((GROUP, 1, rows), lambda s, own: (group(s), 0, 0)),
                pl.BlockSpec(
                    (1, 1, REL_ROWS * seq), lambda s, own: (jnp.clip(s - rel_at, 0, seq // REL_ROWS - 1), 0, 0)
                ),
                once((seq, D), lambda s, own: (both(s), 0)),
                per,
                once((D, D), lambda s, own: (0, 0)),
                swapped,
                swapped,
                once((seq, D), lambda s, own: (early(s), 0)),
                once((seq, D), lambda s, own: (early(s), 0)),
                once((images, 8, D), lambda s, own: (0, 0, 0)),
                once((8, D), lambda s, own: (0, 0)),
                ANY,
                ANY,
            ]
            + extra_in,
            out_specs=[
                pl.BlockSpec((images, D), lambda s, own: (0, part(s))),
                vmem,
                pl.BlockSpec((seq, D), lambda s, own: (late(s), 0)),
                vmem,
                vmem,
                vmem,
                vmem,
            ]
            + extra_out,
            scratch_shapes=[
                pltpu.VMEM((3, HEADS, HD, rows), BF16),
                pltpu.VMEM((rows, D), BF16),
                pltpu.VMEM((HEADS, HD, rows), BF16),
                pltpu.VMEM((seq, D), BF16),
                pltpu.VMEM((8, D), F32),
                pltpu.VMEM((rows, D), F32),
                pltpu.VMEM((HEADS, seq, seq), BF16),
                pltpu.VMEM((rows, D), F32),
                pltpu.VMEM((16, D), F32),
                dma,
                dma,
                dma,
                dma,
            ]
            + extra_scratch,
        ),
        out_shape=[
            jax.ShapeDtypeStruct((images, 3 * D), F32),
            jax.ShapeDtypeStruct((HEADS * 1024 // BUCKETS, BUCKETS), F32),
            jax.ShapeDtypeStruct((rows, D), F32),
            jax.ShapeDtypeStruct((16, D), F32),
            jax.ShapeDtypeStruct((seq, D), F32),
            jax.ShapeDtypeStruct((8, D), F32),
            jax.ShapeDtypeStruct((seq, D), BF16),
        ]
        + extra_shape,
        compiler_params=params(collective_id=5, has_side_effects=True),
        cost_estimate=cost(30 * 10**9, 8 * 10**7),
        name="back_core",
    )(
        own, att, shaped_t, gathered, qkv, bias, lse,
        index_t.reshape(seq // REL_ROWS, 1, REL_ROWS * seq), tok, mod, perm, back_own, back_peer, attn, cot,
        front_sums, gate, send, gate, *reduced,
    )


CHUNKS = 3


def collect_body(nw, nn, nm, seq, images, direct, shared_rows, red_ref, time_ref, rows_ref, b_one_ref, rel_ref, keep_mod, perm_ref, *rest):
    if direct:
        done_ref, mlp_ref, emb_ref, silu_ref = rest[:4]
        rest = rest[4:]
    keep_hbm, mine_hbm, branch_hbm = rest[:3]
    rest = rest[3:]
    if direct:
        att_out, mlp_out, ada_out, norm_out, rel_out, more_out, bias_out = rest[:7]
        final_ref, small_out, out_ref, img_out, slots, ss, sr = rest[7:14]
        rest = rest[14:]
    else:
        img_out, small_out, final_ref = rest[:3]
        rest = rest[3:]
    (from_z, gath, sc, sx, sz, keep, mine, branch,
     zs, zr, ys, yr, ics, icr, ixs, ixr, izs, izr, tcs, tcr, txs, txr, tzs, tzr, ms) = rest
    w, n, m = position()
    nlo, nhi, groups = (2, nn // 2, nw * nn)
    c, x = (lax.rem(n, nlo), lax.div(n, nlo))
    slot = (c * nhi + x) * nw + w
    width = D // CHUNKS
    first_at = pl.multiple_of((1 - m) * 3 * D, 128)
    later_at = (1 - m) * 2 * D + m * D
    sibling = (w, x * nlo + 1 - c, m)
    twin = (w, n, 1 - m)

    def along_x(k):
        there = lax.rem(x + k, nhi)
        return (there, (w, there * nlo + c, m))

    def along_z(k):
        there = lax.rem(w + k, nw)
        return (there, (there, n, m))

    if direct:
        ask_all(nw, nn, nm)
    else:
        greet_group(nw, nn, True)

    def cols(k):
        return pl.ds(pl.multiple_of(later_at + k * width, 128), width)

    def hop_z(k, d):
        there, device = along_z(d)
        return remote(
            red_ref.at[there, :, pl.ds(k * width, width)], from_z.at[k, d - 1], zs.at[k, d - 1], zr.at[k, d - 1], device
        )

    def start_z(k):
        if direct:
            for d in range(1, nw):
                hop_z(k, d).start()

    def hop_y(k):
        at = pl.ds(first_at, D) if k == CHUNKS else cols(k)
        return remote(out_ref.at[:, at], out_ref.at[:, at], ys.at[k], yr.at[k], twin)

    places = ((keep_hbm, keep), (mine_hbm, mine), (branch_hbm, branch))
    loads = [pltpu.make_async_copy(a, b, ms.at[i]) for i, (a, b) in enumerate(places)]
    for copy in loads:
        copy.start()

    def image_rows():
        back = rows_ref[...]
        gath[slot, :, 0 : 3 * D] = time_ref[...]
        for i in range(images):
            for q in range(6):
                gath[slot, i : i + 1, (3 + q) * D : (4 + q) * D] = back[i * 6 + q : i * 6 + q + 1]
        return back

    def small_rows(back):
        mine_small = sc.at[c]
        count = rel_ref.shape[0]
        mine_small[0:count] = rel_ref[...]
        mine_small[count:] = jnp.zeros((SMALL_ROWS - count, 128), F32)
        at = count
        for row in (back[images * 6 : images * 6 + 1], back[images * 6 + 1 : images * 6 + 2], b_one_ref[...]):
            for j in range(row.shape[1] // 128):
                mine_small[at : at + 1] = row[:, j * 128 : (j + 1) * 128]
                at += 1

    img_z = []
    for d in range(1, nw):
        there, device = along_z(d)
        img_z.append(remote(gath.at[slot], gath.at[slot], izs.at[d - 1], izr.at[d - 1], device))
    mine_x = pl.ds((c * nhi + x) * nw, nw)
    img_x = []
    for d in range(1, nhi):
        there, device = along_x(d)
        img_x.append(remote(gath.at[mine_x], gath.at[mine_x], ixs.at[d - 1], ixr.at[d - 1], device))
    mine_c = pl.ds(c * nhi * nw, nhi * nw)
    img_c = remote(gath.at[mine_c], gath.at[mine_c], ics, icr, sibling)
    small_c = remote(sc.at[c], sc.at[c], tcs, tcr, sibling)
    small_x = []
    for d in range(1, nhi):
        there, device = along_x(d)
        small_x.append(remote(sx.at[x], sx.at[x], txs.at[d - 1], txr.at[d - 1], device))
    small_z = []
    for d in range(1, nw):
        there, device = along_z(d)
        small_z.append(remote(sz.at[w], sz.at[w], tzs.at[d - 1], tzr.at[d - 1], device))

    def stage_c(k):
        if not direct:
            return
        for d in range(1, nw):
            hop_z(k, d).wait()
        total = red_ref[w, :, k * width : (k + 1) * width].astype(F32)
        for d in range(1, nw):
            total = total + from_z[k, d - 1].astype(F32)
        out_ref[:, cols(k)] = total.astype(BF16)
        hop_y(k).start()

    back = image_rows()
    small_rows(back)
    if direct:
        pl.semaphore_wait(pltpu.get_barrier_semaphore(), groups * nm - 1)
    for hop in img_z:
        hop.start()
    small_c.start()
    if direct:
        out_ref[:, pl.ds(first_at, D)] = done_ref[...]
        hop_y(CHUNKS).start()
        mlp_sq = mlp_rows(mlp_ref, mlp_out)
    small_c.wait()
    sx[x] = sc[0] + sc[1]
    for hop in small_x:
        hop.start()
    for hop in img_z:
        hop.wait()
    for hop in img_x:
        hop.start()
    start_z(0)
    start_z(1)
    for hop in small_x:
        hop.wait()
    total = sx[0]
    for k in range(1, nhi):
        total = total + sx[k]
    sz[w] = total
    for hop in small_z:
        hop.start()
    start_z(2)
    for copy in loads:
        copy.wait()
    summed = mine[...] + branch[...].astype(F32) + keep_mod[7:8]
    final = (keep[...] + keep_mod[5:6] * summed).astype(BF16)
    final_ref[...] = mm(final, perm_ref[...], NT).astype(BF16)
    stage_c(0)
    for hop in img_x:
        hop.wait()
    img_c.start()
    if direct:
        hop_y(CHUNKS).wait()
        att_sq = space_rows(out_ref, perm_ref, att_out, True, False)
    stage_c(1)
    img_c.wait()
    for g in range(groups):
        img_out[2 * g : 2 * g + 2, :] = gath[g]
    if direct:
        att_sq = att_sq + image_weights(img_out, emb_ref, silu_ref, att_out, ada_out)
    stage_c(2)
    for hop in small_z:
        hop.wait()
    total = sz[0]
    for k in range(1, nw):
        total = total + sz[k]
    small_out[...] = total
    if direct:
        count = rel_out.shape[0]
        rel_out[...] = total[0:count]
        more_out[...] = total[count:shared_rows]
        bias_out[...] = total[shared_rows : shared_rows + bias_out.shape[0]]
        for k in range(CHUNKS):
            hop_y(k).wait()
        att_sq = att_sq + space_rows(out_ref, perm_ref, att_out, False, True)
        norm_of(att_sq, mlp_sq, small_out, ada_out, shared_rows, norm_out, slots, ss, sr, nw, nn, nm)


SMALL_ROWS = 168


def collect(red, time_grad, line, b_one, rel, keep_mod, perm, keep, mine, branch, extra, seq, images, shared_rows, nw, nn, nm):
    groups = nw * nn
    count = groups * nm
    nhi = nn // 2
    img_width = 9 * D
    direct = len(extra) > 0
    blk = D // groups
    half = b_one.shape[1]
    width = D // CHUNKS
    vmem = pl.BlockSpec(memory_space=pltpu.VMEM)
    dma = pltpu.SemaphoreType.DMA
    hi, wi = (max(nhi - 1, 1), max(nw - 1, 1))
    many = dma((CHUNKS + 1,))
    small = jax.ShapeDtypeStruct((SMALL_ROWS, 128), F32)
    final = jax.ShapeDtypeStruct((seq, D), BF16)
    if direct:
        out_shape = [
            jax.ShapeDtypeStruct((blk, 13 * D), F32),
            jax.ShapeDtypeStruct((blk, 2, half), F32),
            jax.ShapeDtypeStruct((1, 6 * D), F32),
            jax.ShapeDtypeStruct((1, 1), F32),
            jax.ShapeDtypeStruct(rel.shape, F32),
            jax.ShapeDtypeStruct((shared_rows - rel.shape[0], 128), F32),
            jax.ShapeDtypeStruct((half // 128, 128), F32),
            final,
        ]
        ahead = [
            pltpu.VMEM((SMALL_ROWS, 128), F32),
            pltpu.VMEM((blk, ATT), BF16),
            pltpu.VMEM((2 * groups, img_width), F32),
            pltpu.VMEM((count, 8, 128), F32),
            dma((count,)),
            dma((count,)),
        ]
    else:
        out_shape = [jax.ShapeDtypeStruct((2 * groups, img_width), F32), small, final]
        ahead = []
    return pl.pallas_call(
        partial(collect_body, nw, nn, nm, seq, images, direct, shared_rows),
        in_specs=[vmem] * (7 + len(extra)) + [ANY] * 3,
        out_specs=[vmem] * len(out_shape),
        out_shape=out_shape,
        scratch_shapes=ahead
        + [
            pltpu.VMEM((CHUNKS, wi, blk, width), BF16),
            pltpu.VMEM((groups, 2, img_width), F32),
            pltpu.VMEM((2, SMALL_ROWS, 128), F32),
            pltpu.VMEM((nhi, SMALL_ROWS, 128), F32),
            pltpu.VMEM((nw, SMALL_ROWS, 128), F32),
            pltpu.VMEM((seq, D), F32),
            pltpu.VMEM((seq, D), F32),
            pltpu.VMEM((seq, D), BF16),
            dma((CHUNKS, wi)), dma((CHUNKS, wi)), many, many,
            dma, dma, dma((hi,)), dma((hi,)), dma((wi,)), dma((wi,)),
            dma, dma, dma((hi,)), dma((hi,)), dma((wi,)), dma((wi,)),
            dma((3,)),
        ],
        compiler_params=params(collective_id=2, has_side_effects=True),
        cost_estimate=cost(10**9, 3 * 10**7),
        name="collect",
    )(
        red, time_grad, line, b_one, rel, keep_mod, perm, *extra, keep, mine, branch,
    )


def who_is(k, nw, nn, nm):
    w, n, m = position()
    count = nw * nn * nm
    other = lax.rem((w * nn + n) * nm + m + k, count)
    pair = lax.div(other, nm)
    return (lax.div(pair, nn), lax.rem(pair, nn), lax.rem(other, nm))


def ask_all(nw, nn, nm):
    bar = pltpu.get_barrier_semaphore()
    count = nw * nn * nm

    def ask(k, carry):
        pl.semaphore_signal(bar, inc=1, device_id=who_is(k, nw, nn, nm), device_id_type=MESH)
        return carry

    lax.fori_loop(1, count, ask, 0)


def greet_all(nw, nn, nm):
    ask_all(nw, nn, nm)
    pl.semaphore_wait(pltpu.get_barrier_semaphore(), nw * nn * nm - 1)


def tally(values):
    return jnp.sum(jnp.sum(values * values, axis=0, keepdims=True), axis=1, keepdims=True)


def mlp_rows(mlp_ref, mlp_out):
    total = jnp.zeros((1, 1), F32)
    for f in range(mlp_ref.shape[1] // (2 * TILE)):
        at = slice(f * TILE, (f + 1) * TILE)
        for half in range(2):
            part = mlp_ref[:, (2 * f + half) * TILE : (2 * f + half + 1) * TILE].astype(F32)
            mlp_out[:, half, at] = part
            total = total + tally(part)
    return total


def image_weights(img_ref, emb_ref, silu_ref, att_out, ada_out):
    def product(rows, values):
        return mm(jnp.concatenate([rows] * 3, axis=0), jnp.concatenate(exact_parts(values), axis=0), TN)

    part = product(emb_ref[...], img_ref[:, 0 : 3 * D])
    att_out[:, 3 * D : 6 * D] = part
    total = tally(part)
    ada = img_ref[:, 3 * D :]
    ada_out[...] = jnp.sum(ada, axis=0, keepdims=True)
    part = product(silu_ref[...], ada)
    att_out[:, 7 * D :] = part
    return total + tally(part)


def space_rows(att_ref, perm_ref, att_out, early, late):
    total = jnp.zeros((1, 1), F32)
    if early:
        part = att_ref[:, 0:D].astype(F32)
        att_out[:, 0:D] = part
        total = total + tally(part)
        part = mm(att_ref[:, 3 * D :], perm_ref[...], NT)
        att_out[:, 6 * D : 7 * D] = part
        total = total + tally(part)
    if late:
        part = att_ref[:, D : 3 * D].astype(F32)
        att_out[:, D : 3 * D] = part
        total = total + tally(part)
    return total


def norm_of(att_sq, mlp_sq, small_ref, ada_out, shared_rows, norm_out, slots, ss, sr, nw, nn, nm):
    w, n, m = position()
    groups = nw * nn
    count = groups * nm
    mine = (w * nn + n) * nm + m
    small_sq = tally(small_ref[0:shared_rows]) + tally(ada_out[...])
    bias_sq = tally(small_ref[shared_rows:])
    local = mlp_sq + att_sq / nm + small_sq / count + bias_sq / groups
    slots[mine] = jnp.broadcast_to(local, (8, 128))

    def copy_to(k):
        return remote(slots.at[mine], slots.at[mine], ss.at[k], sr.at[k], who_is(k, nw, nn, nm))

    def send(k, carry):
        copy_to(k).start()
        return carry

    def finish(k, carry):
        copy_to(k).wait()
        return carry

    lax.fori_loop(1, count, send, 0)
    lax.fori_loop(1, count, finish, 0)
    norm_out[...] = jnp.sqrt(jnp.sum(slots[...], axis=0))[0:1, 0:1]


def norm_body(nw, nn, nm, shared_rows, att_ref, mlp_ref, img_ref, emb_ref, silu_ref, small_ref, perm_ref,
              att_out, mlp_out, ada_out, norm_out, slots, ss, sr):
    greet_all(nw, nn, nm)
    mlp_sq = mlp_rows(mlp_ref, mlp_out)
    att_sq = image_weights(img_ref, emb_ref, silu_ref, att_out, ada_out)
    att_sq = att_sq + space_rows(att_ref, perm_ref, att_out, True, True)
    norm_of(att_sq, mlp_sq, small_ref, ada_out, shared_rows, norm_out, slots, ss, sr, nw, nn, nm)


def collect_norm(att, mlp, imgs, emb, silu, small, perm, shared_rows, nw, nn, nm):
    rows = att.shape[0]
    half = mlp.shape[1] // 2
    count = nw * nn * nm
    dma = pltpu.SemaphoreType.DMA
    return pl.pallas_call(
        partial(norm_body, nw, nn, nm, shared_rows),
        out_shape=[
            jax.ShapeDtypeStruct((rows, 13 * D), F32),
            jax.ShapeDtypeStruct((rows, 2, half), F32),
            jax.ShapeDtypeStruct((1, 6 * D), F32),
            jax.ShapeDtypeStruct((1, 1), F32),
        ],
        scratch_shapes=[pltpu.VMEM((count, 8, 128), F32), dma((count,)), dma((count,))],
        compiler_params=params(collective_id=3, has_side_effects=True),
        cost_estimate=cost(10**8, 10**7),
        name="collect_norm",
    )(att, mlp, imgs, emb, silu, small, perm)


def on_device(
    tokens,
    timesteps,
    owners,
    rel_index,
    cotangent,
    att_master,
    att_moment,
    att_second,
    mlp_master,
    mlp_moment,
    mlp_second,
    small_master,
    small_moment,
    small_second,
    bias_master,
    bias_moment,
    bias_second,
):
    groups = owners.shape[0]
    rows_blk = att_master.shape[0]
    half_ff = mlp_master.shape[2]
    images = timesteps.shape[0]
    tok_rows = tokens.shape[0]
    half_rows = cotangent.shape[0]
    seq_len = tok_rows // images
    nw, nn, nm = (lax.axis_size("wide"), lax.axis_size("narrow"), lax.axis_size("mlp"))
    mlp_at = lax.axis_index("mlp")
    mine = lax.axis_index(GRID)
    moved = rows_blk == HD
    swap = [(i, nm - 1 - i) for i in range(nm)]

    place = (owners[:, None] * rows_blk + jnp.arange(rows_blk)[None, :]).reshape(D)
    pick = (place[:, None] == (mine * rows_blk + jnp.arange(rows_blk))[None, :]).astype(BF16)

    packed, perm = pack_weights(owners, att_master, mlp_master)
    perm_f = perm.astype(F32)
    gathered = lax.all_gather(packed, GRID, axis=0, tiled=True)

    time_emb = time_embed(timesteps)
    emb_rows = jnp.concatenate(
        [time_emb, jax.nn.silu(time_emb), jnp.zeros((8 - 2 * images, D), F32)], axis=0
    ).astype(BF16)
    summed, emb_mine, silu_mine, cot_all = modul_exchange(
        emb_rows, att_master, pick, cotangent, nw, nn
    )
    time_part = summed[:, 0 : 3 * D]
    offset = NREL * HEADS
    table_t = jnp.pad(small_master[0:offset].reshape(NREL, HEADS).T, ((0, 0), (0, 1024 - NREL)))
    b_ada = small_master[offset : offset + 6 * D]
    b_rest = small_master[offset + 6 * D : offset + 8 * D].reshape(1, 2, D)
    modulation = (summed[:, 3 * D :] + b_ada).reshape(images, 6, D)
    mod = jnp.concatenate([modulation, jnp.broadcast_to(b_rest, (images, 2, D))], axis=1)
    mod = mm_exact(mod.reshape(images * 8, D), perm_f).reshape(images, 8, D)
    index_t = rel_index.T
    bias = rel_bias(index_t, table_t.reshape(HEADS, 1, 1024), seq_len)

    tok, shaped, shaped_t, cot, grad_branch, front_sums = front(
        tokens, cot_all, perm, mod, seq_len, images
    )
    heads_at = owners if moved else jnp.arange(HEADS, dtype=jnp.int32)
    qkv, attended, lse = attend_fwd(heads_at, shaped, gathered, time_part, bias, seq_len, images)
    attended = attended.reshape(D, tok_rows)
    if not moved:
        attended = mm(perm, attended, TN).astype(BF16)
    attn_out, shaped_two = middle(attended, gathered, tok, mod, seq_len, images)
    made = mlp_core(
        shaped_two, grad_branch, gathered, bias_master.reshape(1, half_ff), cot, seq_len, nw, nn
    )
    mlp_term, branch_mine, branch_send, gate_own, b_one_grad, back_own, back_peer = made[:7]
    reduced = (mlp_term, made[7]) if len(made) == 8 else ()

    done = back_core(
        heads_at,
        attended,
        shaped_t,
        gathered,
        qkv,
        bias,
        lse,
        index_t,
        tok,
        mod,
        perm,
        back_own,
        back_peer,
        attn_out,
        cot,
        front_sums,
        branch_send,
        gate_own,
        reduced,
        seq_len,
        images,
        nw,
        nn,
        moved,
    )
    time_grad, rel_sum, input_grad, line, keep, keep_mod, branch_peer = done[:7]
    rel_rows = HEADS * 1024 // BUCKETS
    shared_rows = rel_rows + 2 * D // 128
    direct = len(done) == 10
    if direct:
        mlp_part, part_done, red = done[7:]
        extra = (part_done, mlp_part, emb_mine, silu_mine)
    else:
        mlp_part = lax.psum_scatter(mlp_term, GRID, scatter_dimension=0, tiled=True)
        red = jnp.zeros((1, 1, 1), BF16)
        extra = ()
    shared = collect(
        red, time_grad, line, b_one_grad, rel_sum, keep_mod, perm, keep, branch_mine, branch_peer, extra, seq_len, images, shared_rows, nw, nn, nm,
    )
    if direct:
        att_grad, mlp_grad, b_ada_grad, norm, rel_all, rest_all, bias_all, output = shared
    else:
        imgs_all, small_all, output = shared
        att_part = lax.psum_scatter(done[7], GRID, scatter_dimension=0, tiled=True)
        att_grad, mlp_grad, b_ada_grad, norm = collect_norm(
            att_part, mlp_part, imgs_all, emb_mine, silu_mine, small_all, perm, shared_rows, nw, nn, nm
        )
        rel_all = small_all[0:rel_rows]
        rest_all = small_all[rel_rows:shared_rows]
        bias_all = small_all[shared_rows : shared_rows + half_ff // 128]

    grad_norm = norm[0, 0]
    clip_scale = jnp.minimum(1.0, 1.0 / (grad_norm + 1e-06))
    rel_grad = rel_all.reshape(-1, HEADS, BUCKETS).transpose(0, 2, 1).reshape(-1)[0:offset]
    small_grad = jnp.concatenate(
        [rel_grad, b_ada_grad.reshape(-1), rest_all.reshape(-1)]
    )
    bias_grad = bias_all.reshape(-1)
    att_new, att_mom_new, att_sec_new = adam_update(
        att_master, att_moment, att_second, att_grad, clip_scale
    )
    mlp_new, mlp_mom_new, mlp_sec_new = adam_update(
        mlp_master, mlp_moment, mlp_second, mlp_grad, clip_scale
    )
    small_new, small_mom_new, small_sec_new = adam_update(
        small_master, small_moment, small_second, small_grad, clip_scale
    )
    bias_new, bias_mom_new, bias_sec_new = adam_update(
        bias_master, bias_moment, bias_second, bias_grad, clip_scale
    )
    return (
        output,
        input_grad,
        att_new,
        att_mom_new,
        att_sec_new,
        mlp_new,
        mlp_mom_new,
        mlp_sec_new,
        small_new,
        small_mom_new,
        small_sec_new,
        bias_new,
        bias_mom_new,
        bias_sec_new,
        att_new.astype(BF16),
        mlp_new.astype(BF16),
        grad_norm,
    )


def solution(mesh):
    rows = P(GRID, None)
    cube = P(GRID, None, "mlp")
    return jax.shard_map(
        on_device,
        mesh=mesh,
        in_specs=(
            rows,
            P(GRID),
            P(),
            P(),
            P(("wide", "narrow", "mlp"), None),
            rows,
            rows,
            rows,
            cube,
            cube,
            cube,
            P(),
            P(),
            P(),
            P("mlp"),
            P("mlp"),
            P("mlp"),
        ),
        out_specs=(
            P(("wide", "narrow", "mlp"), None),
            rows,
            rows,
            rows,
            rows,
            cube,
            cube,
            cube,
            P(),
            P(),
            P(),
            P("mlp"),
            P("mlp"),
            P("mlp"),
            rows,
            cube,
            P(),
        ),
        check_vma=False,
    )
```
